32 devices in a mesh: ctx: 8 (over y, x, core), fsdp: 4 (over z).
Axes of the slice: x: 2, y: 2, z: 4, core: 2. Of those that a mesh axis runs over, the one named last changes fastest.
Arguments:
- inputs: bfloat16 [4, 3072, 1024], P('fsdp', 'ctx'), may hold values from -6 to 6
- cotangent: bfloat16 [4, 3072, 1024], P('fsdp', 'ctx'), may hold values from -6 to 6
- lengths: int32 [4, 6], P('fsdp'), may hold values from 1 to 1536, 2688 in all within a row
- piece_route: int32 [4, 8, 8], P('fsdp', 'ctx'), may hold values from 0 to 7, each once within a row
- gain_one: bfloat16 [1024], P('fsdp'), may hold values from 0.5 to 1.5
- qkv_weight: bfloat16 [1024, 3072], P('fsdp'), may hold values from -0.1875 to 0.1875
- attn_out: bfloat16 [1024, 1024], P('fsdp'), may hold values from -1.5 to 1.5
- gain_two: bfloat16 [1024], P('fsdp'), may hold values from 0.5 to 1.5
- geglu_in: bfloat16 [1024, 5248], P('fsdp'), may hold values from -0.1875 to 0.1875
- geglu_out: bfloat16 [2624, 1024], P('fsdp'), may hold values from -0.15625 to 0.15625
Outputs:
- block_out: bfloat16 [4, 3072, 1024], P('fsdp', 'ctx')
- grad_inputs: bfloat16 [4, 3072, 1024], P('fsdp', 'ctx')
- grad_gain_one: float32 [1024], P('fsdp')
- grad_qkv_weight: float32 [1024, 3072], P('fsdp')
- grad_attn_out: float32 [1024, 1024], P('fsdp')
- grad_gain_two: float32 [1024], P('fsdp')
- grad_geglu_in: float32 [1024, 5248], P('fsdp')
- grad_geglu_out: float32 [2624, 1024], P('fsdp')
- rms_stats: float32 [4, 3], P('fsdp')
The draws below stay inside these ranges and needn't reach their ends.
Inputs may be any that keep to these rules, and one draw needn't show every extreme that they name: In each pack the 6 lengths sum to 2688 and the largest is 1536. Each row piece_route[b, s, :] names every index of ctx exactly once.
All inputs are finite; a program needn't handle non-finite values.
Results may differ from the reference program's by a relative error of at most 0.02.
Values may be sent and summed in bfloat16 or wider, within the bound.
A program may use at most 192 MiB of HBM per device.

```python
import math
import jax
import jax.numpy as jnp
import numpy as np
from jax import lax

D = 1024
HEADS = 16
HEAD = 64
FF = 2624
TOK_DEV = 384
NSEQ = 6
BATCHES = 4
PIECE = 48
PACK = 3072
LONGEST = 1536
VALID = 2688
N_CTX = 8


def levels(own_key, shape, cuts, low, largest):
    loudness = 1.0
    for axis_at, blocks in cuts:
        draws = jax.random.uniform(jax.random.fold_in(jax.random.fold_in(own_key, 6), axis_at), (blocks,), jnp.float32, low / len(cuts), largest / len(cuts))
        loudness = loudness * jnp.repeat(jnp.exp(draws), shape[axis_at] // blocks).reshape((-1,) + (1,) * (len(shape) - 1 - axis_at))
    return loudness


def profile(number_of, total, reach, skew):
    weights = [(1 << 20) // math.isqrt(standing ** skew) + 1 for standing in range(2, number_of + 1)]
    rest, counts = total - reach - (number_of - 1), [1] * (number_of - 1)
    while rest > 0:
        free = [i for i in range(number_of - 1) if counts[i] < reach]
        pool, remaining = sum([weights[i] for i in free]), rest
        for i in free:
            more = min(reach - counts[i], max(1, remaining * weights[i] // pool), rest)
            counts[i] = counts[i] + more
            rest = rest - more
    return np.array([reach] + counts)


def ragged_sizes(rng, count, total, reach, skew):
    if count == 2:
        one = jax.random.randint(rng, (), max(1, total - reach), min(reach, total - 1) + 1)
        return jnp.stack([one, total - one])
    sizes = jnp.asarray(profile(count, total, reach, skew), jnp.int32)
    pairs = (count - 1) // 2
    source_of, taker = sizes[1:1 + 2 * pairs:2], sizes[2:2 + 2 * pairs:2]
    margin = jnp.minimum(source_of - 1, reach - taker)
    passed = jax.random.randint(jax.random.fold_in(rng, 1), (pairs,), 0, 1 << 20) % (margin + 1)
    sizes = sizes.at[1:1 + 2 * pairs:2].set(source_of - passed).at[2:2 + 2 * pairs:2].set(taker + passed)
    return sizes[jax.random.permutation(jax.random.fold_in(rng, 2), count)]


def noise(rng, dims, width, limit, cuts=(), kind=jnp.bfloat16):
    array = width * jax.random.normal(rng, dims, jnp.float32)
    if cuts:
        array = array * levels(rng, dims, cuts, -0.22, 0.18)
    return jnp.clip(array, -limit, limit).astype(kind)


def setup_inputs(seed: int = 0) -> dict:
    key_of = jax.random.split(jax.random.key(seed), 11)
    return {
        "inputs": noise(key_of[0], (BATCHES, PACK, D), 1.0, 6.0, ((0, 4), (1, 8))),
        "cotangent": noise(key_of[1], (BATCHES, PACK, D), 1.0, 6.0, ((0, 4), (1, 8))),
        "lengths": jax.vmap(lambda own: ragged_sizes(own, NSEQ, VALID, LONGEST, 2))(jax.random.split(key_of[2], BATCHES)).reshape((BATCHES, NSEQ)).astype(jnp.int32),
        "piece_route": jax.vmap(lambda own: jax.random.permutation(own, N_CTX))(jax.random.split(key_of[3], BATCHES * N_CTX)).reshape((BATCHES, N_CTX, N_CTX)).astype(jnp.int32),
        "gain_one": jnp.clip(1.0 + 0.1 * jax.random.normal(key_of[4], (D,), jnp.float32), 0.5, 1.5).astype(jnp.bfloat16),
        "qkv_weight": noise(key_of[5], (D, 3 * D), D ** -0.5, 0.1875, ((0, 4),)),
        "attn_out": noise(key_of[6], (D, D), (max(1, D // 64)) ** -0.5, 1.5, ((0, 4),)),
        "gain_two": jnp.clip(1.0 + 0.1 * jax.random.normal(key_of[7], (D,), jnp.float32), 0.5, 1.5).astype(jnp.bfloat16),
        "geglu_in": noise(key_of[8], (D, 2 * FF), D ** -0.5, 0.1875, ((0, 4),)),
        "geglu_out": noise(key_of[9], (FF, D), (FF // 2) ** -0.5, 0.15625, ((0, 4),)),
    }


rope_base = 160000.0
norm_eps = 1e-05
masked_score = -1e+30

@jax.custom_vjp
def low(v):
    return lax.optimization_barrier(v.astype(jnp.bfloat16)).astype(jnp.float32)

@jax.custom_vjp
def low_back(v):
    return v

def low_keep(v):
    return (low(v), None)

def low_pass(kept, grad):
    return (grad,)

def back_keep(v):
    return (v, None)

def back_low(kept, grad):
    return (low(grad),)
low.defvjp(low_keep, low_pass)
low_back.defvjp(back_keep, back_low)

def layer_norm(rows_in, gain_vec):
    row_mean = lax.optimization_barrier(jnp.mean(rows_in, axis=-1, keepdims=True))
    centred = rows_in - row_mean
    variance = lax.optimization_barrier(jnp.mean(centred * centred, axis=-1, keepdims=True))
    return centred * lax.rsqrt(variance + norm_eps) * gain_vec

def rotate(projected, places, head_count):
    row_count = projected.shape[0]
    head_width = projected.shape[1] // head_count
    half_width = head_width // 2
    inverse_freq = rope_base ** (-2.0 * jnp.arange(half_width, dtype=jnp.float32) / head_width)
    angles = places.astype(jnp.float32)[:, None] * inverse_freq[None, :]
    cosine = jnp.concatenate([jnp.cos(angles), jnp.cos(angles)], axis=1)[:, None, :]
    sine_table = jnp.concatenate([jnp.sin(angles), jnp.sin(angles)], axis=1)[:, None, :]
    by_head = projected.reshape(row_count, head_count, head_width)
    turned = jnp.concatenate([-by_head[..., half_width:], by_head[..., :half_width]], axis=-1)
    return (by_head * cosine + turned * sine_table).reshape(row_count, head_count * head_width)

def describe(places, lengths_row):
    seq_ends = jnp.cumsum(lengths_row).astype(jnp.int32)
    past_end = (places[:, None] >= seq_ends[None, :]).astype(jnp.int32)
    segment = lax.optimization_barrier(jnp.sum(past_end, axis=1)).astype(jnp.int32)
    offset = (places - lax.optimization_barrier(jnp.sum(past_end * lengths_row[None, :], axis=1))).astype(jnp.int32)
    is_valid = places < seq_ends[-1]
    return (segment, offset, is_valid)

def attend_rows(block_in, key_heads, value_heads, key_segment, key_valid):
    query_heads, query_segment, query_valid = block_in
    score_scale = 1.0 / math.sqrt(query_heads.shape[-1])
    scores = low_back(jnp.einsum('qhe,khe->hqk', query_heads, key_heads, precision=lax.Precision.HIGHEST) * score_scale)
    allowed = (query_segment[:, None] == key_segment[None, :]) & query_valid[:, None] & key_valid[None, :]
    masked = jnp.where(allowed[None], scores, masked_score)
    running_top = lax.optimization_barrier(jnp.max(masked, axis=-1, keepdims=True))
    weight_sum = lax.optimization_barrier(jnp.sum(jnp.where(allowed[None], jnp.exp(masked - running_top), 0.0), axis=-1, keepdims=True))
    padding_one = jnp.where(query_valid, 0.0, 1.0)[None, :, None]
    log_total = running_top + jnp.log(weight_sum + padding_one)
    attn_probs = jnp.where(allowed[None], jnp.exp(masked - log_total), 0.0)
    attended = jnp.einsum('hqk,khe->qhe', low(attn_probs), value_heads, precision=lax.Precision.HIGHEST)
    return attended.reshape(attended.shape[0], -1)

def reference(inputs, cotangent, lengths, piece_route, gain_one, qkv_weight, attn_out, gain_two, geglu_in, geglu_out):
    params = tuple((param.astype(jnp.float32) for param in (gain_one, qkv_weight, attn_out, gain_two, geglu_in, geglu_out)))
    stored = jnp.arange(PACK, dtype=jnp.int32)
    shard_of = (stored // TOK_DEV).astype(jnp.int32)
    slot_of = (stored % TOK_DEV // PIECE).astype(jnp.int32)
    within = (stored % PIECE).astype(jnp.int32)
    block_rows = math.gcd(PACK, 512)
    block_count = PACK // block_rows
    highest = lax.Precision.HIGHEST

    def one_pack(so_far, batch_in):
        rows_in, grad_rows, lengths_row, route_row = batch_in
        places = (route_row[shard_of, slot_of] * TOK_DEV + shard_of * PIECE + within).astype(jnp.int32)
        segment, offset, is_valid = describe(places, lengths_row)

        def forward(residual, gain_attn, qkv_full, attn_full, gain_mlp, in_full, out_full):
            act_attn = low(layer_norm(residual, gain_attn))
            projected = low_back(jnp.dot(act_attn, qkv_full, precision=highest))
            queries = low(rotate(projected[:, :D], offset, HEADS)).reshape(PACK, HEADS, HEAD)
            key_heads = low(rotate(projected[:, D:2 * D], offset, HEADS)).reshape(PACK, HEADS, HEAD)
            value_heads = low(projected[:, 2 * D:]).reshape(PACK, HEADS, HEAD)

            def one_block(block_in):
                return attend_rows(block_in, key_heads, value_heads, segment, is_valid)
            attended = lax.map(jax.checkpoint(one_block), (queries.reshape(block_count, block_rows, HEADS, HEAD), segment.reshape(block_count, block_rows), is_valid.reshape(block_count, block_rows)))
            attended = attended.reshape(PACK, D)
            attn_low = low(low_back(attended))
            branch_attn = low_back(jnp.dot(attn_low, attn_full, precision=highest))
            middle = residual + branch_attn
            act_mlp = low(layer_norm(middle, gain_mlp))
            up_both = low_back(jnp.dot(act_mlp, in_full, precision=highest))
            hidden = low(jax.nn.gelu(up_both[:, :FF], approximate=False) * up_both[:, FF:])
            branch_mlp = low_back(jnp.dot(hidden, out_full, precision=highest))
            final_rows = jnp.where(is_valid[:, None], middle + branch_mlp, 0.0)
            square_sums = jnp.stack([jnp.sum(final_rows * final_rows), jnp.sum(jnp.where(is_valid[:, None], branch_attn * branch_attn, 0.0)), jnp.sum(jnp.where(is_valid[:, None], branch_mlp * branch_mlp, 0.0))])
            return (final_rows, square_sums)
        final_rows, pullback, square_sums = jax.vjp(forward, rows_in.astype(jnp.float32), *params, has_aux=True)
        grads = pullback(grad_rows.astype(jnp.float32))
        summed = tuple((before + grad_part for before, grad_part in zip(so_far, grads[1:])))
        valid_count = jnp.sum(lengths_row).astype(jnp.float32)
        stats = jnp.sqrt(square_sums / (valid_count * D))
        return (summed, (final_rows.astype(jnp.bfloat16), grads[0].astype(jnp.bfloat16), stats))
    zero_grads = tuple((jnp.zeros(param.shape, jnp.float32) for param in params))
    totals, outs = lax.scan(one_pack, zero_grads, (inputs, cotangent, lengths, piece_route))
    block_out, grad_inputs, rms_stats = outs
    return (block_out, grad_inputs, totals[0], totals[1], totals[2], totals[3], totals[4], totals[5], rms_stats)
```

```python
import functools
import math
import jax
import jax.numpy as jnp
from jax import lax
from jax.experimental import pallas as pl
from jax.experimental.pallas import tpu as pltpu
from jax.sharding import PartitionSpec as P

HEAD_WIDTH = 64
norm_eps = 1e-05
masked_score = -1e30


def head_stack(rows_in, head_count):
    if head_count == 1:
        return rows_in
    lane_head = lax.broadcasted_iota(jnp.int32, rows_in.shape, 1) // HEAD_WIDTH
    zero = jnp.zeros_like(rows_in)
    return jnp.concatenate(
        [jnp.where(lane_head == h, rows_in, zero) for h in range(head_count)], axis=0
    )


def head_pick(stacked_t, head_count, block):
    return jnp.concatenate(
        [
            stacked_t[h * HEAD_WIDTH : (h + 1) * HEAD_WIDTH, h * block : (h + 1) * block]
            for h in range(head_count)
        ],
        axis=0,
    ).T


NT = (((1,), (1,)), ((), ()))


def forward_kernel(
    head_count, block_q, block_k, low_ref, high_ref, begin_ref, end_ref, qkv_ref, out_ref, log_ref, turned_ref
):
    width = out_ref.shape[1]
    step = pl.program_id(0)

    @pl.when(step == 0)
    def prepare():
        turned_ref[...] = qkv_ref[:, 2 * width :].astype(jnp.float32).T.astype(jnp.bfloat16)

    rows = pl.ds(pl.multiple_of(step * block_q, block_q), block_q)
    scale = 1.0 / math.sqrt(HEAD_WIDTH)
    stacked = head_stack(qkv_ref[rows, :width] * jnp.asarray(scale, jnp.bfloat16), head_count)
    begin = jnp.concatenate([begin_ref[:, rows]] * head_count, axis=1)
    end = jnp.concatenate([end_ref[:, rows]] * head_count, axis=1)

    def body(index, carried):
        top, total, acc = carried
        first = pl.multiple_of(index * block_k, block_k)
        keys = qkv_ref[pl.ds(first, block_k), width : 2 * width]
        scores = lax.dot_general(keys, stacked, NT, preferred_element_type=jnp.float32)
        place = first + lax.broadcasted_iota(jnp.int32, scores.shape, 0)
        scores = jnp.where((place >= begin) & (place < end), scores, masked_score)
        new_top = jnp.maximum(top, jnp.max(scores, axis=0, keepdims=True))
        fresh = jnp.exp(scores - new_top)
        fade = jnp.exp(top - new_top)
        total = total * fade + jnp.sum(fresh, axis=0, keepdims=True)
        acc = acc * fade + jnp.dot(
            turned_ref[:, pl.ds(first, block_k)],
            fresh.astype(jnp.bfloat16),
            preferred_element_type=jnp.float32,
        )
        return (new_top, total, acc)

    lanes = head_count * block_q
    top, total, acc = lax.fori_loop(
        low_ref[step],
        high_ref[step],
        body,
        (
            jnp.full((1, lanes), masked_score, jnp.float32),
            jnp.zeros((1, lanes), jnp.float32),
            jnp.zeros((width, lanes), jnp.float32),
        ),
    )
    valid = end > begin
    safe = jnp.where(valid, total, 1.0)
    acc = jnp.where(valid, acc / safe, 0.0)
    log_total = jnp.where(valid, top + jnp.log(safe), 0.0)
    out_ref[...] = head_pick(acc, head_count, block_q)
    log_ref[0] = log_total


def attention_forward(qkv, begin, end, low, high, head_count, block_q, block_k):
    tokens = qkv.shape[0]
    width = head_count * HEAD_WIDTH
    steps = tokens // block_q
    whole = lambda shape: pl.BlockSpec(shape, lambda i, *_: (0,) * len(shape))
    pairs = tokens * tokens // 4 * head_count
    return pl.pallas_call(
        functools.partial(forward_kernel, head_count, block_q, block_k),
        out_shape=(
            jax.ShapeDtypeStruct((tokens, width), jnp.float32),
            jax.ShapeDtypeStruct((steps, 1, head_count * block_q), jnp.float32),
        ),
        grid_spec=pltpu.PrefetchScalarGridSpec(
            num_scalar_prefetch=2,
            grid=(steps,),
            in_specs=[whole((1, tokens)), whole((1, tokens)), whole((tokens, 3 * width))],
            out_specs=(
                pl.BlockSpec((block_q, width), lambda i, *_: (i, 0)),
                pl.BlockSpec((1, 1, head_count * block_q), lambda i, *_: (i, 0, 0)),
            ),
            scratch_shapes=[pltpu.VMEM((width, tokens), jnp.bfloat16)],
        ),
        cost_estimate=pl.CostEstimate(
            flops=pairs * 512, bytes_accessed=tokens * width * 12, transcendentals=pairs
        ),
        name="attention_forward",
    )(low, high, begin, end, qkv)


def turn_back(grads, cosine, sine, head_count):
    half = HEAD_WIDTH // 2
    pieces = []
    for h in range(head_count):
        base = h * HEAD_WIDTH
        pieces += [grads[:, base + half : base + HEAD_WIDTH], grads[:, base : base + half]]
    return grads * cosine + jnp.concatenate(pieces, axis=1) * sine


def backward_kernel(
    head_count,
    block_q,
    block_k,
    low_ref,
    high_ref,
    begin_ref,
    end_ref,
    qkv_ref,
    attended_ref,
    grad_ref,
    log_ref,
    cosine_ref,
    sine_ref,
    out_ref,
    turned_ref,
    key_acc,
    value_acc,
):
    width = attended_ref.shape[1]
    step = pl.program_id(0)

    @pl.when(step == 0)
    def prepare():
        turned_ref[...] = qkv_ref[:, width : 2 * width].astype(jnp.float32).T.astype(jnp.bfloat16)
        key_acc[...] = jnp.zeros_like(key_acc)
        value_acc[...] = jnp.zeros_like(value_acc)

    rows = pl.ds(pl.multiple_of(step * block_q, block_q), block_q)
    scale = 1.0 / math.sqrt(HEAD_WIDTH)
    stacked = head_stack(qkv_ref[rows, :width] * jnp.asarray(scale, jnp.bfloat16), head_count)
    grads = grad_ref[rows, :]
    grad_stacked = head_stack(grads, head_count)
    begin = jnp.concatenate([begin_ref[:, rows]] * head_count, axis=1)
    end = jnp.concatenate([end_ref[:, rows]] * head_count, axis=1)
    product = (grads.astype(jnp.float32) * attended_ref[rows, :]).T
    delta = jnp.concatenate(
        [
            jnp.sum(product[h * HEAD_WIDTH : (h + 1) * HEAD_WIDTH], axis=0, keepdims=True)
            for h in range(head_count)
        ],
        axis=1,
    )
    log_total = log_ref[0]

    def body(index, acc):
        first = pl.multiple_of(index * block_k, block_k)
        span = pl.ds(first, block_k)
        keys = qkv_ref[span, width : 2 * width]
        values = qkv_ref[span, 2 * width :]
        scores = lax.dot_general(keys, stacked, NT, preferred_element_type=jnp.float32)
        grad_probs = lax.dot_general(values, grad_stacked, NT, preferred_element_type=jnp.float32)
        place = first + lax.broadcasted_iota(jnp.int32, scores.shape, 0)
        scores = jnp.where((place >= begin) & (place < end), scores, masked_score)
        probs = jnp.exp(scores - log_total)
        grad_scores = (probs * (grad_probs - delta)).astype(jnp.bfloat16)
        value_acc[span, :] += jnp.dot(
            probs.astype(jnp.bfloat16), grad_stacked, preferred_element_type=jnp.float32
        )
        key_acc[span, :] += jnp.dot(grad_scores, stacked, preferred_element_type=jnp.float32)
        return acc + jnp.dot(
            turned_ref[:, span], grad_scores, preferred_element_type=jnp.float32
        )

    acc = lax.fori_loop(
        low_ref[step],
        high_ref[step],
        body,
        jnp.zeros((width, head_count * block_q), jnp.float32),
    )
    grad_queries = head_pick(acc, head_count, block_q) * scale
    out_ref[rows, :width] = turn_back(
        grad_queries, cosine_ref[rows, :], sine_ref[rows, :], head_count
    ).astype(jnp.bfloat16)

    @pl.when(step == pl.num_programs(0) - 1)
    def finish():
        @pl.loop(0, pl.num_programs(0))
        def each(index):
            span = pl.ds(pl.multiple_of(index * block_q, block_q), block_q)
            out_ref[span, width : 2 * width] = turn_back(
                key_acc[span, :], cosine_ref[span, :], sine_ref[span, :], head_count
            ).astype(jnp.bfloat16)
            out_ref[span, 2 * width :] = value_acc[span, :].astype(jnp.bfloat16)


def attention_backward(
    qkv, attended, grads, log_total, begin, end, low, high, cosine, sine, head_count, block_q, block_k
):
    tokens = qkv.shape[0]
    width = head_count * HEAD_WIDTH
    steps = tokens // block_q
    whole = lambda shape: pl.BlockSpec(shape, lambda i, *_: (0,) * len(shape))
    pairs = tokens * tokens // 4 * head_count
    return pl.pallas_call(
        functools.partial(backward_kernel, head_count, block_q, block_k),
        out_shape=jax.ShapeDtypeStruct((tokens, 3 * width), jnp.bfloat16),
        grid_spec=pltpu.PrefetchScalarGridSpec(
            num_scalar_prefetch=2,
            grid=(steps,),
            in_specs=[
                whole((1, tokens)),
                whole((1, tokens)),
                whole((tokens, 3 * width)),
                whole((tokens, width)),
                whole((tokens, width)),
                pl.BlockSpec((1, 1, head_count * block_q), lambda i, *_: (i, 0, 0)),
                whole((tokens, width)),
                whole((tokens, width)),
            ],
            out_specs=whole((tokens, 3 * width)),
            scratch_shapes=[
                pltpu.VMEM((width, tokens), jnp.bfloat16),
                pltpu.VMEM((tokens, width), jnp.float32),
                pltpu.VMEM((tokens, width), jnp.float32),
            ],
        ),
        cost_estimate=pl.CostEstimate(
            flops=pairs * 1280, bytes_accessed=tokens * width * 30, transcendentals=pairs
        ),
        name="attention_backward",
    )(low, high, begin, end, qkv, attended, grads, log_total, cosine, sine)


def spans(places, lengths_row):
    ends = jnp.cumsum(lengths_row)
    past = (places[:, None] >= ends[None, :]).astype(jnp.int32)
    begin = jnp.sum(past * lengths_row[None, :], axis=1)
    before = (places[:, None] >= (ends - lengths_row)[None, :]).astype(jnp.int32)
    end = jnp.sum(before * lengths_row[None, :], axis=1)
    valid = places < ends[-1]
    return (jnp.where(valid, begin, 0), jnp.where(valid, end, 0), places - begin, valid)


def key_range(begin, end, block_q, block_k):
    begin_blocks = jnp.where(end > begin, begin, jnp.int32(1 << 30)).reshape(-1, block_q)
    high = (jnp.max(end.reshape(-1, block_q), axis=1) + block_k - 1) // block_k
    low = jnp.minimum(jnp.min(begin_blocks, axis=1) // block_k, high)
    return (low, high)


def rotary_tables(offset, head_count):
    half = HEAD_WIDTH // 2
    inverse = 160000.0 ** (-2.0 * jnp.arange(half, dtype=jnp.float32) / HEAD_WIDTH)
    angles = offset.astype(jnp.float32)[:, None] * inverse[None, :]
    cosine, sine = (jnp.cos(angles), jnp.sin(angles))
    return (
        jnp.concatenate([cosine, cosine] * head_count, axis=1),
        jnp.concatenate([sine, -sine] * head_count, axis=1),
    )


def layer_norm(rows_in, gain_vec):
    row_mean = jnp.mean(rows_in, axis=-1, keepdims=True)
    centred = rows_in - row_mean
    variance = jnp.mean(centred * centred, axis=-1, keepdims=True)
    return centred * lax.rsqrt(variance + norm_eps) * gain_vec


def rotate(projected, cosine, sine):
    row_count, width = projected.shape
    half_width = HEAD_WIDTH // 2
    by_head = projected.reshape(row_count, width // HEAD_WIDTH, HEAD_WIDTH)
    turned = jnp.concatenate([by_head[..., half_width:], by_head[..., :half_width]], axis=-1)
    return (by_head * cosine[:, None, :] - turned * sine[:, None, :]).reshape(row_count, width)


def swap(value, axis, bit):
    pairs = [(i, i ^ bit) for i in range(lax.axis_size(axis))]
    return lax.ppermute(value, axis, pairs)


def bit_of(axis, bit):
    return (lax.axis_index(axis) // bit) % 2 == 1


def bits_below(count):
    return [1 << i for i in range(count.bit_length() - 1)]


def reduce_pieces(pieces, labels, order):
    labels = list(labels)
    for axis, bit in order:
        at = labels.index((axis, bit))
        labels.pop(at)
        first = lax.index_in_dim(pieces, 0, at, keepdims=False)
        second = lax.index_in_dim(pieces, 1, at, keepdims=False)
        upper = bit_of(axis, bit)
        arrived = swap(jnp.where(upper, first, second), axis, bit)
        kept = jnp.where(upper, second, first)
        pieces = (kept.astype(jnp.float32) + arrived.astype(jnp.float32)).astype(jnp.bfloat16)
    return pieces


def gather_pieces(piece, labels, order):
    held = []
    for axis, bit in reversed(order):
        arrived = swap(piece, axis, bit)
        upper = bit_of(axis, bit)
        held = [label for label in labels if label in held or label == (axis, bit)]
        piece = jnp.stack(
            [jnp.where(upper, arrived, piece), jnp.where(upper, piece, arrived)],
            axis=held.index((axis, bit)),
        )
    return piece


def keep_and_send(first, second):
    upper = bit_of("ctx", 1)
    return (jnp.where(upper, second, first), jnp.where(upper, first, second))


def core_product(left, first, second):
    kept, sent = keep_and_send(first, second)
    left_all = jnp.concatenate([left, swap(left, "ctx", 1)], axis=0)
    right_all = jnp.concatenate([kept, swap(sent, "ctx", 1)], axis=0)
    return lax.dot_general(
        left_all, right_all, (((0,), (0,)), ((), ())), preferred_element_type=jnp.float32
    ).astype(jnp.bfloat16)


def shard_sum(product, by_columns):
    shards = lax.axis_size("fsdp")
    slices = lax.axis_size("ctx") // 2
    rows, columns = product.shape
    shard_labels = [("fsdp", bit) for bit in reversed(bits_below(shards))]
    slice_labels = [("ctx", 2 * bit) for bit in reversed(bits_below(slices))]
    if by_columns:
        cut = product.reshape(shards, rows // shards, slices, columns // slices)
        cut = jnp.transpose(cut, (0, 2, 1, 3))
    else:
        cut = product.reshape(shards, slices, rows // shards // slices, columns)
    parts = []
    half = cut.shape[2] // 2
    tail = list(reversed(shard_labels))
    for lead, orders in (
        (cut[:, :, :half], list(reversed(slice_labels))),
        (cut[:, :, half:], slice_labels),
    ):
        pieces = lead.reshape((2,) * (len(shard_labels) + len(slice_labels)) + lead.shape[2:])
        piece = reduce_pieces(pieces, shard_labels + slice_labels, orders + tail)
        whole = gather_pieces(piece, slice_labels, orders)
        parts.append(whole.reshape((slices,) + piece.shape))
    both = jnp.concatenate(parts, axis=1)
    if by_columns:
        return jnp.transpose(both, (1, 0, 2)).reshape(rows // shards, columns)
    return both.reshape(rows // shards, columns)


def join_cores(own):
    other = swap(own, "ctx", 1)
    upper = bit_of("ctx", 1)
    return jnp.concatenate(
        [jnp.where(upper, other, own), jnp.where(upper, own, other)], axis=1
    ).astype(jnp.float32)


def sum_over(value, axes):
    for axis in axes:
        for bit in bits_below(lax.axis_size(axis)):
            value = value + swap(value, axis, bit)
    return value


def own_shard(vector):
    width = vector.shape[0] // lax.axis_size("fsdp")
    return lax.dynamic_slice_in_dim(vector, lax.axis_index("fsdp") * width, width, 0)


def per_device(
    inputs,
    cotangent,
    lengths,
    piece_route,
    gain_one,
    qkv_weight,
    attn_out,
    gain_two,
    geglu_in,
    geglu_out,
):
    ctx_count = lax.axis_size("ctx")
    own_index = lax.axis_index("ctx")
    row_count = inputs.shape[1]
    model_width = inputs.shape[2]
    piece_rows = row_count // ctx_count
    tokens = row_count * ctx_count
    own_heads = model_width // HEAD_WIDTH // ctx_count
    own_width = own_heads * HEAD_WIDTH
    block_q = math.gcd(tokens, 256)
    block_k = math.gcd(tokens, 512)
    lengths_row = lengths[0]
    own_route = piece_route[0, 0]
    slot_ids = jnp.arange(ctx_count, dtype=jnp.int32)
    outgoing = jnp.sum(
        slot_ids[None, :] * (own_route[None, :] == slot_ids[:, None]).astype(jnp.int32), axis=1
    )

    def exchange(blocks):
        return lax.all_to_all(blocks, "ctx", split_axis=0, concat_axis=0, tiled=True)

    def to_slots(rows_in):
        return jnp.take(rows_in.reshape(ctx_count, piece_rows, model_width), outgoing, axis=0)

    def to_heads(rows_in):
        by_heads = rows_in.reshape(row_count, ctx_count, -1)
        return exchange(jnp.transpose(by_heads, (1, 0, 2))).reshape(tokens, -1)

    def to_rows(heads_in):
        return exchange(heads_in.reshape(ctx_count, row_count, -1))

    arrived = exchange(to_slots(inputs[0]))
    grad_arrived = exchange(to_slots(cotangent[0]))
    residual = arrived.reshape(row_count, model_width).astype(jnp.float32)
    places = own_index * row_count + jnp.arange(row_count, dtype=jnp.int32)
    unused_begin, unused_end, offset, is_valid = spans(places, lengths_row)
    pack_begin, pack_end, pack_offset, unused_valid = spans(
        jnp.arange(tokens, dtype=jnp.int32), lengths_row
    )
    grad_final = jnp.where(
        is_valid[:, None], grad_arrived.reshape(row_count, model_width).astype(jnp.float32), 0.0
    )
    gain_attn_low, qkv_full, attn_full = (
        lax.all_gather(gain_one, "fsdp", axis=0, tiled=True),
        lax.all_gather(qkv_weight, "fsdp", axis=0, tiled=True),
        lax.all_gather(attn_out, "fsdp", axis=0, tiled=True),
    )
    gain_mlp_low, in_full, out_full = (
        lax.all_gather(gain_two, "fsdp", axis=0, tiled=True),
        lax.all_gather(geglu_in, "fsdp", axis=0, tiled=True),
        lax.all_gather(geglu_out, "fsdp", axis=0, tiled=True),
    )
    gain_attn = gain_attn_low.astype(jnp.float32)
    act_attn = layer_norm(residual, gain_attn).astype(jnp.bfloat16)
    projected = jnp.dot(act_attn, qkv_full, preferred_element_type=jnp.float32)
    cosine, sine = rotary_tables(offset, 1)
    queries, keys = (
        rotate(projected[:, :model_width], cosine, sine).astype(jnp.bfloat16),
        rotate(projected[:, model_width : 2 * model_width], cosine, sine).astype(jnp.bfloat16),
    )
    values = projected[:, 2 * model_width :].astype(jnp.bfloat16)
    joined = jnp.stack(
        [part.reshape(row_count, ctx_count, own_width) for part in (queries, keys, values)], axis=2
    )
    qkv_heads = to_heads(joined.reshape(row_count, -1))
    low, high = key_range(pack_begin, pack_end, block_q, block_k)
    pack_begin, pack_end = (pack_begin[None, :], pack_end[None, :])
    attended_heads, log_total = attention_forward(
        qkv_heads, pack_begin, pack_end, low, high, own_heads, block_q, block_k
    )
    attn_low = jnp.transpose(to_rows(attended_heads.astype(jnp.bfloat16)), (1, 0, 2)).reshape(
        row_count, model_width
    )
    branch_attn = jnp.dot(attn_low, attn_full, preferred_element_type=jnp.float32)
    middle = residual + branch_attn
    gain_mlp = gain_mlp_low.astype(jnp.float32)
    act_mlp = layer_norm(middle, gain_mlp).astype(jnp.bfloat16)
    up_both = jnp.dot(act_mlp, in_full, preferred_element_type=jnp.float32)
    ff_width = up_both.shape[1] // 2
    hidden = (jax.nn.gelu(up_both[:, :ff_width], approximate=False) * up_both[:, ff_width:]).astype(
        jnp.bfloat16
    )
    branch_mlp = jnp.dot(hidden, out_full, preferred_element_type=jnp.float32)
    final_rows = jnp.where(is_valid[:, None], middle + branch_mlp, 0.0)
    square_sums = jnp.stack(
        [
            jnp.sum(final_rows * final_rows),
            jnp.sum(jnp.where(is_valid[:, None], branch_attn * branch_attn, 0.0)),
            jnp.sum(jnp.where(is_valid[:, None], branch_mlp * branch_mlp, 0.0)),
        ]
    )
    out_slots = final_rows.astype(jnp.bfloat16).reshape(ctx_count, piece_rows, model_width)
    back_out = exchange(out_slots)
    block_out = jnp.take(back_out, own_route, axis=0).reshape(1, row_count, model_width)
    grad_mlp_low = grad_final.astype(jnp.bfloat16)
    half_width = model_width // 2
    grad_out_mlp = core_product(hidden, grad_mlp_low[:, :half_width], grad_mlp_low[:, half_width:])
    grad_hidden = lax.dot_general(
        grad_mlp_low, out_full, NT, preferred_element_type=jnp.float32
    )

    def gated(leading, trailing):
        return jax.nn.gelu(leading, approximate=False) * trailing

    unused_gate, gate_back = jax.vjp(gated, up_both[:, :ff_width], up_both[:, ff_width:])
    grad_leading, grad_trailing = gate_back(grad_hidden)
    grad_leading, grad_trailing = (
        grad_leading.astype(jnp.bfloat16),
        grad_trailing.astype(jnp.bfloat16),
    )
    grad_up = jnp.concatenate([grad_leading, grad_trailing], axis=1)
    grad_in_mlp = core_product(act_mlp, grad_leading, grad_trailing)
    grad_act_mlp = lax.dot_general(grad_up, in_full, NT, preferred_element_type=jnp.float32)
    unused_norm, norm_back_mlp = jax.vjp(layer_norm, middle, gain_mlp)
    grad_middle_norm, grad_gain_mlp = norm_back_mlp(grad_act_mlp)
    grad_middle = grad_final + grad_middle_norm
    grad_attn_low = grad_middle.astype(jnp.bfloat16)
    grad_attn_proj = core_product(
        attn_low, grad_attn_low[:, :half_width], grad_attn_low[:, half_width:]
    )
    grad_attended = lax.dot_general(
        grad_attn_low, attn_full, NT, preferred_element_type=jnp.float32
    ).astype(jnp.bfloat16)
    pack_cosine, pack_sine = rotary_tables(pack_offset, own_heads)
    block_back = math.gcd(tokens, 256)
    low_back, high_back = key_range(pack_begin[0], pack_end[0], block_q, block_back)
    grad_heads = attention_backward(
        qkv_heads,
        attended_heads,
        to_heads(grad_attended),
        log_total,
        pack_begin,
        pack_end,
        low_back,
        high_back,
        pack_cosine,
        pack_sine,
        own_heads,
        block_q,
        block_back,
    )
    grad_projected = jnp.transpose(
        to_rows(grad_heads).reshape(ctx_count, row_count, 3, own_width), (1, 2, 0, 3)
    ).reshape(row_count, 3 * model_width)
    half_three = 3 * model_width // 2
    grad_qkv = core_product(
        act_attn, grad_projected[:, :half_three], grad_projected[:, half_three:]
    )
    grad_act_attn = lax.dot_general(
        grad_projected, qkv_full, NT, preferred_element_type=jnp.float32
    )
    unused_first, norm_back_attn = jax.vjp(layer_norm, residual, gain_attn)
    grad_resid_norm, grad_gain_attn = norm_back_attn(grad_act_attn)
    grad_residual = (grad_middle + grad_resid_norm).astype(jnp.bfloat16)
    back_grad = exchange(grad_residual.reshape(ctx_count, piece_rows, model_width))
    grad_inputs = jnp.take(back_grad, own_route, axis=0).reshape(1, row_count, model_width)
    total_out = join_cores(shard_sum(grad_out_mlp, True))
    total_in = join_cores(shard_sum(grad_in_mlp, False))
    total_attn = join_cores(shard_sum(grad_attn_proj, False))
    total_qkv = join_cores(shard_sum(grad_qkv, False))
    total_gain_one = own_shard(sum_over(grad_gain_attn, ("ctx", "fsdp")))
    total_gain_two = own_shard(sum_over(grad_gain_mlp, ("ctx", "fsdp")))
    total_squares = sum_over(square_sums, ("ctx",))
    valid_count = jnp.sum(lengths_row).astype(jnp.float32)
    rms_stats = jnp.sqrt(total_squares / (valid_count * model_width))[None, :]
    return (
        block_out,
        grad_inputs,
        total_gain_one,
        total_qkv,
        total_attn,
        total_gain_two,
        total_in,
        total_out,
        rms_stats,
    )


def solution(mesh):
    placed = (
        P("fsdp", "ctx", None),
        P("fsdp", "ctx", None),
        P("fsdp", None),
        P("fsdp", "ctx", None),
        P("fsdp"),
        P("fsdp", None),
        P("fsdp", None),
        P("fsdp"),
        P("fsdp", None),
        P("fsdp", None),
    )
    return jax.shard_map(
        per_device,
        mesh=mesh,
        in_specs=placed,
        out_specs=(
            P("fsdp", "ctx", None),
            P("fsdp", "ctx", None),
            P("fsdp"),
            P("fsdp", None),
            P("fsdp", None),
            P("fsdp"),
            P("fsdp", None),
            P("fsdp", None),
            P("fsdp", None),
        ),
        check_vma=False,
    )
```

```python
import functools
import math
import jax
import jax.numpy as jnp
from jax import lax
from jax.experimental import pallas as pl
from jax.experimental.pallas import tpu as pltpu
from jax.sharding import PartitionSpec as P

HEAD_WIDTH = 64
norm_eps = 1e-05
masked_score = -1e30


def head_stack(rows_in, head_count):
    if head_count == 1:
        return rows_in
    lane_head = lax.broadcasted_iota(jnp.int32, rows_in.shape, 1) // HEAD_WIDTH
    zero = jnp.zeros_like(rows_in)
    return jnp.concatenate(
        [jnp.where(lane_head == h, rows_in, zero) for h in range(head_count)], axis=0
    )


def head_pick(stacked_t, head_count, block):
    return jnp.concatenate(
        [
            stacked_t[h * HEAD_WIDTH : (h + 1) * HEAD_WIDTH, h * block : (h + 1) * block]
            for h in range(head_count)
        ],
        axis=0,
    ).T


NT = (((1,), (1,)), ((), ()))


def forward_kernel(
    head_count, block_q, block_k, low_ref, high_ref, begin_ref, end_ref, qkv_ref, out_ref, log_ref, turned_ref
):
    width = out_ref.shape[1]
    step = pl.program_id(0)

    @pl.when(step == 0)
    def prepare():
        turned_ref[...] = qkv_ref[:, 2 * width :].astype(jnp.float32).T.astype(jnp.bfloat16)

    rows = pl.ds(pl.multiple_of(step * block_q, block_q), block_q)
    scale = 1.0 / math.sqrt(HEAD_WIDTH)
    stacked = head_stack(qkv_ref[rows, :width] * jnp.asarray(scale, jnp.bfloat16), head_count)
    begin = jnp.concatenate([begin_ref[:, rows]] * head_count, axis=1)
    end = jnp.concatenate([end_ref[:, rows]] * head_count, axis=1)

    def body(index, carried):
        top, total, acc = carried
        first = pl.multiple_of(index * block_k, block_k)
        keys = qkv_ref[pl.ds(first, block_k), width : 2 * width]
        scores = lax.dot_general(keys, stacked, NT, preferred_element_type=jnp.float32)
        place = first + lax.broadcasted_iota(jnp.int32, scores.shape, 0)
        scores = jnp.where((place >= begin) & (place < end), scores, masked_score)
        new_top = jnp.maximum(top, jnp.max(scores, axis=0, keepdims=True))
        fresh = jnp.exp(scores - new_top)
        fade = jnp.exp(top - new_top)
        total = total * fade + jnp.sum(fresh, axis=0, keepdims=True)
        acc = acc * fade + jnp.dot(
            turned_ref[:, pl.ds(first, block_k)],
            fresh.astype(jnp.bfloat16),
            preferred_element_type=jnp.float32,
        )
        return (new_top, total, acc)

    lanes = head_count * block_q
    top, total, acc = lax.fori_loop(
        low_ref[step],
        high_ref[step],
        body,
        (
            jnp.full((1, lanes), masked_score, jnp.float32),
            jnp.zeros((1, lanes), jnp.float32),
            jnp.zeros((width, lanes), jnp.float32),
        ),
    )
    valid = end > begin
    safe = jnp.where(valid, total, 1.0)
    acc = jnp.where(valid, acc / safe, 0.0)
    log_total = jnp.where(valid, top + jnp.log(safe), 0.0)
    out_ref[...] = head_pick(acc, head_count, block_q)
    log_ref[0] = log_total


def attention_forward(qkv, begin, end, low, high, head_count, block_q, block_k):
    tokens = qkv.shape[0]
    width = head_count * HEAD_WIDTH
    steps = tokens // block_q
    whole = lambda shape: pl.BlockSpec(shape, lambda i, *_: (0,) * len(shape))
    pairs = tokens * tokens // 4 * head_count
    return pl.pallas_call(
        functools.partial(forward_kernel, head_count, block_q, block_k),
        out_shape=(
            jax.ShapeDtypeStruct((tokens, width), jnp.float32),
            jax.ShapeDtypeStruct((steps, 1, head_count * block_q), jnp.float32),
        ),
        grid_spec=pltpu.PrefetchScalarGridSpec(
            num_scalar_prefetch=2,
            grid=(steps,),
            in_specs=[whole((1, tokens)), whole((1, tokens)), whole((tokens, 3 * width))],
            out_specs=(
                pl.BlockSpec((block_q, width), lambda i, *_: (i, 0)),
                pl.BlockSpec((1, 1, head_count * block_q), lambda i, *_: (i, 0, 0)),
            ),
            scratch_shapes=[pltpu.VMEM((width, tokens), jnp.bfloat16)],
        ),
        cost_estimate=pl.CostEstimate(
            flops=pairs * 512, bytes_accessed=tokens * width * 12, transcendentals=pairs
        ),
        name="attention_forward",
    )(low, high, begin, end, qkv)


def turn_back(grads, cosine, sine, head_count):
    half = HEAD_WIDTH // 2
    pieces = []
    for h in range(head_count):
        base = h * HEAD_WIDTH
        pieces += [grads[:, base + half : base + HEAD_WIDTH], grads[:, base : base + half]]
    return grads * cosine + jnp.concatenate(pieces, axis=1) * sine


def backward_kernel(
    head_count,
    block_q,
    block_k,
    low_ref,
    high_ref,
    begin_ref,
    end_ref,
    qkv_ref,
    attended_ref,
    grad_ref,
    log_ref,
    cosine_ref,
    sine_ref,
    out_ref,
    turned_ref,
    key_acc,
    value_acc,
):
    width = attended_ref.shape[1]
    step = pl.program_id(0)

    @pl.when(step == 0)
    def prepare():
        turned_ref[...] = qkv_ref[:, width : 2 * width].astype(jnp.float32).T.astype(jnp.bfloat16)
        key_acc[...] = jnp.zeros_like(key_acc)
        value_acc[...] = jnp.zeros_like(value_acc)

    rows = pl.ds(pl.multiple_of(step * block_q, block_q), block_q)
    scale = 1.0 / math.sqrt(HEAD_WIDTH)
    stacked = head_stack(qkv_ref[rows, :width] * jnp.asarray(scale, jnp.bfloat16), head_count)
    grads = grad_ref[rows, :]
    grad_stacked = head_stack(grads, head_count)
    begin = jnp.concatenate([begin_ref[:, rows]] * head_count, axis=1)
    end = jnp.concatenate([end_ref[:, rows]] * head_count, axis=1)
    product = (grads.astype(jnp.float32) * attended_ref[rows, :]).T
    delta = jnp.concatenate(
        [
            jnp.sum(product[h * HEAD_WIDTH : (h + 1) * HEAD_WIDTH], axis=0, keepdims=True)
            for h in range(head_count)
        ],
        axis=1,
    )
    log_total = log_ref[0]

    def body(index, acc):
        first = pl.multiple_of(index * block_k, block_k)
        span = pl.ds(first, block_k)
        keys = qkv_ref[span, width : 2 * width]
        values = qkv_ref[span, 2 * width :]
        scores = lax.dot_general(keys, stacked, NT, preferred_element_type=jnp.float32)
        grad_probs = lax.dot_general(values, grad_stacked, NT, preferred_element_type=jnp.float32)
        place = first + lax.broadcasted_iota(jnp.int32, scores.shape, 0)
        scores = jnp.where((place >= begin) & (place < end), scores, masked_score)
        probs = jnp.exp(scores - log_total)
        grad_scores = (probs * (grad_probs - delta)).astype(jnp.bfloat16)
        value_acc[span, :] += jnp.dot(
            probs.astype(jnp.bfloat16), grad_stacked, preferred_element_type=jnp.float32
        )
        key_acc[span, :] += jnp.dot(grad_scores, stacked, preferred_element_type=jnp.float32)
        return acc + jnp.dot(
            turned_ref[:, span], grad_scores, preferred_element_type=jnp.float32
        )

    acc = lax.fori_loop(
        low_ref[step],
        high_ref[step],
        body,
        jnp.zeros((width, head_count * block_q), jnp.float32),
    )
    grad_queries = head_pick(acc, head_count, block_q) * scale
    out_ref[rows, :width] = turn_back(
        grad_queries, cosine_ref[rows, :], sine_ref[rows, :], head_count
    ).astype(jnp.bfloat16)

    @pl.when(step == pl.num_programs(0) - 1)
    def finish():
        @pl.loop(0, pl.num_programs(0))
        def each(index):
            span = pl.ds(pl.multiple_of(index * block_q, block_q), block_q)
            out_ref[span, width : 2 * width] = turn_back(
                key_acc[span, :], cosine_ref[span, :], sine_ref[span, :], head_count
            ).astype(jnp.bfloat16)
            out_ref[span, 2 * width :] = value_acc[span, :].astype(jnp.bfloat16)


def attention_backward(
    qkv, attended, grads, log_total, begin, end, low, high, cosine, sine, head_count, block_q, block_k
):
    tokens = qkv.shape[0]
    width = head_count * HEAD_WIDTH
    steps = tokens // block_q
    whole = lambda shape: pl.BlockSpec(shape, lambda i, *_: (0,) * len(shape))
    pairs = tokens * tokens // 4 * head_count
    return pl.pallas_call(
        functools.partial(backward_kernel, head_count, block_q, block_k),
        out_shape=jax.ShapeDtypeStruct((tokens, 3 * width), jnp.bfloat16),
        grid_spec=pltpu.PrefetchScalarGridSpec(
            num_scalar_prefetch=2,
            grid=(steps,),
            in_specs=[
                whole((1, tokens)),
                whole((1, tokens)),
                whole((tokens, 3 * width)),
                whole((tokens, width)),
                whole((tokens, width)),
                pl.BlockSpec((1, 1, head_count * block_q), lambda i, *_: (i, 0, 0)),
                whole((tokens, width)),
                whole((tokens, width)),
            ],
            out_specs=whole((tokens, 3 * width)),
            scratch_shapes=[
                pltpu.VMEM((width, tokens), jnp.bfloat16),
                pltpu.VMEM((tokens, width), jnp.float32),
                pltpu.VMEM((tokens, width), jnp.float32),
            ],
        ),
        cost_estimate=pl.CostEstimate(
            flops=pairs * 1280, bytes_accessed=tokens * width * 30, transcendentals=pairs
        ),
        name="attention_backward",
    )(low, high, begin, end, qkv, attended, grads, log_total, cosine, sine)


def spans(places, lengths_row):
    ends = jnp.cumsum(lengths_row)
    past = (places[:, None] >= ends[None, :]).astype(jnp.int32)
    begin = jnp.sum(past * lengths_row[None, :], axis=1)
    before = (places[:, None] >= (ends - lengths_row)[None, :]).astype(jnp.int32)
    end = jnp.sum(before * lengths_row[None, :], axis=1)
    valid = places < ends[-1]
    return (jnp.where(valid, begin, 0), jnp.where(valid, end, 0), places - begin, valid)


def key_range(begin, end, block_q, block_k):
    begin_blocks = jnp.where(end > begin, begin, jnp.int32(1 << 30)).reshape(-1, block_q)
    high = (jnp.max(end.reshape(-1, block_q), axis=1) + block_k - 1) // block_k
    low = jnp.minimum(jnp.min(begin_blocks, axis=1) // block_k, high)
    return (low, high)


def rotary_tables(offset, head_count):
    half = HEAD_WIDTH // 2
    inverse = 160000.0 ** (-2.0 * jnp.arange(half, dtype=jnp.float32) / HEAD_WIDTH)
    angles = offset.astype(jnp.float32)[:, None] * inverse[None, :]
    cosine, sine = (jnp.cos(angles), jnp.sin(angles))
    return (
        jnp.concatenate([cosine, cosine] * head_count, axis=1),
        jnp.concatenate([sine, -sine] * head_count, axis=1),
    )


def toggled(index, bit):
    return index + bit - 2 * bit * ((index // bit) % 2)


def gather_kernel(shapes, *refs):
    count = len(shapes)
    shard_refs, full_refs = (refs[:count], refs[count : 2 * count])
    send_sem, recv_sem, local_sem = refs[2 * count :]
    shards = lax.axis_size("fsdp")
    slices = lax.axis_size("ctx") // 2
    own_ctx, own_shard = (lax.axis_index("ctx"), lax.axis_index("fsdp"))
    core, chip = (own_ctx % 2, own_ctx // 2)
    barrier = pltpu.get_barrier_semaphore()
    partners = [{"fsdp": toggled(own_shard, bit)} for bit in (1, 2)]
    partners += [{"ctx": toggled(own_ctx, bit)} for bit in (1, 2, 4)]
    for partner in partners:
        pl.semaphore_signal(
            barrier, inc=1, device_id=partner, device_id_type=pl.DeviceIdType.MESH
        )
    pl.semaphore_wait(barrier, len(partners))
    to_one, to_two, to_core, to_x, to_y = partners

    def shard_at(step):
        if step == 0:
            return own_shard
        if step == 3:
            return toggled(toggled(own_shard, 1), 2)
        return toggled(own_shard, step)

    def region(ref, weight, step, chip_at, half):
        if shapes[weight] == "small":
            return ref if len(ref.shape) == 2 else ref.at[shard_at(step)]
        if shapes[weight] == "rows":
            rows = ref.shape[-2]
            span = pl.ds(0, rows) if half is None else pl.ds(half * (rows // 2), rows // 2)
            if len(ref.shape) == 4:
                return ref.at[core, chip_at, span, :]
            return ref.at[shard_at(step), core, chip_at, span, :]
        rows = ref.shape[-2]
        first = (rows // 2) // 16 * 16
        spans_of = {None: pl.ds(0, rows), 0: pl.ds(0, first), 1: pl.ds(first, rows - first)}
        width = ref.shape[-1] // (2 * slices)
        columns = pl.ds(pl.multiple_of((core * slices + chip_at) * width, width), width)
        if len(ref.shape) == 2:
            return ref.at[spans_of[half], columns]
        return ref.at[shard_at(step), spans_of[half], columns]

    def core_region(ref, weight, step):
        if shapes[weight] == "rows":
            return ref.at[shard_at(step), core]
        width = ref.shape[-1] // 2
        return ref.at[shard_at(step), :, pl.ds(pl.multiple_of(core * width, width), width)]

    pending = []

    def send(source, target, slot, partner):
        copy = pltpu.make_async_remote_copy(
            src_ref=source,
            dst_ref=target,
            send_sem=send_sem.at[slot],
            recv_sem=recv_sem.at[slot],
            device_id=partner,
            device_id_type=pl.DeviceIdType.MESH,
        )
        copy.start()
        pending.append(copy)
        return copy

    copies = {}
    local = []

    def slot_of(weight, step, kind):
        return (weight * 3 + step - 1) * 8 + kind

    def shard_sends(weight):
        source = region(shard_refs[weight], weight, 0, chip, None)
        target = region(full_refs[weight], weight, 0, chip, None)
        copies[weight, 2, 0] = send(source, target, slot_of(weight, 2, 0), to_two)
        copies[weight, 1, 0] = send(source, target, slot_of(weight, 1, 0), to_one)
        target = full_refs[weight].at[own_shard]
        copy = pltpu.make_async_copy(shard_refs[weight], target, local_sem.at[weight])
        copy.start()
        local.append(copy)

    def shard_forward(weight):
        copies[weight, 2, 0].wait_recv()
        piece = region(full_refs[weight], weight, 2, chip, None)
        copies[weight, 3, 0] = send(piece, piece, slot_of(weight, 3, 0), to_one)

    def plane_sends(weight, step):
        lead = region(full_refs[weight], weight, step, chip, 0)
        rest = region(full_refs[weight], weight, step, chip, 1)
        for kind, piece, partner in ((1, lead, to_x), (2, rest, to_y), (3, lead, to_y), (4, rest, to_x)):
            copies[weight, step, kind] = send(piece, piece, slot_of(weight, step, kind), partner)

    def plane_forward(weight, step):
        copies[weight, step, 1].wait_recv()
        lead = region(full_refs[weight], weight, step, toggled(chip, 1), 0)
        copies[weight, step, 5] = send(lead, lead, slot_of(weight, step, 5), to_y)
        copies[weight, step, 2].wait_recv()
        rest = region(full_refs[weight], weight, step, toggled(chip, 2), 1)
        copies[weight, step, 6] = send(rest, rest, slot_of(weight, step, 6), to_x)

    def core_send(weight, step):
        for kind in (3, 4, 5, 6):
            copies[weight, step, kind].wait_recv()
        piece = core_region(full_refs[weight], weight, step)
        copies[weight, step, 7] = send(piece, piece, slot_of(weight, step, 7), to_core)

    shard_sends(0)
    for weight in range(count):
        if weight + 1 < count:
            shard_sends(weight + 1)
        shard_forward(weight)
        copies[weight, 1, 0].wait_recv()
        if shapes[weight] == "small":
            copies[weight, 3, 0].wait_recv()
            continue
        plane_sends(weight, 1)
        plane_sends(weight, 2)
        copies[weight, 3, 0].wait_recv()
        plane_sends(weight, 3)
        for step in (1, 2, 3):
            plane_forward(weight, step)
        if weight > 0 and shapes[weight - 1] != "small":
            for step in (1, 2, 3):
                core_send(weight - 1, step)
    for step in (1, 2, 3):
        core_send(count - 1, step)
    for weight in range(count):
        if shapes[weight] != "small":
            for step in (1, 2, 3):
                copies[weight, step, 7].wait_recv()
    for copy in pending:
        copy.wait_send()
    for copy in local:
        copy.wait()


def gather_weights(weights):
    shards, ctx_count = (lax.axis_size("fsdp"), lax.axis_size("ctx"))
    slices = ctx_count // 2
    shapes, views, outs = ([], [], [])
    for weight in weights:
        rows, columns = weight.shape
        if rows % (32 * ctx_count) == 0:
            shapes.append("rows")
            views.append(weight.reshape(2, slices, rows // ctx_count, columns))
            outs.append((shards, 2, slices, rows // ctx_count, columns))
        elif rows == 16:
            shapes.append("small")
            views.append(weight)
            outs.append((shards, rows, columns))
        elif columns % (128 * ctx_count) == 0 and rows % 16 == 0:
            shapes.append("columns")
            views.append(weight)
            outs.append((shards, rows, columns))
    if shards != 4 or ctx_count != 8 or len(views) < len(weights):
        return [lax.all_gather(weight, "fsdp", axis=0, tiled=True) for weight in weights]
    slots = len(views) * 24
    held = pl.pallas_call(
        functools.partial(gather_kernel, shapes),
        out_shape=tuple(jax.ShapeDtypeStruct(out, jnp.bfloat16) for out in outs),
        in_specs=[pl.BlockSpec(memory_space=pltpu.VMEM)] * len(views),
        out_specs=tuple(pl.BlockSpec(memory_space=pl.ANY) for out in outs),
        scratch_shapes=[
            pltpu.SemaphoreType.DMA((slots,)),
            pltpu.SemaphoreType.DMA((slots,)),
            pltpu.SemaphoreType.DMA((len(views),)),
        ],
        compiler_params=pltpu.CompilerParams(collective_id=0, has_side_effects=True),
        name="gather_weights",
    )(*views)
    return [whole.reshape(-1, whole.shape[-1]) for whole in held]


def layer_norm(rows_in, gain_vec):
    row_mean = jnp.mean(rows_in, axis=-1, keepdims=True)
    centred = rows_in - row_mean
    variance = jnp.mean(centred * centred, axis=-1, keepdims=True)
    return centred * lax.rsqrt(variance + norm_eps) * gain_vec


def rotate(projected, cosine, sine):
    row_count, width = projected.shape
    half_width = HEAD_WIDTH // 2
    by_head = projected.reshape(row_count, width // HEAD_WIDTH, HEAD_WIDTH)
    turned = jnp.concatenate([by_head[..., half_width:], by_head[..., :half_width]], axis=-1)
    return (by_head * cosine[:, None, :] - turned * sine[:, None, :]).reshape(row_count, width)


def swap(value, axis, bit):
    pairs = [(i, i ^ bit) for i in range(lax.axis_size(axis))]
    return lax.ppermute(value, axis, pairs)


def bit_of(axis, bit):
    return (lax.axis_index(axis) // bit) % 2 == 1


def bits_below(count):
    return [1 << i for i in range(count.bit_length() - 1)]


def reduce_pieces(pieces, labels, order):
    labels = list(labels)
    for axis, bit in order:
        at = labels.index((axis, bit))
        labels.pop(at)
        first = lax.index_in_dim(pieces, 0, at, keepdims=False)
        second = lax.index_in_dim(pieces, 1, at, keepdims=False)
        upper = bit_of(axis, bit)
        arrived = swap(jnp.where(upper, first, second), axis, bit)
        kept = jnp.where(upper, second, first)
        pieces = (kept.astype(jnp.float32) + arrived.astype(jnp.float32)).astype(jnp.bfloat16)
    return pieces


def gather_pieces(piece, labels, order):
    held = []
    for axis, bit in reversed(order):
        arrived = swap(piece, axis, bit)
        upper = bit_of(axis, bit)
        held = [label for label in labels if label in held or label == (axis, bit)]
        piece = jnp.stack(
            [jnp.where(upper, arrived, piece), jnp.where(upper, piece, arrived)],
            axis=held.index((axis, bit)),
        )
    return piece


def keep_and_send(first, second):
    upper = bit_of("ctx", 1)
    return (jnp.where(upper, second, first), jnp.where(upper, first, second))


def core_product(left, first, second):
    kept, sent = keep_and_send(first, second)
    left_all = jnp.concatenate([left, swap(left, "ctx", 1)], axis=0)
    right_all = jnp.concatenate([kept, swap(sent, "ctx", 1)], axis=0)
    return lax.dot_general(
        left_all, right_all, (((0,), (0,)), ((), ())), preferred_element_type=jnp.float32
    ).astype(jnp.bfloat16)


def shard_sum(product, by_columns):
    shards = lax.axis_size("fsdp")
    slices = lax.axis_size("ctx") // 2
    rows, columns = product.shape
    shard_labels = [("fsdp", bit) for bit in reversed(bits_below(shards))]
    slice_labels = [("ctx", 2 * bit) for bit in reversed(bits_below(slices))]
    if by_columns:
        cut = product.reshape(shards, rows // shards, slices, columns // slices)
        cut = jnp.transpose(cut, (0, 2, 1, 3))
    else:
        cut = product.reshape(shards, slices, rows // shards // slices, columns)
    parts = []
    half = cut.shape[2] // 2
    tail = list(reversed(shard_labels))
    for lead, orders in (
        (cut[:, :, :half], list(reversed(slice_labels))),
        (cut[:, :, half:], slice_labels),
    ):
        pieces = lead.reshape((2,) * (len(shard_labels) + len(slice_labels)) + lead.shape[2:])
        piece = reduce_pieces(pieces, shard_labels + slice_labels, orders + tail)
        whole = gather_pieces(piece, slice_labels, orders)
        parts.append(whole.reshape((slices,) + piece.shape))
    both = jnp.concatenate(parts, axis=1)
    if by_columns:
        return jnp.transpose(both, (1, 0, 2)).reshape(rows // shards, columns)
    return both.reshape(rows // shards, columns)


def join_cores(own):
    other = swap(own, "ctx", 1)
    upper = bit_of("ctx", 1)
    return jnp.concatenate(
        [jnp.where(upper, other, own), jnp.where(upper, own, other)], axis=1
    ).astype(jnp.float32)


def sum_over(value, axes):
    for axis in axes:
        for bit in bits_below(lax.axis_size(axis)):
            value = value + swap(value, axis, bit)
    return value


def own_shard(vector):
    width = vector.shape[0] // lax.axis_size("fsdp")
    return lax.dynamic_slice_in_dim(vector, lax.axis_index("fsdp") * width, width, 0)


def per_device(
    inputs,
    cotangent,
    lengths,
    piece_route,
    gain_one,
    qkv_weight,
    attn_out,
    gain_two,
    geglu_in,
    geglu_out,
):
    ctx_count = lax.axis_size("ctx")
    own_index = lax.axis_index("ctx")
    row_count = inputs.shape[1]
    model_width = inputs.shape[2]
    piece_rows = row_count // ctx_count
    tokens = row_count * ctx_count
    own_heads = model_width // HEAD_WIDTH // ctx_count
    own_width = own_heads * HEAD_WIDTH
    block_q = math.gcd(tokens, 256)
    block_k = math.gcd(tokens, 512)
    lengths_row = lengths[0]
    own_route = piece_route[0, 0]
    slot_ids = jnp.arange(ctx_count, dtype=jnp.int32)
    outgoing = jnp.sum(
        slot_ids[None, :] * (own_route[None, :] == slot_ids[:, None]).astype(jnp.int32), axis=1
    )

    def exchange(blocks):
        return lax.all_to_all(blocks, "ctx", split_axis=0, concat_axis=0, tiled=True)

    def to_slots(rows_in):
        return jnp.take(rows_in.reshape(ctx_count, piece_rows, model_width), outgoing, axis=0)

    def to_heads(rows_in):
        by_heads = rows_in.reshape(row_count, ctx_count, -1)
        return exchange(jnp.transpose(by_heads, (1, 0, 2))).reshape(tokens, -1)

    def to_rows(heads_in):
        return exchange(heads_in.reshape(ctx_count, row_count, -1))

    arrived = exchange(to_slots(inputs[0]))
    grad_arrived = exchange(to_slots(cotangent[0]))
    residual = arrived.reshape(row_count, model_width).astype(jnp.float32)
    places = own_index * row_count + jnp.arange(row_count, dtype=jnp.int32)
    unused_begin, unused_end, offset, is_valid = spans(places, lengths_row)
    pack_begin, pack_end, pack_offset, unused_valid = spans(
        jnp.arange(tokens, dtype=jnp.int32), lengths_row
    )
    grad_final = jnp.where(
        is_valid[:, None], grad_arrived.reshape(row_count, model_width).astype(jnp.float32), 0.0
    )
    gains = jnp.pad(jnp.stack([gain_one, gain_two]), ((0, 14), (0, 0)))
    gains_full, qkv_full, attn_full, in_full, out_full = gather_weights(
        [gains, qkv_weight, attn_out, geglu_in, geglu_out]
    )
    gains_full = gains_full.reshape(-1, 16, gains.shape[1])
    gain_attn = gains_full[:, 0].reshape(-1).astype(jnp.float32)
    gain_mlp = gains_full[:, 1].reshape(-1).astype(jnp.float32)
    act_attn = layer_norm(residual, gain_attn).astype(jnp.bfloat16)
    projected = jnp.dot(act_attn, qkv_full, preferred_element_type=jnp.float32)
    cosine, sine = rotary_tables(offset, 1)
    queries, keys = (
        rotate(projected[:, :model_width], cosine, sine).astype(jnp.bfloat16),
        rotate(projected[:, model_width : 2 * model_width], cosine, sine).astype(jnp.bfloat16),
    )
    values = projected[:, 2 * model_width :].astype(jnp.bfloat16)
    joined = jnp.stack(
        [part.reshape(row_count, ctx_count, own_width) for part in (queries, keys, values)], axis=2
    )
    qkv_heads = to_heads(joined.reshape(row_count, -1))
    low, high = key_range(pack_begin, pack_end, block_q, block_k)
    pack_begin, pack_end = (pack_begin[None, :], pack_end[None, :])
    attended_heads, log_total = attention_forward(
        qkv_heads, pack_begin, pack_end, low, high, own_heads, block_q, block_k
    )
    attn_low = jnp.transpose(to_rows(attended_heads.astype(jnp.bfloat16)), (1, 0, 2)).reshape(
        row_count, model_width
    )
    branch_attn = jnp.dot(attn_low, attn_full, preferred_element_type=jnp.float32)
    middle = residual + branch_attn
    act_mlp = layer_norm(middle, gain_mlp).astype(jnp.bfloat16)
    up_both = jnp.dot(act_mlp, in_full, preferred_element_type=jnp.float32)
    ff_width = up_both.shape[1] // 2
    hidden = (jax.nn.gelu(up_both[:, :ff_width], approximate=False) * up_both[:, ff_width:]).astype(
        jnp.bfloat16
    )
    branch_mlp = jnp.dot(hidden, out_full, preferred_element_type=jnp.float32)
    final_rows = jnp.where(is_valid[:, None], middle + branch_mlp, 0.0)
    square_sums = jnp.stack(
        [
            jnp.sum(final_rows * final_rows),
            jnp.sum(jnp.where(is_valid[:, None], branch_attn * branch_attn, 0.0)),
            jnp.sum(jnp.where(is_valid[:, None], branch_mlp * branch_mlp, 0.0)),
        ]
    )
    out_slots = final_rows.astype(jnp.bfloat16).reshape(ctx_count, piece_rows, model_width)
    back_out = exchange(out_slots)
    block_out = jnp.take(back_out, own_route, axis=0).reshape(1, row_count, model_width)
    grad_mlp_low = grad_final.astype(jnp.bfloat16)
    half_width = model_width // 2
    grad_out_mlp = core_product(hidden, grad_mlp_low[:, :half_width], grad_mlp_low[:, half_width:])
    grad_hidden = lax.dot_general(
        grad_mlp_low, out_full, NT, preferred_element_type=jnp.float32
    )

    def gated(leading, trailing):
        return jax.nn.gelu(leading, approximate=False) * trailing

    unused_gate, gate_back = jax.vjp(gated, up_both[:, :ff_width], up_both[:, ff_width:])
    grad_leading, grad_trailing = gate_back(grad_hidden)
    grad_leading, grad_trailing = (
        grad_leading.astype(jnp.bfloat16),
        grad_trailing.astype(jnp.bfloat16),
    )
    grad_up = jnp.concatenate([grad_leading, grad_trailing], axis=1)
    grad_in_mlp = core_product(act_mlp, grad_leading, grad_trailing)
    grad_act_mlp = lax.dot_general(grad_up, in_full, NT, preferred_element_type=jnp.float32)
    unused_norm, norm_back_mlp = jax.vjp(layer_norm, middle, gain_mlp)
    grad_middle_norm, grad_gain_mlp = norm_back_mlp(grad_act_mlp)
    grad_middle = grad_final + grad_middle_norm
    grad_attn_low = grad_middle.astype(jnp.bfloat16)
    grad_attn_proj = core_product(
        attn_low, grad_attn_low[:, :half_width], grad_attn_low[:, half_width:]
    )
    grad_attended = lax.dot_general(
        grad_attn_low, attn_full, NT, preferred_element_type=jnp.float32
    ).astype(jnp.bfloat16)
    pack_cosine, pack_sine = rotary_tables(pack_offset, own_heads)
    block_back = math.gcd(tokens, 256)
    low_back, high_back = key_range(pack_begin[0], pack_end[0], block_q, block_back)
    grad_heads = attention_backward(
        qkv_heads,
        attended_heads,
        to_heads(grad_attended),
        log_total,
        pack_begin,
        pack_end,
        low_back,
        high_back,
        pack_cosine,
        pack_sine,
        own_heads,
        block_q,
        block_back,
    )
    grad_projected = jnp.transpose(
        to_rows(grad_heads).reshape(ctx_count, row_count, 3, own_width), (1, 2, 0, 3)
    ).reshape(row_count, 3 * model_width)
    half_three = 3 * model_width // 2
    grad_qkv = core_product(
        act_attn, grad_projected[:, :half_three], grad_projected[:, half_three:]
    )
    grad_act_attn = lax.dot_general(
        grad_projected, qkv_full, NT, preferred_element_type=jnp.float32
    )
    unused_first, norm_back_attn = jax.vjp(layer_norm, residual, gain_attn)
    grad_resid_norm, grad_gain_attn = norm_back_attn(grad_act_attn)
    grad_residual = (grad_middle + grad_resid_norm).astype(jnp.bfloat16)
    back_grad = exchange(grad_residual.reshape(ctx_count, piece_rows, model_width))
    grad_inputs = jnp.take(back_grad, own_route, axis=0).reshape(1, row_count, model_width)
    total_out = join_cores(shard_sum(grad_out_mlp, True))
    total_in = join_cores(shard_sum(grad_in_mlp, False))
    total_attn = join_cores(shard_sum(grad_attn_proj, False))
    total_qkv = join_cores(shard_sum(grad_qkv, False))
    total_gain_one = own_shard(sum_over(grad_gain_attn, ("ctx", "fsdp")))
    total_gain_two = own_shard(sum_over(grad_gain_mlp, ("ctx", "fsdp")))
    total_squares = sum_over(square_sums, ("ctx",))
    valid_count = jnp.sum(lengths_row).astype(jnp.float32)
    rms_stats = jnp.sqrt(total_squares / (valid_count * model_width))[None, :]
    return (
        block_out,
        grad_inputs,
        total_gain_one,
        total_qkv,
        total_attn,
        total_gain_two,
        total_in,
        total_out,
        rms_stats,
    )


def solution(mesh):
    placed = (
        P("fsdp", "ctx", None),
        P("fsdp", "ctx", None),
        P("fsdp", None),
        P("fsdp", "ctx", None),
        P("fsdp"),
        P("fsdp", None),
        P("fsdp", None),
        P("fsdp"),
        P("fsdp", None),
        P("fsdp", None),
    )
    return jax.shard_map(
        per_device,
        mesh=mesh,
        in_specs=placed,
        out_specs=(
            P("fsdp", "ctx", None),
            P("fsdp", "ctx", None),
            P("fsdp"),
            P("fsdp", None),
            P("fsdp", None),
            P("fsdp"),
            P("fsdp", None),
            P("fsdp", None),
            P("fsdp", None),
        ),
        check_vma=False,
    )
```

```python
import functools
import math
import jax
import jax.numpy as jnp
from jax import lax
from jax.experimental import pallas as pl
from jax.experimental.pallas import tpu as pltpu
from jax.sharding import PartitionSpec as P

HEAD_WIDTH = 64
norm_eps = 1e-05
masked_score = -1e30


def head_stack(rows_in, head_count):
    if head_count == 1:
        return rows_in
    lane_head = lax.broadcasted_iota(jnp.int32, rows_in.shape, 1) // HEAD_WIDTH
    zero = jnp.zeros_like(rows_in)
    return jnp.concatenate(
        [jnp.where(lane_head == h, rows_in, zero) for h in range(head_count)], axis=0
    )


def head_pick(stacked_t, head_count, block):
    return jnp.concatenate(
        [
            stacked_t[h * HEAD_WIDTH : (h + 1) * HEAD_WIDTH, h * block : (h + 1) * block]
            for h in range(head_count)
        ],
        axis=0,
    ).T


NT = (((1,), (1,)), ((), ()))


def forward_kernel(
    head_count, block_q, block_k, low_ref, high_ref, begin_ref, end_ref, qkv_ref, out_ref, log_ref, turned_ref
):
    width = out_ref.shape[1]
    step = pl.program_id(0)

    @pl.when(step == 0)
    def prepare():
        turned_ref[...] = qkv_ref[:, 2 * width :].astype(jnp.float32).T.astype(jnp.bfloat16)

    rows = pl.ds(pl.multiple_of(step * block_q, block_q), block_q)
    scale = 1.0 / math.sqrt(HEAD_WIDTH)
    stacked = head_stack(qkv_ref[rows, :width] * jnp.asarray(scale, jnp.bfloat16), head_count)
    begin = jnp.concatenate([begin_ref[:, rows]] * head_count, axis=1)
    end = jnp.concatenate([end_ref[:, rows]] * head_count, axis=1)

    def body(index, carried):
        top, total, acc = carried
        first = pl.multiple_of(index * block_k, block_k)
        keys = qkv_ref[pl.ds(first, block_k), width : 2 * width]
        scores = lax.dot_general(keys, stacked, NT, preferred_element_type=jnp.float32)
        place = first + lax.broadcasted_iota(jnp.int32, scores.shape, 0)
        scores = jnp.where((place >= begin) & (place < end), scores, masked_score)
        new_top = jnp.maximum(top, jnp.max(scores, axis=0, keepdims=True))
        fresh = jnp.exp(scores - new_top)
        fade = jnp.exp(top - new_top)
        total = total * fade + jnp.sum(fresh, axis=0, keepdims=True)
        acc = acc * fade + jnp.dot(
            turned_ref[:, pl.ds(first, block_k)],
            fresh.astype(jnp.bfloat16),
            preferred_element_type=jnp.float32,
        )
        return (new_top, total, acc)

    lanes = head_count * block_q
    top, total, acc = lax.fori_loop(
        low_ref[step],
        high_ref[step],
        body,
        (
            jnp.full((1, lanes), masked_score, jnp.float32),
            jnp.zeros((1, lanes), jnp.float32),
            jnp.zeros((width, lanes), jnp.float32),
        ),
    )
    valid = end > begin
    safe = jnp.where(valid, total, 1.0)
    acc = jnp.where(valid, acc / safe, 0.0)
    log_total = jnp.where(valid, top + jnp.log(safe), 0.0)
    out_ref[...] = head_pick(acc, head_count, block_q)
    log_ref[0] = log_total


def attention_forward(qkv, begin, end, low, high, head_count, block_q, block_k):
    tokens = qkv.shape[0]
    width = head_count * HEAD_WIDTH
    steps = tokens // block_q
    whole = lambda shape: pl.BlockSpec(shape, lambda i, *_: (0,) * len(shape))
    pairs = tokens * tokens // 4 * head_count
    return pl.pallas_call(
        functools.partial(forward_kernel, head_count, block_q, block_k),
        out_shape=(
            jax.ShapeDtypeStruct((tokens, width), jnp.float32),
            jax.ShapeDtypeStruct((steps, 1, head_count * block_q), jnp.float32),
        ),
        grid_spec=pltpu.PrefetchScalarGridSpec(
            num_scalar_prefetch=2,
            grid=(steps,),
            in_specs=[whole((1, tokens)), whole((1, tokens)), whole((tokens, 3 * width))],
            out_specs=(
                pl.BlockSpec((block_q, width), lambda i, *_: (i, 0)),
                pl.BlockSpec((1, 1, head_count * block_q), lambda i, *_: (i, 0, 0)),
            ),
            scratch_shapes=[pltpu.VMEM((width, tokens), jnp.bfloat16)],
        ),
        cost_estimate=pl.CostEstimate(
            flops=pairs * 512, bytes_accessed=tokens * width * 12, transcendentals=pairs
        ),
        name="attention_forward",
    )(low, high, begin, end, qkv)


def turn_back(grads, cosine, sine, head_count):
    half = HEAD_WIDTH // 2
    pieces = []
    for h in range(head_count):
        base = h * HEAD_WIDTH
        pieces += [grads[:, base + half : base + HEAD_WIDTH], grads[:, base : base + half]]
    return grads * cosine + jnp.concatenate(pieces, axis=1) * sine


def backward_kernel(
    head_count,
    block_q,
    block_k,
    low_ref,
    high_ref,
    begin_ref,
    end_ref,
    qkv_ref,
    attended_ref,
    grad_ref,
    log_ref,
    cosine_ref,
    sine_ref,
    out_ref,
    turned_ref,
    key_acc,
    value_acc,
):
    width = attended_ref.shape[1]
    step = pl.program_id(0)

    @pl.when(step == 0)
    def prepare():
        turned_ref[...] = qkv_ref[:, width : 2 * width].astype(jnp.float32).T.astype(jnp.bfloat16)
        key_acc[...] = jnp.zeros_like(key_acc)
        value_acc[...] = jnp.zeros_like(value_acc)

    rows = pl.ds(pl.multiple_of(step * block_q, block_q), block_q)
    scale = 1.0 / math.sqrt(HEAD_WIDTH)
    stacked = head_stack(qkv_ref[rows, :width] * jnp.asarray(scale, jnp.bfloat16), head_count)
    grads = grad_ref[rows, :]
    grad_stacked = head_stack(grads, head_count)
    begin = jnp.concatenate([begin_ref[:, rows]] * head_count, axis=1)
    end = jnp.concatenate([end_ref[:, rows]] * head_count, axis=1)
    product = (grads.astype(jnp.float32) * attended_ref[rows, :]).T
    delta = jnp.concatenate(
        [
            jnp.sum(product[h * HEAD_WIDTH : (h + 1) * HEAD_WIDTH], axis=0, keepdims=True)
            for h in range(head_count)
        ],
        axis=1,
    )
    log_total = log_ref[0]

    def body(index, acc):
        first = pl.multiple_of(index * block_k, block_k)
        span = pl.ds(first, block_k)
        keys = qkv_ref[span, width : 2 * width]
        values = qkv_ref[span, 2 * width :]
        scores = lax.dot_general(keys, stacked, NT, preferred_element_type=jnp.float32)
        grad_probs = lax.dot_general(values, grad_stacked, NT, preferred_element_type=jnp.float32)
        place = first + lax.broadcasted_iota(jnp.int32, scores.shape, 0)
        scores = jnp.where((place >= begin) & (place < end), scores, masked_score)
        probs = jnp.exp(scores - log_total)
        grad_scores = (probs * (grad_probs - delta)).astype(jnp.bfloat16)
        value_acc[span, :] += jnp.dot(
            probs.astype(jnp.bfloat16), grad_stacked, preferred_element_type=jnp.float32
        )
        key_acc[span, :] += jnp.dot(grad_scores, stacked, preferred_element_type=jnp.float32)
        return acc + jnp.dot(
            turned_ref[:, span], grad_scores, preferred_element_type=jnp.float32
        )

    acc = lax.fori_loop(
        low_ref[step],
        high_ref[step],
        body,
        jnp.zeros((width, head_count * block_q), jnp.float32),
    )
    grad_queries = head_pick(acc, head_count, block_q) * scale
    out_ref[rows, :width] = turn_back(
        grad_queries, cosine_ref[rows, :], sine_ref[rows, :], head_count
    ).astype(jnp.bfloat16)

    @pl.when(step == pl.num_programs(0) - 1)
    def finish():
        @pl.loop(0, pl.num_programs(0))
        def each(index):
            span = pl.ds(pl.multiple_of(index * block_q, block_q), block_q)
            out_ref[span, width : 2 * width] = turn_back(
                key_acc[span, :], cosine_ref[span, :], sine_ref[span, :], head_count
            ).astype(jnp.bfloat16)
            out_ref[span, 2 * width :] = value_acc[span, :].astype(jnp.bfloat16)


def attention_backward(
    qkv, attended, grads, log_total, begin, end, low, high, cosine, sine, head_count, block_q, block_k
):
    tokens = qkv.shape[0]
    width = head_count * HEAD_WIDTH
    steps = tokens // block_q
    whole = lambda shape: pl.BlockSpec(shape, lambda i, *_: (0,) * len(shape))
    pairs = tokens * tokens // 4 * head_count
    return pl.pallas_call(
        functools.partial(backward_kernel, head_count, block_q, block_k),
        out_shape=jax.ShapeDtypeStruct((tokens, 3 * width), jnp.bfloat16),
        grid_spec=pltpu.PrefetchScalarGridSpec(
            num_scalar_prefetch=2,
            grid=(steps,),
            in_specs=[
                whole((1, tokens)),
                whole((1, tokens)),
                whole((tokens, 3 * width)),
                whole((tokens, width)),
                whole((tokens, width)),
                pl.BlockSpec((1, 1, head_count * block_q), lambda i, *_: (i, 0, 0)),
                whole((tokens, width)),
                whole((tokens, width)),
            ],
            out_specs=whole((tokens, 3 * width)),
            scratch_shapes=[
                pltpu.VMEM((width, tokens), jnp.bfloat16),
                pltpu.VMEM((tokens, width), jnp.float32),
                pltpu.VMEM((tokens, width), jnp.float32),
            ],
        ),
        cost_estimate=pl.CostEstimate(
            flops=pairs * 1280, bytes_accessed=tokens * width * 30, transcendentals=pairs
        ),
        name="attention_backward",
    )(low, high, begin, end, qkv, attended, grads, log_total, cosine, sine)


def spans(places, lengths_row):
    ends = jnp.cumsum(lengths_row)
    past = (places[:, None] >= ends[None, :]).astype(jnp.int32)
    begin = jnp.sum(past * lengths_row[None, :], axis=1)
    before = (places[:, None] >= (ends - lengths_row)[None, :]).astype(jnp.int32)
    end = jnp.sum(before * lengths_row[None, :], axis=1)
    valid = places < ends[-1]
    return (jnp.where(valid, begin, 0), jnp.where(valid, end, 0), places - begin, valid)


def key_range(begin, end, block_q, block_k):
    begin_blocks = jnp.where(end > begin, begin, jnp.int32(1 << 30)).reshape(-1, block_q)
    high = (jnp.max(end.reshape(-1, block_q), axis=1) + block_k - 1) // block_k
    low = jnp.minimum(jnp.min(begin_blocks, axis=1) // block_k, high)
    return (low, high)


def rotary_tables(offset, head_count):
    half = HEAD_WIDTH // 2
    inverse = 160000.0 ** (-2.0 * jnp.arange(half, dtype=jnp.float32) / HEAD_WIDTH)
    angles = offset.astype(jnp.float32)[:, None] * inverse[None, :]
    cosine, sine = (jnp.cos(angles), jnp.sin(angles))
    return (
        jnp.concatenate([cosine, cosine] * head_count, axis=1),
        jnp.concatenate([sine, -sine] * head_count, axis=1),
    )


def toggled(index, bit):
    return index + bit - 2 * bit * ((index // bit) % 2)


def gather_kernel(shapes, *refs):
    count = len(shapes)
    shard_refs, full_refs = (refs[:count], refs[count : 2 * count])
    send_sem, recv_sem, local_sem = refs[2 * count :]
    shards = lax.axis_size("fsdp")
    slices = lax.axis_size("ctx") // 2
    own_ctx, own_shard = (lax.axis_index("ctx"), lax.axis_index("fsdp"))
    core, chip = (own_ctx % 2, own_ctx // 2)
    barrier = pltpu.get_barrier_semaphore()
    partners = [{"fsdp": toggled(own_shard, bit)} for bit in (1, 2)]
    partners += [{"ctx": toggled(own_ctx, bit)} for bit in (1, 2, 4)]
    for partner in partners:
        pl.semaphore_signal(
            barrier, inc=1, device_id=partner, device_id_type=pl.DeviceIdType.MESH
        )
    pl.semaphore_wait(barrier, len(partners))
    to_one, to_two, to_core, to_x, to_y = partners

    def shard_at(step):
        if step == 0:
            return own_shard
        if step == 3:
            return toggled(toggled(own_shard, 1), 2)
        return toggled(own_shard, step)

    def region(ref, weight, step, chip_at, half):
        if shapes[weight] == "small":
            return ref if len(ref.shape) == 2 else ref.at[shard_at(step)]
        if shapes[weight] == "rows":
            rows = ref.shape[-2]
            span = pl.ds(0, rows) if half is None else pl.ds(half * (rows // 2), rows // 2)
            if len(ref.shape) == 4:
                return ref.at[core, chip_at, span, :]
            return ref.at[shard_at(step), core, chip_at, span, :]
        rows = ref.shape[-2]
        first = (rows // 2) // 16 * 16
        spans_of = {None: pl.ds(0, rows), 0: pl.ds(0, first), 1: pl.ds(first, rows - first)}
        width = ref.shape[-1] // (2 * slices)
        columns = pl.ds(pl.multiple_of((core * slices + chip_at) * width, width), width)
        if len(ref.shape) == 2:
            return ref.at[spans_of[half], columns]
        return ref.at[shard_at(step), spans_of[half], columns]

    def core_region(ref, weight, step):
        if shapes[weight] == "rows":
            return ref.at[shard_at(step), core]
        width = ref.shape[-1] // 2
        return ref.at[shard_at(step), :, pl.ds(pl.multiple_of(core * width, width), width)]

    pending = []

    def send(source, target, slot, partner):
        copy = pltpu.make_async_remote_copy(
            src_ref=source,
            dst_ref=target,
            send_sem=send_sem.at[slot],
            recv_sem=recv_sem.at[slot],
            device_id=partner,
            device_id_type=pl.DeviceIdType.MESH,
        )
        copy.start()
        pending.append(copy)
        return copy

    copies = {}
    local = []

    def slot_of(weight, step, kind):
        return (weight * 3 + step - 1) * 8 + kind

    def shard_sends(weight):
        source = region(shard_refs[weight], weight, 0, chip, None)
        target = region(full_refs[weight], weight, 0, chip, None)
        copies[weight, 2, 0] = send(source, target, slot_of(weight, 2, 0), to_two)
        copies[weight, 1, 0] = send(source, target, slot_of(weight, 1, 0), to_one)
        target = full_refs[weight].at[own_shard]
        copy = pltpu.make_async_copy(shard_refs[weight], target, local_sem.at[weight])
        copy.start()
        local.append(copy)

    def shard_forward(weight):
        copies[weight, 2, 0].wait_recv()
        piece = region(full_refs[weight], weight, 2, chip, None)
        copies[weight, 3, 0] = send(piece, piece, slot_of(weight, 3, 0), to_one)

    def plane_sends(weight, step):
        lead = region(full_refs[weight], weight, step, chip, 0)
        rest = region(full_refs[weight], weight, step, chip, 1)
        for kind, piece, partner in ((1, lead, to_x), (2, rest, to_y), (3, lead, to_y), (4, rest, to_x)):
            copies[weight, step, kind] = send(piece, piece, slot_of(weight, step, kind), partner)

    def plane_forward(weight, step):
        copies[weight, step, 1].wait_recv()
        lead = region(full_refs[weight], weight, step, toggled(chip, 1), 0)
        copies[weight, step, 5] = send(lead, lead, slot_of(weight, step, 5), to_y)
        copies[weight, step, 2].wait_recv()
        rest = region(full_refs[weight], weight, step, toggled(chip, 2), 1)
        copies[weight, step, 6] = send(rest, rest, slot_of(weight, step, 6), to_x)

    def core_send(weight, step):
        for kind in (3, 4, 5, 6):
            copies[weight, step, kind].wait_recv()
        piece = core_region(full_refs[weight], weight, step)
        copies[weight, step, 7] = send(piece, piece, slot_of(weight, step, 7), to_core)

    shard_sends(0)
    for weight in range(count):
        if weight + 1 < count:
            shard_sends(weight + 1)
        shard_forward(weight)
        copies[weight, 1, 0].wait_recv()
        if shapes[weight] == "small":
            copies[weight, 3, 0].wait_recv()
            continue
        plane_sends(weight, 1)
        plane_sends(weight, 2)
        copies[weight, 3, 0].wait_recv()
        plane_sends(weight, 3)
        for step in (1, 2, 3):
            plane_forward(weight, step)
        if weight > 0 and shapes[weight - 1] != "small":
            for step in (1, 2, 3):
                core_send(weight - 1, step)
    for step in (1, 2, 3):
        core_send(count - 1, step)
    for weight in range(count):
        if shapes[weight] != "small":
            for step in (1, 2, 3):
                copies[weight, step, 7].wait_recv()
    for copy in pending:
        copy.wait_send()
    for copy in local:
        copy.wait()


def gather_weights(weights):
    shards, ctx_count = (lax.axis_size("fsdp"), lax.axis_size("ctx"))
    slices = ctx_count // 2
    shapes, views, outs = ([], [], [])
    for weight in weights:
        rows, columns = weight.shape
        if rows % (32 * ctx_count) == 0:
            shapes.append("rows")
            views.append(weight.reshape(2, slices, rows // ctx_count, columns))
            outs.append((shards, 2, slices, rows // ctx_count, columns))
        elif rows == 16:
            shapes.append("small")
            views.append(weight)
            outs.append((shards, rows, columns))
        elif columns % (128 * ctx_count) == 0 and rows % 16 == 0:
            shapes.append("columns")
            views.append(weight)
            outs.append((shards, rows, columns))
    if shards != 4 or ctx_count != 8 or len(views) < len(weights):
        return [lax.all_gather(weight, "fsdp", axis=0, tiled=True) for weight in weights]
    slots = len(views) * 24
    held = pl.pallas_call(
        functools.partial(gather_kernel, shapes),
        out_shape=tuple(jax.ShapeDtypeStruct(out, jnp.bfloat16) for out in outs),
        in_specs=[pl.BlockSpec(memory_space=pltpu.VMEM)] * len(views),
        out_specs=tuple(pl.BlockSpec(memory_space=pl.ANY) for out in outs),
        scratch_shapes=[
            pltpu.SemaphoreType.DMA((slots,)),
            pltpu.SemaphoreType.DMA((slots,)),
            pltpu.SemaphoreType.DMA((len(views),)),
        ],
        compiler_params=pltpu.CompilerParams(collective_id=0, has_side_effects=True),
        name="gather_weights",
    )(*views)
    return [whole.reshape(-1, whole.shape[-1]) for whole in held]


def sum_kernel(plan, lead_rows, *refs):
    weights = len(plan)
    left_refs, right_refs = (refs[:weights], refs[weights : 2 * weights])
    small_ref = refs[2 * weights]
    out_refs = refs[2 * weights + 1 : 3 * weights + 1]
    small_out = refs[3 * weights + 1]
    scratch = list(refs[3 * weights + 2 :])
    turned_refs = [scratch.pop(0) for weight in plan]
    whole_refs = [scratch.pop(0) for weight in plan]
    chunks = [(w, t) for w, (kind, count, width) in enumerate(plan) for t in range(count)]
    units = {}
    for number in range(len(chunks)):
        for half in (0, 1):
            units[number, half] = [scratch.pop(0) for stage in range(5)]
    small_held = scratch.pop(0)
    send_sem, recv_sem, local_sem, pair_send, pair_recv, small_send, small_recv, near_sem = scratch
    own_ctx, own_shard = (lax.axis_index("ctx"), lax.axis_index("fsdp"))
    core, chip = (own_ctx % 2, own_ctx // 2)
    own_x, own_y = (chip % 2, chip // 2)
    low_bit, high_bit = (own_shard % 2, own_shard // 2)
    partners = [{"ctx": toggled(own_ctx, bit)} for bit in (1, 2, 4)]
    partners += [{"fsdp": toggled(own_shard, bit)} for bit in (1, 2)]
    barrier = pltpu.get_barrier_semaphore()
    for partner in partners:
        pl.semaphore_signal(
            barrier, inc=1, device_id=partner, device_id_type=pl.DeviceIdType.MESH
        )
    pl.semaphore_wait(barrier, len(partners))
    to_core, to_x, to_y, to_one, to_two = partners
    pending = []

    def send(source, target, sent, got, partner):
        copy = pltpu.make_async_remote_copy(
            src_ref=source,
            dst_ref=target,
            send_sem=sent,
            recv_sem=got,
            device_id=partner,
            device_id_type=pl.DeviceIdType.MESH,
        )
        copy.start()
        pending.append(copy)
        return copy

    rows = left_refs[0].shape[-2]
    pairs = []
    for w, (kind, count, width) in enumerate(plan):
        span = count * width if kind == "rows" else 4 * width
        if len(right_refs[w].shape) == 3:
            own_half, other_half = (right_refs[w].at[core], right_refs[w].at[1 - core])
        else:
            own_half = right_refs[w].at[:, pl.ds(pl.multiple_of(core * span, span), span)]
            other_half = right_refs[w].at[:, pl.ds(pl.multiple_of((1 - core) * span, span), span)]
        near = pltpu.make_async_copy(own_half, whole_refs[w].at[pl.ds(0, rows)], near_sem.at[w])
        near.start()
        far = send(
            other_half,
            whole_refs[w].at[pl.ds(rows, rows)],
            pair_send.at[2 * w],
            pair_recv.at[2 * w],
            to_core,
        )
        pairs.append([near, far])

    def turn(w):
        left, turned = (left_refs[w], turned_refs[w])
        if len(left.shape) == 3:
            for z in range(left.shape[0]):
                turned[z, :, :rows] = left[z].astype(jnp.float32).T.astype(jnp.bfloat16)
        else:
            deep = left.shape[1] // 4
            for z in range(4):
                turned[z, :, :rows] = (
                    left[:, z * deep : (z + 1) * deep].astype(jnp.float32).T.astype(jnp.bfloat16)
                )

    def send_turned(w):
        pairs[w].append(
            send(
                turned_refs[w].at[:, :, pl.ds(0, rows)],
                turned_refs[w].at[:, :, pl.ds(rows, rows)],
                pair_send.at[2 * w + 1],
                pair_recv.at[2 * w + 1],
                to_core,
            )
        )

    copies = {}

    def hop(number, half, stage, source, target, partner):
        slot = (number * 2 + half) * 8 + stage
        copies[number, half, stage] = send(
            source, target, send_sem.at[slot], recv_sem.at[slot], partner
        )

    def product(number):
        w, t = chunks[number]
        kind, count, width = plan[w]
        if t == 0:
            near, far, turned = pairs[w]
            near.wait()
            far.wait_recv()
            turned.wait_recv()
        first, second = (units[number, 0][0], units[number, 1][0])

        def each(z, carried):
            if kind == "rows":
                part = jnp.dot(
                    turned_refs[w][z],
                    whole_refs[w][:, t * width : (t + 1) * width],
                    preferred_element_type=jnp.float32,
                ).astype(jnp.bfloat16)
                deep = first.shape[3]
                for s in range(4):
                    first[z, s // 2, s % 2] = part[2 * s * deep : (2 * s + 1) * deep]
                    second[z, s // 2, s % 2] = part[(2 * s + 1) * deep : (2 * s + 2) * deep]
            else:
                part = jnp.dot(
                    turned_refs[w][z], whole_refs[w][...], preferred_element_type=jnp.float32
                ).astype(jnp.bfloat16)
                column = first.shape[4]
                for s in range(4):
                    piece = part[:, s * column : (s + 1) * column]
                    first[z, s // 2, s % 2] = piece[:lead_rows]
                    second[z, s // 2, s % 2] = piece[lead_rows:]
            return carried

        lax.fori_loop(0, 4, each, 0)

    def stage_one(number):
        hop(number, 0, 0, units[number, 0][0].at[:, :, 1 - own_x], units[number, 0][1], to_x)
        hop(number, 1, 0, units[number, 1][0].at[:, 1 - own_y], units[number, 1][1], to_y)

    def add(target, source_at, count):
        def each(i, carried):
            target[i] = (
                target[i].astype(jnp.float32) + source_at(i).astype(jnp.float32)
            ).astype(jnp.bfloat16)
            return carried

        lax.fori_loop(0, count, each, 0)

    def stage_two(number):
        held, got = (units[number, 0][0], units[number, 0][1])
        copies[number, 0, 0].wait_recv()
        add(got, lambda z: held[z, :, own_x], 4)
        held_b, got_b = (units[number, 1][0], units[number, 1][1])
        copies[number, 1, 0].wait_recv()
        add(got_b, lambda z: held_b[z, own_y], 4)
        hop(number, 0, 1, got.at[:, 1 - own_y], units[number, 0][2], to_y)
        hop(number, 1, 1, got_b.at[:, 1 - own_x], units[number, 1][2], to_x)

    def stage_three(number):
        for half in (0, 1):
            held, got = (units[number, half][1], units[number, half][2])
            own = own_y if half == 0 else own_x
            copies[number, half, 1].wait_recv()
            add(got, lambda z: held[z, own], 4)
        for half in (0, 1):
            got = units[number, half][2]
            for high in (0, 1):
                hop(
                    number,
                    half,
                    2 + 4 * high,
                    got.at[2 * high + 1 - low_bit],
                    units[number, half][3].at[high],
                    to_one,
                )

    def stage_four(number):
        for half in (0, 1):
            held, got = (units[number, half][2], units[number, half][3])
            copies[number, half, 2].wait_recv()
            copies[number, half, 6].wait_recv()
            add(got, lambda high: held[2 * high + low_bit], 2)
        for half in (0, 1):
            got = units[number, half][3]
            hop(number, half, 3, got.at[1 - high_bit], units[number, half][4].at[0], to_two)

    def final_region(number, half, chip_at):
        w, t = chunks[number]
        kind, count, width = plan[w]
        deep = units[number, half][4].shape[1]
        if kind == "rows":
            start = pl.multiple_of((2 * chip_at + half) * deep, deep)
            column = pl.multiple_of((core * count + t) * width, width)
            return out_refs[w].at[pl.ds(start, deep), pl.ds(column, width)]
        column = pl.multiple_of((core * 4 + chip_at) * width, width)
        return out_refs[w].at[pl.ds(half * lead_rows, deep), pl.ds(column, width)]

    local = []

    def stage_five(number):
        for half in (0, 1):
            held, got = (units[number, half][3], units[number, half][4])
            copies[number, half, 3].wait_recv()
            add(got, lambda i: held[high_bit], 1)
        for half in (0, 1):
            got = units[number, half][4].at[0]
            target = final_region(number, half, chip)
            hop(number, half, 4, got, target, to_x if half == 0 else to_y)
            hop(number, half, 5, got, target, to_y if half == 0 else to_x)
            copy = pltpu.make_async_copy(got, target, local_sem.at[number * 2 + half])
            copy.start()
            local.append(copy)

    def stage_six(number):
        for half in (0, 1):
            copies[number, half, 4].wait_recv()
            piece = final_region(number, half, toggled(chip, 1 if half == 0 else 2))
            hop(number, half, 7, piece, piece, to_y if half == 0 else to_x)

    def stage_seven(number):
        w, t = chunks[number]
        kind, count, width = plan[w]
        for half in (0, 1):
            copies[number, half, 5].wait_recv()
            copies[number, half, 7].wait_recv()
            local[number * 2 + half].wait()
        span = width if kind == "rows" else 4 * width
        at = core * count + t if kind == "rows" else core
        piece = out_refs[w].at[:, pl.ds(pl.multiple_of(at * span, span), span)]
        slot = len(chunks) * 16 + number
        copies[number, 2, 0] = send(
            piece, piece, send_sem.at[slot], recv_sem.at[slot], to_core
        )

    small_copies = []

    def small_step(step):
        if step > 0:
            small_copies[step - 1].wait_recv()
            small_held[2 * step] = small_held[2 * step - 2] + small_held[2 * step - 1]
            if step == 3:
                small_out[0] = small_held[6]
        else:
            small_held[0] = small_ref[...]
        if step < 5:
            small_copies.append(
                send(
                    small_held.at[2 * step],
                    small_held.at[2 * step + 1],
                    small_send.at[step],
                    small_recv.at[step],
                    partners[step],
                )
            )
        else:
            small_out[1] = small_held[10]

    turn(0)
    for w in range(1, weights):
        turn(w)
        send_turned(w - 1)
    stages = [
        (stage_two, 1),
        (stage_three, 2),
        (stage_four, 3),
        (stage_five, 4),
        (stage_six, 5),
        (stage_seven, 6),
    ]
    small_at = 0
    for tick in range(len(chunks) + 7):
        if tick < len(chunks):
            product(tick)
            if tick == 0:
                send_turned(weights - 1)
            stage_one(tick)
        for stage, lag in stages:
            if 0 <= tick - lag < len(chunks):
                stage(tick - lag)
        if small_at < 6:
            small_step(small_at)
            small_at += 1
    for number in range(len(chunks)):
        copies[number, 2, 0].wait_recv()
    for copy in pending:
        copy.wait_send()


def sum_weights(products, small):
    rows = small.shape[0]
    plan, scratch, outs, lefts, rights, turned, whole, pieces = ([], [], [], [], [], [], [], [])
    lead_rows = 0
    for kind, left, right, count in products:
        tokens = left.shape[-2]
        if kind == "rows":
            deep = left.shape[1] // 4
            span = right.shape[-1] // (1 if right.ndim == 3 else 2)
            width = span // count
            outs.append(jax.ShapeDtypeStruct((deep, 2 * span), jnp.bfloat16))
            halves = (deep // 8, deep // 8)
        else:
            deep = left.shape[2]
            span = right.shape[-1] // 2
            width = span // 4
            lead_rows = deep // 2 // 16 * 16
            outs.append(jax.ShapeDtypeStruct((deep, 2 * span), jnp.bfloat16))
            halves = (lead_rows, deep - lead_rows)
        plan.append((kind, count, width))
        lefts.append(left)
        rights.append(right)
        turned.append(pltpu.VMEM((4, deep, 2 * tokens), jnp.bfloat16))
        whole.append(pltpu.VMEM((2 * tokens, span), jnp.bfloat16))
        for chunk in range(count):
            for deep_half in halves:
                for lead in ((4, 2, 2), (4, 2), (4,), (2,), (1,)):
                    pieces.append(pltpu.VMEM(lead + (deep_half, width), jnp.bfloat16))
    chunk_count = sum(count for kind, count, width in plan)
    scratch = turned + whole + pieces
    scratch += [pltpu.VMEM((11,) + small.shape, jnp.float32)]
    dma = pltpu.SemaphoreType.DMA
    slots = chunk_count * 17
    scratch += [dma((slots,)), dma((slots,)), dma((2 * chunk_count,))]
    scratch += [dma((2 * len(plan),)), dma((2 * len(plan),)), dma((5,)), dma((5,)), dma((len(plan),))]
    vmem, anywhere = (
        pl.BlockSpec(memory_space=pltpu.VMEM),
        pl.BlockSpec(memory_space=pl.ANY),
    )
    return pl.pallas_call(
        functools.partial(sum_kernel, plan, lead_rows),
        out_shape=tuple(outs) + (jax.ShapeDtypeStruct((2,) + small.shape, jnp.float32),),
        in_specs=[vmem] * len(plan) + [anywhere] * len(plan) + [vmem],
        out_specs=(anywhere,) * len(plan) + (vmem,),
        scratch_shapes=scratch,
        compiler_params=pltpu.CompilerParams(
            collective_id=1, has_side_effects=True, vmem_limit_bytes=60 * 1024 * 1024
        ),
        name="sum_weights",
    )(*lefts, *rights, small)


def layer_norm(rows_in, gain_vec):
    row_mean = jnp.mean(rows_in, axis=-1, keepdims=True)
    centred = rows_in - row_mean
    variance = jnp.mean(centred * centred, axis=-1, keepdims=True)
    return centred * lax.rsqrt(variance + norm_eps) * gain_vec


def rotate(projected, cosine, sine):
    row_count, width = projected.shape
    half_width = HEAD_WIDTH // 2
    by_head = projected.reshape(row_count, width // HEAD_WIDTH, HEAD_WIDTH)
    turned = jnp.concatenate([by_head[..., half_width:], by_head[..., :half_width]], axis=-1)
    return (by_head * cosine[:, None, :] - turned * sine[:, None, :]).reshape(row_count, width)


def swap(value, axis, bit):
    pairs = [(i, i ^ bit) for i in range(lax.axis_size(axis))]
    return lax.ppermute(value, axis, pairs)


def bit_of(axis, bit):
    return (lax.axis_index(axis) // bit) % 2 == 1


def bits_below(count):
    return [1 << i for i in range(count.bit_length() - 1)]


def reduce_pieces(pieces, labels, order):
    labels = list(labels)
    for axis, bit in order:
        at = labels.index((axis, bit))
        labels.pop(at)
        first = lax.index_in_dim(pieces, 0, at, keepdims=False)
        second = lax.index_in_dim(pieces, 1, at, keepdims=False)
        upper = bit_of(axis, bit)
        arrived = swap(jnp.where(upper, first, second), axis, bit)
        kept = jnp.where(upper, second, first)
        pieces = (kept.astype(jnp.float32) + arrived.astype(jnp.float32)).astype(jnp.bfloat16)
    return pieces


def gather_pieces(piece, labels, order):
    held = []
    for axis, bit in reversed(order):
        arrived = swap(piece, axis, bit)
        upper = bit_of(axis, bit)
        held = [label for label in labels if label in held or label == (axis, bit)]
        piece = jnp.stack(
            [jnp.where(upper, arrived, piece), jnp.where(upper, piece, arrived)],
            axis=held.index((axis, bit)),
        )
    return piece


def keep_and_send(first, second):
    upper = bit_of("ctx", 1)
    return (jnp.where(upper, second, first), jnp.where(upper, first, second))


def core_product(left, first, second):
    kept, sent = keep_and_send(first, second)
    left_all = jnp.concatenate([left, swap(left, "ctx", 1)], axis=0)
    right_all = jnp.concatenate([kept, swap(sent, "ctx", 1)], axis=0)
    return lax.dot_general(
        left_all, right_all, (((0,), (0,)), ((), ())), preferred_element_type=jnp.float32
    ).astype(jnp.bfloat16)


def shard_sum(product, by_columns):
    shards = lax.axis_size("fsdp")
    slices = lax.axis_size("ctx") // 2
    rows, columns = product.shape
    shard_labels = [("fsdp", bit) for bit in reversed(bits_below(shards))]
    slice_labels = [("ctx", 2 * bit) for bit in reversed(bits_below(slices))]
    if by_columns:
        cut = product.reshape(shards, rows // shards, slices, columns // slices)
        cut = jnp.transpose(cut, (0, 2, 1, 3))
    else:
        cut = product.reshape(shards, slices, rows // shards // slices, columns)
    parts = []
    half = cut.shape[2] // 2
    tail = list(reversed(shard_labels))
    for lead, orders in (
        (cut[:, :, :half], list(reversed(slice_labels))),
        (cut[:, :, half:], slice_labels),
    ):
        pieces = lead.reshape((2,) * (len(shard_labels) + len(slice_labels)) + lead.shape[2:])
        piece = reduce_pieces(pieces, shard_labels + slice_labels, orders + tail)
        whole = gather_pieces(piece, slice_labels, orders)
        parts.append(whole.reshape((slices,) + piece.shape))
    both = jnp.concatenate(parts, axis=1)
    if by_columns:
        return jnp.transpose(both, (1, 0, 2)).reshape(rows // shards, columns)
    return both.reshape(rows // shards, columns)


def join_cores(own):
    other = swap(own, "ctx", 1)
    upper = bit_of("ctx", 1)
    return jnp.concatenate(
        [jnp.where(upper, other, own), jnp.where(upper, own, other)], axis=1
    ).astype(jnp.float32)


def sum_over(value, axes):
    for axis in axes:
        for bit in bits_below(lax.axis_size(axis)):
            value = value + swap(value, axis, bit)
    return value


def own_shard(vector):
    width = vector.shape[0] // lax.axis_size("fsdp")
    return lax.dynamic_slice_in_dim(vector, lax.axis_index("fsdp") * width, width, 0)


def weight_sums(
    hidden,
    grad_mlp_low,
    act_mlp,
    grad_leading,
    grad_trailing,
    act_attn,
    grad_projected,
    attn_low,
    grad_attn_low,
    small,
):
    shards, ctx_count = (lax.axis_size("fsdp"), lax.axis_size("ctx"))
    rows, ff_width = hidden.shape
    model_width = act_mlp.shape[1]
    if shards != 4 or ctx_count != 8 or model_width % 1024 != 0 or ff_width % 64 != 0:
        half, half_three = (model_width // 2, 3 * model_width // 2)
        pairs = (
            (hidden, grad_mlp_low[:, :half], grad_mlp_low[:, half:]),
            (act_mlp, grad_leading, grad_trailing),
            (act_attn, grad_projected[:, :half_three], grad_projected[:, half_three:]),
            (attn_low, grad_attn_low[:, :half], grad_attn_low[:, half:]),
        )
        totals = [
            join_cores(shard_sum(core_product(*pair), at == 0)) for at, pair in enumerate(pairs)
        ]
        over_pack = sum_over(small, ("ctx",))
        return totals + [jnp.stack([over_pack, sum_over(over_pack, ("fsdp",))])]
    padded = -(-ff_width // 384) * 384
    sides = jnp.stack(
        [
            jnp.pad(side, ((0, 0), (0, padded - ff_width)))
            for side in (grad_leading, grad_trailing)
        ]
    )
    by_shard = jnp.transpose(hidden.reshape(rows, shards, ff_width // shards), (1, 0, 2))
    total_out, total_in, total_qkv, total_attn, small_sums = sum_weights(
        [
            ("columns", by_shard, grad_mlp_low, 1),
            ("rows", act_mlp, sides, 3),
            ("rows", act_attn, grad_projected, 3),
            ("rows", attn_low, grad_attn_low, 1),
        ],
        small,
    )
    total_in = jnp.concatenate(
        [total_in[:, :ff_width], total_in[:, padded : padded + ff_width]], axis=1
    )
    return [
        total.astype(jnp.float32) for total in (total_out, total_in, total_qkv, total_attn)
    ] + [small_sums]


def per_device(
    inputs,
    cotangent,
    lengths,
    piece_route,
    gain_one,
    qkv_weight,
    attn_out,
    gain_two,
    geglu_in,
    geglu_out,
):
    ctx_count = lax.axis_size("ctx")
    own_index = lax.axis_index("ctx")
    row_count = inputs.shape[1]
    model_width = inputs.shape[2]
    piece_rows = row_count // ctx_count
    tokens = row_count * ctx_count
    own_heads = model_width // HEAD_WIDTH // ctx_count
    own_width = own_heads * HEAD_WIDTH
    block_q = math.gcd(tokens, 256)
    block_k = math.gcd(tokens, 512)
    lengths_row = lengths[0]
    own_route = piece_route[0, 0]
    slot_ids = jnp.arange(ctx_count, dtype=jnp.int32)
    outgoing = jnp.sum(
        slot_ids[None, :] * (own_route[None, :] == slot_ids[:, None]).astype(jnp.int32), axis=1
    )

    def exchange(blocks):
        return lax.all_to_all(blocks, "ctx", split_axis=0, concat_axis=0, tiled=True)

    def to_slots(rows_in):
        return jnp.take(rows_in.reshape(ctx_count, piece_rows, model_width), outgoing, axis=0)

    def to_heads(rows_in):
        by_heads = rows_in.reshape(row_count, ctx_count, -1)
        return exchange(jnp.transpose(by_heads, (1, 0, 2))).reshape(tokens, -1)

    def to_rows(heads_in):
        return exchange(heads_in.reshape(ctx_count, row_count, -1))

    arrived = exchange(to_slots(inputs[0]))
    grad_arrived = exchange(to_slots(cotangent[0]))
    residual = arrived.reshape(row_count, model_width).astype(jnp.float32)
    places = own_index * row_count + jnp.arange(row_count, dtype=jnp.int32)
    unused_begin, unused_end, offset, is_valid = spans(places, lengths_row)
    pack_begin, pack_end, pack_offset, unused_valid = spans(
        jnp.arange(tokens, dtype=jnp.int32), lengths_row
    )
    grad_final = jnp.where(
        is_valid[:, None], grad_arrived.reshape(row_count, model_width).astype(jnp.float32), 0.0
    )
    gains = jnp.pad(jnp.stack([gain_one, gain_two]), ((0, 14), (0, 0)))
    gains_full, qkv_full, attn_full, in_full, out_full = gather_weights(
        [gains, qkv_weight, attn_out, geglu_in, geglu_out]
    )
    gains_full = gains_full.reshape(-1, 16, gains.shape[1])
    gain_attn = gains_full[:, 0].reshape(-1).astype(jnp.float32)
    gain_mlp = gains_full[:, 1].reshape(-1).astype(jnp.float32)
    act_attn = layer_norm(residual, gain_attn).astype(jnp.bfloat16)
    projected = jnp.dot(act_attn, qkv_full, preferred_element_type=jnp.float32)
    cosine, sine = rotary_tables(offset, 1)
    queries, keys = (
        rotate(projected[:, :model_width], cosine, sine).astype(jnp.bfloat16),
        rotate(projected[:, model_width : 2 * model_width], cosine, sine).astype(jnp.bfloat16),
    )
    values = projected[:, 2 * model_width :].astype(jnp.bfloat16)
    joined = jnp.stack(
        [part.reshape(row_count, ctx_count, own_width) for part in (queries, keys, values)], axis=2
    )
    qkv_heads = to_heads(joined.reshape(row_count, -1))
    low, high = key_range(pack_begin, pack_end, block_q, block_k)
    pack_begin, pack_end = (pack_begin[None, :], pack_end[None, :])
    attended_heads, log_total = attention_forward(
        qkv_heads, pack_begin, pack_end, low, high, own_heads, block_q, block_k
    )
    attn_low = jnp.transpose(to_rows(attended_heads.astype(jnp.bfloat16)), (1, 0, 2)).reshape(
        row_count, model_width
    )
    branch_attn = jnp.dot(attn_low, attn_full, preferred_element_type=jnp.float32)
    middle = residual + branch_attn
    act_mlp = layer_norm(middle, gain_mlp).astype(jnp.bfloat16)
    up_both = jnp.dot(act_mlp, in_full, preferred_element_type=jnp.float32)
    ff_width = up_both.shape[1] // 2
    hidden = (jax.nn.gelu(up_both[:, :ff_width], approximate=False) * up_both[:, ff_width:]).astype(
        jnp.bfloat16
    )
    branch_mlp = jnp.dot(hidden, out_full, preferred_element_type=jnp.float32)
    final_rows = jnp.where(is_valid[:, None], middle + branch_mlp, 0.0)
    square_sums = jnp.stack(
        [
            jnp.sum(final_rows * final_rows),
            jnp.sum(jnp.where(is_valid[:, None], branch_attn * branch_attn, 0.0)),
            jnp.sum(jnp.where(is_valid[:, None], branch_mlp * branch_mlp, 0.0)),
        ]
    )
    out_slots = final_rows.astype(jnp.bfloat16).reshape(ctx_count, piece_rows, model_width)
    back_out = exchange(out_slots)
    block_out = jnp.take(back_out, own_route, axis=0).reshape(1, row_count, model_width)
    grad_mlp_low = grad_final.astype(jnp.bfloat16)
    grad_hidden = lax.dot_general(
        grad_mlp_low, out_full, NT, preferred_element_type=jnp.float32
    )

    def gated(leading, trailing):
        return jax.nn.gelu(leading, approximate=False) * trailing

    unused_gate, gate_back = jax.vjp(gated, up_both[:, :ff_width], up_both[:, ff_width:])
    grad_leading, grad_trailing = gate_back(grad_hidden)
    grad_leading, grad_trailing = (
        grad_leading.astype(jnp.bfloat16),
        grad_trailing.astype(jnp.bfloat16),
    )
    grad_up = jnp.concatenate([grad_leading, grad_trailing], axis=1)
    grad_act_mlp = lax.dot_general(grad_up, in_full, NT, preferred_element_type=jnp.float32)
    unused_norm, norm_back_mlp = jax.vjp(layer_norm, middle, gain_mlp)
    grad_middle_norm, grad_gain_mlp = norm_back_mlp(grad_act_mlp)
    grad_middle = grad_final + grad_middle_norm
    grad_attn_low = grad_middle.astype(jnp.bfloat16)
    grad_attended = lax.dot_general(
        grad_attn_low, attn_full, NT, preferred_element_type=jnp.float32
    ).astype(jnp.bfloat16)
    pack_cosine, pack_sine = rotary_tables(pack_offset, own_heads)
    block_back = math.gcd(tokens, 256)
    low_back, high_back = key_range(pack_begin[0], pack_end[0], block_q, block_back)
    grad_heads = attention_backward(
        qkv_heads,
        attended_heads,
        to_heads(grad_attended),
        log_total,
        pack_begin,
        pack_end,
        low_back,
        high_back,
        pack_cosine,
        pack_sine,
        own_heads,
        block_q,
        block_back,
    )
    grad_projected = jnp.transpose(
        to_rows(grad_heads).reshape(ctx_count, row_count, 3, own_width), (1, 2, 0, 3)
    ).reshape(row_count, 3 * model_width)
    grad_act_attn = lax.dot_general(
        grad_projected, qkv_full, NT, preferred_element_type=jnp.float32
    )
    unused_first, norm_back_attn = jax.vjp(layer_norm, residual, gain_attn)
    grad_resid_norm, grad_gain_attn = norm_back_attn(grad_act_attn)
    grad_residual = (grad_middle + grad_resid_norm).astype(jnp.bfloat16)
    back_grad = exchange(grad_residual.reshape(ctx_count, piece_rows, model_width))
    grad_inputs = jnp.take(back_grad, own_route, axis=0).reshape(1, row_count, model_width)
    small = jnp.stack(
        [grad_gain_attn, grad_gain_mlp, jnp.pad(square_sums, (0, model_width - 3))]
        + [jnp.zeros((model_width,), jnp.float32)] * 5
    )
    total_out, total_in, total_qkv, total_attn, small_sums = weight_sums(
        hidden,
        grad_mlp_low,
        act_mlp,
        grad_leading,
        grad_trailing,
        act_attn,
        grad_projected,
        attn_low,
        grad_attn_low,
        small,
    )
    total_gain_one = own_shard(small_sums[1, 0])
    total_gain_two = own_shard(small_sums[1, 1])
    total_squares = small_sums[0, 2, :3]
    valid_count = jnp.sum(lengths_row).astype(jnp.float32)
    rms_stats = jnp.sqrt(total_squares / (valid_count * model_width))[None, :]
    return (
        block_out,
        grad_inputs,
        total_gain_one,
        total_qkv,
        total_attn,
        total_gain_two,
        total_in,
        total_out,
        rms_stats,
    )


def solution(mesh):
    placed = (
        P("fsdp", "ctx", None),
        P("fsdp", "ctx", None),
        P("fsdp", None),
        P("fsdp", "ctx", None),
        P("fsdp"),
        P("fsdp", None),
        P("fsdp", None),
        P("fsdp"),
        P("fsdp", None),
        P("fsdp", None),
    )
    return jax.shard_map(
        per_device,
        mesh=mesh,
        in_specs=placed,
        out_specs=(
            P("fsdp", "ctx", None),
            P("fsdp", "ctx", None),
            P("fsdp"),
            P("fsdp", None),
            P("fsdp", None),
            P("fsdp"),
            P("fsdp", None),
            P("fsdp", None),
            P("fsdp", None),
        ),
        check_vma=False,
    )
```

```python
import functools
import math
import jax
import jax.numpy as jnp
from jax import lax
from jax.experimental import pallas as pl
from jax.experimental.pallas import tpu as pltpu
from jax.sharding import PartitionSpec as P

HEAD_WIDTH = 64
norm_eps = 1e-05
masked_score = -1e30


def head_stack(rows_in, head_count):
    if head_count == 1:
        return rows_in
    lane_head = lax.broadcasted_iota(jnp.int32, rows_in.shape, 1) // HEAD_WIDTH
    zero = jnp.zeros_like(rows_in)
    return jnp.concatenate(
        [jnp.where(lane_head == h, rows_in, zero) for h in range(head_count)], axis=0
    )


def head_pick(stacked_t, head_count, block):
    return jnp.concatenate(
        [
            stacked_t[h * HEAD_WIDTH : (h + 1) * HEAD_WIDTH, h * block : (h + 1) * block]
            for h in range(head_count)
        ],
        axis=0,
    ).T


NT = (((1,), (1,)), ((), ()))


def forward_kernel(
    head_count, block_q, block_k, low_ref, high_ref, begin_ref, end_ref, qkv_ref, out_ref, log_ref, turned_ref
):
    width = out_ref.shape[1]
    step = pl.program_id(0)

    @pl.when(step == 0)
    def prepare():
        turned_ref[...] = qkv_ref[:, 2 * width :].astype(jnp.float32).T.astype(jnp.bfloat16)

    rows = pl.ds(pl.multiple_of(step * block_q, block_q), block_q)
    scale = 1.0 / math.sqrt(HEAD_WIDTH)
    stacked = head_stack(qkv_ref[rows, :width] * jnp.asarray(scale, jnp.bfloat16), head_count)
    begin = jnp.concatenate([begin_ref[:, rows]] * head_count, axis=1)
    end = jnp.concatenate([end_ref[:, rows]] * head_count, axis=1)

    def body(index, carried):
        top, total, acc = carried
        first = pl.multiple_of(index * block_k, block_k)
        keys = qkv_ref[pl.ds(first, block_k), width : 2 * width]
        scores = lax.dot_general(keys, stacked, NT, preferred_element_type=jnp.float32)
        place = first + lax.broadcasted_iota(jnp.int32, scores.shape, 0)
        scores = jnp.where((place >= begin) & (place < end), scores, masked_score)
        new_top = jnp.maximum(top, jnp.max(scores, axis=0, keepdims=True))
        fresh = jnp.exp(scores - new_top)
        fade = jnp.exp(top - new_top)
        total = total * fade + jnp.sum(fresh, axis=0, keepdims=True)
        acc = acc * fade + jnp.dot(
            turned_ref[:, pl.ds(first, block_k)],
            fresh.astype(jnp.bfloat16),
            preferred_element_type=jnp.float32,
        )
        return (new_top, total, acc)

    lanes = head_count * block_q
    top, total, acc = lax.fori_loop(
        low_ref[step],
        high_ref[step],
        body,
        (
            jnp.full((1, lanes), masked_score, jnp.float32),
            jnp.zeros((1, lanes), jnp.float32),
            jnp.zeros((width, lanes), jnp.float32),
        ),
    )
    valid = end > begin
    safe = jnp.where(valid, total, 1.0)
    acc = jnp.where(valid, acc / safe, 0.0)
    log_total = jnp.where(valid, top + jnp.log(safe), 0.0)
    out_ref[...] = head_pick(acc, head_count, block_q)
    log_ref[0] = log_total


def attention_forward(qkv, begin, end, low, high, head_count, block_q, block_k):
    tokens = qkv.shape[0]
    width = head_count * HEAD_WIDTH
    steps = tokens // block_q
    whole = lambda shape: pl.BlockSpec(shape, lambda i, *_: (0,) * len(shape))
    pairs = tokens * tokens // 4 * head_count
    return pl.pallas_call(
        functools.partial(forward_kernel, head_count, block_q, block_k),
        out_shape=(
            jax.ShapeDtypeStruct((tokens, width), jnp.float32),
            jax.ShapeDtypeStruct((steps, 1, head_count * block_q), jnp.float32),
        ),
        grid_spec=pltpu.PrefetchScalarGridSpec(
            num_scalar_prefetch=2,
            grid=(steps,),
            in_specs=[whole((1, tokens)), whole((1, tokens)), whole((tokens, 3 * width))],
            out_specs=(
                pl.BlockSpec((block_q, width), lambda i, *_: (i, 0)),
                pl.BlockSpec((1, 1, head_count * block_q), lambda i, *_: (i, 0, 0)),
            ),
            scratch_shapes=[pltpu.VMEM((width, tokens), jnp.bfloat16)],
        ),
        cost_estimate=pl.CostEstimate(
            flops=pairs * 512, bytes_accessed=tokens * width * 12, transcendentals=pairs
        ),
        name="attention_forward",
    )(low, high, begin, end, qkv)


def turn_back(grads, cosine, sine, head_count):
    half = HEAD_WIDTH // 2
    pieces = []
    for h in range(head_count):
        base = h * HEAD_WIDTH
        pieces += [grads[:, base + half : base + HEAD_WIDTH], grads[:, base : base + half]]
    return grads * cosine + jnp.concatenate(pieces, axis=1) * sine


def backward_kernel(
    head_count,
    block_q,
    block_k,
    low_ref,
    high_ref,
    begin_ref,
    end_ref,
    qkv_ref,
    attended_ref,
    grad_ref,
    log_ref,
    cosine_ref,
    sine_ref,
    out_ref,
    turned_ref,
    key_acc,
    value_acc,
):
    width = attended_ref.shape[1]
    step = pl.program_id(0)

    @pl.when(step == 0)
    def prepare():
        turned_ref[...] = qkv_ref[:, width : 2 * width].astype(jnp.float32).T.astype(jnp.bfloat16)
        key_acc[...] = jnp.zeros_like(key_acc)
        value_acc[...] = jnp.zeros_like(value_acc)

    rows = pl.ds(pl.multiple_of(step * block_q, block_q), block_q)
    scale = 1.0 / math.sqrt(HEAD_WIDTH)
    stacked = head_stack(qkv_ref[rows, :width] * jnp.asarray(scale, jnp.bfloat16), head_count)
    grads = grad_ref[rows, :]
    grad_stacked = head_stack(grads, head_count)
    begin = jnp.concatenate([begin_ref[:, rows]] * head_count, axis=1)
    end = jnp.concatenate([end_ref[:, rows]] * head_count, axis=1)
    product = (grads.astype(jnp.float32) * attended_ref[rows, :]).T
    delta = jnp.concatenate(
        [
            jnp.sum(product[h * HEAD_WIDTH : (h + 1) * HEAD_WIDTH], axis=0, keepdims=True)
            for h in range(head_count)
        ],
        axis=1,
    )
    log_total = log_ref[0]

    def body(index, acc):
        first = pl.multiple_of(index * block_k, block_k)
        span = pl.ds(first, block_k)
        keys = qkv_ref[span, width : 2 * width]
        values = qkv_ref[span, 2 * width :]
        scores = lax.dot_general(keys, stacked, NT, preferred_element_type=jnp.float32)
        grad_probs = lax.dot_general(values, grad_stacked, NT, preferred_element_type=jnp.float32)
        place = first + lax.broadcasted_iota(jnp.int32, scores.shape, 0)
        scores = jnp.where((place >= begin) & (place < end), scores, masked_score)
        probs = jnp.exp(scores - log_total)
        grad_scores = (probs * (grad_probs - delta)).astype(jnp.bfloat16)
        value_acc[span, :] += jnp.dot(
            probs.astype(jnp.bfloat16), grad_stacked, preferred_element_type=jnp.float32
        )
        key_acc[span, :] += jnp.dot(grad_scores, stacked, preferred_element_type=jnp.float32)
        return acc + jnp.dot(
            turned_ref[:, span], grad_scores, preferred_element_type=jnp.float32
        )

    acc = lax.fori_loop(
        low_ref[step],
        high_ref[step],
        body,
        jnp.zeros((width, head_count * block_q), jnp.float32),
    )
    grad_queries = head_pick(acc, head_count, block_q) * scale
    out_ref[rows, :width] = turn_back(
        grad_queries, cosine_ref[rows, :], sine_ref[rows, :], head_count
    ).astype(jnp.bfloat16)

    @pl.when(step == pl.num_programs(0) - 1)
    def finish():
        @pl.loop(0, pl.num_programs(0))
        def each(index):
            span = pl.ds(pl.multiple_of(index * block_q, block_q), block_q)
            out_ref[span, width : 2 * width] = turn_back(
                key_acc[span, :], cosine_ref[span, :], sine_ref[span, :], head_count
            ).astype(jnp.bfloat16)
            out_ref[span, 2 * width :] = value_acc[span, :].astype(jnp.bfloat16)


def attention_backward(
    qkv, attended, grads, log_total, begin, end, low, high, cosine, sine, head_count, block_q, block_k
):
    tokens = qkv.shape[0]
    width = head_count * HEAD_WIDTH
    steps = tokens // block_q
    whole = lambda shape: pl.BlockSpec(shape, lambda i, *_: (0,) * len(shape))
    pairs = tokens * tokens // 4 * head_count
    return pl.pallas_call(
        functools.partial(backward_kernel, head_count, block_q, block_k),
        out_shape=jax.ShapeDtypeStruct((tokens, 3 * width), jnp.bfloat16),
        grid_spec=pltpu.PrefetchScalarGridSpec(
            num_scalar_prefetch=2,
            grid=(steps,),
            in_specs=[
                whole((1, tokens)),
                whole((1, tokens)),
                whole((tokens, 3 * width)),
                whole((tokens, width)),
                whole((tokens, width)),
                pl.BlockSpec((1, 1, head_count * block_q), lambda i, *_: (i, 0, 0)),
                whole((tokens, width)),
                whole((tokens, width)),
            ],
            out_specs=whole((tokens, 3 * width)),
            scratch_shapes=[
                pltpu.VMEM((width, tokens), jnp.bfloat16),
                pltpu.VMEM((tokens, width), jnp.float32),
                pltpu.VMEM((tokens, width), jnp.float32),
            ],
        ),
        cost_estimate=pl.CostEstimate(
            flops=pairs * 1280, bytes_accessed=tokens * width * 30, transcendentals=pairs
        ),
        name="attention_backward",
    )(low, high, begin, end, qkv, attended, grads, log_total, cosine, sine)


def spans(places, lengths_row):
    ends = jnp.cumsum(lengths_row)
    past = (places[:, None] >= ends[None, :]).astype(jnp.int32)
    begin = jnp.sum(past * lengths_row[None, :], axis=1)
    before = (places[:, None] >= (ends - lengths_row)[None, :]).astype(jnp.int32)
    end = jnp.sum(before * lengths_row[None, :], axis=1)
    valid = places < ends[-1]
    return (jnp.where(valid, begin, 0), jnp.where(valid, end, 0), places - begin, valid)


def key_range(begin, end, block_q, block_k):
    begin_blocks = jnp.where(end > begin, begin, jnp.int32(1 << 30)).reshape(-1, block_q)
    high = (jnp.max(end.reshape(-1, block_q), axis=1) + block_k - 1) // block_k
    low = jnp.minimum(jnp.min(begin_blocks, axis=1) // block_k, high)
    return (low, high)


def rotary_tables(offset, head_count):
    half = HEAD_WIDTH // 2
    inverse = 160000.0 ** (-2.0 * jnp.arange(half, dtype=jnp.float32) / HEAD_WIDTH)
    angles = offset.astype(jnp.float32)[:, None] * inverse[None, :]
    cosine, sine = (jnp.cos(angles), jnp.sin(angles))
    return (
        jnp.concatenate([cosine, cosine] * head_count, axis=1),
        jnp.concatenate([sine, -sine] * head_count, axis=1),
    )


def toggled(index, bit):
    return index + bit - 2 * bit * ((index // bit) % 2)


def gather_kernel(shapes, projects, *refs):
    count = len(shapes)
    shard_refs, refs = (refs[:count], refs[count:])
    if projects:
        act_ref, qkv_ref, cosine_ref, sine_ref = refs[:4]
        heads_ref = refs[4 + count]
        columns_ref, held_ref, load_sem, head_send, head_recv, own_sem = refs[count + 8 :]
        refs = refs[4 : 4 + count] + refs[count + 5 : count + 8]
    full_refs = refs[:count]
    send_sem, recv_sem, local_sem = refs[count:]
    shards = lax.axis_size("fsdp")
    slices = lax.axis_size("ctx") // 2
    own_ctx, own_shard = (lax.axis_index("ctx"), lax.axis_index("fsdp"))
    core, chip = (own_ctx % 2, own_ctx // 2)
    barrier = pltpu.get_barrier_semaphore()
    partners = [{"fsdp": toggled(own_shard, bit)} for bit in (1, 2)]
    partners += [{"ctx": toggled(own_ctx, bit)} for bit in (1, 2, 4)]

    def owner_at(relation):
        owner = own_ctx
        for bit in (1, 2, 4):
            if relation & bit:
                owner = toggled(owner, bit)
        return owner

    if projects:
        partners += [{"ctx": owner_at(relation)} for relation in (3, 5, 6, 7)]
    for partner in partners:
        pl.semaphore_signal(
            barrier, inc=1, device_id=partner, device_id_type=pl.DeviceIdType.MESH
        )
    pl.semaphore_wait(barrier, len(partners))
    to_one, to_two, to_core, to_x, to_y = partners[:5]

    def shard_at(step):
        if step == 0:
            return own_shard
        if step == 3:
            return toggled(toggled(own_shard, 1), 2)
        return toggled(own_shard, step)

    def region(ref, weight, step, chip_at, half):
        if shapes[weight] == "small":
            return ref if len(ref.shape) == 2 else ref.at[shard_at(step)]
        if shapes[weight] == "rows":
            rows = ref.shape[-2]
            span = pl.ds(0, rows) if half is None else pl.ds(half * (rows // 2), rows // 2)
            if len(ref.shape) == 4:
                return ref.at[core, chip_at, span, :]
            return ref.at[shard_at(step), core, chip_at, span, :]
        rows = ref.shape[-2]
        first = (rows // 2) // 16 * 16
        spans_of = {None: pl.ds(0, rows), 0: pl.ds(0, first), 1: pl.ds(first, rows - first)}
        width = ref.shape[-1] // (2 * slices)
        columns = pl.ds(pl.multiple_of((core * slices + chip_at) * width, width), width)
        if len(ref.shape) == 2:
            return ref.at[spans_of[half], columns]
        return ref.at[shard_at(step), spans_of[half], columns]

    def core_region(ref, weight, step):
        if shapes[weight] == "rows":
            return ref.at[shard_at(step), core]
        width = ref.shape[-1] // 2
        return ref.at[shard_at(step), :, pl.ds(pl.multiple_of(core * width, width), width)]

    pending = []

    def send(source, target, slot, partner):
        copy = pltpu.make_async_remote_copy(
            src_ref=source,
            dst_ref=target,
            send_sem=send_sem.at[slot],
            recv_sem=recv_sem.at[slot],
            device_id=partner,
            device_id_type=pl.DeviceIdType.MESH,
        )
        copy.start()
        pending.append(copy)
        return copy

    copies = {}
    local = []

    def slot_of(weight, step, kind):
        return (weight * 3 + step - 1) * 8 + kind

    def shard_sends(weight):
        source = region(shard_refs[weight], weight, 0, chip, None)
        target = region(full_refs[weight], weight, 0, chip, None)
        copies[weight, 2, 0] = send(source, target, slot_of(weight, 2, 0), to_two)
        copies[weight, 1, 0] = send(source, target, slot_of(weight, 1, 0), to_one)
        target = full_refs[weight].at[own_shard]
        copy = pltpu.make_async_copy(shard_refs[weight], target, local_sem.at[weight])
        copy.start()
        local.append(copy)

    def shard_forward(weight):
        copies[weight, 2, 0].wait_recv()
        piece = region(full_refs[weight], weight, 2, chip, None)
        copies[weight, 3, 0] = send(piece, piece, slot_of(weight, 3, 0), to_one)

    def plane_sends(weight, step):
        lead = region(full_refs[weight], weight, step, chip, 0)
        rest = region(full_refs[weight], weight, step, chip, 1)
        for kind, piece, partner in ((1, lead, to_x), (2, rest, to_y), (3, lead, to_y), (4, rest, to_x)):
            copies[weight, step, kind] = send(piece, piece, slot_of(weight, step, kind), partner)

    def plane_forward(weight, step):
        copies[weight, step, 1].wait_recv()
        lead = region(full_refs[weight], weight, step, toggled(chip, 1), 0)
        copies[weight, step, 5] = send(lead, lead, slot_of(weight, step, 5), to_y)
        copies[weight, step, 2].wait_recv()
        rest = region(full_refs[weight], weight, step, toggled(chip, 2), 1)
        copies[weight, step, 6] = send(rest, rest, slot_of(weight, step, 6), to_x)

    def core_send(weight, step):
        for kind in (3, 4, 5, 6):
            copies[weight, step, kind].wait_recv()
        piece = core_region(full_refs[weight], weight, step)
        copies[weight, step, 7] = send(piece, piece, slot_of(weight, step, 7), to_core)

    chip_order = (3, 1, 2, 0)

    def start_loads():
        loads = {}
        for chip_bits in chip_order:
            owner_chip = owner_at(2 * chip_bits) // 2
            for part in range(3):
                width = columns_ref.shape[2] // 3
                total = qkv_ref.shape[1] // 3
                first = pl.multiple_of(part * total + owner_chip * width, width)
                loads[chip_bits, part] = pltpu.make_async_copy(
                    qkv_ref.at[:, pl.ds(first, width)],
                    columns_ref.at[chip_bits, :, pl.ds(part * width, width)],
                    load_sem.at[chip_bits * 3 + part],
                )
                loads[chip_bits, part].start()
        return loads

    def project(chip_bits, loads):
        for part in range(3):
            loads[chip_bits, part].wait()
        rows, own_width = (act_ref.shape[0], held_ref.shape[2] // 3)
        product = jnp.dot(
            act_ref[...], columns_ref[chip_bits], preferred_element_type=jnp.float32
        )
        for core_at in (0, 1):
            slot = 2 * chip_bits + core + core_at - 2 * core * core_at
            for part in range(3):
                first = (2 * part + core_at) * own_width
                piece = product[:, first : first + own_width]
                if part < 2:
                    half = HEAD_WIDTH // 2
                    turned = []
                    for base in range(0, own_width, HEAD_WIDTH):
                        turned += [piece[:, base + half : base + HEAD_WIDTH], piece[:, base : base + half]]
                    piece = piece * cosine_ref[...] - jnp.concatenate(turned, axis=1) * sine_ref[...]
                held_ref[slot, :, part * own_width : (part + 1) * own_width] = piece.astype(jnp.bfloat16)
        target = heads_ref.at[pl.ds(pl.multiple_of(own_ctx * rows, rows), rows), :]
        for core_bit in (0, 1):
            relation = 2 * chip_bits + core_bit
            if relation == 0:
                copy = pltpu.make_async_copy(held_ref.at[0], target, own_sem.at[0])
                copy.start()
                local.append(copy)
                continue
            copy = pltpu.make_async_remote_copy(
                src_ref=held_ref.at[relation],
                dst_ref=target,
                send_sem=head_send.at[relation],
                recv_sem=head_recv.at[relation],
                device_id={"ctx": owner_at(relation)},
                device_id_type=pl.DeviceIdType.MESH,
            )
            copy.start()
            pending.append(copy)
            arriving.append(copy)

    arriving = []
    sent = 1
    if projects:
        loads = start_loads()
        for weight in range(count):
            shard_sends(weight)
        sent = count
        for chip_bits in chip_order:
            project(chip_bits, loads)
    else:
        shard_sends(0)
    for weight in range(count):
        if weight + 1 >= sent and weight + 1 < count:
            shard_sends(weight + 1)
        shard_forward(weight)
        copies[weight, 1, 0].wait_recv()
        if shapes[weight] == "small":
            copies[weight, 3, 0].wait_recv()
            continue
        plane_sends(weight, 1)
        plane_sends(weight, 2)
        copies[weight, 3, 0].wait_recv()
        plane_sends(weight, 3)
        for step in (1, 2, 3):
            plane_forward(weight, step)
        if weight > 0 and shapes[weight - 1] != "small":
            for step in (1, 2, 3):
                core_send(weight - 1, step)
    for step in (1, 2, 3):
        core_send(count - 1, step)
    for weight in range(count):
        if shapes[weight] != "small":
            for step in (1, 2, 3):
                copies[weight, step, 7].wait_recv()
    for copy in arriving:
        copy.wait_recv()
    for copy in pending:
        copy.wait_send()
    for copy in local:
        copy.wait()


def gather_weights(weights, projection=None):
    shards, ctx_count = (lax.axis_size("fsdp"), lax.axis_size("ctx"))
    slices = ctx_count // 2
    shapes, views, outs = ([], [], [])
    for weight in weights:
        rows, columns = weight.shape
        if rows % (32 * ctx_count) == 0:
            shapes.append("rows")
            views.append(weight.reshape(2, slices, rows // ctx_count, columns))
            outs.append((shards, 2, slices, rows // ctx_count, columns))
        elif rows == 16:
            shapes.append("small")
            views.append(weight)
            outs.append((shards, rows, columns))
        elif columns % (128 * ctx_count) == 0 and rows % 16 == 0:
            shapes.append("columns")
            views.append(weight)
            outs.append((shards, rows, columns))
    if shards != 4 or ctx_count != 8 or len(views) < len(weights):
        return [lax.all_gather(weight, "fsdp", axis=0, tiled=True) for weight in weights]
    slots = len(views) * 24
    vmem, anywhere, dma = (
        pl.BlockSpec(memory_space=pltpu.VMEM),
        pl.BlockSpec(memory_space=pl.ANY),
        pltpu.SemaphoreType.DMA,
    )
    in_specs = [vmem] * len(views)
    scratch = [dma((slots,)), dma((slots,)), dma((len(views),))]
    if projection is not None:
        act_attn, qkv_full = projection[:2]
        rows, own_columns = (act_attn.shape[0], qkv_full.shape[1] // ctx_count)
        views += list(projection)
        in_specs += [vmem, anywhere, vmem, vmem]
        outs.append((ctx_count * rows, own_columns))
        scratch += [
            pltpu.VMEM((slices, qkv_full.shape[0], 2 * own_columns), jnp.bfloat16),
            pltpu.VMEM((ctx_count, rows, own_columns), jnp.bfloat16),
            dma((3 * slices,)),
            dma((ctx_count,)),
            dma((ctx_count,)),
            dma((1,)),
        ]
    held = pl.pallas_call(
        functools.partial(gather_kernel, shapes, projection is not None),
        out_shape=tuple(jax.ShapeDtypeStruct(out, jnp.bfloat16) for out in outs),
        in_specs=in_specs,
        out_specs=tuple(anywhere for out in outs),
        scratch_shapes=scratch,
        compiler_params=pltpu.CompilerParams(
            collective_id=0 if projection is None else 2,
            has_side_effects=True,
            vmem_limit_bytes=60 * 1024 * 1024,
        ),
        name="gather_weights" if projection is None else "gather_and_project",
    )(*views)
    return [whole.reshape(-1, whole.shape[-1]) for whole in held]


def sum_kernel(plan, lead_rows, *refs):
    weights = len(plan)
    left_refs, right_refs = (refs[:weights], refs[weights : 2 * weights])
    small_ref = refs[2 * weights]
    out_refs = refs[2 * weights + 1 : 3 * weights + 1]
    small_out = refs[3 * weights + 1]
    scratch = list(refs[3 * weights + 2 :])
    turned_refs = [scratch.pop(0) for weight in plan]
    whole_refs = [scratch.pop(0) for weight in plan]
    chunks = [(w, t) for w, (kind, count, width) in enumerate(plan) for t in range(count)]
    units = {}
    for number in range(len(chunks)):
        for half in (0, 1):
            units[number, half] = [scratch.pop(0) for stage in range(5)]
    small_held = scratch.pop(0)
    send_sem, recv_sem, local_sem, pair_send, pair_recv, small_send, small_recv, near_sem = scratch
    own_ctx, own_shard = (lax.axis_index("ctx"), lax.axis_index("fsdp"))
    core, chip = (own_ctx % 2, own_ctx // 2)
    own_x, own_y = (chip % 2, chip // 2)
    low_bit, high_bit = (own_shard % 2, own_shard // 2)
    partners = [{"ctx": toggled(own_ctx, bit)} for bit in (1, 2, 4)]
    partners += [{"fsdp": toggled(own_shard, bit)} for bit in (1, 2)]
    barrier = pltpu.get_barrier_semaphore()
    for partner in partners:
        pl.semaphore_signal(
            barrier, inc=1, device_id=partner, device_id_type=pl.DeviceIdType.MESH
        )
    pl.semaphore_wait(barrier, len(partners))
    to_core, to_x, to_y, to_one, to_two = partners
    pending = []

    def send(source, target, sent, got, partner):
        copy = pltpu.make_async_remote_copy(
            src_ref=source,
            dst_ref=target,
            send_sem=sent,
            recv_sem=got,
            device_id=partner,
            device_id_type=pl.DeviceIdType.MESH,
        )
        copy.start()
        pending.append(copy)
        return copy

    rows = left_refs[0].shape[-2]
    pairs = []
    for w, (kind, count, width) in enumerate(plan):
        span = count * width if kind == "rows" else 4 * width
        if len(right_refs[w].shape) == 3:
            own_half, other_half = (right_refs[w].at[core], right_refs[w].at[1 - core])
        else:
            own_half = right_refs[w].at[:, pl.ds(pl.multiple_of(core * span, span), span)]
            other_half = right_refs[w].at[:, pl.ds(pl.multiple_of((1 - core) * span, span), span)]
        near = pltpu.make_async_copy(own_half, whole_refs[w].at[pl.ds(0, rows)], near_sem.at[w])
        near.start()
        far = send(
            other_half,
            whole_refs[w].at[pl.ds(rows, rows)],
            pair_send.at[2 * w],
            pair_recv.at[2 * w],
            to_core,
        )
        pairs.append([near, far])

    def turn(w):
        left, turned = (left_refs[w], turned_refs[w])
        if len(left.shape) == 3:
            for z in range(left.shape[0]):
                turned[z, :, :rows] = left[z].astype(jnp.float32).T.astype(jnp.bfloat16)
        else:
            deep = left.shape[1] // 4
            for z in range(4):
                turned[z, :, :rows] = (
                    left[:, z * deep : (z + 1) * deep].astype(jnp.float32).T.astype(jnp.bfloat16)
                )

    def send_turned(w):
        pairs[w].append(
            send(
                turned_refs[w].at[:, :, pl.ds(0, rows)],
                turned_refs[w].at[:, :, pl.ds(rows, rows)],
                pair_send.at[2 * w + 1],
                pair_recv.at[2 * w + 1],
                to_core,
            )
        )

    copies = {}

    def hop(number, half, stage, source, target, partner):
        slot = (number * 2 + half) * 8 + stage
        copies[number, half, stage] = send(
            source, target, send_sem.at[slot], recv_sem.at[slot], partner
        )

    def product(number):
        w, t = chunks[number]
        kind, count, width = plan[w]
        if t == 0:
            near, far, turned = pairs[w]
            near.wait()
            far.wait_recv()
            turned.wait_recv()
        first, second = (units[number, 0][0], units[number, 1][0])

        def each(z, carried):
            if kind == "rows":
                part = jnp.dot(
                    turned_refs[w][z],
                    whole_refs[w][:, t * width : (t + 1) * width],
                    preferred_element_type=jnp.float32,
                ).astype(jnp.bfloat16)
                deep = first.shape[3]
                for s in range(4):
                    first[z, s // 2, s % 2] = part[2 * s * deep : (2 * s + 1) * deep]
                    second[z, s // 2, s % 2] = part[(2 * s + 1) * deep : (2 * s + 2) * deep]
            else:
                part = jnp.dot(
                    turned_refs[w][z], whole_refs[w][...], preferred_element_type=jnp.float32
                ).astype(jnp.bfloat16)
                column = first.shape[4]
                for s in range(4):
                    piece = part[:, s * column : (s + 1) * column]
                    first[z, s // 2, s % 2] = piece[:lead_rows]
                    second[z, s // 2, s % 2] = piece[lead_rows:]
            return carried

        lax.fori_loop(0, 4, each, 0)

    def stage_one(number):
        hop(number, 0, 0, units[number, 0][0].at[:, :, 1 - own_x], units[number, 0][1], to_x)
        hop(number, 1, 0, units[number, 1][0].at[:, 1 - own_y], units[number, 1][1], to_y)

    def add(target, source_at, count):
        def each(i, carried):
            target[i] = (
                target[i].astype(jnp.float32) + source_at(i).astype(jnp.float32)
            ).astype(jnp.bfloat16)
            return carried

        lax.fori_loop(0, count, each, 0)

    def stage_two(number):
        held, got = (units[number, 0][0], units[number, 0][1])
        copies[number, 0, 0].wait_recv()
        add(got, lambda z: held[z, :, own_x], 4)
        held_b, got_b = (units[number, 1][0], units[number, 1][1])
        copies[number, 1, 0].wait_recv()
        add(got_b, lambda z: held_b[z, own_y], 4)
        hop(number, 0, 1, got.at[:, 1 - own_y], units[number, 0][2], to_y)
        hop(number, 1, 1, got_b.at[:, 1 - own_x], units[number, 1][2], to_x)

    def stage_three(number):
        for half in (0, 1):
            held, got = (units[number, half][1], units[number, half][2])
            own = own_y if half == 0 else own_x
            copies[number, half, 1].wait_recv()
            add(got, lambda z: held[z, own], 4)
        for half in (0, 1):
            got = units[number, half][2]
            for high in (0, 1):
                hop(
                    number,
                    half,
                    2 + 4 * high,
                    got.at[2 * high + 1 - low_bit],
                    units[number, half][3].at[high],
                    to_one,
                )

    def stage_four(number):
        for half in (0, 1):
            held, got = (units[number, half][2], units[number, half][3])
            copies[number, half, 2].wait_recv()
            copies[number, half, 6].wait_recv()
            add(got, lambda high: held[2 * high + low_bit], 2)
        for half in (0, 1):
            got = units[number, half][3]
            hop(number, half, 3, got.at[1 - high_bit], units[number, half][4].at[0], to_two)

    def final_region(number, half, chip_at):
        w, t = chunks[number]
        kind, count, width = plan[w]
        deep = units[number, half][4].shape[1]
        if kind == "rows":
            start = pl.multiple_of((2 * chip_at + half) * deep, deep)
            column = pl.multiple_of((core * count + t) * width, width)
            return out_refs[w].at[pl.ds(start, deep), pl.ds(column, width)]
        column = pl.multiple_of((core * 4 + chip_at) * width, width)
        return out_refs[w].at[pl.ds(half * lead_rows, deep), pl.ds(column, width)]

    local = []

    def stage_five(number):
        for half in (0, 1):
            held, got = (units[number, half][3], units[number, half][4])
            copies[number, half, 3].wait_recv()
            add(got, lambda i: held[high_bit], 1)
        for half in (0, 1):
            got = units[number, half][4].at[0]
            target = final_region(number, half, chip)
            hop(number, half, 4, got, target, to_x if half == 0 else to_y)
            hop(number, half, 5, got, target, to_y if half == 0 else to_x)
            copy = pltpu.make_async_copy(got, target, local_sem.at[number * 2 + half])
            copy.start()
            local.append(copy)

    def stage_six(number):
        for half in (0, 1):
            copies[number, half, 4].wait_recv()
            piece = final_region(number, half, toggled(chip, 1 if half == 0 else 2))
            hop(number, half, 7, piece, piece, to_y if half == 0 else to_x)

    def stage_seven(number):
        w, t = chunks[number]
        kind, count, width = plan[w]
        for half in (0, 1):
            copies[number, half, 5].wait_recv()
            copies[number, half, 7].wait_recv()
            local[number * 2 + half].wait()
        span = width if kind == "rows" else 4 * width
        at = core * count + t if kind == "rows" else core
        piece = out_refs[w].at[:, pl.ds(pl.multiple_of(at * span, span), span)]
        slot = len(chunks) * 16 + number
        copies[number, 2, 0] = send(
            piece, piece, send_sem.at[slot], recv_sem.at[slot], to_core
        )

    small_copies = []

    def small_step(step):
        if step > 0:
            small_copies[step - 1].wait_recv()
            small_held[2 * step] = small_held[2 * step - 2] + small_held[2 * step - 1]
            if step == 3:
                small_out[0] = small_held[6]
        else:
            small_held[0] = small_ref[...]
        if step < 5:
            small_copies.append(
                send(
                    small_held.at[2 * step],
                    small_held.at[2 * step + 1],
                    small_send.at[step],
                    small_recv.at[step],
                    partners[step],
                )
            )
        else:
            small_out[1] = small_held[10]

    turn(0)
    for w in range(1, weights):
        turn(w)
        send_turned(w - 1)
    stages = [
        (stage_two, 1),
        (stage_three, 2),
        (stage_four, 3),
        (stage_five, 4),
        (stage_six, 5),
        (stage_seven, 6),
    ]
    small_at = 0
    for tick in range(len(chunks) + 7):
        if tick < len(chunks):
            product(tick)
            if tick == 0:
                send_turned(weights - 1)
            stage_one(tick)
        for stage, lag in stages:
            if 0 <= tick - lag < len(chunks):
                stage(tick - lag)
        if small_at < 6:
            small_step(small_at)
            small_at += 1
    for number in range(len(chunks)):
        copies[number, 2, 0].wait_recv()
    for copy in pending:
        copy.wait_send()


def sum_weights(products, small):
    rows = small.shape[0]
    plan, scratch, outs, lefts, rights, turned, whole, pieces = ([], [], [], [], [], [], [], [])
    lead_rows = 0
    for kind, left, right, count in products:
        tokens = left.shape[-2]
        if kind == "rows":
            deep = left.shape[1] // 4
            span = right.shape[-1] // (1 if right.ndim == 3 else 2)
            width = span // count
            outs.append(jax.ShapeDtypeStruct((deep, 2 * span), jnp.bfloat16))
            halves = (deep // 8, deep // 8)
        else:
            deep = left.shape[2]
            span = right.shape[-1] // 2
            width = span // 4
            lead_rows = deep // 2 // 16 * 16
            outs.append(jax.ShapeDtypeStruct((deep, 2 * span), jnp.bfloat16))
            halves = (lead_rows, deep - lead_rows)
        plan.append((kind, count, width))
        lefts.append(left)
        rights.append(right)
        turned.append(pltpu.VMEM((4, deep, 2 * tokens), jnp.bfloat16))
        whole.append(pltpu.VMEM((2 * tokens, span), jnp.bfloat16))
        for chunk in range(count):
            for deep_half in halves:
                for lead in ((4, 2, 2), (4, 2), (4,), (2,), (1,)):
                    pieces.append(pltpu.VMEM(lead + (deep_half, width), jnp.bfloat16))
    chunk_count = sum(count for kind, count, width in plan)
    scratch = turned + whole + pieces
    scratch += [pltpu.VMEM((11,) + small.shape, jnp.float32)]
    dma = pltpu.SemaphoreType.DMA
    slots = chunk_count * 17
    scratch += [dma((slots,)), dma((slots,)), dma((2 * chunk_count,))]
    scratch += [dma((2 * len(plan),)), dma((2 * len(plan),)), dma((5,)), dma((5,)), dma((len(plan),))]
    vmem, anywhere = (
        pl.BlockSpec(memory_space=pltpu.VMEM),
        pl.BlockSpec(memory_space=pl.ANY),
    )
    return pl.pallas_call(
        functools.partial(sum_kernel, plan, lead_rows),
        out_shape=tuple(outs) + (jax.ShapeDtypeStruct((2,) + small.shape, jnp.float32),),
        in_specs=[vmem] * len(plan) + [anywhere] * len(plan) + [vmem],
        out_specs=(anywhere,) * len(plan) + (vmem,),
        scratch_shapes=scratch,
        compiler_params=pltpu.CompilerParams(
            collective_id=1, has_side_effects=True, vmem_limit_bytes=60 * 1024 * 1024
        ),
        name="sum_weights",
    )(*lefts, *rights, small)


def layer_norm(rows_in, gain_vec):
    row_mean = jnp.mean(rows_in, axis=-1, keepdims=True)
    centred = rows_in - row_mean
    variance = jnp.mean(centred * centred, axis=-1, keepdims=True)
    return centred * lax.rsqrt(variance + norm_eps) * gain_vec


def rotate(projected, cosine, sine):
    row_count, width = projected.shape
    half_width = HEAD_WIDTH // 2
    by_head = projected.reshape(row_count, width // HEAD_WIDTH, HEAD_WIDTH)
    turned = jnp.concatenate([by_head[..., half_width:], by_head[..., :half_width]], axis=-1)
    return (by_head * cosine[:, None, :] - turned * sine[:, None, :]).reshape(row_count, width)


def swap(value, axis, bit):
    pairs = [(i, i ^ bit) for i in range(lax.axis_size(axis))]
    return lax.ppermute(value, axis, pairs)


def bit_of(axis, bit):
    return (lax.axis_index(axis) // bit) % 2 == 1


def bits_below(count):
    return [1 << i for i in range(count.bit_length() - 1)]


def reduce_pieces(pieces, labels, order):
    labels = list(labels)
    for axis, bit in order:
        at = labels.index((axis, bit))
        labels.pop(at)
        first = lax.index_in_dim(pieces, 0, at, keepdims=False)
        second = lax.index_in_dim(pieces, 1, at, keepdims=False)
        upper = bit_of(axis, bit)
        arrived = swap(jnp.where(upper, first, second), axis, bit)
        kept = jnp.where(upper, second, first)
        pieces = (kept.astype(jnp.float32) + arrived.astype(jnp.float32)).astype(jnp.bfloat16)
    return pieces


def gather_pieces(piece, labels, order):
    held = []
    for axis, bit in reversed(order):
        arrived = swap(piece, axis, bit)
        upper = bit_of(axis, bit)
        held = [label for label in labels if label in held or label == (axis, bit)]
        piece = jnp.stack(
            [jnp.where(upper, arrived, piece), jnp.where(upper, piece, arrived)],
            axis=held.index((axis, bit)),
        )
    return piece


def keep_and_send(first, second):
    upper = bit_of("ctx", 1)
    return (jnp.where(upper, second, first), jnp.where(upper, first, second))


def core_product(left, first, second):
    kept, sent = keep_and_send(first, second)
    left_all = jnp.concatenate([left, swap(left, "ctx", 1)], axis=0)
    right_all = jnp.concatenate([kept, swap(sent, "ctx", 1)], axis=0)
    return lax.dot_general(
        left_all, right_all, (((0,), (0,)), ((), ())), preferred_element_type=jnp.float32
    ).astype(jnp.bfloat16)


def shard_sum(product, by_columns):
    shards = lax.axis_size("fsdp")
    slices = lax.axis_size("ctx") // 2
    rows, columns = product.shape
    shard_labels = [("fsdp", bit) for bit in reversed(bits_below(shards))]
    slice_labels = [("ctx", 2 * bit) for bit in reversed(bits_below(slices))]
    if by_columns:
        cut = product.reshape(shards, rows // shards, slices, columns // slices)
        cut = jnp.transpose(cut, (0, 2, 1, 3))
    else:
        cut = product.reshape(shards, slices, rows // shards // slices, columns)
    parts = []
    half = cut.shape[2] // 2
    tail = list(reversed(shard_labels))
    for lead, orders in (
        (cut[:, :, :half], list(reversed(slice_labels))),
        (cut[:, :, half:], slice_labels),
    ):
        pieces = lead.reshape((2,) * (len(shard_labels) + len(slice_labels)) + lead.shape[2:])
        piece = reduce_pieces(pieces, shard_labels + slice_labels, orders + tail)
        whole = gather_pieces(piece, slice_labels, orders)
        parts.append(whole.reshape((slices,) + piece.shape))
    both = jnp.concatenate(parts, axis=1)
    if by_columns:
        return jnp.transpose(both, (1, 0, 2)).reshape(rows // shards, columns)
    return both.reshape(rows // shards, columns)


def join_cores(own):
    other = swap(own, "ctx", 1)
    upper = bit_of("ctx", 1)
    return jnp.concatenate(
        [jnp.where(upper, other, own), jnp.where(upper, own, other)], axis=1
    ).astype(jnp.float32)


def sum_over(value, axes):
    for axis in axes:
        for bit in bits_below(lax.axis_size(axis)):
            value = value + swap(value, axis, bit)
    return value


def own_shard(vector):
    width = vector.shape[0] // lax.axis_size("fsdp")
    return lax.dynamic_slice_in_dim(vector, lax.axis_index("fsdp") * width, width, 0)


def weight_sums(
    hidden,
    grad_mlp_low,
    act_mlp,
    grad_leading,
    grad_trailing,
    act_attn,
    grad_projected,
    attn_low,
    grad_attn_low,
    small,
):
    shards, ctx_count = (lax.axis_size("fsdp"), lax.axis_size("ctx"))
    rows, ff_width = hidden.shape
    model_width = act_mlp.shape[1]
    if shards != 4 or ctx_count != 8 or model_width % 1024 != 0 or ff_width % 64 != 0:
        half, half_three = (model_width // 2, 3 * model_width // 2)
        pairs = (
            (hidden, grad_mlp_low[:, :half], grad_mlp_low[:, half:]),
            (act_mlp, grad_leading, grad_trailing),
            (act_attn, grad_projected[:, :half_three], grad_projected[:, half_three:]),
            (attn_low, grad_attn_low[:, :half], grad_attn_low[:, half:]),
        )
        totals = [
            join_cores(shard_sum(core_product(*pair), at == 0)) for at, pair in enumerate(pairs)
        ]
        over_pack = sum_over(small, ("ctx",))
        return totals + [jnp.stack([over_pack, sum_over(over_pack, ("fsdp",))])]
    padded = -(-ff_width // 384) * 384
    sides = jnp.stack(
        [
            jnp.pad(side, ((0, 0), (0, padded - ff_width)))
            for side in (grad_leading, grad_trailing)
        ]
    )
    by_shard = jnp.transpose(hidden.reshape(rows, shards, ff_width // shards), (1, 0, 2))
    total_out, total_in, total_qkv, total_attn, small_sums = sum_weights(
        [
            ("columns", by_shard, grad_mlp_low, 1),
            ("rows", act_mlp, sides, 3),
            ("rows", act_attn, grad_projected, 3),
            ("rows", attn_low, grad_attn_low, 1),
        ],
        small,
    )
    total_in = jnp.concatenate(
        [total_in[:, :ff_width], total_in[:, padded : padded + ff_width]], axis=1
    )
    return [
        total.astype(jnp.float32) for total in (total_out, total_in, total_qkv, total_attn)
    ] + [small_sums]


def per_device(
    inputs,
    cotangent,
    lengths,
    piece_route,
    gain_one,
    qkv_weight,
    attn_out,
    gain_two,
    geglu_in,
    geglu_out,
):
    ctx_count = lax.axis_size("ctx")
    own_index = lax.axis_index("ctx")
    row_count = inputs.shape[1]
    model_width = inputs.shape[2]
    piece_rows = row_count // ctx_count
    tokens = row_count * ctx_count
    own_heads = model_width // HEAD_WIDTH // ctx_count
    own_width = own_heads * HEAD_WIDTH
    block_q = math.gcd(tokens, 256)
    block_k = math.gcd(tokens, 512)
    lengths_row = lengths[0]
    own_route = piece_route[0, 0]
    slot_ids = jnp.arange(ctx_count, dtype=jnp.int32)
    outgoing = jnp.sum(
        slot_ids[None, :] * (own_route[None, :] == slot_ids[:, None]).astype(jnp.int32), axis=1
    )

    def exchange(blocks):
        return lax.all_to_all(blocks, "ctx", split_axis=0, concat_axis=0, tiled=True)

    def to_slots(rows_in):
        return jnp.take(rows_in.reshape(ctx_count, piece_rows, model_width), outgoing, axis=0)

    def to_heads(rows_in):
        by_heads = rows_in.reshape(row_count, ctx_count, -1)
        return exchange(jnp.transpose(by_heads, (1, 0, 2))).reshape(tokens, -1)

    def to_rows(heads_in):
        return exchange(heads_in.reshape(ctx_count, row_count, -1))

    arrived = exchange(to_slots(inputs[0]))
    grad_arrived = exchange(to_slots(cotangent[0]))
    residual = arrived.reshape(row_count, model_width).astype(jnp.float32)
    places = own_index * row_count + jnp.arange(row_count, dtype=jnp.int32)
    unused_begin, unused_end, offset, is_valid = spans(places, lengths_row)
    pack_begin, pack_end, pack_offset, unused_valid = spans(
        jnp.arange(tokens, dtype=jnp.int32), lengths_row
    )
    grad_final = jnp.where(
        is_valid[:, None], grad_arrived.reshape(row_count, model_width).astype(jnp.float32), 0.0
    )
    gains = jnp.pad(jnp.stack([gain_one, gain_two]), ((0, 14), (0, 0)))
    gains_full, qkv_full = gather_weights([gains, qkv_weight])
    gains_full = gains_full.reshape(-1, 16, gains.shape[1])
    gain_attn = gains_full[:, 0].reshape(-1).astype(jnp.float32)
    gain_mlp = gains_full[:, 1].reshape(-1).astype(jnp.float32)
    act_attn = layer_norm(residual, gain_attn).astype(jnp.bfloat16)
    later = [attn_out, geglu_in, geglu_out]
    if lax.axis_size("fsdp") == 4 and ctx_count == 8 and own_width == 128:
        attn_full, in_full, out_full, qkv_heads = gather_weights(
            later, (act_attn, qkv_full) + rotary_tables(offset, own_heads)
        )
    else:
        attn_full, in_full, out_full = gather_weights(later)
        projected = jnp.dot(act_attn, qkv_full, preferred_element_type=jnp.float32)
        cosine, sine = rotary_tables(offset, 1)
        queries, keys = (
            rotate(projected[:, :model_width], cosine, sine).astype(jnp.bfloat16),
            rotate(projected[:, model_width : 2 * model_width], cosine, sine).astype(jnp.bfloat16),
        )
        values = projected[:, 2 * model_width :].astype(jnp.bfloat16)
        joined = jnp.stack(
            [part.reshape(row_count, ctx_count, own_width) for part in (queries, keys, values)], axis=2
        )
        qkv_heads = to_heads(joined.reshape(row_count, -1))
    low, high = key_range(pack_begin, pack_end, block_q, block_k)
    pack_begin, pack_end = (pack_begin[None, :], pack_end[None, :])
    attended_heads, log_total = attention_forward(
        qkv_heads, pack_begin, pack_end, low, high, own_heads, block_q, block_k
    )
    attn_low = jnp.transpose(to_rows(attended_heads.astype(jnp.bfloat16)), (1, 0, 2)).reshape(
        row_count, model_width
    )
    branch_attn = jnp.dot(attn_low, attn_full, preferred_element_type=jnp.float32)
    middle = residual + branch_attn
    act_mlp = layer_norm(middle, gain_mlp).astype(jnp.bfloat16)
    up_both = jnp.dot(act_mlp, in_full, preferred_element_type=jnp.float32)
    ff_width = up_both.shape[1] // 2
    hidden = (jax.nn.gelu(up_both[:, :ff_width], approximate=False) * up_both[:, ff_width:]).astype(
        jnp.bfloat16
    )
    branch_mlp = jnp.dot(hidden, out_full, preferred_element_type=jnp.float32)
    final_rows = jnp.where(is_valid[:, None], middle + branch_mlp, 0.0)
    square_sums = jnp.stack(
        [
            jnp.sum(final_rows * final_rows),
            jnp.sum(jnp.where(is_valid[:, None], branch_attn * branch_attn, 0.0)),
            jnp.sum(jnp.where(is_valid[:, None], branch_mlp * branch_mlp, 0.0)),
        ]
    )
    out_slots = final_rows.astype(jnp.bfloat16).reshape(ctx_count, piece_rows, model_width)
    back_out = exchange(out_slots)
    block_out = jnp.take(back_out, own_route, axis=0).reshape(1, row_count, model_width)
    grad_mlp_low = grad_final.astype(jnp.bfloat16)
    grad_hidden = lax.dot_general(
        grad_mlp_low, out_full, NT, preferred_element_type=jnp.float32
    )

    def gated(leading, trailing):
        return jax.nn.gelu(leading, approximate=False) * trailing

    unused_gate, gate_back = jax.vjp(gated, up_both[:, :ff_width], up_both[:, ff_width:])
    grad_leading, grad_trailing = gate_back(grad_hidden)
    grad_leading, grad_trailing = (
        grad_leading.astype(jnp.bfloat16),
        grad_trailing.astype(jnp.bfloat16),
    )
    grad_up = jnp.concatenate([grad_leading, grad_trailing], axis=1)
    grad_act_mlp = lax.dot_general(grad_up, in_full, NT, preferred_element_type=jnp.float32)
    unused_norm, norm_back_mlp = jax.vjp(layer_norm, middle, gain_mlp)
    grad_middle_norm, grad_gain_mlp = norm_back_mlp(grad_act_mlp)
    grad_middle = grad_final + grad_middle_norm
    grad_attn_low = grad_middle.astype(jnp.bfloat16)
    grad_attended = lax.dot_general(
        grad_attn_low, attn_full, NT, preferred_element_type=jnp.float32
    ).astype(jnp.bfloat16)
    pack_cosine, pack_sine = rotary_tables(pack_offset, own_heads)
    block_back = math.gcd(tokens, 256)
    low_back, high_back = key_range(pack_begin[0], pack_end[0], block_q, block_back)
    grad_heads = attention_backward(
        qkv_heads,
        attended_heads,
        to_heads(grad_attended),
        log_total,
        pack_begin,
        pack_end,
        low_back,
        high_back,
        pack_cosine,
        pack_sine,
        own_heads,
        block_q,
        block_back,
    )
    grad_projected = jnp.transpose(
        to_rows(grad_heads).reshape(ctx_count, row_count, 3, own_width), (1, 2, 0, 3)
    ).reshape(row_count, 3 * model_width)
    grad_act_attn = lax.dot_general(
        grad_projected, qkv_full, NT, preferred_element_type=jnp.float32
    )
    unused_first, norm_back_attn = jax.vjp(layer_norm, residual, gain_attn)
    grad_resid_norm, grad_gain_attn = norm_back_attn(grad_act_attn)
    grad_residual = (grad_middle + grad_resid_norm).astype(jnp.bfloat16)
    back_grad = exchange(grad_residual.reshape(ctx_count, piece_rows, model_width))
    grad_inputs = jnp.take(back_grad, own_route, axis=0).reshape(1, row_count, model_width)
    small = jnp.stack(
        [grad_gain_attn, grad_gain_mlp, jnp.pad(square_sums, (0, model_width - 3))]
        + [jnp.zeros((model_width,), jnp.float32)] * 5
    )
    total_out, total_in, total_qkv, total_attn, small_sums = weight_sums(
        hidden,
        grad_mlp_low,
        act_mlp,
        grad_leading,
        grad_trailing,
        act_attn,
        grad_projected,
        attn_low,
        grad_attn_low,
        small,
    )
    total_gain_one = own_shard(small_sums[1, 0])
    total_gain_two = own_shard(small_sums[1, 1])
    total_squares = small_sums[0, 2, :3]
    valid_count = jnp.sum(lengths_row).astype(jnp.float32)
    rms_stats = jnp.sqrt(total_squares / (valid_count * model_width))[None, :]
    return (
        block_out,
        grad_inputs,
        total_gain_one,
        total_qkv,
        total_attn,
        total_gain_two,
        total_in,
        total_out,
        rms_stats,
    )


def solution(mesh):
    placed = (
        P("fsdp", "ctx", None),
        P("fsdp", "ctx", None),
        P("fsdp", None),
        P("fsdp", "ctx", None),
        P("fsdp"),
        P("fsdp", None),
        P("fsdp", None),
        P("fsdp"),
        P("fsdp", None),
        P("fsdp", None),
    )
    return jax.shard_map(
        per_device,
        mesh=mesh,
        in_specs=placed,
        out_specs=(
            P("fsdp", "ctx", None),
            P("fsdp", "ctx", None),
            P("fsdp"),
            P("fsdp", None),
            P("fsdp", None),
            P("fsdp"),
            P("fsdp", None),
            P("fsdp", None),
            P("fsdp", None),
        ),
        check_vma=False,
    )
```

```python
import functools
import math
import jax
import jax.numpy as jnp
from jax import lax
from jax.experimental import pallas as pl
from jax.experimental.pallas import tpu as pltpu
from jax.sharding import PartitionSpec as P

HEAD_WIDTH = 64
norm_eps = 1e-05
masked_score = -1e30


def head_stack(rows_in, head_count):
    if head_count == 1:
        return rows_in
    lane_head = lax.broadcasted_iota(jnp.int32, rows_in.shape, 1) // HEAD_WIDTH
    zero = jnp.zeros_like(rows_in)
    return jnp.concatenate(
        [jnp.where(lane_head == h, rows_in, zero) for h in range(head_count)], axis=0
    )


def head_pick(stacked_t, head_count, block):
    return jnp.concatenate(
        [
            stacked_t[h * HEAD_WIDTH : (h + 1) * HEAD_WIDTH, h * block : (h + 1) * block]
            for h in range(head_count)
        ],
        axis=0,
    ).T


NT = (((1,), (1,)), ((), ()))


def forward_kernel(
    head_count, block_q, block_k, low_ref, high_ref, begin_ref, end_ref, qkv_ref, out_ref, log_ref, turned_ref
):
    width = out_ref.shape[1]
    step = pl.program_id(0)

    @pl.when(step == 0)
    def prepare():
        turned_ref[...] = qkv_ref[:, 2 * width :].astype(jnp.float32).T.astype(jnp.bfloat16)

    rows = pl.ds(pl.multiple_of(step * block_q, block_q), block_q)
    scale = 1.0 / math.sqrt(HEAD_WIDTH)
    stacked = head_stack(qkv_ref[rows, :width] * jnp.asarray(scale, jnp.bfloat16), head_count)
    begin = jnp.concatenate([begin_ref[:, rows]] * head_count, axis=1)
    end = jnp.concatenate([end_ref[:, rows]] * head_count, axis=1)

    def body(index, carried):
        top, total, acc = carried
        first = pl.multiple_of(index * block_k, block_k)
        keys = qkv_ref[pl.ds(first, block_k), width : 2 * width]
        scores = lax.dot_general(keys, stacked, NT, preferred_element_type=jnp.float32)
        place = first + lax.broadcasted_iota(jnp.int32, scores.shape, 0)
        scores = jnp.where((place >= begin) & (place < end), scores, masked_score)
        new_top = jnp.maximum(top, jnp.max(scores, axis=0, keepdims=True))
        fresh = jnp.exp(scores - new_top)
        fade = jnp.exp(top - new_top)
        total = total * fade + jnp.sum(fresh, axis=0, keepdims=True)
        acc = acc * fade + jnp.dot(
            turned_ref[:, pl.ds(first, block_k)],
            fresh.astype(jnp.bfloat16),
            preferred_element_type=jnp.float32,
        )
        return (new_top, total, acc)

    lanes = head_count * block_q
    top, total, acc = lax.fori_loop(
        low_ref[step],
        high_ref[step],
        body,
        (
            jnp.full((1, lanes), masked_score, jnp.float32),
            jnp.zeros((1, lanes), jnp.float32),
            jnp.zeros((width, lanes), jnp.float32),
        ),
    )
    valid = end > begin
    safe = jnp.where(valid, total, 1.0)
    acc = jnp.where(valid, acc / safe, 0.0)
    log_total = jnp.where(valid, top + jnp.log(safe), 0.0)
    out_ref[...] = head_pick(acc, head_count, block_q)
    log_ref[0] = log_total


def attention_forward(qkv, begin, end, low, high, head_count, block_q, block_k):
    tokens = qkv.shape[0]
    width = head_count * HEAD_WIDTH
    steps = tokens // block_q
    whole = lambda shape: pl.BlockSpec(shape, lambda i, *_: (0,) * len(shape))
    pairs = tokens * tokens // 4 * head_count
    return pl.pallas_call(
        functools.partial(forward_kernel, head_count, block_q, block_k),
        out_shape=(
            jax.ShapeDtypeStruct((tokens, width), jnp.float32),
            jax.ShapeDtypeStruct((steps, 1, head_count * block_q), jnp.float32),
        ),
        grid_spec=pltpu.PrefetchScalarGridSpec(
            num_scalar_prefetch=2,
            grid=(steps,),
            in_specs=[whole((1, tokens)), whole((1, tokens)), whole((tokens, 3 * width))],
            out_specs=(
                pl.BlockSpec((block_q, width), lambda i, *_: (i, 0)),
                pl.BlockSpec((1, 1, head_count * block_q), lambda i, *_: (i, 0, 0)),
            ),
            scratch_shapes=[pltpu.VMEM((width, tokens), jnp.bfloat16)],
        ),
        cost_estimate=pl.CostEstimate(
            flops=pairs * 512, bytes_accessed=tokens * width * 12, transcendentals=pairs
        ),
        name="attention_forward",
    )(low, high, begin, end, qkv)


def turn_back(grads, cosine, sine, head_count):
    half = HEAD_WIDTH // 2
    pieces = []
    for h in range(head_count):
        base = h * HEAD_WIDTH
        pieces += [grads[:, base + half : base + HEAD_WIDTH], grads[:, base : base + half]]
    return grads * cosine + jnp.concatenate(pieces, axis=1) * sine


def backward_kernel(
    head_count,
    block_q,
    block_k,
    low_ref,
    high_ref,
    begin_ref,
    end_ref,
    qkv_ref,
    attended_ref,
    grad_ref,
    log_ref,
    cosine_ref,
    sine_ref,
    *refs,
):
    out_ref, turned_ref, key_acc, value_acc = refs[-4:]
    width = attended_ref.shape[1]
    step = pl.program_id(0)

    @pl.when(step == 0)
    def prepare():
        turned_ref[...] = qkv_ref[:, width : 2 * width].astype(jnp.float32).T.astype(jnp.bfloat16)
        key_acc[...] = jnp.zeros_like(key_acc)
        value_acc[...] = jnp.zeros_like(value_acc)

    rows = pl.ds(pl.multiple_of(step * block_q, block_q), block_q)
    scale = 1.0 / math.sqrt(HEAD_WIDTH)
    stacked = head_stack(qkv_ref[rows, :width] * jnp.asarray(scale, jnp.bfloat16), head_count)
    grads = grad_ref[rows, :]
    grad_stacked = head_stack(grads, head_count)
    begin = jnp.concatenate([begin_ref[:, rows]] * head_count, axis=1)
    end = jnp.concatenate([end_ref[:, rows]] * head_count, axis=1)
    product = (grads.astype(jnp.float32) * attended_ref[rows, :]).T
    delta = jnp.concatenate(
        [
            jnp.sum(product[h * HEAD_WIDTH : (h + 1) * HEAD_WIDTH], axis=0, keepdims=True)
            for h in range(head_count)
        ],
        axis=1,
    )
    log_total = log_ref[0]

    def body(index, acc):
        first = pl.multiple_of(index * block_k, block_k)
        span = pl.ds(first, block_k)
        keys = qkv_ref[span, width : 2 * width]
        values = qkv_ref[span, 2 * width :]
        scores = lax.dot_general(keys, stacked, NT, preferred_element_type=jnp.float32)
        grad_probs = lax.dot_general(values, grad_stacked, NT, preferred_element_type=jnp.float32)
        place = first + lax.broadcasted_iota(jnp.int32, scores.shape, 0)
        scores = jnp.where((place >= begin) & (place < end), scores, masked_score)
        probs = jnp.exp(scores - log_total)
        grad_scores = (probs * (grad_probs - delta)).astype(jnp.bfloat16)
        value_acc[span, :] += jnp.dot(
            probs.astype(jnp.bfloat16), grad_stacked, preferred_element_type=jnp.float32
        )
        key_acc[span, :] += jnp.dot(grad_scores, stacked, preferred_element_type=jnp.float32)
        return acc + jnp.dot(
            turned_ref[:, span], grad_scores, preferred_element_type=jnp.float32
        )

    acc = lax.fori_loop(
        low_ref[step],
        high_ref[step],
        body,
        jnp.zeros((width, head_count * block_q), jnp.float32),
    )
    grad_queries = head_pick(acc, head_count, block_q) * scale
    out_ref[rows, :width] = turn_back(
        grad_queries, cosine_ref[rows, :], sine_ref[rows, :], head_count
    ).astype(jnp.bfloat16)

    @pl.when(step == pl.num_programs(0) - 1)
    def finish():
        @pl.loop(0, pl.num_programs(0))
        def each(index):
            span = pl.ds(pl.multiple_of(index * block_q, block_q), block_q)
            out_ref[span, width : 2 * width] = turn_back(
                key_acc[span, :], cosine_ref[span, :], sine_ref[span, :], head_count
            ).astype(jnp.bfloat16)
            out_ref[span, 2 * width :] = value_acc[span, :].astype(jnp.bfloat16)


def attention_backward(
    qkv, attended, grads, log_total, begin, end, low, high, cosine, sine, after, head_count, block_q, block_k
):
    tokens = qkv.shape[0]
    width = head_count * HEAD_WIDTH
    steps = tokens // block_q
    whole = lambda shape: pl.BlockSpec(shape, lambda i, *_: (0,) * len(shape))
    pairs = tokens * tokens // 4 * head_count
    return pl.pallas_call(
        functools.partial(backward_kernel, head_count, block_q, block_k),
        out_shape=jax.ShapeDtypeStruct((tokens, 3 * width), jnp.bfloat16),
        grid_spec=pltpu.PrefetchScalarGridSpec(
            num_scalar_prefetch=2,
            grid=(steps,),
            in_specs=[
                whole((1, tokens)),
                whole((1, tokens)),
                whole((tokens, 3 * width)),
                whole((tokens, width)),
                whole((tokens, width)),
                pl.BlockSpec((1, 1, head_count * block_q), lambda i, *_: (i, 0, 0)),
                whole((tokens, width)),
                whole((tokens, width)),
            ]
            + [pl.BlockSpec(memory_space=pl.ANY)] * len(after),
            out_specs=whole((tokens, 3 * width)),
            scratch_shapes=[
                pltpu.VMEM((width, tokens), jnp.bfloat16),
                pltpu.VMEM((tokens, width), jnp.float32),
                pltpu.VMEM((tokens, width), jnp.float32),
            ],
        ),
        cost_estimate=pl.CostEstimate(
            flops=pairs * 1280, bytes_accessed=tokens * width * 30, transcendentals=pairs
        ),
        name="attention_backward",
    )(low, high, begin, end, qkv, attended, grads, log_total, cosine, sine, *after)


def spans(places, lengths_row):
    ends = jnp.cumsum(lengths_row)
    past = (places[:, None] >= ends[None, :]).astype(jnp.int32)
    begin = jnp.sum(past * lengths_row[None, :], axis=1)
    before = (places[:, None] >= (ends - lengths_row)[None, :]).astype(jnp.int32)
    end = jnp.sum(before * lengths_row[None, :], axis=1)
    valid = places < ends[-1]
    return (jnp.where(valid, begin, 0), jnp.where(valid, end, 0), places - begin, valid)


def key_range(begin, end, block_q, block_k):
    begin_blocks = jnp.where(end > begin, begin, jnp.int32(1 << 30)).reshape(-1, block_q)
    high = (jnp.max(end.reshape(-1, block_q), axis=1) + block_k - 1) // block_k
    low = jnp.minimum(jnp.min(begin_blocks, axis=1) // block_k, high)
    return (low, high)


def rotary_tables(offset, head_count):
    half = HEAD_WIDTH // 2
    inverse = 160000.0 ** (-2.0 * jnp.arange(half, dtype=jnp.float32) / HEAD_WIDTH)
    angles = offset.astype(jnp.float32)[:, None] * inverse[None, :]
    cosine, sine = (jnp.cos(angles), jnp.sin(angles))
    return (
        jnp.concatenate([cosine, cosine] * head_count, axis=1),
        jnp.concatenate([sine, -sine] * head_count, axis=1),
    )


def toggled(index, bit):
    return index + bit - 2 * bit * ((index // bit) % 2)


def gather_kernel(shapes, projects, *refs):
    count = len(shapes)
    shard_refs, refs = (refs[:count], refs[count:])
    if projects:
        act_ref, qkv_ref, cosine_ref, sine_ref = refs[:4]
        heads_ref = refs[4 + count]
        columns_ref, held_ref, load_sem, head_send, head_recv, own_sem = refs[count + 8 :]
        refs = refs[4 : 4 + count] + refs[count + 5 : count + 8]
    full_refs = refs[:count]
    send_sem, recv_sem, local_sem = refs[count:]
    shards = lax.axis_size("fsdp")
    slices = lax.axis_size("ctx") // 2
    own_ctx, own_shard = (lax.axis_index("ctx"), lax.axis_index("fsdp"))
    core, chip = (own_ctx % 2, own_ctx // 2)
    barrier = pltpu.get_barrier_semaphore()
    partners = [{"fsdp": toggled(own_shard, bit)} for bit in (1, 2)]
    partners += [{"ctx": toggled(own_ctx, bit)} for bit in (1, 2, 4)]

    def owner_at(relation):
        owner = own_ctx
        for bit in (1, 2, 4):
            if relation & bit:
                owner = toggled(owner, bit)
        return owner

    if projects:
        partners += [{"ctx": owner_at(relation)} for relation in (3, 5, 6, 7)]
    for partner in partners:
        pl.semaphore_signal(
            barrier, inc=1, device_id=partner, device_id_type=pl.DeviceIdType.MESH
        )
    pl.semaphore_wait(barrier, len(partners))
    to_one, to_two, to_core, to_x, to_y = partners[:5]

    def shard_at(step):
        if step == 0:
            return own_shard
        if step == 3:
            return toggled(toggled(own_shard, 1), 2)
        return toggled(own_shard, step)

    def region(ref, weight, step, chip_at, half):
        if shapes[weight] == "small":
            return ref if len(ref.shape) == 2 else ref.at[shard_at(step)]
        if shapes[weight] == "rows":
            rows = ref.shape[-2]
            span = pl.ds(0, rows) if half is None else pl.ds(half * (rows // 2), rows // 2)
            if len(ref.shape) == 4:
                return ref.at[core, chip_at, span, :]
            return ref.at[shard_at(step), core, chip_at, span, :]
        rows = ref.shape[-2]
        first = (rows // 2) // 16 * 16
        spans_of = {None: pl.ds(0, rows), 0: pl.ds(0, first), 1: pl.ds(first, rows - first)}
        width = ref.shape[-1] // (2 * slices)
        columns = pl.ds(pl.multiple_of((core * slices + chip_at) * width, width), width)
        if len(ref.shape) == 2:
            return ref.at[spans_of[half], columns]
        return ref.at[shard_at(step), spans_of[half], columns]

    def core_region(ref, weight, step):
        if shapes[weight] == "rows":
            return ref.at[shard_at(step), core]
        width = ref.shape[-1] // 2
        return ref.at[shard_at(step), :, pl.ds(pl.multiple_of(core * width, width), width)]

    pending = []

    def send(source, target, slot, partner):
        copy = pltpu.make_async_remote_copy(
            src_ref=source,
            dst_ref=target,
            send_sem=send_sem.at[slot],
            recv_sem=recv_sem.at[slot],
            device_id=partner,
            device_id_type=pl.DeviceIdType.MESH,
        )
        copy.start()
        pending.append(copy)
        return copy

    copies = {}
    local = []

    def slot_of(weight, step, kind):
        return (weight * 3 + step - 1) * 8 + kind

    def shard_sends(weight):
        source = region(shard_refs[weight], weight, 0, chip, None)
        target = region(full_refs[weight], weight, 0, chip, None)
        copies[weight, 2, 0] = send(source, target, slot_of(weight, 2, 0), to_two)
        copies[weight, 1, 0] = send(source, target, slot_of(weight, 1, 0), to_one)
        target = full_refs[weight].at[own_shard]
        copy = pltpu.make_async_copy(shard_refs[weight], target, local_sem.at[weight])
        copy.start()
        local.append(copy)

    def shard_forward(weight):
        copies[weight, 2, 0].wait_recv()
        piece = region(full_refs[weight], weight, 2, chip, None)
        copies[weight, 3, 0] = send(piece, piece, slot_of(weight, 3, 0), to_one)

    def plane_sends(weight, step):
        lead = region(full_refs[weight], weight, step, chip, 0)
        rest = region(full_refs[weight], weight, step, chip, 1)
        for kind, piece, partner in ((1, lead, to_x), (2, rest, to_y), (3, lead, to_y), (4, rest, to_x)):
            copies[weight, step, kind] = send(piece, piece, slot_of(weight, step, kind), partner)

    def plane_forward(weight, step):
        copies[weight, step, 1].wait_recv()
        lead = region(full_refs[weight], weight, step, toggled(chip, 1), 0)
        copies[weight, step, 5] = send(lead, lead, slot_of(weight, step, 5), to_y)
        copies[weight, step, 2].wait_recv()
        rest = region(full_refs[weight], weight, step, toggled(chip, 2), 1)
        copies[weight, step, 6] = send(rest, rest, slot_of(weight, step, 6), to_x)

    def core_send(weight, step):
        for kind in (3, 4, 5, 6):
            copies[weight, step, kind].wait_recv()
        piece = core_region(full_refs[weight], weight, step)
        copies[weight, step, 7] = send(piece, piece, slot_of(weight, step, 7), to_core)

    chip_order = (3, 1, 2, 0)

    def start_loads():
        loads = {}
        for chip_bits in chip_order:
            owner_chip = owner_at(2 * chip_bits) // 2
            for part in range(3):
                width = columns_ref.shape[2] // 3
                total = qkv_ref.shape[1] // 3
                first = pl.multiple_of(part * total + owner_chip * width, width)
                loads[chip_bits, part] = pltpu.make_async_copy(
                    qkv_ref.at[:, pl.ds(first, width)],
                    columns_ref.at[chip_bits, :, pl.ds(part * width, width)],
                    load_sem.at[chip_bits * 3 + part],
                )
                loads[chip_bits, part].start()
        return loads

    def project(chip_bits, loads):
        for part in range(3):
            loads[chip_bits, part].wait()
        rows, own_width = (act_ref.shape[0], held_ref.shape[2] // 3)
        product = jnp.dot(
            act_ref[...], columns_ref[chip_bits], preferred_element_type=jnp.float32
        )
        for core_at in (0, 1):
            slot = 2 * chip_bits + core + core_at - 2 * core * core_at
            for part in range(3):
                first = (2 * part + core_at) * own_width
                piece = product[:, first : first + own_width]
                if part < 2:
                    half = HEAD_WIDTH // 2
                    turned = []
                    for base in range(0, own_width, HEAD_WIDTH):
                        turned += [piece[:, base + half : base + HEAD_WIDTH], piece[:, base : base + half]]
                    piece = piece * cosine_ref[...] - jnp.concatenate(turned, axis=1) * sine_ref[...]
                held_ref[slot, :, part * own_width : (part + 1) * own_width] = piece.astype(jnp.bfloat16)
        target = heads_ref.at[pl.ds(pl.multiple_of(own_ctx * rows, rows), rows), :]
        for core_bit in (0, 1):
            relation = 2 * chip_bits + core_bit
            if relation == 0:
                copy = pltpu.make_async_copy(held_ref.at[0], target, own_sem.at[0])
                copy.start()
                local.append(copy)
                continue
            copy = pltpu.make_async_remote_copy(
                src_ref=held_ref.at[relation],
                dst_ref=target,
                send_sem=head_send.at[relation],
                recv_sem=head_recv.at[relation],
                device_id={"ctx": owner_at(relation)},
                device_id_type=pl.DeviceIdType.MESH,
            )
            copy.start()
            pending.append(copy)
            arriving.append(copy)

    arriving = []
    sent = 1
    if projects:
        loads = start_loads()
        for weight in range(count):
            shard_sends(weight)
        sent = count
        for chip_bits in chip_order:
            project(chip_bits, loads)
    else:
        shard_sends(0)
    for weight in range(count):
        if weight + 1 >= sent and weight + 1 < count:
            shard_sends(weight + 1)
        shard_forward(weight)
        copies[weight, 1, 0].wait_recv()
        if shapes[weight] == "small":
            copies[weight, 3, 0].wait_recv()
            continue
        plane_sends(weight, 1)
        plane_sends(weight, 2)
        copies[weight, 3, 0].wait_recv()
        plane_sends(weight, 3)
        for step in (1, 2, 3):
            plane_forward(weight, step)
        if weight > 0 and shapes[weight - 1] != "small":
            for step in (1, 2, 3):
                core_send(weight - 1, step)
    for step in (1, 2, 3):
        core_send(count - 1, step)
    for weight in range(count):
        if shapes[weight] != "small":
            for step in (1, 2, 3):
                copies[weight, step, 7].wait_recv()
    for copy in arriving:
        copy.wait_recv()
    for copy in pending:
        copy.wait_send()
    for copy in local:
        copy.wait()


def gather_weights(weights, projection=None):
    shards, ctx_count = (lax.axis_size("fsdp"), lax.axis_size("ctx"))
    slices = ctx_count // 2
    shapes, views, outs = ([], [], [])
    for weight in weights:
        rows, columns = weight.shape
        if rows % (32 * ctx_count) == 0:
            shapes.append("rows")
            views.append(weight.reshape(2, slices, rows // ctx_count, columns))
            outs.append((shards, 2, slices, rows // ctx_count, columns))
        elif rows == 16:
            shapes.append("small")
            views.append(weight)
            outs.append((shards, rows, columns))
        elif columns % (128 * ctx_count) == 0 and rows % 16 == 0:
            shapes.append("columns")
            views.append(weight)
            outs.append((shards, rows, columns))
    if shards != 4 or ctx_count != 8 or len(views) < len(weights):
        return [lax.all_gather(weight, "fsdp", axis=0, tiled=True) for weight in weights]
    slots = len(views) * 24
    vmem, anywhere, dma = (
        pl.BlockSpec(memory_space=pltpu.VMEM),
        pl.BlockSpec(memory_space=pl.ANY),
        pltpu.SemaphoreType.DMA,
    )
    in_specs = [vmem] * len(views)
    scratch = [dma((slots,)), dma((slots,)), dma((len(views),))]
    if projection is not None:
        act_attn, qkv_full = projection[:2]
        rows, own_columns = (act_attn.shape[0], qkv_full.shape[1] // ctx_count)
        views += list(projection)
        in_specs += [vmem, anywhere, vmem, vmem]
        outs.append((ctx_count * rows, own_columns))
        scratch += [
            pltpu.VMEM((slices, qkv_full.shape[0], 2 * own_columns), jnp.bfloat16),
            pltpu.VMEM((ctx_count, rows, own_columns), jnp.bfloat16),
            dma((3 * slices,)),
            dma((ctx_count,)),
            dma((ctx_count,)),
            dma((1,)),
        ]
    held = pl.pallas_call(
        functools.partial(gather_kernel, shapes, projection is not None),
        out_shape=tuple(jax.ShapeDtypeStruct(out, jnp.bfloat16) for out in outs),
        in_specs=in_specs,
        out_specs=tuple(anywhere for out in outs),
        scratch_shapes=scratch,
        compiler_params=pltpu.CompilerParams(
            collective_id=0 if projection is None else 2,
            has_side_effects=True,
            vmem_limit_bytes=60 * 1024 * 1024,
        ),
        name="gather_weights" if projection is None else "gather_and_project",
    )(*views)
    return [whole.reshape(-1, whole.shape[-1]) for whole in held]


def pair_steps(plan, lead_rows, left_refs, right_refs, turned_refs, whole_refs, sems, core, send_core):
    pair_send, pair_recv, near_sem = sems
    rows = left_refs[0].shape[0] if left_refs else 0
    pairs = []
    for w, (kind, count, width, deep, halves) in enumerate(plan):
        span = count * width if kind == "rows" else 4 * width
        if len(right_refs[w].shape) == 3:
            own_half, other_half = (right_refs[w].at[core], right_refs[w].at[1 - core])
        else:
            own_half = right_refs[w].at[:, pl.ds(pl.multiple_of(core * span, span), span)]
            other_half = right_refs[w].at[:, pl.ds(pl.multiple_of((1 - core) * span, span), span)]
        near = pltpu.make_async_copy(own_half, whole_refs[w].at[pl.ds(0, rows)], near_sem.at[w])
        near.start()
        target = whole_refs[w].at[pl.ds(rows, rows)]
        far = send_core(other_half, target, pair_send.at[2 * w], pair_recv.at[2 * w])
        pairs.append([near, far])

    def turn(w):
        left, turned = (left_refs[w], turned_refs[w])
        block = 512
        for first in range(0, left.shape[1], block):
            last = min(first + block, left.shape[1])
            turned[first:last, :rows] = (
                left[:, first:last].astype(jnp.float32).T.astype(jnp.bfloat16)
            )
        pairs[w].append(
            send_core(
                turned.at[:, pl.ds(0, rows)],
                turned.at[:, pl.ds(rows, rows)],
                pair_send.at[2 * w + 1],
                pair_recv.at[2 * w + 1],
            )
        )

    def multiply(w, t, first, second):
        kind, count, width, deep, halves = plan[w]
        if t == 0:
            near, far, turned = pairs[w]
            near.wait()
            far.wait_recv()
            turned.wait_recv()

        def each(z, carried):
            left = turned_refs[w][pl.ds(pl.multiple_of(z * deep, 16), deep), :]
            if kind == "rows":
                part = jnp.dot(
                    left,
                    whole_refs[w][:, t * width : (t + 1) * width],
                    preferred_element_type=jnp.float32,
                ).astype(jnp.bfloat16)
                piece_rows = first.shape[3]
                for s in range(4):
                    first[z, s // 2, s % 2] = part[2 * s * piece_rows : (2 * s + 1) * piece_rows]
                    second[z, s // 2, s % 2] = part[(2 * s + 1) * piece_rows : (2 * s + 2) * piece_rows]
            else:
                part = jnp.dot(
                    left, whole_refs[w][...], preferred_element_type=jnp.float32
                ).astype(jnp.bfloat16)
                for s in range(4):
                    piece = part[:, s * width : (s + 1) * width]
                    first[z, s // 2, s % 2] = piece[:lead_rows]
                    second[z, s // 2, s % 2] = piece[lead_rows:]
            return carried

        lax.fori_loop(0, 4, each, 0)

    return (turn, multiply)


def remote_send(pending):
    def send(source, target, sent, got, partner):
        copy = pltpu.make_async_remote_copy(
            src_ref=source,
            dst_ref=target,
            send_sem=sent,
            recv_sem=got,
            device_id=partner,
            device_id_type=pl.DeviceIdType.MESH,
        )
        copy.start()
        pending.append(copy)
        return copy

    return send


def product_kernel(plan, lead_rows, *refs):
    weights = len(plan)
    left_refs, right_refs = (refs[:weights], refs[weights : 2 * weights])
    out_refs = refs[2 * weights : 6 * weights]
    scratch = list(refs[6 * weights :])
    turned_refs = [scratch.pop(0) for weight in plan]
    whole_refs = [scratch.pop(0) for weight in plan]
    chunks = [(w, t) for w, entry in enumerate(plan) for t in range(entry[1])]
    held = [(scratch.pop(0), scratch.pop(0)) for chunk in chunks]
    pair_send, pair_recv, near_sem, store_sem = scratch
    own_ctx = lax.axis_index("ctx")
    core, chip = (own_ctx % 2, own_ctx // 2)
    own_x, own_y = (chip % 2, chip // 2)
    to_core = {"ctx": toggled(own_ctx, 1)}
    barrier = pltpu.get_barrier_semaphore()
    pl.semaphore_signal(barrier, inc=1, device_id=to_core, device_id_type=pl.DeviceIdType.MESH)
    pl.semaphore_wait(barrier, 1)
    pending = []
    send = remote_send(pending)
    turn, multiply = pair_steps(
        plan,
        lead_rows,
        left_refs,
        right_refs,
        turned_refs,
        whole_refs,
        (pair_send, pair_recv, near_sem),
        core,
        lambda *copied: send(*copied, to_core),
    )
    for w in range(weights):
        turn(w)
    stores = []
    for number, (w, t) in enumerate(chunks):
        first, second = held[number]
        multiply(w, t, first, second)
        sides = (
            lambda at: first.at[:, at, own_x],
            lambda at: first.at[:, at, 1 - own_x],
            lambda at: second.at[:, own_y, at],
            lambda at: second.at[:, 1 - own_y, at],
        )
        for side, source_at in enumerate(sides):
            for at in (0, 1):
                copy = pltpu.make_async_copy(
                    source_at(at),
                    out_refs[4 * w + side].at[at, t],
                    store_sem.at[8 * number + 2 * side + at],
                )
                copy.start()
                stores.append(copy)
    for copy in stores:
        copy.wait()
    for copy in pending:
        copy.wait_send()


def weight_plan(kind, left, right, count):
    deep = left.shape[1] // 4
    if kind == "rows":
        span = right.shape[-1] // (1 if right.ndim == 3 else 2)
        return (kind, count, span // count, deep, (deep // 8, deep // 8))
    lead_rows = deep // 2 // 16 * 16
    return (kind, count, right.shape[-1] // 8, deep, (lead_rows, deep - lead_rows))


def plan_span(entry):
    return entry[1] * entry[2] if entry[0] == "rows" else 4 * entry[2]


def plan_lead(plan):
    return max([0] + [entry[4][0] for entry in plan if entry[0] == "columns"])


def pair_scratch(plan, tokens):
    turned = [pltpu.VMEM((4 * entry[3], 2 * tokens), jnp.bfloat16) for entry in plan]
    return turned + [pltpu.VMEM((2 * tokens, plan_span(entry)), jnp.bfloat16) for entry in plan]


def early_sums(products):
    plan = [weight_plan(*product) for product in products]
    lefts, rights = ([product[1] for product in products], [product[2] for product in products])
    vmem, anywhere, dma = (
        pl.BlockSpec(memory_space=pltpu.VMEM),
        pl.BlockSpec(memory_space=pl.ANY),
        pltpu.SemaphoreType.DMA,
    )
    outs, held = ([], [])
    for kind, count, width, deep, halves in plan:
        for half in halves:
            outs += [jax.ShapeDtypeStruct((2, count, 4, half, width), jnp.bfloat16)] * 2
        for chunk in range(count):
            held += [pltpu.VMEM((4, 2, 2, half, width), jnp.bfloat16) for half in halves]
    chunk_count = sum(entry[1] for entry in plan)
    scratch = pair_scratch(plan, lefts[0].shape[0]) + held
    scratch += [dma((2 * len(plan),)), dma((2 * len(plan),)), dma((len(plan),)), dma((8 * chunk_count,))]
    sides = pl.pallas_call(
        functools.partial(product_kernel, plan, plan_lead(plan)),
        out_shape=tuple(outs),
        in_specs=[vmem] * len(plan) + [anywhere] * len(plan),
        out_specs=(anywhere,) * len(outs),
        scratch_shapes=scratch,
        compiler_params=pltpu.CompilerParams(
            collective_id=3, has_side_effects=True, vmem_limit_bytes=60 * 1024 * 1024
        ),
        name="early_products",
    )(*lefts, *rights)
    arrays = []
    for w in range(len(plan)):
        for part, bit in ((0, 2), (2, 4)):
            kept, sent = sides[4 * w + part : 4 * w + part + 2]
            arrays.append((kept, swap(sent, "ctx", bit)))
    return (plan, arrays)


def second_step(held, early):
    plan, arrays = early
    held, arrays = lax.optimization_barrier((held, arrays))
    chip = lax.axis_index("ctx") // 2
    flat = []
    for at, (kept, arrived) in enumerate(arrays):
        bit, own = ((4, chip // 2), (2, chip % 2))[at % 2]
        other = [
            lax.dynamic_index_in_dim(side, 1 - own, 0, keepdims=False).astype(jnp.float32)
            for side in (kept, arrived)
        ]
        flat += [kept, arrived, swap((other[0] + other[1]).astype(jnp.bfloat16), "ctx", bit)]
    return (held, (plan, flat))


def sum_kernel(early, late, lead_rows, *refs):
    weights, products = (len(early) + len(late), len(late))
    left_refs, right_refs = (refs[:products], refs[products : 2 * products])
    refs = refs[2 * products :]
    early_refs, refs = (refs[: 6 * len(early)], refs[6 * len(early) :])
    small_ref, out_refs, small_out = (refs[0], refs[1 : weights + 1], refs[weights + 1])
    scratch = list(refs[weights + 2 :])
    turned_refs = [scratch.pop(0) for weight in late]
    whole_refs = [scratch.pop(0) for weight in late]
    plan = early + late
    chunks = [(w, t) for w, entry in enumerate(plan) for t in range(entry[1])]
    early_count = sum(entry[1] for entry in early)
    units = {}
    for number in range(len(chunks)):
        for half in (0, 1):
            units[number, half] = [scratch.pop(0) for stage in range(5)]
    small_held = scratch.pop(0)
    send_sem, recv_sem, local_sem, load_sem, pair_send, pair_recv, small_send, small_recv, near_sem = scratch
    own_ctx, own_shard = (lax.axis_index("ctx"), lax.axis_index("fsdp"))
    core, chip = (own_ctx % 2, own_ctx // 2)
    own_x, own_y = (chip % 2, chip // 2)
    low_bit, high_bit = (own_shard % 2, own_shard // 2)
    loads = {}
    for number in range(early_count):
        w, t = chunks[number]
        for half in (0, 1):
            own = own_y if half == 0 else own_x
            kept, arrived, twice = early_refs[6 * w + 3 * half : 6 * w + 3 * half + 3]
            for at, source in enumerate((kept.at[own, t], arrived.at[own, t], twice.at[t])):
                slot = (number * 2 + half) * 3 + at
                copy = pltpu.make_async_copy(source, units[number, half][at], load_sem.at[slot])
                copy.start()
                loads[number, half, at] = copy
    partners = [{"ctx": toggled(own_ctx, bit)} for bit in (1, 2, 4)]
    partners += [{"fsdp": toggled(own_shard, bit)} for bit in (1, 2)]
    barrier = pltpu.get_barrier_semaphore()
    for partner in partners:
        pl.semaphore_signal(
            barrier, inc=1, device_id=partner, device_id_type=pl.DeviceIdType.MESH
        )
    pl.semaphore_wait(barrier, len(partners))
    to_core, to_x, to_y, to_one, to_two = partners
    pending = []
    send = remote_send(pending)
    turn, multiply = pair_steps(
        late,
        lead_rows,
        left_refs,
        right_refs,
        turned_refs,
        whole_refs,
        (pair_send, pair_recv, near_sem),
        core,
        lambda *copied: send(*copied, to_core),
    )
    copies = {}

    def hop(number, half, stage, source, target, partner):
        slot = (number * 2 + half) * 8 + stage
        copies[number, half, stage] = send(
            source, target, send_sem.at[slot], recv_sem.at[slot], partner
        )

    def stage_one(number):
        w, t = chunks[number]
        multiply(w - len(early), t, units[number, 0][0], units[number, 1][0])
        hop(number, 0, 0, units[number, 0][0].at[:, :, 1 - own_x], units[number, 0][1], to_x)
        hop(number, 1, 0, units[number, 1][0].at[:, 1 - own_y], units[number, 1][1], to_y)

    def add(target, source_at, count):
        def each(i, carried):
            target[i] = (
                target[i].astype(jnp.float32) + source_at(i).astype(jnp.float32)
            ).astype(jnp.bfloat16)
            return carried

        lax.fori_loop(0, count, each, 0)

    def stage_two(number):
        held, got = (units[number, 0][0], units[number, 0][1])
        copies[number, 0, 0].wait_recv()
        add(got, lambda z: held[z, :, own_x], 4)
        held_b, got_b = (units[number, 1][0], units[number, 1][1])
        copies[number, 1, 0].wait_recv()
        add(got_b, lambda z: held_b[z, own_y], 4)
        hop(number, 0, 1, got.at[:, 1 - own_y], units[number, 0][2], to_y)
        hop(number, 1, 1, got_b.at[:, 1 - own_x], units[number, 1][2], to_x)

    def stage_three(number):
        for half in (0, 1):
            kept, held, got = units[number, half][:3]
            own = own_y if half == 0 else own_x
            if number < early_count:
                for at in range(3):
                    loads[number, half, at].wait()
                add(held, lambda z: kept[z], 4)
                add(got, lambda z: held[z], 4)
            else:
                copies[number, half, 1].wait_recv()
                add(got, lambda z: held[z, own], 4)
        for half in (0, 1):
            got = units[number, half][2]
            for high in (0, 1):
                hop(
                    number,
                    half,
                    2 + 4 * high,
                    got.at[2 * high + 1 - low_bit],
                    units[number, half][3].at[high],
                    to_one,
                )

    def stage_four(number):
        for half in (0, 1):
            held, got = (units[number, half][2], units[number, half][3])
            copies[number, half, 2].wait_recv()
            copies[number, half, 6].wait_recv()
            add(got, lambda high: held[2 * high + low_bit], 2)
        for half in (0, 1):
            got = units[number, half][3]
            hop(number, half, 3, got.at[1 - high_bit], units[number, half][4].at[0], to_two)

    def final_region(number, half, chip_at):
        w, t = chunks[number]
        kind, count, width = plan[w][:3]
        deep = units[number, half][4].shape[1]
        if kind == "rows":
            start = pl.multiple_of((2 * chip_at + half) * deep, deep)
            column = pl.multiple_of((core * count + t) * width, width)
            return out_refs[w].at[pl.ds(start, deep), pl.ds(column, width)]
        column = pl.multiple_of((core * 4 + chip_at) * width, width)
        return out_refs[w].at[pl.ds(half * lead_rows, deep), pl.ds(column, width)]

    local = {}

    def stage_five(number):
        for half in (0, 1):
            held, got = (units[number, half][3], units[number, half][4])
            copies[number, half, 3].wait_recv()
            add(got, lambda i: held[high_bit], 1)
        for half in (0, 1):
            got = units[number, half][4].at[0]
            target = final_region(number, half, chip)
            hop(number, half, 4, got, target, to_x if half == 0 else to_y)
            hop(number, half, 5, got, target, to_y if half == 0 else to_x)
            copy = pltpu.make_async_copy(got, target, local_sem.at[number * 2 + half])
            copy.start()
            local[number, half] = copy

    def stage_six(number):
        for half in (0, 1):
            copies[number, half, 4].wait_recv()
            piece = final_region(number, half, toggled(chip, 1 if half == 0 else 2))
            hop(number, half, 7, piece, piece, to_y if half == 0 else to_x)

    def stage_seven(number):
        w, t = chunks[number]
        kind, count, width = plan[w][:3]
        for half in (0, 1):
            copies[number, half, 5].wait_recv()
            copies[number, half, 7].wait_recv()
            local[number, half].wait()
        span = width if kind == "rows" else 4 * width
        at = core * count + t if kind == "rows" else core
        piece = out_refs[w].at[:, pl.ds(pl.multiple_of(at * span, span), span)]
        slot = len(chunks) * 16 + number
        copies[number, 2, 0] = send(
            piece, piece, send_sem.at[slot], recv_sem.at[slot], to_core
        )

    small_copies = []

    def small_step(step):
        if step > 0:
            small_copies[step - 1].wait_recv()
            small_held[2 * step] = small_held[2 * step - 2] + small_held[2 * step - 1]
            if step == 3:
                small_out[0] = small_held[6]
        else:
            small_held[0] = small_ref[...]
        if step < 5:
            small_copies.append(
                send(
                    small_held.at[2 * step],
                    small_held.at[2 * step + 1],
                    small_send.at[step],
                    small_recv.at[step],
                    partners[step],
                )
            )
        else:
            small_out[1] = small_held[10]

    stages = (stage_one, stage_two, stage_three, stage_four, stage_five, stage_six, stage_seven)
    small_at = 0
    stage_three(0)
    for w in range(len(late)):
        turn(w)
    for tick in range(len(chunks) + len(stages)):
        for lag, stage in enumerate(stages):
            for number in range(len(chunks)):
                start = number - 2 if number < early_count else number - early_count
                if start + lag == tick and (number >= early_count or (lag >= 2 and number + lag > 2)):
                    stage(number)
        if small_at < 6:
            small_step(small_at)
            small_at += 1
    for number in range(len(chunks)):
        copies[number, 2, 0].wait_recv()
    for copy in pending:
        copy.wait_send()


def sum_weights(early, early_arrays, products, small):
    late = [weight_plan(*product) for product in products]
    lefts, rights = ([product[1] for product in products], [product[2] for product in products])
    plan = early + late
    pieces = []
    for w, (kind, count, width, deep, halves) in enumerate(plan):
        leads = [(4, 2, 2), (4, 2), (4,), (2,), (1,)]
        if w < len(early):
            leads[:2] = [(4,), (4,)]
        for chunk in range(count):
            for half in halves:
                pieces += [pltpu.VMEM(lead + (half, width), jnp.bfloat16) for lead in leads]
    outs = [jax.ShapeDtypeStruct((entry[3], 2 * plan_span(entry)), jnp.bfloat16) for entry in plan]
    chunk_count = sum(entry[1] for entry in plan)
    scratch = pair_scratch(late, lefts[0].shape[0]) + pieces
    scratch += [pltpu.VMEM((11,) + small.shape, jnp.float32)]
    dma = pltpu.SemaphoreType.DMA
    slots = chunk_count * 17
    scratch += [dma((slots,)), dma((slots,)), dma((2 * chunk_count,)), dma((6 * chunk_count,))]
    scratch += [dma((2 * len(late),)), dma((2 * len(late),)), dma((5,)), dma((5,)), dma((len(late),))]
    vmem, anywhere = (
        pl.BlockSpec(memory_space=pltpu.VMEM),
        pl.BlockSpec(memory_space=pl.ANY),
    )
    return pl.pallas_call(
        functools.partial(sum_kernel, early, late, plan_lead(plan)),
        out_shape=tuple(outs) + (jax.ShapeDtypeStruct((2,) + small.shape, jnp.float32),),
        in_specs=[vmem] * len(late) + [anywhere] * (len(late) + len(early_arrays)) + [vmem],
        out_specs=(anywhere,) * len(plan) + (vmem,),
        scratch_shapes=scratch,
        compiler_params=pltpu.CompilerParams(
            collective_id=1, has_side_effects=True, vmem_limit_bytes=60 * 1024 * 1024
        ),
        name="sum_weights",
    )(*lefts, *rights, *early_arrays, small)


def layer_norm(rows_in, gain_vec):
    row_mean = jnp.mean(rows_in, axis=-1, keepdims=True)
    centred = rows_in - row_mean
    variance = jnp.mean(centred * centred, axis=-1, keepdims=True)
    return centred * lax.rsqrt(variance + norm_eps) * gain_vec


def rotate(projected, cosine, sine):
    row_count, width = projected.shape
    half_width = HEAD_WIDTH // 2
    by_head = projected.reshape(row_count, width // HEAD_WIDTH, HEAD_WIDTH)
    turned = jnp.concatenate([by_head[..., half_width:], by_head[..., :half_width]], axis=-1)
    return (by_head * cosine[:, None, :] - turned * sine[:, None, :]).reshape(row_count, width)


def swap(value, axis, bit):
    pairs = [(i, i ^ bit) for i in range(lax.axis_size(axis))]
    return lax.ppermute(value, axis, pairs)


def bit_of(axis, bit):
    return (lax.axis_index(axis) // bit) % 2 == 1


def bits_below(count):
    return [1 << i for i in range(count.bit_length() - 1)]


def reduce_pieces(pieces, labels, order):
    labels = list(labels)
    for axis, bit in order:
        at = labels.index((axis, bit))
        labels.pop(at)
        first = lax.index_in_dim(pieces, 0, at, keepdims=False)
        second = lax.index_in_dim(pieces, 1, at, keepdims=False)
        upper = bit_of(axis, bit)
        arrived = swap(jnp.where(upper, first, second), axis, bit)
        kept = jnp.where(upper, second, first)
        pieces = (kept.astype(jnp.float32) + arrived.astype(jnp.float32)).astype(jnp.bfloat16)
    return pieces


def gather_pieces(piece, labels, order):
    held = []
    for axis, bit in reversed(order):
        arrived = swap(piece, axis, bit)
        upper = bit_of(axis, bit)
        held = [label for label in labels if label in held or label == (axis, bit)]
        piece = jnp.stack(
            [jnp.where(upper, arrived, piece), jnp.where(upper, piece, arrived)],
            axis=held.index((axis, bit)),
        )
    return piece


def keep_and_send(first, second):
    upper = bit_of("ctx", 1)
    return (jnp.where(upper, second, first), jnp.where(upper, first, second))


def core_product(left, first, second):
    kept, sent = keep_and_send(first, second)
    left_all = jnp.concatenate([left, swap(left, "ctx", 1)], axis=0)
    right_all = jnp.concatenate([kept, swap(sent, "ctx", 1)], axis=0)
    return lax.dot_general(
        left_all, right_all, (((0,), (0,)), ((), ())), preferred_element_type=jnp.float32
    ).astype(jnp.bfloat16)


def shard_sum(product, by_columns):
    shards = lax.axis_size("fsdp")
    slices = lax.axis_size("ctx") // 2
    rows, columns = product.shape
    shard_labels = [("fsdp", bit) for bit in reversed(bits_below(shards))]
    slice_labels = [("ctx", 2 * bit) for bit in reversed(bits_below(slices))]
    if by_columns:
        cut = product.reshape(shards, rows // shards, slices, columns // slices)
        cut = jnp.transpose(cut, (0, 2, 1, 3))
    else:
        cut = product.reshape(shards, slices, rows // shards // slices, columns)
    parts = []
    half = cut.shape[2] // 2
    tail = list(reversed(shard_labels))
    for lead, orders in (
        (cut[:, :, :half], list(reversed(slice_labels))),
        (cut[:, :, half:], slice_labels),
    ):
        pieces = lead.reshape((2,) * (len(shard_labels) + len(slice_labels)) + lead.shape[2:])
        piece = reduce_pieces(pieces, shard_labels + slice_labels, orders + tail)
        whole = gather_pieces(piece, slice_labels, orders)
        parts.append(whole.reshape((slices,) + piece.shape))
    both = jnp.concatenate(parts, axis=1)
    if by_columns:
        return jnp.transpose(both, (1, 0, 2)).reshape(rows // shards, columns)
    return both.reshape(rows // shards, columns)


def join_cores(own):
    other = swap(own, "ctx", 1)
    upper = bit_of("ctx", 1)
    return jnp.concatenate(
        [jnp.where(upper, other, own), jnp.where(upper, own, other)], axis=1
    ).astype(jnp.float32)


def sum_over(value, axes):
    for axis in axes:
        for bit in bits_below(lax.axis_size(axis)):
            value = value + swap(value, axis, bit)
    return value


def own_shard(vector):
    width = vector.shape[0] // lax.axis_size("fsdp")
    return lax.dynamic_slice_in_dim(vector, lax.axis_index("fsdp") * width, width, 0)


def weight_sums(
    hidden,
    grad_mlp_low,
    act_mlp,
    grad_leading,
    grad_trailing,
    act_attn,
    grad_projected,
    attn_low,
    grad_attn_low,
    small,
    early,
):
    shards, ctx_count = (lax.axis_size("fsdp"), lax.axis_size("ctx"))
    rows, ff_width = hidden.shape
    model_width = act_mlp.shape[1]
    if early is None:
        half, half_three = (model_width // 2, 3 * model_width // 2)
        pairs = (
            (hidden, grad_mlp_low[:, :half], grad_mlp_low[:, half:]),
            (act_mlp, grad_leading, grad_trailing),
            (act_attn, grad_projected[:, :half_three], grad_projected[:, half_three:]),
            (attn_low, grad_attn_low[:, :half], grad_attn_low[:, half:]),
        )
        totals = [
            join_cores(shard_sum(core_product(*pair), at == 0)) for at, pair in enumerate(pairs)
        ]
        over_pack = sum_over(small, ("ctx",))
        return totals + [jnp.stack([over_pack, sum_over(over_pack, ("fsdp",))])]
    total_out, total_in, total_attn, total_qkv, small_sums = sum_weights(
        *early, [("rows", act_attn, grad_projected, 3)], small
    )
    padded = total_in.shape[1] // 2
    total_in = jnp.concatenate(
        [total_in[:, :ff_width], total_in[:, padded : padded + ff_width]], axis=1
    )
    return [
        total.astype(jnp.float32) for total in (total_out, total_in, total_qkv, total_attn)
    ] + [small_sums]


def weight_sums_early(hidden, grad_mlp_low, act_mlp, grad_leading, grad_trailing, attn_low, grad_attn_low):
    shards, ctx_count = (lax.axis_size("fsdp"), lax.axis_size("ctx"))
    ff_width = hidden.shape[1]
    if shards != 4 or ctx_count != 8 or act_mlp.shape[1] % 1024 != 0 or ff_width % 64 != 0:
        return None
    padded = -(-ff_width // 384) * 384
    sides = jnp.stack(
        [
            jnp.pad(side, ((0, 0), (0, padded - ff_width)))
            for side in (grad_leading, grad_trailing)
        ]
    )
    return early_sums(
        [
            ("columns", hidden, grad_mlp_low, 1),
            ("rows", act_mlp, sides, 3),
            ("rows", attn_low, grad_attn_low, 1),
        ]
    )


def per_device(
    inputs,
    cotangent,
    lengths,
    piece_route,
    gain_one,
    qkv_weight,
    attn_out,
    gain_two,
    geglu_in,
    geglu_out,
):
    ctx_count = lax.axis_size("ctx")
    own_index = lax.axis_index("ctx")
    row_count = inputs.shape[1]
    model_width = inputs.shape[2]
    piece_rows = row_count // ctx_count
    tokens = row_count * ctx_count
    own_heads = model_width // HEAD_WIDTH // ctx_count
    own_width = own_heads * HEAD_WIDTH
    block_q = math.gcd(tokens, 256)
    block_k = math.gcd(tokens, 512)
    lengths_row = lengths[0]
    own_route = piece_route[0, 0]
    slot_ids = jnp.arange(ctx_count, dtype=jnp.int32)
    outgoing = jnp.sum(
        slot_ids[None, :] * (own_route[None, :] == slot_ids[:, None]).astype(jnp.int32), axis=1
    )

    def exchange(blocks):
        return lax.all_to_all(blocks, "ctx", split_axis=0, concat_axis=0, tiled=True)

    def to_slots(rows_in):
        return jnp.take(rows_in.reshape(ctx_count, piece_rows, model_width), outgoing, axis=0)

    def to_heads(rows_in):
        by_heads = rows_in.reshape(row_count, ctx_count, -1)
        return exchange(jnp.transpose(by_heads, (1, 0, 2))).reshape(tokens, -1)

    def to_rows(heads_in):
        return exchange(heads_in.reshape(ctx_count, row_count, -1))

    arrived = exchange(to_slots(inputs[0]))
    grad_arrived = exchange(to_slots(cotangent[0]))
    residual = arrived.reshape(row_count, model_width).astype(jnp.float32)
    places = own_index * row_count + jnp.arange(row_count, dtype=jnp.int32)
    unused_begin, unused_end, offset, is_valid = spans(places, lengths_row)
    pack_begin, pack_end, pack_offset, unused_valid = spans(
        jnp.arange(tokens, dtype=jnp.int32), lengths_row
    )
    grad_final = jnp.where(
        is_valid[:, None], grad_arrived.reshape(row_count, model_width).astype(jnp.float32), 0.0
    )
    gains = jnp.pad(jnp.stack([gain_one, gain_two]), ((0, 14), (0, 0)))
    gains_full, qkv_full = gather_weights([gains, qkv_weight])
    gains_full = gains_full.reshape(-1, 16, gains.shape[1])
    gain_attn = gains_full[:, 0].reshape(-1).astype(jnp.float32)
    gain_mlp = gains_full[:, 1].reshape(-1).astype(jnp.float32)
    act_attn = layer_norm(residual, gain_attn).astype(jnp.bfloat16)
    later = [attn_out, geglu_in, geglu_out]
    if lax.axis_size("fsdp") == 4 and ctx_count == 8 and own_width == 128:
        attn_full, in_full, out_full, qkv_heads = gather_weights(
            later, (act_attn, qkv_full) + rotary_tables(offset, own_heads)
        )
    else:
        attn_full, in_full, out_full = gather_weights(later)
        projected = jnp.dot(act_attn, qkv_full, preferred_element_type=jnp.float32)
        cosine, sine = rotary_tables(offset, 1)
        queries, keys = (
            rotate(projected[:, :model_width], cosine, sine).astype(jnp.bfloat16),
            rotate(projected[:, model_width : 2 * model_width], cosine, sine).astype(jnp.bfloat16),
        )
        values = projected[:, 2 * model_width :].astype(jnp.bfloat16)
        joined = jnp.stack(
            [part.reshape(row_count, ctx_count, own_width) for part in (queries, keys, values)], axis=2
        )
        qkv_heads = to_heads(joined.reshape(row_count, -1))
    low, high = key_range(pack_begin, pack_end, block_q, block_k)
    pack_begin, pack_end = (pack_begin[None, :], pack_end[None, :])
    attended_heads, log_total = attention_forward(
        qkv_heads, pack_begin, pack_end, low, high, own_heads, block_q, block_k
    )
    attn_low = jnp.transpose(to_rows(attended_heads.astype(jnp.bfloat16)), (1, 0, 2)).reshape(
        row_count, model_width
    )
    branch_attn = jnp.dot(attn_low, attn_full, preferred_element_type=jnp.float32)
    middle = residual + branch_attn
    act_mlp = layer_norm(middle, gain_mlp).astype(jnp.bfloat16)
    up_both = jnp.dot(act_mlp, in_full, preferred_element_type=jnp.float32)
    ff_width = up_both.shape[1] // 2
    hidden = (jax.nn.gelu(up_both[:, :ff_width], approximate=False) * up_both[:, ff_width:]).astype(
        jnp.bfloat16
    )
    branch_mlp = jnp.dot(hidden, out_full, preferred_element_type=jnp.float32)
    final_rows = jnp.where(is_valid[:, None], middle + branch_mlp, 0.0)
    square_sums = jnp.stack(
        [
            jnp.sum(final_rows * final_rows),
            jnp.sum(jnp.where(is_valid[:, None], branch_attn * branch_attn, 0.0)),
            jnp.sum(jnp.where(is_valid[:, None], branch_mlp * branch_mlp, 0.0)),
        ]
    )
    out_slots = final_rows.astype(jnp.bfloat16).reshape(ctx_count, piece_rows, model_width)
    back_out = exchange(out_slots)
    block_out = jnp.take(back_out, own_route, axis=0).reshape(1, row_count, model_width)
    grad_mlp_low = grad_final.astype(jnp.bfloat16)
    grad_hidden = lax.dot_general(
        grad_mlp_low, out_full, NT, preferred_element_type=jnp.float32
    )

    def gated(leading, trailing):
        return jax.nn.gelu(leading, approximate=False) * trailing

    unused_gate, gate_back = jax.vjp(gated, up_both[:, :ff_width], up_both[:, ff_width:])
    grad_leading, grad_trailing = gate_back(grad_hidden)
    grad_leading, grad_trailing = (
        grad_leading.astype(jnp.bfloat16),
        grad_trailing.astype(jnp.bfloat16),
    )
    grad_up = jnp.concatenate([grad_leading, grad_trailing], axis=1)
    grad_act_mlp = lax.dot_general(grad_up, in_full, NT, preferred_element_type=jnp.float32)
    unused_norm, norm_back_mlp = jax.vjp(layer_norm, middle, gain_mlp)
    grad_middle_norm, grad_gain_mlp = norm_back_mlp(grad_act_mlp)
    grad_middle = grad_final + grad_middle_norm
    grad_attn_low = grad_middle.astype(jnp.bfloat16)
    grad_attended = lax.dot_general(
        grad_attn_low, attn_full, NT, preferred_element_type=jnp.float32
    ).astype(jnp.bfloat16)
    early = weight_sums_early(
        hidden, grad_mlp_low, act_mlp, grad_leading, grad_trailing, attn_low, grad_attn_low
    )
    pack_cosine, pack_sine = rotary_tables(pack_offset, own_heads)
    block_back = math.gcd(tokens, 256)
    low_back, high_back = key_range(pack_begin[0], pack_end[0], block_q, block_back)
    grad_heads = attention_backward(
        qkv_heads,
        attended_heads,
        to_heads(grad_attended),
        log_total,
        pack_begin,
        pack_end,
        low_back,
        high_back,
        pack_cosine,
        pack_sine,
        [] if early is None else [early[1][0][0]],
        own_heads,
        block_q,
        block_back,
    )
    if early is not None:
        grad_heads, early = second_step(grad_heads, early)
    grad_projected = jnp.transpose(
        to_rows(grad_heads).reshape(ctx_count, row_count, 3, own_width), (1, 2, 0, 3)
    ).reshape(row_count, 3 * model_width)
    grad_act_attn = lax.dot_general(
        grad_projected, qkv_full, NT, preferred_element_type=jnp.float32
    )
    unused_first, norm_back_attn = jax.vjp(layer_norm, residual, gain_attn)
    grad_resid_norm, grad_gain_attn = norm_back_attn(grad_act_attn)
    grad_residual = (grad_middle + grad_resid_norm).astype(jnp.bfloat16)
    back_grad = exchange(grad_residual.reshape(ctx_count, piece_rows, model_width))
    grad_inputs = jnp.take(back_grad, own_route, axis=0).reshape(1, row_count, model_width)
    small = jnp.stack(
        [grad_gain_attn, grad_gain_mlp, jnp.pad(square_sums, (0, model_width - 3))]
        + [jnp.zeros((model_width,), jnp.float32)] * 5
    )
    total_out, total_in, total_qkv, total_attn, small_sums = weight_sums(
        hidden,
        grad_mlp_low,
        act_mlp,
        grad_leading,
        grad_trailing,
        act_attn,
        grad_projected,
        attn_low,
        grad_attn_low,
        small,
        early,
    )
    total_gain_one = own_shard(small_sums[1, 0])
    total_gain_two = own_shard(small_sums[1, 1])
    total_squares = small_sums[0, 2, :3]
    valid_count = jnp.sum(lengths_row).astype(jnp.float32)
    rms_stats = jnp.sqrt(total_squares / (valid_count * model_width))[None, :]
    return (
        block_out,
        grad_inputs,
        total_gain_one,
        total_qkv,
        total_attn,
        total_gain_two,
        total_in,
        total_out,
        rms_stats,
    )


def solution(mesh):
    placed = (
        P("fsdp", "ctx", None),
        P("fsdp", "ctx", None),
        P("fsdp", None),
        P("fsdp", "ctx", None),
        P("fsdp"),
        P("fsdp", None),
        P("fsdp", None),
        P("fsdp"),
        P("fsdp", None),
        P("fsdp", None),
    )
    return jax.shard_map(
        per_device,
        mesh=mesh,
        in_specs=placed,
        out_specs=(
            P("fsdp", "ctx", None),
            P("fsdp", "ctx", None),
            P("fsdp"),
            P("fsdp", None),
            P("fsdp", None),
            P("fsdp"),
            P("fsdp", None),
            P("fsdp", None),
            P("fsdp", None),
        ),
        check_vma=False,
    )
```

```python
import functools
import math
import jax
import jax.numpy as jnp
from jax import lax
from jax.experimental import pallas as pl
from jax.experimental.pallas import tpu as pltpu
from jax.sharding import PartitionSpec as P

HEAD_WIDTH = 64
norm_eps = 1e-05
masked_score = -1e30


def head_stack(rows_in, head_count):
    if head_count == 1:
        return rows_in
    lane_head = lax.broadcasted_iota(jnp.int32, rows_in.shape, 1) // HEAD_WIDTH
    zero = jnp.zeros_like(rows_in)
    return jnp.concatenate(
        [jnp.where(lane_head == h, rows_in, zero) for h in range(head_count)], axis=0
    )


def head_pick(stacked_t, head_count, block):
    return jnp.concatenate(
        [
            stacked_t[h * HEAD_WIDTH : (h + 1) * HEAD_WIDTH, h * block : (h + 1) * block]
            for h in range(head_count)
        ],
        axis=0,
    ).T


NT = (((1,), (1,)), ((), ()))


def forward_kernel(
    head_count, block_q, block_k, low_ref, high_ref, begin_ref, end_ref, qkv_ref, out_ref, log_ref, turned_ref
):
    width = out_ref.shape[1]
    step = pl.program_id(0)

    @pl.when(step == 0)
    def prepare():
        turned_ref[...] = qkv_ref[:, 2 * width :].astype(jnp.float32).T.astype(jnp.bfloat16)

    rows = pl.ds(pl.multiple_of(step * block_q, block_q), block_q)
    scale = 1.0 / math.sqrt(HEAD_WIDTH)
    stacked = head_stack(qkv_ref[rows, :width] * jnp.asarray(scale, jnp.bfloat16), head_count)
    begin = jnp.concatenate([begin_ref[:, rows]] * head_count, axis=1)
    end = jnp.concatenate([end_ref[:, rows]] * head_count, axis=1)

    def body(index, carried):
        top, total, acc = carried
        first = pl.multiple_of(index * block_k, block_k)
        keys = qkv_ref[pl.ds(first, block_k), width : 2 * width]
        scores = lax.dot_general(keys, stacked, NT, preferred_element_type=jnp.float32)
        place = first + lax.broadcasted_iota(jnp.int32, scores.shape, 0)
        scores = jnp.where((place >= begin) & (place < end), scores, masked_score)
        new_top = jnp.maximum(top, jnp.max(scores, axis=0, keepdims=True))
        fresh = jnp.exp(scores - new_top)
        fade = jnp.exp(top - new_top)
        total = total * fade + jnp.sum(fresh, axis=0, keepdims=True)
        acc = acc * fade + jnp.dot(
            turned_ref[:, pl.ds(first, block_k)],
            fresh.astype(jnp.bfloat16),
            preferred_element_type=jnp.float32,
        )
        return (new_top, total, acc)

    lanes = head_count * block_q
    top, total, acc = lax.fori_loop(
        low_ref[step],
        high_ref[step],
        body,
        (
            jnp.full((1, lanes), masked_score, jnp.float32),
            jnp.zeros((1, lanes), jnp.float32),
            jnp.zeros((width, lanes), jnp.float32),
        ),
    )
    valid = end > begin
    safe = jnp.where(valid, total, 1.0)
    acc = jnp.where(valid, acc / safe, 0.0)
    log_total = jnp.where(valid, top + jnp.log(safe), 0.0)
    out_ref[...] = head_pick(acc, head_count, block_q)
    log_ref[0] = log_total


def attention_forward(qkv, begin, end, low, high, head_count, block_q, block_k):
    tokens = qkv.shape[0]
    width = head_count * HEAD_WIDTH
    steps = tokens // block_q
    whole = lambda shape: pl.BlockSpec(shape, lambda i, *_: (0,) * len(shape))
    pairs = tokens * tokens // 4 * head_count
    return pl.pallas_call(
        functools.partial(forward_kernel, head_count, block_q, block_k),
        out_shape=(
            jax.ShapeDtypeStruct((tokens, width), jnp.float32),
            jax.ShapeDtypeStruct((steps, 1, head_count * block_q), jnp.float32),
        ),
        grid_spec=pltpu.PrefetchScalarGridSpec(
            num_scalar_prefetch=2,
            grid=(steps,),
            in_specs=[whole((1, tokens)), whole((1, tokens)), whole((tokens, 3 * width))],
            out_specs=(
                pl.BlockSpec((block_q, width), lambda i, *_: (i, 0)),
                pl.BlockSpec((1, 1, head_count * block_q), lambda i, *_: (i, 0, 0)),
            ),
            scratch_shapes=[pltpu.VMEM((width, tokens), jnp.bfloat16)],
        ),
        cost_estimate=pl.CostEstimate(
            flops=pairs * 512, bytes_accessed=tokens * width * 12, transcendentals=pairs
        ),
        name="attention_forward",
    )(low, high, begin, end, qkv)


def turn_back(grads, cosine, sine, head_count):
    half = HEAD_WIDTH // 2
    pieces = []
    for h in range(head_count):
        base = h * HEAD_WIDTH
        pieces += [grads[:, base + half : base + HEAD_WIDTH], grads[:, base : base + half]]
    return grads * cosine + jnp.concatenate(pieces, axis=1) * sine


def backward_kernel(
    head_count,
    block_q,
    block_k,
    low_ref,
    high_ref,
    begin_ref,
    end_ref,
    qkv_ref,
    attended_ref,
    grad_ref,
    log_ref,
    cosine_ref,
    sine_ref,
    *refs,
):
    out_ref, turned_ref, key_acc, value_acc = refs[-4:]
    width = attended_ref.shape[1]
    step = pl.program_id(0)

    @pl.when(step == 0)
    def prepare():
        turned_ref[...] = qkv_ref[:, width : 2 * width].astype(jnp.float32).T.astype(jnp.bfloat16)
        key_acc[...] = jnp.zeros_like(key_acc)
        value_acc[...] = jnp.zeros_like(value_acc)

    rows = pl.ds(pl.multiple_of(step * block_q, block_q), block_q)
    scale = 1.0 / math.sqrt(HEAD_WIDTH)
    stacked = head_stack(qkv_ref[rows, :width] * jnp.asarray(scale, jnp.bfloat16), head_count)
    grads = grad_ref[rows, :]
    grad_stacked = head_stack(grads, head_count)
    begin = jnp.concatenate([begin_ref[:, rows]] * head_count, axis=1)
    end = jnp.concatenate([end_ref[:, rows]] * head_count, axis=1)
    product = (grads.astype(jnp.float32) * attended_ref[rows, :]).T
    delta = jnp.concatenate(
        [
            jnp.sum(product[h * HEAD_WIDTH : (h + 1) * HEAD_WIDTH], axis=0, keepdims=True)
            for h in range(head_count)
        ],
        axis=1,
    )
    log_total = log_ref[0]

    def body(index, acc):
        first = pl.multiple_of(index * block_k, block_k)
        span = pl.ds(first, block_k)
        keys = qkv_ref[span, width : 2 * width]
        values = qkv_ref[span, 2 * width :]
        scores = lax.dot_general(keys, stacked, NT, preferred_element_type=jnp.float32)
        grad_probs = lax.dot_general(values, grad_stacked, NT, preferred_element_type=jnp.float32)
        place = first + lax.broadcasted_iota(jnp.int32, scores.shape, 0)
        scores = jnp.where((place >= begin) & (place < end), scores, masked_score)
        probs = jnp.exp(scores - log_total)
        grad_scores = (probs * (grad_probs - delta)).astype(jnp.bfloat16)
        value_acc[span, :] += jnp.dot(
            probs.astype(jnp.bfloat16), grad_stacked, preferred_element_type=jnp.float32
        )
        key_acc[span, :] += jnp.dot(grad_scores, stacked, preferred_element_type=jnp.float32)
        return acc + jnp.dot(
            turned_ref[:, span], grad_scores, preferred_element_type=jnp.float32
        )

    acc = lax.fori_loop(
        low_ref[step],
        high_ref[step],
        body,
        jnp.zeros((width, head_count * block_q), jnp.float32),
    )
    grad_queries = head_pick(acc, head_count, block_q) * scale
    out_ref[rows, :width] = turn_back(
        grad_queries, cosine_ref[rows, :], sine_ref[rows, :], head_count
    ).astype(jnp.bfloat16)

    @pl.when(step == pl.num_programs(0) - 1)
    def finish():
        @pl.loop(0, pl.num_programs(0))
        def each(index):
            span = pl.ds(pl.multiple_of(index * block_q, block_q), block_q)
            out_ref[span, width : 2 * width] = turn_back(
                key_acc[span, :], cosine_ref[span, :], sine_ref[span, :], head_count
            ).astype(jnp.bfloat16)
            out_ref[span, 2 * width :] = value_acc[span, :].astype(jnp.bfloat16)


def attention_backward(
    qkv, attended, grads, log_total, begin, end, low, high, cosine, sine, after, head_count, block_q, block_k
):
    tokens = qkv.shape[0]
    width = head_count * HEAD_WIDTH
    steps = tokens // block_q
    whole = lambda shape: pl.BlockSpec(shape, lambda i, *_: (0,) * len(shape))
    pairs = tokens * tokens // 4 * head_count
    return pl.pallas_call(
        functools.partial(backward_kernel, head_count, block_q, block_k),
        out_shape=jax.ShapeDtypeStruct((tokens, 3 * width), jnp.bfloat16),
        grid_spec=pltpu.PrefetchScalarGridSpec(
            num_scalar_prefetch=2,
            grid=(steps,),
            in_specs=[
                whole((1, tokens)),
                whole((1, tokens)),
                whole((tokens, 3 * width)),
                whole((tokens, width)),
                whole((tokens, width)),
                pl.BlockSpec((1, 1, head_count * block_q), lambda i, *_: (i, 0, 0)),
                whole((tokens, width)),
                whole((tokens, width)),
            ]
            + [pl.BlockSpec(memory_space=pl.ANY)] * len(after),
            out_specs=whole((tokens, 3 * width)),
            scratch_shapes=[
                pltpu.VMEM((width, tokens), jnp.bfloat16),
                pltpu.VMEM((tokens, width), jnp.float32),
                pltpu.VMEM((tokens, width), jnp.float32),
            ],
        ),
        cost_estimate=pl.CostEstimate(
            flops=pairs * 1280, bytes_accessed=tokens * width * 30, transcendentals=pairs
        ),
        name="attention_backward",
    )(low, high, begin, end, qkv, attended, grads, log_total, cosine, sine, *after)


def spans(places, lengths_row):
    ends = jnp.cumsum(lengths_row)
    past = (places[:, None] >= ends[None, :]).astype(jnp.int32)
    begin = jnp.sum(past * lengths_row[None, :], axis=1)
    before = (places[:, None] >= (ends - lengths_row)[None, :]).astype(jnp.int32)
    end = jnp.sum(before * lengths_row[None, :], axis=1)
    valid = places < ends[-1]
    return (jnp.where(valid, begin, 0), jnp.where(valid, end, 0), places - begin, valid)


def key_range(begin, end, block_q, block_k):
    begin_blocks = jnp.where(end > begin, begin, jnp.int32(1 << 30)).reshape(-1, block_q)
    high = (jnp.max(end.reshape(-1, block_q), axis=1) + block_k - 1) // block_k
    low = jnp.minimum(jnp.min(begin_blocks, axis=1) // block_k, high)
    return (low, high)


def rotary_tables(offset, head_count):
    half = HEAD_WIDTH // 2
    inverse = 160000.0 ** (-2.0 * jnp.arange(half, dtype=jnp.float32) / HEAD_WIDTH)
    angles = offset.astype(jnp.float32)[:, None] * inverse[None, :]
    cosine, sine = (jnp.cos(angles), jnp.sin(angles))
    return (
        jnp.concatenate([cosine, cosine] * head_count, axis=1),
        jnp.concatenate([sine, -sine] * head_count, axis=1),
    )


def pack_rotary_tables(lengths_row, tokens, head_count):
    half, step = (HEAD_WIDTH // 2, math.gcd(tokens, 128))
    inverse = 160000.0 ** (-2.0 * jnp.arange(half, dtype=jnp.float32) / HEAD_WIDTH)
    inverse = jnp.tile(inverse, 2 * head_count)[None, :]
    sign = jnp.tile(jnp.repeat(jnp.asarray([1.0, -1.0], jnp.float32), half), head_count)[None, :]
    coarse = jnp.arange(0, tokens, step).astype(jnp.float32)[:, None] * inverse
    fine = jnp.arange(step).astype(jnp.float32)[:, None] * inverse
    begins = jnp.cumsum(lengths_row) - lengths_row
    start = begins.astype(jnp.float32)[:, None] * inverse
    cos_a, sin_a = (jnp.cos(coarse)[:, None, :], jnp.sin(coarse)[:, None, :])
    cos_b, sin_b = (jnp.cos(fine)[None], jnp.sin(fine)[None])
    cos_place = (cos_a * cos_b - sin_a * sin_b).reshape(tokens, -1)
    sin_place = (sin_a * cos_b + cos_a * sin_b).reshape(tokens, -1)
    place = lax.broadcasted_iota(jnp.int32, cos_place.shape, 0)
    cos_all, sin_all = (jnp.cos(start), jnp.sin(start))
    cos_start, sin_start = (cos_all[:1], sin_all[:1])
    for at in range(1, lengths_row.shape[0]):
        later = place >= begins[at]
        cos_start = jnp.where(later, cos_all[at][None, :], cos_start)
        sin_start = jnp.where(later, sin_all[at][None, :], sin_start)
    cosine = cos_place * cos_start + sin_place * sin_start
    sine = sin_place * cos_start - cos_place * sin_start
    return (cosine, sine * sign)


def toggled(index, bit):
    return index + bit - 2 * bit * ((index // bit) % 2)


def gather_kernel(shapes, projects, *refs):
    count = len(shapes)
    shard_refs, refs = (refs[:count], refs[count:])
    if projects:
        act_ref, qkv_ref, cosine_ref, sine_ref = refs[:4]
        heads_ref = refs[4 + count]
        columns_ref, held_ref, load_sem, head_send, head_recv, own_sem = refs[count + 8 :]
        refs = refs[4 : 4 + count] + refs[count + 5 : count + 8]
    full_refs = refs[:count]
    send_sem, recv_sem, local_sem = refs[count:]
    shards = lax.axis_size("fsdp")
    slices = lax.axis_size("ctx") // 2
    own_ctx, own_shard = (lax.axis_index("ctx"), lax.axis_index("fsdp"))
    core, chip = (own_ctx % 2, own_ctx // 2)
    barrier = pltpu.get_barrier_semaphore()
    partners = [{"fsdp": toggled(own_shard, bit)} for bit in (1, 2)]
    partners += [{"ctx": toggled(own_ctx, bit)} for bit in (1, 2, 4)]

    def owner_at(relation):
        owner = own_ctx
        for bit in (1, 2, 4):
            if relation & bit:
                owner = toggled(owner, bit)
        return owner

    if projects:
        partners += [{"ctx": owner_at(relation)} for relation in (3, 5, 6, 7)]
    for partner in partners:
        pl.semaphore_signal(
            barrier, inc=1, device_id=partner, device_id_type=pl.DeviceIdType.MESH
        )
    pl.semaphore_wait(barrier, len(partners))
    to_one, to_two, to_core, to_x, to_y = partners[:5]

    def shard_at(step):
        if step == 0:
            return own_shard
        if step == 3:
            return toggled(toggled(own_shard, 1), 2)
        return toggled(own_shard, step)

    def region(ref, weight, step, chip_at, half):
        if shapes[weight] == "small":
            return ref if len(ref.shape) == 2 else ref.at[shard_at(step)]
        if shapes[weight] == "rows":
            rows = ref.shape[-2]
            span = pl.ds(0, rows) if half is None else pl.ds(half * (rows // 2), rows // 2)
            if len(ref.shape) == 4:
                return ref.at[core, chip_at, span, :]
            return ref.at[shard_at(step), core, chip_at, span, :]
        rows = ref.shape[-2]
        first = (rows // 2) // 16 * 16
        spans_of = {None: pl.ds(0, rows), 0: pl.ds(0, first), 1: pl.ds(first, rows - first)}
        width = ref.shape[-1] // (2 * slices)
        columns = pl.ds(pl.multiple_of((core * slices + chip_at) * width, width), width)
        if len(ref.shape) == 2:
            return ref.at[spans_of[half], columns]
        return ref.at[shard_at(step), spans_of[half], columns]

    def core_region(ref, weight, step):
        if shapes[weight] == "rows":
            return ref.at[shard_at(step), core]
        width = ref.shape[-1] // 2
        return ref.at[shard_at(step), :, pl.ds(pl.multiple_of(core * width, width), width)]

    pending = []

    def send(source, target, slot, partner):
        copy = pltpu.make_async_remote_copy(
            src_ref=source,
            dst_ref=target,
            send_sem=send_sem.at[slot],
            recv_sem=recv_sem.at[slot],
            device_id=partner,
            device_id_type=pl.DeviceIdType.MESH,
        )
        copy.start()
        pending.append(copy)
        return copy

    copies = {}
    local = []

    def slot_of(weight, step, kind):
        return (weight * 3 + step - 1) * 8 + kind

    def shard_sends(weight):
        source = region(shard_refs[weight], weight, 0, chip, None)
        target = region(full_refs[weight], weight, 0, chip, None)
        copies[weight, 2, 0] = send(source, target, slot_of(weight, 2, 0), to_two)
        copies[weight, 1, 0] = send(source, target, slot_of(weight, 1, 0), to_one)
        target = full_refs[weight].at[own_shard]
        copy = pltpu.make_async_copy(shard_refs[weight], target, local_sem.at[weight])
        copy.start()
        local.append(copy)

    def shard_forward(weight):
        copies[weight, 2, 0].wait_recv()
        piece = region(full_refs[weight], weight, 2, chip, None)
        copies[weight, 3, 0] = send(piece, piece, slot_of(weight, 3, 0), to_one)

    def plane_sends(weight, step):
        lead = region(full_refs[weight], weight, step, chip, 0)
        rest = region(full_refs[weight], weight, step, chip, 1)
        for kind, piece, partner in ((1, lead, to_x), (2, rest, to_y), (3, lead, to_y), (4, rest, to_x)):
            copies[weight, step, kind] = send(piece, piece, slot_of(weight, step, kind), partner)

    def plane_forward(weight, step):
        copies[weight, step, 1].wait_recv()
        lead = region(full_refs[weight], weight, step, toggled(chip, 1), 0)
        copies[weight, step, 5] = send(lead, lead, slot_of(weight, step, 5), to_y)
        copies[weight, step, 2].wait_recv()
        rest = region(full_refs[weight], weight, step, toggled(chip, 2), 1)
        copies[weight, step, 6] = send(rest, rest, slot_of(weight, step, 6), to_x)

    def core_send(weight, step):
        for kind in (3, 4, 5, 6):
            copies[weight, step, kind].wait_recv()
        piece = core_region(full_refs[weight], weight, step)
        copies[weight, step, 7] = send(piece, piece, slot_of(weight, step, 7), to_core)

    chip_order = (3, 1, 2, 0)

    def start_loads():
        loads = {}
        for chip_bits in chip_order:
            owner_chip = owner_at(2 * chip_bits) // 2
            for part in range(3):
                width = columns_ref.shape[2] // 3
                total = qkv_ref.shape[1] // 3
                first = pl.multiple_of(part * total + owner_chip * width, width)
                loads[chip_bits, part] = pltpu.make_async_copy(
                    qkv_ref.at[:, pl.ds(first, width)],
                    columns_ref.at[chip_bits, :, pl.ds(part * width, width)],
                    load_sem.at[chip_bits * 3 + part],
                )
                loads[chip_bits, part].start()
        return loads

    def project(chip_bits, loads):
        for part in range(3):
            loads[chip_bits, part].wait()
        rows, own_width = (act_ref.shape[0], held_ref.shape[2] // 3)
        product = jnp.dot(
            act_ref[...], columns_ref[chip_bits], preferred_element_type=jnp.float32
        )
        for core_at in (0, 1):
            slot = 2 * chip_bits + core + core_at - 2 * core * core_at
            for part in range(3):
                first = (2 * part + core_at) * own_width
                piece = product[:, first : first + own_width]
                if part < 2:
                    half = HEAD_WIDTH // 2
                    turned = []
                    for base in range(0, own_width, HEAD_WIDTH):
                        turned += [piece[:, base + half : base + HEAD_WIDTH], piece[:, base : base + half]]
                    piece = piece * cosine_ref[...] - jnp.concatenate(turned, axis=1) * sine_ref[...]
                held_ref[slot, :, part * own_width : (part + 1) * own_width] = piece.astype(jnp.bfloat16)
        target = heads_ref.at[pl.ds(pl.multiple_of(own_ctx * rows, rows), rows), :]
        for core_bit in (0, 1):
            relation = 2 * chip_bits + core_bit
            if relation == 0:
                copy = pltpu.make_async_copy(held_ref.at[0], target, own_sem.at[0])
                copy.start()
                local.append(copy)
                continue
            copy = pltpu.make_async_remote_copy(
                src_ref=held_ref.at[relation],
                dst_ref=target,
                send_sem=head_send.at[relation],
                recv_sem=head_recv.at[relation],
                device_id={"ctx": owner_at(relation)},
                device_id_type=pl.DeviceIdType.MESH,
            )
            copy.start()
            pending.append(copy)
            arriving.append(copy)

    arriving = []
    sent = 1
    if projects:
        loads = start_loads()
        for weight in range(count):
            shard_sends(weight)
        sent = count
        for chip_bits in chip_order:
            project(chip_bits, loads)
    else:
        shard_sends(0)
    for weight in range(count):
        if weight + 1 >= sent and weight + 1 < count:
            shard_sends(weight + 1)
        shard_forward(weight)
        copies[weight, 1, 0].wait_recv()
        if shapes[weight] == "small":
            copies[weight, 3, 0].wait_recv()
            continue
        plane_sends(weight, 1)
        plane_sends(weight, 2)
        copies[weight, 3, 0].wait_recv()
        plane_sends(weight, 3)
        for step in (1, 2, 3):
            plane_forward(weight, step)
        if weight > 0 and shapes[weight - 1] != "small":
            for step in (1, 2, 3):
                core_send(weight - 1, step)
    for step in (1, 2, 3):
        core_send(count - 1, step)
    for weight in range(count):
        if shapes[weight] != "small":
            for step in (1, 2, 3):
                copies[weight, step, 7].wait_recv()
    for copy in arriving:
        copy.wait_recv()
    for copy in pending:
        copy.wait_send()
    for copy in local:
        copy.wait()


def gather_weights(weights, projection=None):
    shards, ctx_count = (lax.axis_size("fsdp"), lax.axis_size("ctx"))
    slices = ctx_count // 2
    shapes, views, outs = ([], [], [])
    for weight in weights:
        rows, columns = weight.shape
        if rows % (32 * ctx_count) == 0:
            shapes.append("rows")
            views.append(weight.reshape(2, slices, rows // ctx_count, columns))
            outs.append((shards, 2, slices, rows // ctx_count, columns))
        elif rows == 16:
            shapes.append("small")
            views.append(weight)
            outs.append((shards, rows, columns))
        elif columns % (128 * ctx_count) == 0 and rows % 16 == 0:
            shapes.append("columns")
            views.append(weight)
            outs.append((shards, rows, columns))
    if shards != 4 or ctx_count != 8 or len(views) < len(weights):
        return [lax.all_gather(weight, "fsdp", axis=0, tiled=True) for weight in weights]
    slots = len(views) * 24
    vmem, anywhere, dma = (
        pl.BlockSpec(memory_space=pltpu.VMEM),
        pl.BlockSpec(memory_space=pl.ANY),
        pltpu.SemaphoreType.DMA,
    )
    in_specs = [vmem] * len(views)
    scratch = [dma((slots,)), dma((slots,)), dma((len(views),))]
    if projection is not None:
        act_attn, qkv_full = projection[:2]
        rows, own_columns = (act_attn.shape[0], qkv_full.shape[1] // ctx_count)
        views += list(projection)
        in_specs += [vmem, anywhere, vmem, vmem]
        outs.append((ctx_count * rows, own_columns))
        scratch += [
            pltpu.VMEM((slices, qkv_full.shape[0], 2 * own_columns), jnp.bfloat16),
            pltpu.VMEM((ctx_count, rows, own_columns), jnp.bfloat16),
            dma((3 * slices,)),
            dma((ctx_count,)),
            dma((ctx_count,)),
            dma((1,)),
        ]
    held = pl.pallas_call(
        functools.partial(gather_kernel, shapes, projection is not None),
        out_shape=tuple(jax.ShapeDtypeStruct(out, jnp.bfloat16) for out in outs),
        in_specs=in_specs,
        out_specs=tuple(anywhere for out in outs),
        scratch_shapes=scratch,
        compiler_params=pltpu.CompilerParams(
            collective_id=0 if projection is None else 2,
            has_side_effects=True,
            vmem_limit_bytes=60 * 1024 * 1024,
        ),
        name="gather_weights" if projection is None else "gather_and_project",
    )(*views)
    return [whole.reshape(-1, whole.shape[-1]) for whole in held]


def pair_steps(plan, lead_rows, left_refs, right_refs, turned_refs, whole_refs, sems, core, pending, send):
    pair_send, pair_recv, near_sem = sems
    to_core = {"ctx": toggled(lax.axis_index("ctx"), 1)}

    def send_core(source, target, sent, got, start=True):
        return send(source, target, sent, got, to_core, start)

    rows = left_refs[0].shape[0] if left_refs else 0
    pairs = []
    for w, entry in enumerate(plan):
        span, right = (plan_span(entry), right_refs[w])
        own_part, other_part = (whole_refs[w].at[pl.ds(0, rows)], whole_refs[w].at[pl.ds(rows, rows)])

        def exchange(own_half, other_half, start=True):
            near = pltpu.make_async_copy(own_half, own_part, near_sem.at[w])
            if start:
                near.start()
            sems = (pair_send.at[2 * w], pair_recv.at[2 * w])
            return [near, send_core(other_half, other_part, *sems, start)]

        if entry[5]:
            ways = [exchange(right[at], right[1 - at], False) for at in (0, 1)]
            for at in (0, 1):

                @pl.when(core == at)
                def begin():
                    for copy in ways[at]:
                        copy.start()

            pairs.append(ways[0])
            pending.append(ways[0][1])
        else:
            halves = [
                right.at[:, pl.ds(pl.multiple_of(at * span, span), span)] for at in (core, 1 - core)
            ]
            pairs.append(exchange(*halves))

    def turn(w):
        left, turned = (left_refs[w], turned_refs[w])
        block = 512
        for first in range(0, left.shape[1], block):
            last = min(first + block, left.shape[1])
            turned[first:last, :rows] = (
                left[:, first:last].astype(jnp.float32).T.astype(jnp.bfloat16)
            )
        pairs[w].append(
            send_core(
                turned.at[:, pl.ds(0, rows)],
                turned.at[:, pl.ds(rows, rows)],
                pair_send.at[2 * w + 1],
                pair_recv.at[2 * w + 1],
            )
        )

    def multiply(w, t, first, second):
        kind, count, width, deep, halves, parted = plan[w]
        if t == 0:
            near, far, turned = pairs[w]
            near.wait()
            far.wait_recv()
            turned.wait_recv()

        def each(z, carried):
            left = turned_refs[w][pl.ds(pl.multiple_of(z * deep, 16), deep), :]
            if kind == "rows":
                last = min((t + 1) * width, whole_refs[w].shape[1])
                part = jnp.dot(
                    left, whole_refs[w][:, t * width : last], preferred_element_type=jnp.float32
                ).astype(jnp.bfloat16)
                if last < (t + 1) * width:
                    empty = jnp.zeros((deep, (t + 1) * width - last), jnp.bfloat16)
                    part = jnp.concatenate([part, empty], axis=1)
                piece_rows = first.shape[3]
                for s in range(4):
                    first[z, s // 2, s % 2] = part[2 * s * piece_rows : (2 * s + 1) * piece_rows]
                    second[z, s // 2, s % 2] = part[(2 * s + 1) * piece_rows : (2 * s + 2) * piece_rows]
            else:
                part = jnp.dot(
                    left, whole_refs[w][...], preferred_element_type=jnp.float32
                ).astype(jnp.bfloat16)
                for s in range(4):
                    piece = part[:, s * width : (s + 1) * width]
                    first[z, s // 2, s % 2] = piece[:lead_rows]
                    second[z, s // 2, s % 2] = piece[lead_rows:]
            return carried

        lax.fori_loop(0, 4, each, 0)

    return (turn, multiply)


def remote_send(pending):
    def send(source, target, sent, got, partner, start=True):
        copy = pltpu.make_async_remote_copy(
            src_ref=source,
            dst_ref=target,
            send_sem=sent,
            recv_sem=got,
            device_id=partner,
            device_id_type=pl.DeviceIdType.MESH,
        )
        if start:
            copy.start()
            pending.append(copy)
        return copy

    return send


def product_kernel(plan, lead_rows, *refs):
    groups, places = early_places(plan)
    weights, outs = (len(plan), 4 * len(groups))
    left_refs, refs = (refs[:weights], refs[weights:])
    right_refs = []
    for entry in plan:
        held = 2 if entry[5] else 1
        right_refs.append(refs[:held] if held == 2 else refs[0])
        refs = refs[held:]
    out_refs = refs[:outs]
    scratch = list(refs[outs:])
    turned_refs = [scratch.pop(0) for weight in plan]
    whole_refs = [scratch.pop(0) for weight in plan]
    chunks = [(w, t) for w, entry in enumerate(plan) for t in range(entry[1])]
    held = [(scratch.pop(0), scratch.pop(0)) for chunk in chunks]
    pair_send, pair_recv, near_sem, store_sem = scratch
    own_ctx = lax.axis_index("ctx")
    core, chip = (own_ctx % 2, own_ctx // 2)
    own_x, own_y = (chip % 2, chip // 2)
    to_core = {"ctx": toggled(own_ctx, 1)}
    barrier = pltpu.get_barrier_semaphore()
    pl.semaphore_signal(barrier, inc=1, device_id=to_core, device_id_type=pl.DeviceIdType.MESH)
    pl.semaphore_wait(barrier, 1)
    pending = []
    send = remote_send(pending)
    turn, multiply = pair_steps(
        plan,
        lead_rows,
        left_refs,
        right_refs,
        turned_refs,
        whole_refs,
        (pair_send, pair_recv, near_sem),
        core,
        pending,
        send,
    )
    for w in range(weights):
        turn(w)
    stores = []
    for number, (w, t) in enumerate(chunks):
        first, second = held[number]
        multiply(w, t, first, second)
        group, offset = places[number]
        sides = (
            lambda at: first.at[:, at, own_x],
            lambda at: first.at[:, at, 1 - own_x],
            lambda at: second.at[:, own_y, at],
            lambda at: second.at[:, 1 - own_y, at],
        )
        for side, source_at in enumerate(sides):
            for at in (0, 1):
                copy = pltpu.make_async_copy(
                    source_at(at),
                    out_refs[4 * group + side].at[at, :, :, pl.ds(offset, plan[w][2])],
                    store_sem.at[8 * number + 2 * side + at],
                )
                copy.start()
                stores.append(copy)
    for copy in stores:
        copy.wait()
    for copy in pending:
        copy.wait_send()


def weight_plan(kind, left, right, count):
    deep = left.shape[1] // 4
    if kind == "rows":
        parted = isinstance(right, tuple)
        span = right[0].shape[1] if parted else right.shape[1] // 2
        width = -(-span // (128 * count)) * 128
        return (kind, count, width, deep, (deep // 8, deep // 8), span if parted else 0)
    lead_rows = deep // 2 // 16 * 16
    return (kind, count, right.shape[-1] // 8, deep, (lead_rows, deep - lead_rows), 0)


def early_places(plan):
    groups, places = ([], [])
    for kind, count, width, deep, halves, parted in plan:
        found = [at for at, group in enumerate(groups) if group[0] == halves]
        if not found:
            groups.append([halves, 0])
            found = [len(groups) - 1]
        for chunk in range(count):
            places.append((found[0], groups[found[0]][1]))
            groups[found[0]][1] += width
    return (groups, places)


def plan_span(entry):
    return entry[1] * entry[2] if entry[0] == "rows" else 4 * entry[2]


def plan_lead(plan):
    return max([0] + [entry[4][0] for entry in plan if entry[0] == "columns"])


def pair_scratch(plan, tokens):
    turned = [pltpu.VMEM((4 * entry[3], 2 * tokens), jnp.bfloat16) for entry in plan]
    return turned + [
        pltpu.VMEM((2 * tokens, entry[5] or plan_span(entry)), jnp.bfloat16) for entry in plan
    ]


def early_sums(products):
    plan = [weight_plan(*product) for product in products]
    lefts, rights = ([product[1] for product in products], [product[2] for product in products])
    vmem, anywhere, dma = (
        pl.BlockSpec(memory_space=pltpu.VMEM),
        pl.BlockSpec(memory_space=pl.ANY),
        pltpu.SemaphoreType.DMA,
    )
    rights = [part for right in rights for part in (right if isinstance(right, tuple) else [right])]
    groups = early_places(plan)[0]
    outs, held = ([], [])
    for halves, columns in groups:
        for half in halves:
            outs += [jax.ShapeDtypeStruct((2, 4, half, columns), jnp.bfloat16)] * 2
    for kind, count, width, deep, halves, parted in plan:
        for chunk in range(count):
            held += [pltpu.VMEM((4, 2, 2, half, width), jnp.bfloat16) for half in halves]
    chunk_count = sum(entry[1] for entry in plan)
    scratch = pair_scratch(plan, lefts[0].shape[0]) + held
    scratch += [dma((2 * len(plan),)), dma((2 * len(plan),)), dma((len(plan),)), dma((8 * chunk_count,))]
    sides = pl.pallas_call(
        functools.partial(product_kernel, plan, plan_lead(plan)),
        out_shape=tuple(outs),
        in_specs=[vmem] * len(plan) + [anywhere] * len(rights),
        out_specs=(anywhere,) * len(outs),
        scratch_shapes=scratch,
        compiler_params=pltpu.CompilerParams(
            collective_id=3, has_side_effects=True, vmem_limit_bytes=60 * 1024 * 1024
        ),
        name="early_products",
    )(*lefts, *rights)
    arrays = []
    for group in range(len(groups)):
        for part, bit in ((0, 2), (2, 4)):
            kept, sent = sides[4 * group + part : 4 * group + part + 2]
            arrays.append((kept, swap(sent, "ctx", bit)))
    return (plan, arrays)


def second_step(held, early):
    plan, arrays = early
    held, arrays = lax.optimization_barrier((held, arrays))
    chip = lax.axis_index("ctx") // 2
    flat = []
    for at, (kept, arrived) in enumerate(arrays):
        bit, own = ((4, chip // 2), (2, chip % 2))[at % 2]
        other = [
            lax.dynamic_index_in_dim(side, 1 - own, 0, keepdims=False).astype(jnp.float32)
            for side in (kept, arrived)
        ]
        flat += [kept, arrived, swap((other[0] + other[1]).astype(jnp.bfloat16), "ctx", bit)]
    return (held, (plan, flat))


def sum_kernel(early, late, lead_rows, *refs):
    weights, products = (len(early) + len(late), len(late))
    left_refs, right_refs = (refs[:products], refs[products : 2 * products])
    refs = refs[2 * products :]
    groups, places = early_places(early)
    early_refs, refs = (refs[: 6 * len(groups)], refs[6 * len(groups) :])
    small_ref, out_refs, small_out = (refs[0], refs[1 : weights + 1], refs[weights + 1])
    scratch = list(refs[weights + 2 :])
    turned_refs = [scratch.pop(0) for weight in late]
    whole_refs = [scratch.pop(0) for weight in late]
    plan = early + late
    chunks = [(w, t) for w, entry in enumerate(plan) for t in range(entry[1])]
    early_count = sum(entry[1] for entry in early)
    units = {}
    for number in range(len(chunks)):
        for half in (0, 1):
            units[number, half] = [scratch.pop(0) for stage in range(5)]
    small_held = scratch.pop(0)
    send_sem, recv_sem, local_sem, load_sem, pair_send, pair_recv, small_send, small_recv, near_sem = scratch
    own_ctx, own_shard = (lax.axis_index("ctx"), lax.axis_index("fsdp"))
    core, chip = (own_ctx % 2, own_ctx // 2)
    own_x, own_y = (chip % 2, chip // 2)
    low_bit, high_bit = (own_shard % 2, own_shard // 2)
    loads = {}
    for number in range(early_count):
        w, (group, offset) = (chunks[number][0], places[number])
        for half in (0, 1):
            own = own_y if half == 0 else own_x
            kept, arrived, twice = early_refs[6 * group + 3 * half : 6 * group + 3 * half + 3]
            columns = pl.ds(offset, plan[w][2])
            sources = (kept.at[own, :, :, columns], arrived.at[own, :, :, columns], twice.at[:, :, columns])
            for at, source in enumerate(sources):
                slot = (number * 2 + half) * 3 + at
                copy = pltpu.make_async_copy(source, units[number, half][at], load_sem.at[slot])
                copy.start()
                loads[number, half, at] = copy
    partners = [{"ctx": toggled(own_ctx, bit)} for bit in (1, 2, 4)]
    partners += [{"fsdp": toggled(own_shard, bit)} for bit in (1, 2)]
    barrier = pltpu.get_barrier_semaphore()
    for partner in partners:
        pl.semaphore_signal(
            barrier, inc=1, device_id=partner, device_id_type=pl.DeviceIdType.MESH
        )
    pl.semaphore_wait(barrier, len(partners))
    to_core, to_x, to_y, to_one, to_two = partners
    pending = []
    send = remote_send(pending)
    turn, multiply = pair_steps(
        late,
        lead_rows,
        left_refs,
        right_refs,
        turned_refs,
        whole_refs,
        (pair_send, pair_recv, near_sem),
        core,
        pending,
        send,
    )
    copies = {}

    def hop(number, half, stage, source, target, partner):
        slot = (number * 2 + half) * 8 + stage
        copies[number, half, stage] = send(
            source, target, send_sem.at[slot], recv_sem.at[slot], partner
        )

    def stage_one(number):
        w, t = chunks[number]
        multiply(w - len(early), t, units[number, 0][0], units[number, 1][0])
        hop(number, 0, 0, units[number, 0][0].at[:, :, 1 - own_x], units[number, 0][1], to_x)
        hop(number, 1, 0, units[number, 1][0].at[:, 1 - own_y], units[number, 1][1], to_y)

    def add(target, source_at, count):
        def each(i, carried):
            target[i] = (
                target[i].astype(jnp.float32) + source_at(i).astype(jnp.float32)
            ).astype(jnp.bfloat16)
            return carried

        lax.fori_loop(0, count, each, 0)

    def stage_two(number):
        held, got = (units[number, 0][0], units[number, 0][1])
        copies[number, 0, 0].wait_recv()
        add(got, lambda z: held[z, :, own_x], 4)
        held_b, got_b = (units[number, 1][0], units[number, 1][1])
        copies[number, 1, 0].wait_recv()
        add(got_b, lambda z: held_b[z, own_y], 4)
        hop(number, 0, 1, got.at[:, 1 - own_y], units[number, 0][2], to_y)
        hop(number, 1, 1, got_b.at[:, 1 - own_x], units[number, 1][2], to_x)

    def stage_three(number):
        for half in (0, 1):
            kept, held, got = units[number, half][:3]
            own = own_y if half == 0 else own_x
            if number < early_count:
                for at in range(3):
                    loads[number, half, at].wait()
                add(held, lambda z: kept[z], 4)
                add(got, lambda z: held[z], 4)
            else:
                copies[number, half, 1].wait_recv()
                add(got, lambda z: held[z, own], 4)
        for half in (0, 1):
            got = units[number, half][2]
            for high in (0, 1):
                hop(
                    number,
                    half,
                    2 + 4 * high,
                    got.at[2 * high + 1 - low_bit],
                    units[number, half][3].at[high],
                    to_one,
                )

    def stage_four(number):
        for half in (0, 1):
            held, got = (units[number, half][2], units[number, half][3])
            copies[number, half, 2].wait_recv()
            copies[number, half, 6].wait_recv()
            add(got, lambda high: held[2 * high + low_bit], 2)
        for half in (0, 1):
            got = units[number, half][3]
            hop(number, half, 3, got.at[1 - high_bit], units[number, half][4].at[0], to_two)

    def final_region(number, half, chip_at):
        w, t = chunks[number]
        kind, count, width = plan[w][:3]
        deep = units[number, half][4].shape[1]
        if kind == "rows":
            start = pl.multiple_of((2 * chip_at + half) * deep, deep)
            column = pl.multiple_of((core * count + t) * width, width)
            return out_refs[w].at[pl.ds(start, deep), pl.ds(column, width)]
        column = pl.multiple_of((core * 4 + chip_at) * width, width)
        return out_refs[w].at[pl.ds(half * lead_rows, deep), pl.ds(column, width)]

    local = {}

    def stage_five(number):
        for half in (0, 1):
            held, got = (units[number, half][3], units[number, half][4])
            copies[number, half, 3].wait_recv()
            add(got, lambda i: held[high_bit], 1)
        for half in (0, 1):
            got = units[number, half][4].at[0]
            target = final_region(number, half, chip)
            hop(number, half, 4, got, target, to_x if half == 0 else to_y)
            hop(number, half, 5, got, target, to_y if half == 0 else to_x)
            copy = pltpu.make_async_copy(got, target, local_sem.at[number * 2 + half])
            copy.start()
            local[number, half] = copy

    def stage_six(number):
        for half in (0, 1):
            copies[number, half, 4].wait_recv()
            piece = final_region(number, half, toggled(chip, 1 if half == 0 else 2))
            hop(number, half, 7, piece, piece, to_y if half == 0 else to_x)

    def stage_seven(number):
        w, t = chunks[number]
        kind, count, width = plan[w][:3]
        for half in (0, 1):
            copies[number, half, 5].wait_recv()
            copies[number, half, 7].wait_recv()
            local[number, half].wait()
        span = width if kind == "rows" else 4 * width
        at = core * count + t if kind == "rows" else core
        piece = out_refs[w].at[:, pl.ds(pl.multiple_of(at * span, span), span)]
        slot = len(chunks) * 16 + number
        copies[number, 2, 0] = send(
            piece, piece, send_sem.at[slot], recv_sem.at[slot], to_core
        )

    small_copies = []

    def small_step(step):
        if step > 0:
            small_copies[step - 1].wait_recv()
            small_held[2 * step] = small_held[2 * step - 2] + small_held[2 * step - 1]
            if step == 3:
                small_out[0] = small_held[6]
        else:
            small_held[0] = small_ref[...]
        if step < 5:
            small_copies.append(
                send(
                    small_held.at[2 * step],
                    small_held.at[2 * step + 1],
                    small_send.at[step],
                    small_recv.at[step],
                    partners[step],
                )
            )
        else:
            small_out[1] = small_held[10]

    stages = (stage_one, stage_two, stage_three, stage_four, stage_five, stage_six, stage_seven)
    small_at = 0
    stage_three(0)
    for w in range(len(late)):
        turn(w)
    for tick in range(len(chunks) + len(stages)):
        for lag, stage in enumerate(stages):
            for number in range(len(chunks)):
                start = number - 2 if number < early_count else number - early_count
                if start + lag == tick and (number >= early_count or (lag >= 2 and number + lag > 2)):
                    stage(number)
        if small_at < 6:
            small_step(small_at)
            small_at += 1
    for number in range(len(chunks)):
        copies[number, 2, 0].wait_recv()
    for copy in pending:
        copy.wait_send()


def sum_weights(early, early_arrays, products, small):
    late = [weight_plan(*product) for product in products]
    lefts, rights = ([product[1] for product in products], [product[2] for product in products])
    plan = early + late
    pieces = []
    for w, (kind, count, width, deep, halves, parted) in enumerate(plan):
        leads = [(4, 2, 2), (4, 2), (4,), (2,), (1,)]
        if w < len(early):
            leads[:2] = [(4,), (4,)]
        for chunk in range(count):
            for half in halves:
                pieces += [pltpu.VMEM(lead + (half, width), jnp.bfloat16) for lead in leads]
    outs = [jax.ShapeDtypeStruct((entry[3], 2 * plan_span(entry)), jnp.bfloat16) for entry in plan]
    chunk_count = sum(entry[1] for entry in plan)
    scratch = pair_scratch(late, lefts[0].shape[0]) + pieces
    scratch += [pltpu.VMEM((11,) + small.shape, jnp.float32)]
    dma = pltpu.SemaphoreType.DMA
    slots = chunk_count * 17
    scratch += [dma((slots,)), dma((slots,)), dma((2 * chunk_count,)), dma((6 * chunk_count,))]
    scratch += [dma((2 * len(late),)), dma((2 * len(late),)), dma((5,)), dma((5,)), dma((len(late),))]
    vmem, anywhere = (
        pl.BlockSpec(memory_space=pltpu.VMEM),
        pl.BlockSpec(memory_space=pl.ANY),
    )
    return pl.pallas_call(
        functools.partial(sum_kernel, early, late, plan_lead(plan)),
        out_shape=tuple(outs) + (jax.ShapeDtypeStruct((2,) + small.shape, jnp.float32),),
        in_specs=[vmem] * len(late) + [anywhere] * (len(late) + len(early_arrays)) + [vmem],
        out_specs=(anywhere,) * len(plan) + (vmem,),
        scratch_shapes=scratch,
        compiler_params=pltpu.CompilerParams(
            collective_id=1, has_side_effects=True, vmem_limit_bytes=60 * 1024 * 1024
        ),
        name="sum_weights",
    )(*lefts, *rights, *early_arrays, small)


def layer_norm(rows_in, gain_vec):
    row_mean = jnp.mean(rows_in, axis=-1, keepdims=True)
    centred = rows_in - row_mean
    variance = jnp.mean(centred * centred, axis=-1, keepdims=True)
    return centred * lax.rsqrt(variance + norm_eps) * gain_vec


def rotate(projected, cosine, sine):
    row_count, width = projected.shape
    half_width = HEAD_WIDTH // 2
    by_head = projected.reshape(row_count, width // HEAD_WIDTH, HEAD_WIDTH)
    turned = jnp.concatenate([by_head[..., half_width:], by_head[..., :half_width]], axis=-1)
    return (by_head * cosine[:, None, :] - turned * sine[:, None, :]).reshape(row_count, width)


def swap(value, axis, bit):
    pairs = [(i, i ^ bit) for i in range(lax.axis_size(axis))]
    return lax.ppermute(value, axis, pairs)


def bit_of(axis, bit):
    return (lax.axis_index(axis) // bit) % 2 == 1


def bits_below(count):
    return [1 << i for i in range(count.bit_length() - 1)]


def reduce_pieces(pieces, labels, order):
    labels = list(labels)
    for axis, bit in order:
        at = labels.index((axis, bit))
        labels.pop(at)
        first = lax.index_in_dim(pieces, 0, at, keepdims=False)
        second = lax.index_in_dim(pieces, 1, at, keepdims=False)
        upper = bit_of(axis, bit)
        arrived = swap(jnp.where(upper, first, second), axis, bit)
        kept = jnp.where(upper, second, first)
        pieces = (kept.astype(jnp.float32) + arrived.astype(jnp.float32)).astype(jnp.bfloat16)
    return pieces


def gather_pieces(piece, labels, order):
    held = []
    for axis, bit in reversed(order):
        arrived = swap(piece, axis, bit)
        upper = bit_of(axis, bit)
        held = [label for label in labels if label in held or label == (axis, bit)]
        piece = jnp.stack(
            [jnp.where(upper, arrived, piece), jnp.where(upper, piece, arrived)],
            axis=held.index((axis, bit)),
        )
    return piece


def keep_and_send(first, second):
    upper = bit_of("ctx", 1)
    return (jnp.where(upper, second, first), jnp.where(upper, first, second))


def core_product(left, first, second):
    kept, sent = keep_and_send(first, second)
    left_all = jnp.concatenate([left, swap(left, "ctx", 1)], axis=0)
    right_all = jnp.concatenate([kept, swap(sent, "ctx", 1)], axis=0)
    return lax.dot_general(
        left_all, right_all, (((0,), (0,)), ((), ())), preferred_element_type=jnp.float32
    ).astype(jnp.bfloat16)


def shard_sum(product, by_columns):
    shards = lax.axis_size("fsdp")
    slices = lax.axis_size("ctx") // 2
    rows, columns = product.shape
    shard_labels = [("fsdp", bit) for bit in reversed(bits_below(shards))]
    slice_labels = [("ctx", 2 * bit) for bit in reversed(bits_below(slices))]
    if by_columns:
        cut = product.reshape(shards, rows // shards, slices, columns // slices)
        cut = jnp.transpose(cut, (0, 2, 1, 3))
    else:
        cut = product.reshape(shards, slices, rows // shards // slices, columns)
    parts = []
    half = cut.shape[2] // 2
    tail = list(reversed(shard_labels))
    for lead, orders in (
        (cut[:, :, :half], list(reversed(slice_labels))),
        (cut[:, :, half:], slice_labels),
    ):
        pieces = lead.reshape((2,) * (len(shard_labels) + len(slice_labels)) + lead.shape[2:])
        piece = reduce_pieces(pieces, shard_labels + slice_labels, orders + tail)
        whole = gather_pieces(piece, slice_labels, orders)
        parts.append(whole.reshape((slices,) + piece.shape))
    both = jnp.concatenate(parts, axis=1)
    if by_columns:
        return jnp.transpose(both, (1, 0, 2)).reshape(rows // shards, columns)
    return both.reshape(rows // shards, columns)


def join_cores(own):
    other = swap(own, "ctx", 1)
    upper = bit_of("ctx", 1)
    return jnp.concatenate(
        [jnp.where(upper, other, own), jnp.where(upper, own, other)], axis=1
    ).astype(jnp.float32)


def sum_over(value, axes):
    for axis in axes:
        for bit in bits_below(lax.axis_size(axis)):
            value = value + swap(value, axis, bit)
    return value


def own_shard(vector):
    width = vector.shape[0] // lax.axis_size("fsdp")
    return lax.dynamic_slice_in_dim(vector, lax.axis_index("fsdp") * width, width, 0)


def weight_sums(
    hidden,
    grad_mlp_low,
    act_mlp,
    grad_leading,
    grad_trailing,
    act_attn,
    grad_projected,
    attn_low,
    grad_attn_low,
    small,
    early,
):
    shards, ctx_count = (lax.axis_size("fsdp"), lax.axis_size("ctx"))
    rows, ff_width = hidden.shape
    model_width = act_mlp.shape[1]
    if early is None:
        half, half_three = (model_width // 2, 3 * model_width // 2)
        pairs = (
            (hidden, grad_mlp_low[:, :half], grad_mlp_low[:, half:]),
            (act_mlp, grad_leading, grad_trailing),
            (act_attn, grad_projected[:, :half_three], grad_projected[:, half_three:]),
            (attn_low, grad_attn_low[:, :half], grad_attn_low[:, half:]),
        )
        totals = [
            join_cores(shard_sum(core_product(*pair), at == 0)) for at, pair in enumerate(pairs)
        ]
        over_pack = sum_over(small, ("ctx",))
        return totals + [jnp.stack([over_pack, sum_over(over_pack, ("fsdp",))])]
    total_out, total_in, total_attn, total_qkv, small_sums = sum_weights(
        *early, [("rows", act_attn, grad_projected, 3)], small
    )
    padded = total_in.shape[1] // 2
    total_in = jnp.concatenate(
        [total_in[:, :ff_width], total_in[:, padded : padded + ff_width]], axis=1
    )
    return [
        total.astype(jnp.float32) for total in (total_out, total_in, total_qkv, total_attn)
    ] + [small_sums]


def weight_sums_early(hidden, grad_mlp_low, act_mlp, grad_leading, grad_trailing, attn_low, grad_attn_low):
    shards, ctx_count = (lax.axis_size("fsdp"), lax.axis_size("ctx"))
    ff_width = hidden.shape[1]
    if shards != 4 or ctx_count != 8 or act_mlp.shape[1] % 1024 != 0 or ff_width % 64 != 0:
        return None
    return early_sums(
        [
            ("columns", hidden, grad_mlp_low, 1),
            ("rows", act_mlp, (grad_leading, grad_trailing), 3),
            ("rows", attn_low, grad_attn_low, 1),
        ]
    )


def per_device(
    inputs,
    cotangent,
    lengths,
    piece_route,
    gain_one,
    qkv_weight,
    attn_out,
    gain_two,
    geglu_in,
    geglu_out,
):
    ctx_count = lax.axis_size("ctx")
    own_index = lax.axis_index("ctx")
    row_count = inputs.shape[1]
    model_width = inputs.shape[2]
    piece_rows = row_count // ctx_count
    tokens = row_count * ctx_count
    own_heads = model_width // HEAD_WIDTH // ctx_count
    own_width = own_heads * HEAD_WIDTH
    block_q = math.gcd(tokens, 256)
    block_k = math.gcd(tokens, 512)
    lengths_row = lengths[0]
    own_route = piece_route[0, 0]
    slot_ids = jnp.arange(ctx_count, dtype=jnp.int32)
    outgoing = jnp.sum(
        slot_ids[None, :] * (own_route[None, :] == slot_ids[:, None]).astype(jnp.int32), axis=1
    )

    def exchange(blocks):
        return lax.all_to_all(blocks, "ctx", split_axis=0, concat_axis=0, tiled=True)

    def to_slots(rows_in):
        return jnp.take(rows_in.reshape(ctx_count, piece_rows, model_width), outgoing, axis=0)

    def to_heads(rows_in):
        by_heads = rows_in.reshape(row_count, ctx_count, -1)
        return exchange(jnp.transpose(by_heads, (1, 0, 2))).reshape(tokens, -1)

    def to_rows(heads_in):
        return exchange(heads_in.reshape(ctx_count, row_count, -1))

    arrived = exchange(to_slots(inputs[0]))
    grad_arrived = exchange(to_slots(cotangent[0]))
    residual = arrived.reshape(row_count, model_width).astype(jnp.float32)
    places = own_index * row_count + jnp.arange(row_count, dtype=jnp.int32)
    unused_begin, unused_end, offset, is_valid = spans(places, lengths_row)
    pack_begin, pack_end, unused_offset, unused_valid = spans(
        jnp.arange(tokens, dtype=jnp.int32), lengths_row
    )
    grad_final = jnp.where(
        is_valid[:, None], grad_arrived.reshape(row_count, model_width).astype(jnp.float32), 0.0
    )
    gains = jnp.pad(jnp.stack([gain_one, gain_two]), ((0, 14), (0, 0)))
    gains_full, qkv_full = gather_weights([gains, qkv_weight])
    gains_full = gains_full.reshape(-1, 16, gains.shape[1])
    gain_attn = gains_full[:, 0].reshape(-1).astype(jnp.float32)
    gain_mlp = gains_full[:, 1].reshape(-1).astype(jnp.float32)
    act_attn = layer_norm(residual, gain_attn).astype(jnp.bfloat16)
    later = [attn_out, geglu_in, geglu_out]
    if lax.axis_size("fsdp") == 4 and ctx_count == 8 and own_width == 128:
        attn_full, in_full, out_full, qkv_heads = gather_weights(
            later, (act_attn, qkv_full) + rotary_tables(offset, own_heads)
        )
    else:
        attn_full, in_full, out_full = gather_weights(later)
        projected = jnp.dot(act_attn, qkv_full, preferred_element_type=jnp.float32)
        cosine, sine = rotary_tables(offset, 1)
        queries, keys = (
            rotate(projected[:, :model_width], cosine, sine).astype(jnp.bfloat16),
            rotate(projected[:, model_width : 2 * model_width], cosine, sine).astype(jnp.bfloat16),
        )
        values = projected[:, 2 * model_width :].astype(jnp.bfloat16)
        joined = jnp.stack(
            [part.reshape(row_count, ctx_count, own_width) for part in (queries, keys, values)], axis=2
        )
        qkv_heads = to_heads(joined.reshape(row_count, -1))
    low, high = key_range(pack_begin, pack_end, block_q, block_k)
    pack_begin, pack_end = (pack_begin[None, :], pack_end[None, :])
    attended_heads, log_total = attention_forward(
        qkv_heads, pack_begin, pack_end, low, high, own_heads, block_q, block_k
    )
    attn_low = jnp.transpose(to_rows(attended_heads.astype(jnp.bfloat16)), (1, 0, 2)).reshape(
        row_count, model_width
    )
    branch_attn = jnp.dot(attn_low, attn_full, preferred_element_type=jnp.float32)
    middle = residual + branch_attn
    act_mlp = layer_norm(middle, gain_mlp).astype(jnp.bfloat16)
    up_both = jnp.dot(act_mlp, in_full, preferred_element_type=jnp.float32)
    ff_width = up_both.shape[1] // 2
    hidden = (jax.nn.gelu(up_both[:, :ff_width], approximate=False) * up_both[:, ff_width:]).astype(
        jnp.bfloat16
    )
    branch_mlp = jnp.dot(hidden, out_full, preferred_element_type=jnp.float32)
    final_rows = jnp.where(is_valid[:, None], middle + branch_mlp, 0.0)
    square_sums = jnp.stack(
        [
            jnp.sum(final_rows * final_rows),
            jnp.sum(jnp.where(is_valid[:, None], branch_attn * branch_attn, 0.0)),
            jnp.sum(jnp.where(is_valid[:, None], branch_mlp * branch_mlp, 0.0)),
        ]
    )
    out_slots = final_rows.astype(jnp.bfloat16).reshape(ctx_count, piece_rows, model_width)
    back_out = exchange(out_slots)
    block_out = jnp.take(back_out, own_route, axis=0).reshape(1, row_count, model_width)
    grad_mlp_low = grad_final.astype(jnp.bfloat16)
    grad_hidden = lax.dot_general(
        grad_mlp_low, out_full, NT, preferred_element_type=jnp.float32
    )

    def gated(leading, trailing):
        return jax.nn.gelu(leading, approximate=False) * trailing

    unused_gate, gate_back = jax.vjp(gated, up_both[:, :ff_width], up_both[:, ff_width:])
    grad_leading, grad_trailing = gate_back(grad_hidden)
    grad_leading, grad_trailing = (
        grad_leading.astype(jnp.bfloat16),
        grad_trailing.astype(jnp.bfloat16),
    )
    grad_up = jnp.concatenate([grad_leading, grad_trailing], axis=1)
    grad_act_mlp = lax.dot_general(grad_up, in_full, NT, preferred_element_type=jnp.float32)
    unused_norm, norm_back_mlp = jax.vjp(layer_norm, middle, gain_mlp)
    grad_middle_norm, grad_gain_mlp = norm_back_mlp(grad_act_mlp)
    grad_middle = grad_final + grad_middle_norm
    grad_attn_low = grad_middle.astype(jnp.bfloat16)
    grad_attended = lax.dot_general(
        grad_attn_low, attn_full, NT, preferred_element_type=jnp.float32
    ).astype(jnp.bfloat16)
    early = weight_sums_early(
        hidden, grad_mlp_low, act_mlp, grad_leading, grad_trailing, attn_low, grad_attn_low
    )
    pack_cosine, pack_sine = pack_rotary_tables(lengths_row, tokens, own_heads)
    block_back = math.gcd(tokens, 256)
    low_back, high_back = key_range(pack_begin[0], pack_end[0], block_q, block_back)
    grad_heads = attention_backward(
        qkv_heads,
        attended_heads,
        to_heads(grad_attended),
        log_total,
        pack_begin,
        pack_end,
        low_back,
        high_back,
        pack_cosine,
        pack_sine,
        [] if early is None else [early[1][0][0]],
        own_heads,
        block_q,
        block_back,
    )
    if early is not None:
        grad_heads, early = second_step(grad_heads, early)
    grad_projected = jnp.transpose(
        to_rows(grad_heads).reshape(ctx_count, row_count, 3, own_width), (1, 2, 0, 3)
    ).reshape(row_count, 3 * model_width)
    grad_act_attn = lax.dot_general(
        grad_projected, qkv_full, NT, preferred_element_type=jnp.float32
    )
    unused_first, norm_back_attn = jax.vjp(layer_norm, residual, gain_attn)
    grad_resid_norm, grad_gain_attn = norm_back_attn(grad_act_attn)
    grad_residual = (grad_middle + grad_resid_norm).astype(jnp.bfloat16)
    back_grad = exchange(grad_residual.reshape(ctx_count, piece_rows, model_width))
    grad_inputs = jnp.take(back_grad, own_route, axis=0).reshape(1, row_count, model_width)
    small = jnp.stack(
        [grad_gain_attn, grad_gain_mlp, jnp.pad(square_sums, (0, model_width - 3))]
        + [jnp.zeros((model_width,), jnp.float32)] * 5
    )
    total_out, total_in, total_qkv, total_attn, small_sums = weight_sums(
        hidden,
        grad_mlp_low,
        act_mlp,
        grad_leading,
        grad_trailing,
        act_attn,
        grad_projected,
        attn_low,
        grad_attn_low,
        small,
        early,
    )
    total_gain_one = own_shard(small_sums[1, 0])
    total_gain_two = own_shard(small_sums[1, 1])
    total_squares = small_sums[0, 2, :3]
    valid_count = jnp.sum(lengths_row).astype(jnp.float32)
    rms_stats = jnp.sqrt(total_squares / (valid_count * model_width))[None, :]
    return (
        block_out,
        grad_inputs,
        total_gain_one,
        total_qkv,
        total_attn,
        total_gain_two,
        total_in,
        total_out,
        rms_stats,
    )


def solution(mesh):
    placed = (
        P("fsdp", "ctx", None),
        P("fsdp", "ctx", None),
        P("fsdp", None),
        P("fsdp", "ctx", None),
        P("fsdp"),
        P("fsdp", None),
        P("fsdp", None),
        P("fsdp"),
        P("fsdp", None),
        P("fsdp", None),
    )
    return jax.shard_map(
        per_device,
        mesh=mesh,
        in_specs=placed,
        out_specs=(
            P("fsdp", "ctx", None),
            P("fsdp", "ctx", None),
            P("fsdp"),
            P("fsdp", None),
            P("fsdp", None),
            P("fsdp"),
            P("fsdp", None),
            P("fsdp", None),
            P("fsdp", None),
        ),
        check_vma=False,
    )
```

```python
import functools
import math
import jax
import jax.numpy as jnp
from jax import lax
from jax.experimental import pallas as pl
from jax.experimental.pallas import tpu as pltpu
from jax.sharding import PartitionSpec as P

HEAD_WIDTH = 64
norm_eps = 1e-05
masked_score = -1e30


def head_stack(rows_in, head_count):
    if head_count == 1:
        return rows_in
    lane_head = lax.broadcasted_iota(jnp.int32, rows_in.shape, 1) // HEAD_WIDTH
    zero = jnp.zeros_like(rows_in)
    return jnp.concatenate(
        [jnp.where(lane_head == h, rows_in, zero) for h in range(head_count)], axis=0
    )


def head_pick(stacked_t, head_count, block):
    return jnp.concatenate(
        [
            stacked_t[h * HEAD_WIDTH : (h + 1) * HEAD_WIDTH, h * block : (h + 1) * block]
            for h in range(head_count)
        ],
        axis=0,
    ).T


NT = (((1,), (1,)), ((), ()))


def forward_kernel(
    head_count, block_q, block_k, low_ref, high_ref, begin_ref, end_ref, qkv_ref, out_ref, log_ref, turned_ref
):
    width = out_ref.shape[1]
    step = pl.program_id(0)

    @pl.when(step == 0)
    def prepare():
        turned_ref[...] = qkv_ref[:, 2 * width :].astype(jnp.float32).T.astype(jnp.bfloat16)

    rows = pl.ds(pl.multiple_of(step * block_q, block_q), block_q)
    scale = 1.0 / math.sqrt(HEAD_WIDTH)
    stacked = head_stack(qkv_ref[rows, :width] * jnp.asarray(scale, jnp.bfloat16), head_count)
    begin = jnp.concatenate([begin_ref[:, rows]] * head_count, axis=1)
    end = jnp.concatenate([end_ref[:, rows]] * head_count, axis=1)

    def body(index, carried):
        top, total, acc = carried
        first = pl.multiple_of(index * block_k, block_k)
        keys = qkv_ref[pl.ds(first, block_k), width : 2 * width]
        scores = lax.dot_general(keys, stacked, NT, preferred_element_type=jnp.float32)
        place = first + lax.broadcasted_iota(jnp.int32, scores.shape, 0)
        scores = jnp.where((place >= begin) & (place < end), scores, masked_score)
        new_top = jnp.maximum(top, jnp.max(scores, axis=0, keepdims=True))
        fresh = jnp.exp(scores - new_top)
        fade = jnp.exp(top - new_top)
        total = total * fade + jnp.sum(fresh, axis=0, keepdims=True)
        acc = acc * fade + jnp.dot(
            turned_ref[:, pl.ds(first, block_k)],
            fresh.astype(jnp.bfloat16),
            preferred_element_type=jnp.float32,
        )
        return (new_top, total, acc)

    lanes = head_count * block_q
    top, total, acc = lax.fori_loop(
        low_ref[step],
        high_ref[step],
        body,
        (
            jnp.full((1, lanes), masked_score, jnp.float32),
            jnp.zeros((1, lanes), jnp.float32),
            jnp.zeros((width, lanes), jnp.float32),
        ),
    )
    valid = end > begin
    safe = jnp.where(valid, total, 1.0)
    acc = jnp.where(valid, acc / safe, 0.0)
    log_total = jnp.where(valid, top + jnp.log(safe), 0.0)
    out_ref[...] = head_pick(acc, head_count, block_q)
    log_ref[0] = log_total


def attention_forward(qkv, begin, end, low, high, head_count, block_q, block_k):
    tokens = qkv.shape[0]
    width = head_count * HEAD_WIDTH
    steps = tokens // block_q
    whole = lambda shape: pl.BlockSpec(shape, lambda i, *_: (0,) * len(shape))
    pairs = tokens * tokens // 4 * head_count
    return pl.pallas_call(
        functools.partial(forward_kernel, head_count, block_q, block_k),
        out_shape=(
            jax.ShapeDtypeStruct((tokens, width), jnp.float32),
            jax.ShapeDtypeStruct((steps, 1, head_count * block_q), jnp.float32),
        ),
        grid_spec=pltpu.PrefetchScalarGridSpec(
            num_scalar_prefetch=2,
            grid=(steps,),
            in_specs=[whole((1, tokens)), whole((1, tokens)), whole((tokens, 3 * width))],
            out_specs=(
                pl.BlockSpec((block_q, width), lambda i, *_: (i, 0)),
                pl.BlockSpec((1, 1, head_count * block_q), lambda i, *_: (i, 0, 0)),
            ),
            scratch_shapes=[pltpu.VMEM((width, tokens), jnp.bfloat16)],
        ),
        cost_estimate=pl.CostEstimate(
            flops=pairs * 512, bytes_accessed=tokens * width * 12, transcendentals=pairs
        ),
        name="attention_forward",
    )(low, high, begin, end, qkv)


def turn_back(grads, cosine, sine, head_count):
    half = HEAD_WIDTH // 2
    pieces = []
    for h in range(head_count):
        base = h * HEAD_WIDTH
        pieces += [grads[:, base + half : base + HEAD_WIDTH], grads[:, base : base + half]]
    return grads * cosine + jnp.concatenate(pieces, axis=1) * sine


def backward_kernel(
    head_count,
    block_q,
    block_k,
    low_ref,
    high_ref,
    begin_ref,
    end_ref,
    qkv_ref,
    attended_ref,
    grad_ref,
    log_ref,
    *refs,
):
    out_ref, turned_ref, key_acc, value_acc = refs[-4:]
    width = attended_ref.shape[1]
    step = pl.program_id(0)

    @pl.when(step == 0)
    def prepare():
        turned_ref[...] = qkv_ref[:, width : 2 * width].astype(jnp.float32).T.astype(jnp.bfloat16)
        key_acc[...] = jnp.zeros_like(key_acc)
        value_acc[...] = jnp.zeros_like(value_acc)

    rows = pl.ds(pl.multiple_of(step * block_q, block_q), block_q)
    scale = 1.0 / math.sqrt(HEAD_WIDTH)
    stacked = head_stack(qkv_ref[rows, :width] * jnp.asarray(scale, jnp.bfloat16), head_count)
    grads = grad_ref[rows, :]
    grad_stacked = head_stack(grads, head_count)
    begin = jnp.concatenate([begin_ref[:, rows]] * head_count, axis=1)
    end = jnp.concatenate([end_ref[:, rows]] * head_count, axis=1)
    product = (grads.astype(jnp.float32) * attended_ref[rows, :]).T
    delta = jnp.concatenate(
        [
            jnp.sum(product[h * HEAD_WIDTH : (h + 1) * HEAD_WIDTH], axis=0, keepdims=True)
            for h in range(head_count)
        ],
        axis=1,
    )
    log_total = log_ref[0]

    def body(index, acc):
        first = pl.multiple_of(index * block_k, block_k)
        span = pl.ds(first, block_k)
        keys = qkv_ref[span, width : 2 * width]
        values = qkv_ref[span, 2 * width :]
        scores = lax.dot_general(keys, stacked, NT, preferred_element_type=jnp.float32)
        grad_probs = lax.dot_general(values, grad_stacked, NT, preferred_element_type=jnp.float32)
        place = first + lax.broadcasted_iota(jnp.int32, scores.shape, 0)
        scores = jnp.where((place >= begin) & (place < end), scores, masked_score)
        probs = jnp.exp(scores - log_total)
        grad_scores = (probs * (grad_probs - delta)).astype(jnp.bfloat16)
        value_acc[span, :] += jnp.dot(
            probs.astype(jnp.bfloat16), grad_stacked, preferred_element_type=jnp.float32
        )
        key_acc[span, :] += jnp.dot(grad_scores, stacked, preferred_element_type=jnp.float32)
        return acc + jnp.dot(
            turned_ref[:, span], grad_scores, preferred_element_type=jnp.float32
        )

    acc = lax.fori_loop(
        low_ref[step],
        high_ref[step],
        body,
        jnp.zeros((width, head_count * block_q), jnp.float32),
    )
    grad_queries = head_pick(acc, head_count, block_q) * scale
    out_ref[rows, :width] = grad_queries.astype(jnp.bfloat16)

    @pl.when(step == pl.num_programs(0) - 1)
    def finish():
        @pl.loop(0, pl.num_programs(0))
        def each(index):
            span = pl.ds(pl.multiple_of(index * block_q, block_q), block_q)
            out_ref[span, width : 2 * width] = key_acc[span, :].astype(jnp.bfloat16)
            out_ref[span, 2 * width :] = value_acc[span, :].astype(jnp.bfloat16)


def attention_backward(
    qkv, attended, grads, log_total, begin, end, low, high, after, head_count, block_q, block_k
):
    tokens = qkv.shape[0]
    width = head_count * HEAD_WIDTH
    steps = tokens // block_q
    whole = lambda shape: pl.BlockSpec(shape, lambda i, *_: (0,) * len(shape))
    pairs = tokens * tokens // 4 * head_count
    return pl.pallas_call(
        functools.partial(backward_kernel, head_count, block_q, block_k),
        out_shape=jax.ShapeDtypeStruct((tokens, 3 * width), jnp.bfloat16),
        grid_spec=pltpu.PrefetchScalarGridSpec(
            num_scalar_prefetch=2,
            grid=(steps,),
            in_specs=[
                whole((1, tokens)),
                whole((1, tokens)),
                whole((tokens, 3 * width)),
                whole((tokens, width)),
                whole((tokens, width)),
                pl.BlockSpec((1, 1, head_count * block_q), lambda i, *_: (i, 0, 0)),
            ]
            + [pl.BlockSpec(memory_space=pl.ANY)] * len(after),
            out_specs=whole((tokens, 3 * width)),
            scratch_shapes=[
                pltpu.VMEM((width, tokens), jnp.bfloat16),
                pltpu.VMEM((tokens, width), jnp.float32),
                pltpu.VMEM((tokens, width), jnp.float32),
            ],
        ),
        cost_estimate=pl.CostEstimate(
            flops=pairs * 1280, bytes_accessed=tokens * width * 30, transcendentals=pairs
        ),
        name="attention_backward",
    )(low, high, begin, end, qkv, attended, grads, log_total, *after)


def rows_kernel(head_count, heads_ref, cosine_ref, sine_ref, query_ref, key_ref, value_ref, out_ref, act_ref):
    width = heads_ref.shape[2] // 3
    step = pl.program_id(0)
    total = out_ref.shape[1] // 3
    pieces = []
    for part in range(3):
        piece = heads_ref[0, :, part * width : (part + 1) * width]
        if part < 2:
            piece = turn_back(
                piece.astype(jnp.float32), cosine_ref[...], sine_ref[...], head_count
            ).astype(jnp.bfloat16)
        first = pl.multiple_of(part * total + step * width, width)
        out_ref[:, pl.ds(first, width)] = piece
        pieces.append(piece)
    weights = jnp.concatenate([query_ref[...], key_ref[...], value_ref[...]], axis=1)
    product = lax.dot_general(
        jnp.concatenate(pieces, axis=1), weights, NT, preferred_element_type=jnp.float32
    )

    @pl.when(step == 0)
    def begin():
        act_ref[...] = product

    @pl.when(step > 0)
    def add():
        act_ref[...] += product


def finish_rows(heads, cosine, sine, qkv_full, head_count):
    owners, rows, columns = heads.shape
    width = columns // 3
    depth = qkv_full.shape[0]
    whole = lambda shape: pl.BlockSpec(shape, lambda i: (0,) * len(shape))
    part_of = lambda part: pl.BlockSpec((depth, width), lambda i: (0, part * owners + i))
    return pl.pallas_call(
        functools.partial(rows_kernel, head_count),
        out_shape=(
            jax.ShapeDtypeStruct((rows, owners * columns), jnp.bfloat16),
            jax.ShapeDtypeStruct((rows, depth), jnp.float32),
        ),
        grid=(owners,),
        in_specs=[
            pl.BlockSpec((1, rows, columns), lambda i: (i, 0, 0)),
            whole((rows, width)),
            whole((rows, width)),
            part_of(0),
            part_of(1),
            part_of(2),
        ],
        out_specs=(whole((rows, owners * columns)), whole((rows, depth))),
        cost_estimate=pl.CostEstimate(
            flops=2 * rows * depth * owners * columns,
            bytes_accessed=2 * depth * owners * columns + 4 * rows * owners * columns,
            transcendentals=0,
        ),
        name="finish_rows",
    )(heads, cosine, sine, qkv_full, qkv_full, qkv_full)


def spans(places, lengths_row):
    ends = jnp.cumsum(lengths_row)
    past = (places[:, None] >= ends[None, :]).astype(jnp.int32)
    begin = jnp.sum(past * lengths_row[None, :], axis=1)
    before = (places[:, None] >= (ends - lengths_row)[None, :]).astype(jnp.int32)
    end = jnp.sum(before * lengths_row[None, :], axis=1)
    valid = places < ends[-1]
    return (jnp.where(valid, begin, 0), jnp.where(valid, end, 0), places - begin, valid)


def key_range(begin, end, block_q, block_k):
    begin_blocks = jnp.where(end > begin, begin, jnp.int32(1 << 30)).reshape(-1, block_q)
    high = (jnp.max(end.reshape(-1, block_q), axis=1) + block_k - 1) // block_k
    low = jnp.minimum(jnp.min(begin_blocks, axis=1) // block_k, high)
    return (low, high)


def rotary_tables(offset, head_count):
    half = HEAD_WIDTH // 2
    inverse = 160000.0 ** (-2.0 * jnp.arange(half, dtype=jnp.float32) / HEAD_WIDTH)
    angles = offset.astype(jnp.float32)[:, None] * inverse[None, :]
    cosine, sine = (jnp.cos(angles), jnp.sin(angles))
    return (
        jnp.concatenate([cosine, cosine] * head_count, axis=1),
        jnp.concatenate([sine, -sine] * head_count, axis=1),
    )


def toggled(index, bit):
    return index + bit - 2 * bit * ((index // bit) % 2)


def gather_kernel(shapes, projects, *refs):
    count = len(shapes)
    shard_refs, refs = (refs[:count], refs[count:])
    if projects:
        act_ref, qkv_ref, cosine_ref, sine_ref = refs[:4]
        heads_ref = refs[4 + count]
        columns_ref, held_ref, load_sem, head_send, head_recv, own_sem = refs[count + 8 :]
        refs = refs[4 : 4 + count] + refs[count + 5 : count + 8]
    full_refs = refs[:count]
    send_sem, recv_sem, local_sem = refs[count:]
    shards = lax.axis_size("fsdp")
    slices = lax.axis_size("ctx") // 2
    own_ctx, own_shard = (lax.axis_index("ctx"), lax.axis_index("fsdp"))
    core, chip = (own_ctx % 2, own_ctx // 2)
    barrier = pltpu.get_barrier_semaphore()
    partners = [{"fsdp": toggled(own_shard, bit)} for bit in (1, 2)]
    partners += [{"ctx": toggled(own_ctx, bit)} for bit in (1, 2, 4)]

    def owner_at(relation):
        owner = own_ctx
        for bit in (1, 2, 4):
            if relation & bit:
                owner = toggled(owner, bit)
        return owner

    if projects:
        partners += [{"ctx": owner_at(relation)} for relation in (3, 5, 6, 7)]
    for partner in partners:
        pl.semaphore_signal(
            barrier, inc=1, device_id=partner, device_id_type=pl.DeviceIdType.MESH
        )
    pl.semaphore_wait(barrier, len(partners))
    to_one, to_two, to_core, to_x, to_y = partners[:5]

    def shard_at(step):
        if step == 0:
            return own_shard
        if step == 3:
            return toggled(toggled(own_shard, 1), 2)
        return toggled(own_shard, step)

    def region(ref, weight, step, chip_at, half):
        if shapes[weight] == "small":
            return ref if len(ref.shape) == 2 else ref.at[shard_at(step)]
        if shapes[weight] == "rows":
            rows = ref.shape[-2]
            span = pl.ds(0, rows) if half is None else pl.ds(half * (rows // 2), rows // 2)
            if len(ref.shape) == 4:
                return ref.at[core, chip_at, span, :]
            return ref.at[shard_at(step), core, chip_at, span, :]
        rows = ref.shape[-2]
        first = (rows // 2) // 16 * 16
        spans_of = {None: pl.ds(0, rows), 0: pl.ds(0, first), 1: pl.ds(first, rows - first)}
        width = ref.shape[-1] // (2 * slices)
        columns = pl.ds(pl.multiple_of((core * slices + chip_at) * width, width), width)
        if len(ref.shape) == 2:
            return ref.at[spans_of[half], columns]
        return ref.at[shard_at(step), spans_of[half], columns]

    def core_region(ref, weight, step):
        if shapes[weight] == "rows":
            return ref.at[shard_at(step), core]
        width = ref.shape[-1] // 2
        return ref.at[shard_at(step), :, pl.ds(pl.multiple_of(core * width, width), width)]

    pending = []

    def send(source, target, slot, partner):
        copy = pltpu.make_async_remote_copy(
            src_ref=source,
            dst_ref=target,
            send_sem=send_sem.at[slot],
            recv_sem=recv_sem.at[slot],
            device_id=partner,
            device_id_type=pl.DeviceIdType.MESH,
        )
        copy.start()
        pending.append(copy)
        return copy

    copies = {}
    local = []

    def slot_of(weight, step, kind):
        return (weight * 3 + step - 1) * 8 + kind

    def shard_sends(weight):
        source = region(shard_refs[weight], weight, 0, chip, None)
        target = region(full_refs[weight], weight, 0, chip, None)
        copies[weight, 2, 0] = send(source, target, slot_of(weight, 2, 0), to_two)
        copies[weight, 1, 0] = send(source, target, slot_of(weight, 1, 0), to_one)
        target = full_refs[weight].at[own_shard]
        copy = pltpu.make_async_copy(shard_refs[weight], target, local_sem.at[weight])
        copy.start()
        local.append(copy)

    def shard_forward(weight):
        copies[weight, 2, 0].wait_recv()
        piece = region(full_refs[weight], weight, 2, chip, None)
        copies[weight, 3, 0] = send(piece, piece, slot_of(weight, 3, 0), to_one)

    def plane_sends(weight, step):
        lead = region(full_refs[weight], weight, step, chip, 0)
        rest = region(full_refs[weight], weight, step, chip, 1)
        for kind, piece, partner in ((1, lead, to_x), (2, rest, to_y), (3, lead, to_y), (4, rest, to_x)):
            copies[weight, step, kind] = send(piece, piece, slot_of(weight, step, kind), partner)

    def plane_forward(weight, step):
        copies[weight, step, 1].wait_recv()
        lead = region(full_refs[weight], weight, step, toggled(chip, 1), 0)
        copies[weight, step, 5] = send(lead, lead, slot_of(weight, step, 5), to_y)
        copies[weight, step, 2].wait_recv()
        rest = region(full_refs[weight], weight, step, toggled(chip, 2), 1)
        copies[weight, step, 6] = send(rest, rest, slot_of(weight, step, 6), to_x)

    def core_send(weight, step):
        for kind in (3, 4, 5, 6):
            copies[weight, step, kind].wait_recv()
        piece = core_region(full_refs[weight], weight, step)
        copies[weight, step, 7] = send(piece, piece, slot_of(weight, step, 7), to_core)

    chip_order = (3, 1, 2, 0)

    def start_loads():
        loads = {}
        for chip_bits in chip_order:
            owner_chip = owner_at(2 * chip_bits) // 2
            for part in range(3):
                width = columns_ref.shape[2] // 3
                total = qkv_ref.shape[1] // 3
                first = pl.multiple_of(part * total + owner_chip * width, width)
                loads[chip_bits, part] = pltpu.make_async_copy(
                    qkv_ref.at[:, pl.ds(first, width)],
                    columns_ref.at[chip_bits, :, pl.ds(part * width, width)],
                    load_sem.at[chip_bits * 3 + part],
                )
                loads[chip_bits, part].start()
        return loads

    def project(chip_bits, loads):
        for part in range(3):
            loads[chip_bits, part].wait()
        rows, own_width = (act_ref.shape[0], held_ref.shape[2] // 3)
        product = jnp.dot(
            act_ref[...], columns_ref[chip_bits], preferred_element_type=jnp.float32
        )
        for core_at in (0, 1):
            slot = 2 * chip_bits + core + core_at - 2 * core * core_at
            for part in range(3):
                first = (2 * part + core_at) * own_width
                piece = product[:, first : first + own_width]
                if part < 2:
                    half = HEAD_WIDTH // 2
                    turned = []
                    for base in range(0, own_width, HEAD_WIDTH):
                        turned += [piece[:, base + half : base + HEAD_WIDTH], piece[:, base : base + half]]
                    piece = piece * cosine_ref[...] - jnp.concatenate(turned, axis=1) * sine_ref[...]
                held_ref[slot, :, part * own_width : (part + 1) * own_width] = piece.astype(jnp.bfloat16)
        target = heads_ref.at[pl.ds(pl.multiple_of(own_ctx * rows, rows), rows), :]
        for core_bit in (0, 1):
            relation = 2 * chip_bits + core_bit
            if relation == 0:
                copy = pltpu.make_async_copy(held_ref.at[0], target, own_sem.at[0])
                copy.start()
                local.append(copy)
                continue
            copy = pltpu.make_async_remote_copy(
                src_ref=held_ref.at[relation],
                dst_ref=target,
                send_sem=head_send.at[relation],
                recv_sem=head_recv.at[relation],
                device_id={"ctx": owner_at(relation)},
                device_id_type=pl.DeviceIdType.MESH,
            )
            copy.start()
            pending.append(copy)
            arriving.append(copy)

    arriving = []
    sent = 1
    if projects:
        loads = start_loads()
        for weight in range(count):
            shard_sends(weight)
        sent = count
        for chip_bits in chip_order:
            project(chip_bits, loads)
    else:
        shard_sends(0)
    for weight in range(count):
        if weight + 1 >= sent and weight + 1 < count:
            shard_sends(weight + 1)
        shard_forward(weight)
        copies[weight, 1, 0].wait_recv()
        if shapes[weight] == "small":
            copies[weight, 3, 0].wait_recv()
            continue
        plane_sends(weight, 1)
        plane_sends(weight, 2)
        copies[weight, 3, 0].wait_recv()
        plane_sends(weight, 3)
        for step in (1, 2, 3):
            plane_forward(weight, step)
        if weight > 0 and shapes[weight - 1] != "small":
            for step in (1, 2, 3):
                core_send(weight - 1, step)
    for step in (1, 2, 3):
        core_send(count - 1, step)
    for weight in range(count):
        if shapes[weight] != "small":
            for step in (1, 2, 3):
                copies[weight, step, 7].wait_recv()
    for copy in arriving:
        copy.wait_recv()
    for copy in pending:
        copy.wait_send()
    for copy in local:
        copy.wait()


def gather_weights(weights, projection=None):
    shards, ctx_count = (lax.axis_size("fsdp"), lax.axis_size("ctx"))
    slices = ctx_count // 2
    shapes, views, outs = ([], [], [])
    for weight in weights:
        rows, columns = weight.shape
        if rows % (32 * ctx_count) == 0:
            shapes.append("rows")
            views.append(weight.reshape(2, slices, rows // ctx_count, columns))
            outs.append((shards, 2, slices, rows // ctx_count, columns))
        elif rows == 16:
            shapes.append("small")
            views.append(weight)
            outs.append((shards, rows, columns))
        elif columns % (128 * ctx_count) == 0 and rows % 16 == 0:
            shapes.append("columns")
            views.append(weight)
            outs.append((shards, rows, columns))
    if shards != 4 or ctx_count != 8 or len(views) < len(weights):
        return [lax.all_gather(weight, "fsdp", axis=0, tiled=True) for weight in weights]
    slots = len(views) * 24
    vmem, anywhere, dma = (
        pl.BlockSpec(memory_space=pltpu.VMEM),
        pl.BlockSpec(memory_space=pl.ANY),
        pltpu.SemaphoreType.DMA,
    )
    in_specs = [vmem] * len(views)
    scratch = [dma((slots,)), dma((slots,)), dma((len(views),))]
    if projection is not None:
        act_attn, qkv_full = projection[:2]
        rows, own_columns = (act_attn.shape[0], qkv_full.shape[1] // ctx_count)
        views += list(projection)
        in_specs += [vmem, anywhere, vmem, vmem]
        outs.append((ctx_count * rows, own_columns))
        scratch += [
            pltpu.VMEM((slices, qkv_full.shape[0], 2 * own_columns), jnp.bfloat16),
            pltpu.VMEM((ctx_count, rows, own_columns), jnp.bfloat16),
            dma((3 * slices,)),
            dma((ctx_count,)),
            dma((ctx_count,)),
            dma((1,)),
        ]
    held = pl.pallas_call(
        functools.partial(gather_kernel, shapes, projection is not None),
        out_shape=tuple(jax.ShapeDtypeStruct(out, jnp.bfloat16) for out in outs),
        in_specs=in_specs,
        out_specs=tuple(anywhere for out in outs),
        scratch_shapes=scratch,
        compiler_params=pltpu.CompilerParams(
            collective_id=0 if projection is None else 2,
            has_side_effects=True,
            vmem_limit_bytes=60 * 1024 * 1024,
        ),
        name="gather_weights" if projection is None else "gather_and_project",
    )(*views)
    return [whole.reshape(-1, whole.shape[-1]) for whole in held]


def pair_steps(plan, lead_rows, left_refs, right_refs, turned_refs, whole_refs, sems, core, pending, send):
    pair_send, pair_recv, near_sem = sems
    to_core = {"ctx": toggled(lax.axis_index("ctx"), 1)}

    def send_core(source, target, sent, got, start=True):
        return send(source, target, sent, got, to_core, start)

    rows = left_refs[0].shape[0] if left_refs else 0
    pairs = []
    for w, entry in enumerate(plan):
        span, right = (plan_span(entry), right_refs[w])
        own_part, other_part = (whole_refs[w].at[pl.ds(0, rows)], whole_refs[w].at[pl.ds(rows, rows)])

        def exchange(own_half, other_half, start=True):
            near = pltpu.make_async_copy(own_half, own_part, near_sem.at[w])
            if start:
                near.start()
            sems = (pair_send.at[2 * w], pair_recv.at[2 * w])
            return [near, send_core(other_half, other_part, *sems, start)]

        if entry[5]:
            ways = [exchange(right[at], right[1 - at], False) for at in (0, 1)]
            for at in (0, 1):

                @pl.when(core == at)
                def begin():
                    for copy in ways[at]:
                        copy.start()

            pairs.append(ways[0])
            pending.append(ways[0][1])
        else:
            halves = [
                right.at[:, pl.ds(pl.multiple_of(at * span, span), span)] for at in (core, 1 - core)
            ]
            pairs.append(exchange(*halves))

    def turn(w):
        left, turned = (left_refs[w], turned_refs[w])
        block = 512
        for first in range(0, left.shape[1], block):
            last = min(first + block, left.shape[1])
            turned[first:last, :rows] = (
                left[:, first:last].astype(jnp.float32).T.astype(jnp.bfloat16)
            )
        pairs[w].append(
            send_core(
                turned.at[:, pl.ds(0, rows)],
                turned.at[:, pl.ds(rows, rows)],
                pair_send.at[2 * w + 1],
                pair_recv.at[2 * w + 1],
            )
        )

    def multiply(w, t, first, second):
        kind, count, width, deep, halves, parted = plan[w]
        if t == 0:
            near, far, turned = pairs[w]
            near.wait()
            far.wait_recv()
            turned.wait_recv()

        def each(z, carried):
            left = turned_refs[w][pl.ds(pl.multiple_of(z * deep, 16), deep), :]
            if kind == "rows":
                last = min((t + 1) * width, whole_refs[w].shape[1])
                part = jnp.dot(
                    left, whole_refs[w][:, t * width : last], preferred_element_type=jnp.float32
                ).astype(jnp.bfloat16)
                if last < (t + 1) * width:
                    empty = jnp.zeros((deep, (t + 1) * width - last), jnp.bfloat16)
                    part = jnp.concatenate([part, empty], axis=1)
                piece_rows = first.shape[3]
                for s in range(4):
                    first[z, s // 2, s % 2] = part[2 * s * piece_rows : (2 * s + 1) * piece_rows]
                    second[z, s // 2, s % 2] = part[(2 * s + 1) * piece_rows : (2 * s + 2) * piece_rows]
            else:
                part = jnp.dot(
                    left, whole_refs[w][...], preferred_element_type=jnp.float32
                ).astype(jnp.bfloat16)
                for s in range(4):
                    piece = part[:, s * width : (s + 1) * width]
                    first[z, s // 2, s % 2] = piece[:lead_rows]
                    second[z, s // 2, s % 2] = piece[lead_rows:]
            return carried

        lax.fori_loop(0, 4, each, 0)

    return (turn, multiply)


def remote_send(pending):
    def send(source, target, sent, got, partner, start=True):
        copy = pltpu.make_async_remote_copy(
            src_ref=source,
            dst_ref=target,
            send_sem=sent,
            recv_sem=got,
            device_id=partner,
            device_id_type=pl.DeviceIdType.MESH,
        )
        if start:
            copy.start()
            pending.append(copy)
        return copy

    return send


def product_kernel(plan, lead_rows, *refs):
    groups, places = early_places(plan)
    weights, outs = (len(plan), 4 * len(groups))
    left_refs, refs = (refs[:weights], refs[weights:])
    right_refs = []
    for entry in plan:
        held = 2 if entry[5] else 1
        right_refs.append(refs[:held] if held == 2 else refs[0])
        refs = refs[held:]
    out_refs = refs[:outs]
    scratch = list(refs[outs:])
    turned_refs = [scratch.pop(0) for weight in plan]
    whole_refs = [scratch.pop(0) for weight in plan]
    chunks = [(w, t) for w, entry in enumerate(plan) for t in range(entry[1])]
    held = [(scratch.pop(0), scratch.pop(0)) for chunk in chunks]
    pair_send, pair_recv, near_sem, store_sem = scratch
    own_ctx = lax.axis_index("ctx")
    core, chip = (own_ctx % 2, own_ctx // 2)
    own_x, own_y = (chip % 2, chip // 2)
    to_core = {"ctx": toggled(own_ctx, 1)}
    barrier = pltpu.get_barrier_semaphore()
    pl.semaphore_signal(barrier, inc=1, device_id=to_core, device_id_type=pl.DeviceIdType.MESH)
    pl.semaphore_wait(barrier, 1)
    pending = []
    send = remote_send(pending)
    turn, multiply = pair_steps(
        plan,
        lead_rows,
        left_refs,
        right_refs,
        turned_refs,
        whole_refs,
        (pair_send, pair_recv, near_sem),
        core,
        pending,
        send,
    )
    for w in range(weights):
        turn(w)
    stores = []
    for number, (w, t) in enumerate(chunks):
        first, second = held[number]
        multiply(w, t, first, second)
        group, offset = places[number]
        sides = (
            lambda at: first.at[:, at, own_x],
            lambda at: first.at[:, at, 1 - own_x],
            lambda at: second.at[:, own_y, at],
            lambda at: second.at[:, 1 - own_y, at],
        )
        for side, source_at in enumerate(sides):
            for at in (0, 1):
                copy = pltpu.make_async_copy(
                    source_at(at),
                    out_refs[4 * group + side].at[at, :, :, pl.ds(offset, plan[w][2])],
                    store_sem.at[8 * number + 2 * side + at],
                )
                copy.start()
                stores.append(copy)
    for copy in stores:
        copy.wait()
    for copy in pending:
        copy.wait_send()


def weight_plan(kind, left, right, count):
    deep = left.shape[1] // 4
    if kind == "rows":
        parted = isinstance(right, tuple)
        span = right[0].shape[1] if parted else right.shape[1] // 2
        width = -(-span // (128 * count)) * 128
        return (kind, count, width, deep, (deep // 8, deep // 8), span if parted else 0)
    lead_rows = deep // 2 // 16 * 16
    return (kind, count, right.shape[-1] // 8, deep, (lead_rows, deep - lead_rows), 0)


def early_places(plan):
    groups, places = ([], [])
    for kind, count, width, deep, halves, parted in plan:
        found = [at for at, group in enumerate(groups) if group[0] == halves]
        if not found:
            groups.append([halves, 0])
            found = [len(groups) - 1]
        for chunk in range(count):
            places.append((found[0], groups[found[0]][1]))
            groups[found[0]][1] += width
    return (groups, places)


def plan_span(entry):
    return entry[1] * entry[2] if entry[0] == "rows" else 4 * entry[2]


def plan_lead(plan):
    return max([0] + [entry[4][0] for entry in plan if entry[0] == "columns"])


def pair_scratch(plan, tokens):
    turned = [pltpu.VMEM((4 * entry[3], 2 * tokens), jnp.bfloat16) for entry in plan]
    return turned + [
        pltpu.VMEM((2 * tokens, entry[5] or plan_span(entry)), jnp.bfloat16) for entry in plan
    ]


def early_sums(products):
    plan = [weight_plan(*product) for product in products]
    lefts, rights = ([product[1] for product in products], [product[2] for product in products])
    vmem, anywhere, dma = (
        pl.BlockSpec(memory_space=pltpu.VMEM),
        pl.BlockSpec(memory_space=pl.ANY),
        pltpu.SemaphoreType.DMA,
    )
    rights = [part for right in rights for part in (right if isinstance(right, tuple) else [right])]
    groups = early_places(plan)[0]
    outs, held = ([], [])
    for halves, columns in groups:
        for half in halves:
            outs += [jax.ShapeDtypeStruct((2, 4, half, columns), jnp.bfloat16)] * 2
    for kind, count, width, deep, halves, parted in plan:
        for chunk in range(count):
            held += [pltpu.VMEM((4, 2, 2, half, width), jnp.bfloat16) for half in halves]
    chunk_count = sum(entry[1] for entry in plan)
    scratch = pair_scratch(plan, lefts[0].shape[0]) + held
    scratch += [dma((2 * len(plan),)), dma((2 * len(plan),)), dma((len(plan),)), dma((8 * chunk_count,))]
    sides = pl.pallas_call(
        functools.partial(product_kernel, plan, plan_lead(plan)),
        out_shape=tuple(outs),
        in_specs=[vmem] * len(plan) + [anywhere] * len(rights),
        out_specs=(anywhere,) * len(outs),
        scratch_shapes=scratch,
        compiler_params=pltpu.CompilerParams(
            collective_id=3, has_side_effects=True, vmem_limit_bytes=60 * 1024 * 1024
        ),
        name="early_products",
    )(*lefts, *rights)
    arrays = []
    for group in range(len(groups)):
        for part, bit in ((0, 2), (2, 4)):
            kept, sent = sides[4 * group + part : 4 * group + part + 2]
            arrays.append((kept, swap(sent, "ctx", bit)))
    return (plan, arrays)


def second_step(held, early):
    plan, arrays = early
    held, arrays = lax.optimization_barrier((held, arrays))
    chip = lax.axis_index("ctx") // 2
    flat = []
    for at, (kept, arrived) in enumerate(arrays):
        bit, own = ((4, chip // 2), (2, chip % 2))[at % 2]
        other = [
            lax.dynamic_index_in_dim(side, 1 - own, 0, keepdims=False).astype(jnp.float32)
            for side in (kept, arrived)
        ]
        flat += [kept, arrived, swap((other[0] + other[1]).astype(jnp.bfloat16), "ctx", bit)]
    return (held, (plan, flat))


def sum_kernel(early, late, lead_rows, *refs):
    weights, products = (len(early) + len(late), len(late))
    left_refs, right_refs = (refs[:products], refs[products : 2 * products])
    refs = refs[2 * products :]
    groups, places = early_places(early)
    early_refs, refs = (refs[: 6 * len(groups)], refs[6 * len(groups) :])
    small_ref, out_refs, small_out = (refs[0], refs[1 : weights + 1], refs[weights + 1])
    scratch = list(refs[weights + 2 :])
    turned_refs = [scratch.pop(0) for weight in late]
    whole_refs = [scratch.pop(0) for weight in late]
    plan = early + late
    chunks = [(w, t) for w, entry in enumerate(plan) for t in range(entry[1])]
    early_count = sum(entry[1] for entry in early)
    units = {}
    for number in range(len(chunks)):
        for half in (0, 1):
            units[number, half] = [scratch.pop(0) for stage in range(5)]
    small_held = scratch.pop(0)
    send_sem, recv_sem, local_sem, load_sem, pair_send, pair_recv, small_send, small_recv, near_sem = scratch
    own_ctx, own_shard = (lax.axis_index("ctx"), lax.axis_index("fsdp"))
    core, chip = (own_ctx % 2, own_ctx // 2)
    own_x, own_y = (chip % 2, chip // 2)
    low_bit, high_bit = (own_shard % 2, own_shard // 2)
    loads = {}
    for number in range(early_count):
        w, (group, offset) = (chunks[number][0], places[number])
        for half in (0, 1):
            own = own_y if half == 0 else own_x
            kept, arrived, twice = early_refs[6 * group + 3 * half : 6 * group + 3 * half + 3]
            columns = pl.ds(offset, plan[w][2])
            sources = (kept.at[own, :, :, columns], arrived.at[own, :, :, columns], twice.at[:, :, columns])
            for at, source in enumerate(sources):
                slot = (number * 2 + half) * 3 + at
                copy = pltpu.make_async_copy(source, units[number, half][at], load_sem.at[slot])
                copy.start()
                loads[number, half, at] = copy
    partners = [{"ctx": toggled(own_ctx, bit)} for bit in (1, 2, 4)]
    partners += [{"fsdp": toggled(own_shard, bit)} for bit in (1, 2)]
    barrier = pltpu.get_barrier_semaphore()
    for partner in partners:
        pl.semaphore_signal(
            barrier, inc=1, device_id=partner, device_id_type=pl.DeviceIdType.MESH
        )
    pl.semaphore_wait(barrier, len(partners))
    to_core, to_x, to_y, to_one, to_two = partners
    pending = []
    send = remote_send(pending)
    turn, multiply = pair_steps(
        late,
        lead_rows,
        left_refs,
        right_refs,
        turned_refs,
        whole_refs,
        (pair_send, pair_recv, near_sem),
        core,
        pending,
        send,
    )
    copies = {}

    def hop(number, half, stage, source, target, partner):
        slot = (number * 2 + half) * 8 + stage
        copies[number, half, stage] = send(
            source, target, send_sem.at[slot], recv_sem.at[slot], partner
        )

    def stage_one(number):
        w, t = chunks[number]
        multiply(w - len(early), t, units[number, 0][0], units[number, 1][0])
        hop(number, 0, 0, units[number, 0][0].at[:, :, 1 - own_x], units[number, 0][1], to_x)
        hop(number, 1, 0, units[number, 1][0].at[:, 1 - own_y], units[number, 1][1], to_y)

    def add(target, source_at, count):
        def each(i, carried):
            target[i] = (
                target[i].astype(jnp.float32) + source_at(i).astype(jnp.float32)
            ).astype(jnp.bfloat16)
            return carried

        lax.fori_loop(0, count, each, 0)

    def stage_two(number):
        held, got = (units[number, 0][0], units[number, 0][1])
        copies[number, 0, 0].wait_recv()
        add(got, lambda z: held[z, :, own_x], 4)
        held_b, got_b = (units[number, 1][0], units[number, 1][1])
        copies[number, 1, 0].wait_recv()
        add(got_b, lambda z: held_b[z, own_y], 4)
        hop(number, 0, 1, got.at[:, 1 - own_y], units[number, 0][2], to_y)
        hop(number, 1, 1, got_b.at[:, 1 - own_x], units[number, 1][2], to_x)

    def stage_three(number):
        for half in (0, 1):
            kept, held, got = units[number, half][:3]
            own = own_y if half == 0 else own_x
            if number < early_count:
                for at in range(3):
                    loads[number, half, at].wait()
                add(held, lambda z: kept[z], 4)
                add(got, lambda z: held[z], 4)
            else:
                copies[number, half, 1].wait_recv()
                add(got, lambda z: held[z, own], 4)
        for half in (0, 1):
            got = units[number, half][2]
            for high in (0, 1):
                hop(
                    number,
                    half,
                    2 + 4 * high,
                    got.at[2 * high + 1 - low_bit],
                    units[number, half][3].at[high],
                    to_one,
                )

    def stage_four(number):
        for half in (0, 1):
            held, got = (units[number, half][2], units[number, half][3])
            copies[number, half, 2].wait_recv()
            copies[number, half, 6].wait_recv()
            add(got, lambda high: held[2 * high + low_bit], 2)
        for half in (0, 1):
            got = units[number, half][3]
            hop(number, half, 3, got.at[1 - high_bit], units[number, half][4].at[0], to_two)

    def final_region(number, half, chip_at):
        w, t = chunks[number]
        kind, count, width = plan[w][:3]
        deep = units[number, half][4].shape[1]
        if kind == "rows":
            start = pl.multiple_of((2 * chip_at + half) * deep, deep)
            column = pl.multiple_of((core * count + t) * width, width)
            return out_refs[w].at[pl.ds(start, deep), pl.ds(column, width)]
        column = pl.multiple_of((core * 4 + chip_at) * width, width)
        return out_refs[w].at[pl.ds(half * lead_rows, deep), pl.ds(column, width)]

    local = {}

    def stage_five(number):
        for half in (0, 1):
            held, got = (units[number, half][3], units[number, half][4])
            copies[number, half, 3].wait_recv()
            add(got, lambda i: held[high_bit], 1)
        for half in (0, 1):
            got = units[number, half][4].at[0]
            target = final_region(number, half, chip)
            hop(number, half, 4, got, target, to_x if half == 0 else to_y)
            hop(number, half, 5, got, target, to_y if half == 0 else to_x)
            copy = pltpu.make_async_copy(got, target, local_sem.at[number * 2 + half])
            copy.start()
            local[number, half] = copy

    def stage_six(number):
        for half in (0, 1):
            copies[number, half, 4].wait_recv()
            piece = final_region(number, half, toggled(chip, 1 if half == 0 else 2))
            hop(number, half, 7, piece, piece, to_y if half == 0 else to_x)

    def stage_seven(number):
        w, t = chunks[number]
        kind, count, width = plan[w][:3]
        for half in (0, 1):
            copies[number, half, 5].wait_recv()
            copies[number, half, 7].wait_recv()
            local[number, half].wait()
        span = width if kind == "rows" else 4 * width
        at = core * count + t if kind == "rows" else core
        piece = out_refs[w].at[:, pl.ds(pl.multiple_of(at * span, span), span)]
        slot = len(chunks) * 16 + number
        copies[number, 2, 0] = send(
            piece, piece, send_sem.at[slot], recv_sem.at[slot], to_core
        )

    small_copies = []

    def small_step(step):
        if step > 0:
            small_copies[step - 1].wait_recv()
            small_held[2 * step] = small_held[2 * step - 2] + small_held[2 * step - 1]
            if step == 3:
                small_out[0] = small_held[6]
        else:
            small_held[0] = small_ref[...]
        if step < 5:
            small_copies.append(
                send(
                    small_held.at[2 * step],
                    small_held.at[2 * step + 1],
                    small_send.at[step],
                    small_recv.at[step],
                    partners[step],
                )
            )
        else:
            small_out[1] = small_held[10]

    stages = (stage_one, stage_two, stage_three, stage_four, stage_five, stage_six, stage_seven)
    small_at = 0
    stage_three(0)
    for w in range(len(late)):
        turn(w)
    for tick in range(len(chunks) + len(stages)):
        for lag, stage in enumerate(stages):
            for number in range(len(chunks)):
                start = number - 2 if number < early_count else number - early_count
                if start + lag == tick and (number >= early_count or (lag >= 2 and number + lag > 2)):
                    stage(number)
        if small_at < 6:
            small_step(small_at)
            small_at += 1
    for number in range(len(chunks)):
        copies[number, 2, 0].wait_recv()
    for copy in pending:
        copy.wait_send()


def sum_weights(early, early_arrays, products, small):
    late = [weight_plan(*product) for product in products]
    lefts, rights = ([product[1] for product in products], [product[2] for product in products])
    plan = early + late
    pieces = []
    for w, (kind, count, width, deep, halves, parted) in enumerate(plan):
        leads = [(4, 2, 2), (4, 2), (4,), (2,), (1,)]
        if w < len(early):
            leads[:2] = [(4,), (4,)]
        for chunk in range(count):
            for half in halves:
                pieces += [pltpu.VMEM(lead + (half, width), jnp.bfloat16) for lead in leads]
    outs = [jax.ShapeDtypeStruct((entry[3], 2 * plan_span(entry)), jnp.bfloat16) for entry in plan]
    chunk_count = sum(entry[1] for entry in plan)
    scratch = pair_scratch(late, lefts[0].shape[0]) + pieces
    scratch += [pltpu.VMEM((11,) + small.shape, jnp.float32)]
    dma = pltpu.SemaphoreType.DMA
    slots = chunk_count * 17
    scratch += [dma((slots,)), dma((slots,)), dma((2 * chunk_count,)), dma((6 * chunk_count,))]
    scratch += [dma((2 * len(late),)), dma((2 * len(late),)), dma((5,)), dma((5,)), dma((len(late),))]
    vmem, anywhere = (
        pl.BlockSpec(memory_space=pltpu.VMEM),
        pl.BlockSpec(memory_space=pl.ANY),
    )
    return pl.pallas_call(
        functools.partial(sum_kernel, early, late, plan_lead(plan)),
        out_shape=tuple(outs) + (jax.ShapeDtypeStruct((2,) + small.shape, jnp.float32),),
        in_specs=[vmem] * len(late) + [anywhere] * (len(late) + len(early_arrays)) + [vmem],
        out_specs=(anywhere,) * len(plan) + (vmem,),
        scratch_shapes=scratch,
        compiler_params=pltpu.CompilerParams(
            collective_id=1, has_side_effects=True, vmem_limit_bytes=60 * 1024 * 1024
        ),
        name="sum_weights",
    )(*lefts, *rights, *early_arrays, small)


def layer_norm(rows_in, gain_vec):
    row_mean = jnp.mean(rows_in, axis=-1, keepdims=True)
    centred = rows_in - row_mean
    variance = jnp.mean(centred * centred, axis=-1, keepdims=True)
    return centred * lax.rsqrt(variance + norm_eps) * gain_vec


def rotate(projected, cosine, sine):
    row_count, width = projected.shape
    half_width = HEAD_WIDTH // 2
    by_head = projected.reshape(row_count, width // HEAD_WIDTH, HEAD_WIDTH)
    turned = jnp.concatenate([by_head[..., half_width:], by_head[..., :half_width]], axis=-1)
    return (by_head * cosine[:, None, :] - turned * sine[:, None, :]).reshape(row_count, width)


def swap(value, axis, bit):
    pairs = [(i, i ^ bit) for i in range(lax.axis_size(axis))]
    return lax.ppermute(value, axis, pairs)


def bit_of(axis, bit):
    return (lax.axis_index(axis) // bit) % 2 == 1


def bits_below(count):
    return [1 << i for i in range(count.bit_length() - 1)]


def reduce_pieces(pieces, labels, order):
    labels = list(labels)
    for axis, bit in order:
        at = labels.index((axis, bit))
        labels.pop(at)
        first = lax.index_in_dim(pieces, 0, at, keepdims=False)
        second = lax.index_in_dim(pieces, 1, at, keepdims=False)
        upper = bit_of(axis, bit)
        arrived = swap(jnp.where(upper, first, second), axis, bit)
        kept = jnp.where(upper, second, first)
        pieces = (kept.astype(jnp.float32) + arrived.astype(jnp.float32)).astype(jnp.bfloat16)
    return pieces


def gather_pieces(piece, labels, order):
    held = []
    for axis, bit in reversed(order):
        arrived = swap(piece, axis, bit)
        upper = bit_of(axis, bit)
        held = [label for label in labels if label in held or label == (axis, bit)]
        piece = jnp.stack(
            [jnp.where(upper, arrived, piece), jnp.where(upper, piece, arrived)],
            axis=held.index((axis, bit)),
        )
    return piece


def keep_and_send(first, second):
    upper = bit_of("ctx", 1)
    return (jnp.where(upper, second, first), jnp.where(upper, first, second))


def core_product(left, first, second):
    kept, sent = keep_and_send(first, second)
    left_all = jnp.concatenate([left, swap(left, "ctx", 1)], axis=0)
    right_all = jnp.concatenate([kept, swap(sent, "ctx", 1)], axis=0)
    return lax.dot_general(
        left_all, right_all, (((0,), (0,)), ((), ())), preferred_element_type=jnp.float32
    ).astype(jnp.bfloat16)


def shard_sum(product, by_columns):
    shards = lax.axis_size("fsdp")
    slices = lax.axis_size("ctx") // 2
    rows, columns = product.shape
    shard_labels = [("fsdp", bit) for bit in reversed(bits_below(shards))]
    slice_labels = [("ctx", 2 * bit) for bit in reversed(bits_below(slices))]
    if by_columns:
        cut = product.reshape(shards, rows // shards, slices, columns // slices)
        cut = jnp.transpose(cut, (0, 2, 1, 3))
    else:
        cut = product.reshape(shards, slices, rows // shards // slices, columns)
    parts = []
    half = cut.shape[2] // 2
    tail = list(reversed(shard_labels))
    for lead, orders in (
        (cut[:, :, :half], list(reversed(slice_labels))),
        (cut[:, :, half:], slice_labels),
    ):
        pieces = lead.reshape((2,) * (len(shard_labels) + len(slice_labels)) + lead.shape[2:])
        piece = reduce_pieces(pieces, shard_labels + slice_labels, orders + tail)
        whole = gather_pieces(piece, slice_labels, orders)
        parts.append(whole.reshape((slices,) + piece.shape))
    both = jnp.concatenate(parts, axis=1)
    if by_columns:
        return jnp.transpose(both, (1, 0, 2)).reshape(rows // shards, columns)
    return both.reshape(rows // shards, columns)


def join_cores(own):
    other = swap(own, "ctx", 1)
    upper = bit_of("ctx", 1)
    return jnp.concatenate(
        [jnp.where(upper, other, own), jnp.where(upper, own, other)], axis=1
    ).astype(jnp.float32)


def sum_over(value, axes):
    for axis in axes:
        for bit in bits_below(lax.axis_size(axis)):
            value = value + swap(value, axis, bit)
    return value


def own_shard(vector):
    width = vector.shape[0] // lax.axis_size("fsdp")
    return lax.dynamic_slice_in_dim(vector, lax.axis_index("fsdp") * width, width, 0)


def weight_sums(
    hidden,
    grad_mlp_low,
    act_mlp,
    grad_leading,
    grad_trailing,
    act_attn,
    grad_projected,
    attn_low,
    grad_attn_low,
    small,
    early,
):
    shards, ctx_count = (lax.axis_size("fsdp"), lax.axis_size("ctx"))
    rows, ff_width = hidden.shape
    model_width = act_mlp.shape[1]
    if early is None:
        half, half_three = (model_width // 2, 3 * model_width // 2)
        pairs = (
            (hidden, grad_mlp_low[:, :half], grad_mlp_low[:, half:]),
            (act_mlp, grad_leading, grad_trailing),
            (act_attn, grad_projected[:, :half_three], grad_projected[:, half_three:]),
            (attn_low, grad_attn_low[:, :half], grad_attn_low[:, half:]),
        )
        totals = [
            join_cores(shard_sum(core_product(*pair), at == 0)) for at, pair in enumerate(pairs)
        ]
        over_pack = sum_over(small, ("ctx",))
        return totals + [jnp.stack([over_pack, sum_over(over_pack, ("fsdp",))])]
    total_out, total_in, total_attn, total_qkv, small_sums = sum_weights(
        *early, [("rows", act_attn, grad_projected, 3)], small
    )
    padded = total_in.shape[1] // 2
    total_in = jnp.concatenate(
        [total_in[:, :ff_width], total_in[:, padded : padded + ff_width]], axis=1
    )
    return [
        total.astype(jnp.float32) for total in (total_out, total_in, total_qkv, total_attn)
    ] + [small_sums]


def weight_sums_early(hidden, grad_mlp_low, act_mlp, grad_leading, grad_trailing, attn_low, grad_attn_low):
    shards, ctx_count = (lax.axis_size("fsdp"), lax.axis_size("ctx"))
    ff_width = hidden.shape[1]
    if shards != 4 or ctx_count != 8 or act_mlp.shape[1] % 1024 != 0 or ff_width % 64 != 0:
        return None
    return early_sums(
        [
            ("columns", hidden, grad_mlp_low, 1),
            ("rows", act_mlp, (grad_leading, grad_trailing), 3),
            ("rows", attn_low, grad_attn_low, 1),
        ]
    )


def per_device(
    inputs,
    cotangent,
    lengths,
    piece_route,
    gain_one,
    qkv_weight,
    attn_out,
    gain_two,
    geglu_in,
    geglu_out,
):
    ctx_count = lax.axis_size("ctx")
    own_index = lax.axis_index("ctx")
    row_count = inputs.shape[1]
    model_width = inputs.shape[2]
    piece_rows = row_count // ctx_count
    tokens = row_count * ctx_count
    own_heads = model_width // HEAD_WIDTH // ctx_count
    own_width = own_heads * HEAD_WIDTH
    block_q = math.gcd(tokens, 256)
    block_k = math.gcd(tokens, 512)
    lengths_row = lengths[0]
    own_route = piece_route[0, 0]
    slot_ids = jnp.arange(ctx_count, dtype=jnp.int32)
    outgoing = jnp.sum(
        slot_ids[None, :] * (own_route[None, :] == slot_ids[:, None]).astype(jnp.int32), axis=1
    )

    def exchange(blocks):
        return lax.all_to_all(blocks, "ctx", split_axis=0, concat_axis=0, tiled=True)

    def to_slots(rows_in):
        return jnp.take(rows_in.reshape(ctx_count, piece_rows, model_width), outgoing, axis=0)

    def to_heads(rows_in):
        by_heads = rows_in.reshape(row_count, ctx_count, -1)
        return exchange(jnp.transpose(by_heads, (1, 0, 2))).reshape(tokens, -1)

    def to_rows(heads_in):
        return exchange(heads_in.reshape(ctx_count, row_count, -1))

    both_arrived = exchange(
        jnp.concatenate([to_slots(inputs[0]), to_slots(cotangent[0])], axis=1)
    )
    arrived, grad_arrived = (both_arrived[:, :piece_rows], both_arrived[:, piece_rows:])
    residual = arrived.reshape(row_count, model_width).astype(jnp.float32)
    places = own_index * row_count + jnp.arange(row_count, dtype=jnp.int32)
    unused_begin, unused_end, offset, is_valid = spans(places, lengths_row)
    pack_begin, pack_end, unused_offset, unused_valid = spans(
        jnp.arange(tokens, dtype=jnp.int32), lengths_row
    )
    grad_final = jnp.where(
        is_valid[:, None], grad_arrived.reshape(row_count, model_width).astype(jnp.float32), 0.0
    )
    gains = jnp.pad(jnp.stack([gain_one, gain_two]), ((0, 14), (0, 0)))
    gains_full, qkv_full = gather_weights([gains, qkv_weight])
    gains_full = gains_full.reshape(-1, 16, gains.shape[1])
    gain_attn = gains_full[:, 0].reshape(-1).astype(jnp.float32)
    gain_mlp = gains_full[:, 1].reshape(-1).astype(jnp.float32)
    act_attn = layer_norm(residual, gain_attn).astype(jnp.bfloat16)
    later = [attn_out, geglu_in, geglu_out]
    row_cosine, row_sine = rotary_tables(offset, own_heads)
    if lax.axis_size("fsdp") == 4 and ctx_count == 8 and own_width == 128:
        attn_full, in_full, out_full, qkv_heads = gather_weights(
            later, (act_attn, qkv_full, row_cosine, row_sine)
        )
    else:
        attn_full, in_full, out_full = gather_weights(later)
        projected = jnp.dot(act_attn, qkv_full, preferred_element_type=jnp.float32)
        cosine, sine = rotary_tables(offset, 1)
        queries, keys = (
            rotate(projected[:, :model_width], cosine, sine).astype(jnp.bfloat16),
            rotate(projected[:, model_width : 2 * model_width], cosine, sine).astype(jnp.bfloat16),
        )
        values = projected[:, 2 * model_width :].astype(jnp.bfloat16)
        joined = jnp.stack(
            [part.reshape(row_count, ctx_count, own_width) for part in (queries, keys, values)], axis=2
        )
        qkv_heads = to_heads(joined.reshape(row_count, -1))
    low, high = key_range(pack_begin, pack_end, block_q, block_k)
    pack_begin, pack_end = (pack_begin[None, :], pack_end[None, :])
    attended_heads, log_total = attention_forward(
        qkv_heads, pack_begin, pack_end, low, high, own_heads, block_q, block_k
    )
    attn_low = jnp.transpose(to_rows(attended_heads.astype(jnp.bfloat16)), (1, 0, 2)).reshape(
        row_count, model_width
    )
    branch_attn = jnp.dot(attn_low, attn_full, preferred_element_type=jnp.float32)
    middle = residual + branch_attn
    act_mlp = layer_norm(middle, gain_mlp).astype(jnp.bfloat16)
    up_both = jnp.dot(act_mlp, in_full, preferred_element_type=jnp.float32)
    ff_width = up_both.shape[1] // 2
    hidden = (jax.nn.gelu(up_both[:, :ff_width], approximate=False) * up_both[:, ff_width:]).astype(
        jnp.bfloat16
    )
    branch_mlp = jnp.dot(hidden, out_full, preferred_element_type=jnp.float32)
    final_rows = jnp.where(is_valid[:, None], middle + branch_mlp, 0.0)
    square_sums = jnp.stack(
        [
            jnp.sum(final_rows * final_rows),
            jnp.sum(jnp.where(is_valid[:, None], branch_attn * branch_attn, 0.0)),
            jnp.sum(jnp.where(is_valid[:, None], branch_mlp * branch_mlp, 0.0)),
        ]
    )
    out_slots = final_rows.astype(jnp.bfloat16).reshape(ctx_count, piece_rows, model_width)
    grad_mlp_low = grad_final.astype(jnp.bfloat16)
    grad_hidden = lax.dot_general(
        grad_mlp_low, out_full, NT, preferred_element_type=jnp.float32
    )

    def gated(leading, trailing):
        return jax.nn.gelu(leading, approximate=False) * trailing

    unused_gate, gate_back = jax.vjp(gated, up_both[:, :ff_width], up_both[:, ff_width:])
    grad_leading, grad_trailing = gate_back(grad_hidden)
    grad_leading, grad_trailing = (
        grad_leading.astype(jnp.bfloat16),
        grad_trailing.astype(jnp.bfloat16),
    )
    grad_up = jnp.concatenate([grad_leading, grad_trailing], axis=1)
    grad_act_mlp = lax.dot_general(grad_up, in_full, NT, preferred_element_type=jnp.float32)
    unused_norm, norm_back_mlp = jax.vjp(layer_norm, middle, gain_mlp)
    grad_middle_norm, grad_gain_mlp = norm_back_mlp(grad_act_mlp)
    grad_middle = grad_final + grad_middle_norm
    grad_attn_low = grad_middle.astype(jnp.bfloat16)
    grad_attended = lax.dot_general(
        grad_attn_low, attn_full, NT, preferred_element_type=jnp.float32
    ).astype(jnp.bfloat16)
    early = weight_sums_early(
        hidden, grad_mlp_low, act_mlp, grad_leading, grad_trailing, attn_low, grad_attn_low
    )
    block_back = math.gcd(tokens, 256)
    low_back, high_back = key_range(pack_begin[0], pack_end[0], block_q, block_back)
    grad_heads = attention_backward(
        qkv_heads,
        attended_heads,
        to_heads(grad_attended),
        log_total,
        pack_begin,
        pack_end,
        low_back,
        high_back,
        [] if early is None else [early[1][0][0]],
        own_heads,
        block_q,
        block_back,
    )
    if early is not None:
        grad_heads, early = second_step(grad_heads, early)
    grad_rows = to_rows(grad_heads)
    if own_width % 128 == 0:
        grad_projected, grad_act_attn = finish_rows(
            grad_rows, row_cosine, row_sine, qkv_full, own_heads
        )
    else:
        by_part = jnp.transpose(
            grad_rows.reshape(ctx_count, row_count, 3, own_width), (2, 1, 0, 3)
        ).reshape(3, row_count, model_width)
        cosine, sine = rotary_tables(offset, 1)
        grad_projected = jnp.concatenate(
            [
                rotate(by_part[part].astype(jnp.float32), cosine, -sine).astype(jnp.bfloat16)
                for part in (0, 1)
            ]
            + [by_part[2]],
            axis=1,
        )
        grad_act_attn = lax.dot_general(
            grad_projected, qkv_full, NT, preferred_element_type=jnp.float32
        )
    unused_first, norm_back_attn = jax.vjp(layer_norm, residual, gain_attn)
    grad_resid_norm, grad_gain_attn = norm_back_attn(grad_act_attn)
    grad_residual = (grad_middle + grad_resid_norm).astype(jnp.bfloat16)
    grad_slots = grad_residual.reshape(ctx_count, piece_rows, model_width)
    back = exchange(jnp.concatenate([out_slots, grad_slots], axis=1))
    block_out, grad_inputs = (
        jnp.take(half, own_route, axis=0).reshape(1, row_count, model_width)
        for half in (back[:, :piece_rows], back[:, piece_rows:])
    )
    small = jnp.stack(
        [grad_gain_attn, grad_gain_mlp, jnp.pad(square_sums, (0, model_width - 3))]
        + [jnp.zeros((model_width,), jnp.float32)] * 5
    )
    total_out, total_in, total_qkv, total_attn, small_sums = weight_sums(
        hidden,
        grad_mlp_low,
        act_mlp,
        grad_leading,
        grad_trailing,
        act_attn,
        grad_projected,
        attn_low,
        grad_attn_low,
        small,
        early,
    )
    total_gain_one = own_shard(small_sums[1, 0])
    total_gain_two = own_shard(small_sums[1, 1])
    total_squares = small_sums[0, 2, :3]
    valid_count = jnp.sum(lengths_row).astype(jnp.float32)
    rms_stats = jnp.sqrt(total_squares / (valid_count * model_width))[None, :]
    return (
        block_out,
        grad_inputs,
        total_gain_one,
        total_qkv,
        total_attn,
        total_gain_two,
        total_in,
        total_out,
        rms_stats,
    )


def solution(mesh):
    placed = (
        P("fsdp", "ctx", None),
        P("fsdp", "ctx", None),
        P("fsdp", None),
        P("fsdp", "ctx", None),
        P("fsdp"),
        P("fsdp", None),
        P("fsdp", None),
        P("fsdp"),
        P("fsdp", None),
        P("fsdp", None),
    )
    return jax.shard_map(
        per_device,
        mesh=mesh,
        in_specs=placed,
        out_specs=(
            P("fsdp", "ctx", None),
            P("fsdp", "ctx", None),
            P("fsdp"),
            P("fsdp", None),
            P("fsdp", None),
            P("fsdp"),
            P("fsdp", None),
            P("fsdp", None),
            P("fsdp", None),
        ),
        check_vma=False,
    )
```

```python
import functools
import math
import jax
import jax.numpy as jnp
from jax import lax
from jax.experimental import pallas as pl
from jax.experimental.pallas import tpu as pltpu
from jax.sharding import PartitionSpec as P

HEAD_WIDTH = 64
norm_eps = 1e-05
masked_score = -1e30


def head_stack(rows_in, head_count):
    if head_count == 1:
        return rows_in
    lane_head = lax.broadcasted_iota(jnp.int32, rows_in.shape, 1) // HEAD_WIDTH
    zero = jnp.zeros_like(rows_in)
    return jnp.concatenate(
        [jnp.where(lane_head == h, rows_in, zero) for h in range(head_count)], axis=0
    )


def head_pick(stacked_t, head_count, block):
    return jnp.concatenate(
        [
            stacked_t[h * HEAD_WIDTH : (h + 1) * HEAD_WIDTH, h * block : (h + 1) * block]
            for h in range(head_count)
        ],
        axis=0,
    ).T


NT = (((1,), (1,)), ((), ()))


def forward_kernel(
    head_count, block_q, block_k, low_ref, high_ref, begin_ref, end_ref, qkv_ref, out_ref, log_ref, turned_ref
):
    width = out_ref.shape[1]
    step = pl.program_id(0)

    @pl.when(step == 0)
    def prepare():
        turned_ref[...] = qkv_ref[:, 2 * width :].astype(jnp.float32).T.astype(jnp.bfloat16)

    rows = pl.ds(pl.multiple_of(step * block_q, block_q), block_q)
    scale = 1.0 / math.sqrt(HEAD_WIDTH)
    stacked = head_stack(qkv_ref[rows, :width] * jnp.asarray(scale, jnp.bfloat16), head_count)
    begin = jnp.concatenate([begin_ref[:, rows]] * head_count, axis=1)
    end = jnp.concatenate([end_ref[:, rows]] * head_count, axis=1)

    def body(index, carried):
        top, total, acc = carried
        first = pl.multiple_of(index * block_k, block_k)
        keys = qkv_ref[pl.ds(first, block_k), width : 2 * width]
        scores = lax.dot_general(keys, stacked, NT, preferred_element_type=jnp.float32)
        place = first + lax.broadcasted_iota(jnp.int32, scores.shape, 0)
        scores = jnp.where((place >= begin) & (place < end), scores, masked_score)
        new_top = jnp.maximum(top, jnp.max(scores, axis=0, keepdims=True))
        fresh = jnp.exp(scores - new_top)
        fade = jnp.exp(top - new_top)
        total = total * fade + jnp.sum(fresh, axis=0, keepdims=True)
        acc = acc * fade + jnp.dot(
            turned_ref[:, pl.ds(first, block_k)],
            fresh.astype(jnp.bfloat16),
            preferred_element_type=jnp.float32,
        )
        return (new_top, total, acc)

    lanes = head_count * block_q
    top, total, acc = lax.fori_loop(
        low_ref[step],
        high_ref[step],
        body,
        (
            jnp.full((1, lanes), masked_score, jnp.float32),
            jnp.zeros((1, lanes), jnp.float32),
            jnp.zeros((width, lanes), jnp.float32),
        ),
    )
    valid = end > begin
    safe = jnp.where(valid, total, 1.0)
    acc = jnp.where(valid, acc / safe, 0.0)
    log_total = jnp.where(valid, top + jnp.log(safe), 0.0)
    out_ref[...] = head_pick(acc, head_count, block_q)
    log_ref[0] = log_total


def attention_forward(qkv, begin, end, low, high, head_count, block_q, block_k):
    tokens = qkv.shape[0]
    width = head_count * HEAD_WIDTH
    steps = tokens // block_q
    whole = lambda shape: pl.BlockSpec(shape, lambda i, *_: (0,) * len(shape))
    pairs = tokens * tokens // 4 * head_count
    return pl.pallas_call(
        functools.partial(forward_kernel, head_count, block_q, block_k),
        out_shape=(
            jax.ShapeDtypeStruct((tokens, width), jnp.float32),
            jax.ShapeDtypeStruct((steps, 1, head_count * block_q), jnp.float32),
        ),
        grid_spec=pltpu.PrefetchScalarGridSpec(
            num_scalar_prefetch=2,
            grid=(steps,),
            in_specs=[whole((1, tokens)), whole((1, tokens)), whole((tokens, 3 * width))],
            out_specs=(
                pl.BlockSpec((block_q, width), lambda i, *_: (i, 0)),
                pl.BlockSpec((1, 1, head_count * block_q), lambda i, *_: (i, 0, 0)),
            ),
            scratch_shapes=[pltpu.VMEM((width, tokens), jnp.bfloat16)],
        ),
        cost_estimate=pl.CostEstimate(
            flops=pairs * 512, bytes_accessed=tokens * width * 12, transcendentals=pairs
        ),
        name="attention_forward",
    )(low, high, begin, end, qkv)


def turn_back(grads, cosine, sine, head_count):
    half = HEAD_WIDTH // 2
    pieces = []
    for h in range(head_count):
        base = h * HEAD_WIDTH
        pieces += [grads[:, base + half : base + HEAD_WIDTH], grads[:, base : base + half]]
    return grads * cosine + jnp.concatenate(pieces, axis=1) * sine


def backward_kernel(
    head_count,
    block_q,
    block_k,
    low_ref,
    high_ref,
    begin_ref,
    end_ref,
    qkv_ref,
    attended_ref,
    grad_ref,
    log_ref,
    *refs,
):
    out_ref, turned_ref, key_acc, value_acc = refs[-4:]
    width = attended_ref.shape[1]
    step = pl.program_id(0)

    @pl.when(step == 0)
    def prepare():
        turned_ref[...] = qkv_ref[:, width : 2 * width].astype(jnp.float32).T.astype(jnp.bfloat16)
        key_acc[...] = jnp.zeros_like(key_acc)
        value_acc[...] = jnp.zeros_like(value_acc)

    rows = pl.ds(pl.multiple_of(step * block_q, block_q), block_q)
    scale = 1.0 / math.sqrt(HEAD_WIDTH)
    stacked = head_stack(qkv_ref[rows, :width] * jnp.asarray(scale, jnp.bfloat16), head_count)
    grads = grad_ref[rows, :]
    grad_stacked = head_stack(grads, head_count)
    begin = jnp.concatenate([begin_ref[:, rows]] * head_count, axis=1)
    end = jnp.concatenate([end_ref[:, rows]] * head_count, axis=1)
    product = (grads.astype(jnp.float32) * attended_ref[rows, :]).T
    delta = jnp.concatenate(
        [
            jnp.sum(product[h * HEAD_WIDTH : (h + 1) * HEAD_WIDTH], axis=0, keepdims=True)
            for h in range(head_count)
        ],
        axis=1,
    )
    log_total = log_ref[0]

    def body(index, acc):
        first = pl.multiple_of(index * block_k, block_k)
        span = pl.ds(first, block_k)
        keys = qkv_ref[span, width : 2 * width]
        values = qkv_ref[span, 2 * width :]
        scores = lax.dot_general(keys, stacked, NT, preferred_element_type=jnp.float32)
        grad_probs = lax.dot_general(values, grad_stacked, NT, preferred_element_type=jnp.float32)
        place = first + lax.broadcasted_iota(jnp.int32, scores.shape, 0)
        scores = jnp.where((place >= begin) & (place < end), scores, masked_score)
        probs = jnp.exp(scores - log_total)
        grad_scores = (probs * (grad_probs - delta)).astype(jnp.bfloat16)
        value_acc[span, :] += jnp.dot(
            probs.astype(jnp.bfloat16), grad_stacked, preferred_element_type=jnp.float32
        )
        key_acc[span, :] += jnp.dot(grad_scores, stacked, preferred_element_type=jnp.float32)
        return acc + jnp.dot(
            turned_ref[:, span], grad_scores, preferred_element_type=jnp.float32
        )

    acc = lax.fori_loop(
        low_ref[step],
        high_ref[step],
        body,
        jnp.zeros((width, head_count * block_q), jnp.float32),
    )
    grad_queries = head_pick(acc, head_count, block_q) * scale
    out_ref[rows, :width] = grad_queries.astype(jnp.bfloat16)

    @pl.when(step == pl.num_programs(0) - 1)
    def finish():
        @pl.loop(0, pl.num_programs(0))
        def each(index):
            span = pl.ds(pl.multiple_of(index * block_q, block_q), block_q)
            out_ref[span, width : 2 * width] = key_acc[span, :].astype(jnp.bfloat16)
            out_ref[span, 2 * width :] = value_acc[span, :].astype(jnp.bfloat16)


def attention_backward(
    qkv, attended, grads, log_total, begin, end, low, high, after, head_count, block_q, block_k
):
    tokens = qkv.shape[0]
    width = head_count * HEAD_WIDTH
    steps = tokens // block_q
    whole = lambda shape: pl.BlockSpec(shape, lambda i, *_: (0,) * len(shape))
    pairs = tokens * tokens // 4 * head_count
    return pl.pallas_call(
        functools.partial(backward_kernel, head_count, block_q, block_k),
        out_shape=jax.ShapeDtypeStruct((tokens, 3 * width), jnp.bfloat16),
        grid_spec=pltpu.PrefetchScalarGridSpec(
            num_scalar_prefetch=2,
            grid=(steps,),
            in_specs=[
                whole((1, tokens)),
                whole((1, tokens)),
                whole((tokens, 3 * width)),
                whole((tokens, width)),
                whole((tokens, width)),
                pl.BlockSpec((1, 1, head_count * block_q), lambda i, *_: (i, 0, 0)),
            ]
            + [pl.BlockSpec(memory_space=pl.ANY)] * len(after),
            out_specs=whole((tokens, 3 * width)),
            scratch_shapes=[
                pltpu.VMEM((width, tokens), jnp.bfloat16),
                pltpu.VMEM((tokens, width), jnp.float32),
                pltpu.VMEM((tokens, width), jnp.float32),
            ],
        ),
        cost_estimate=pl.CostEstimate(
            flops=pairs * 1280, bytes_accessed=tokens * width * 30, transcendentals=pairs
        ),
        name="attention_backward",
    )(low, high, begin, end, qkv, attended, grads, log_total, *after)


def rows_kernel(head_count, heads_ref, cosine_ref, sine_ref, query_ref, key_ref, value_ref, out_ref, act_ref):
    width = heads_ref.shape[2] // 3
    step = pl.program_id(0)
    total = out_ref.shape[1] // 3
    pieces = []
    for part in range(3):
        piece = heads_ref[0, :, part * width : (part + 1) * width]
        if part < 2:
            piece = turn_back(
                piece.astype(jnp.float32), cosine_ref[...], sine_ref[...], head_count
            ).astype(jnp.bfloat16)
        first = pl.multiple_of(part * total + step * width, width)
        out_ref[:, pl.ds(first, width)] = piece
        pieces.append(piece)
    weights = jnp.concatenate([query_ref[...], key_ref[...], value_ref[...]], axis=1)
    product = lax.dot_general(
        jnp.concatenate(pieces, axis=1), weights, NT, preferred_element_type=jnp.float32
    )

    @pl.when(step == 0)
    def begin():
        act_ref[...] = product

    @pl.when(step > 0)
    def add():
        act_ref[...] += product


def finish_rows(heads, cosine, sine, qkv_full, head_count):
    owners, rows, columns = heads.shape
    width = columns // 3
    depth = qkv_full.shape[0]
    whole = lambda shape: pl.BlockSpec(shape, lambda i: (0,) * len(shape))
    part_of = lambda part: pl.BlockSpec((depth, width), lambda i: (0, part * owners + i))
    return pl.pallas_call(
        functools.partial(rows_kernel, head_count),
        out_shape=(
            jax.ShapeDtypeStruct((rows, owners * columns), jnp.bfloat16),
            jax.ShapeDtypeStruct((rows, depth), jnp.float32),
        ),
        grid=(owners,),
        in_specs=[
            pl.BlockSpec((1, rows, columns), lambda i: (i, 0, 0)),
            whole((rows, width)),
            whole((rows, width)),
            part_of(0),
            part_of(1),
            part_of(2),
        ],
        out_specs=(whole((rows, owners * columns)), whole((rows, depth))),
        cost_estimate=pl.CostEstimate(
            flops=2 * rows * depth * owners * columns,
            bytes_accessed=2 * depth * owners * columns + 4 * rows * owners * columns,
            transcendentals=0,
        ),
        name="finish_rows",
    )(heads, cosine, sine, qkv_full, qkv_full, qkv_full)


def spans(places, lengths_row):
    ends = jnp.cumsum(lengths_row)
    past = (places[:, None] >= ends[None, :]).astype(jnp.int32)
    begin = jnp.sum(past * lengths_row[None, :], axis=1)
    before = (places[:, None] >= (ends - lengths_row)[None, :]).astype(jnp.int32)
    end = jnp.sum(before * lengths_row[None, :], axis=1)
    valid = places < ends[-1]
    return (jnp.where(valid, begin, 0), jnp.where(valid, end, 0), places - begin, valid)


def key_range(begin, end, block_q, block_k):
    begin_blocks = jnp.where(end > begin, begin, jnp.int32(1 << 30)).reshape(-1, block_q)
    high = (jnp.max(end.reshape(-1, block_q), axis=1) + block_k - 1) // block_k
    low = jnp.minimum(jnp.min(begin_blocks, axis=1) // block_k, high)
    return (low, high)


def rotary_tables(offset, head_count):
    half = HEAD_WIDTH // 2
    inverse = 160000.0 ** (-2.0 * jnp.arange(half, dtype=jnp.float32) / HEAD_WIDTH)
    angles = offset.astype(jnp.float32)[:, None] * inverse[None, :]
    cosine, sine = (jnp.cos(angles), jnp.sin(angles))
    return (
        jnp.concatenate([cosine, cosine] * head_count, axis=1),
        jnp.concatenate([sine, -sine] * head_count, axis=1),
    )


def toggled(index, bit):
    return index + bit - 2 * bit * ((index // bit) % 2)


def gather_kernel(arrays, parts, projects, *refs):
    count = len(parts)
    array_shards, refs = (refs[:arrays], refs[arrays:])
    if projects:
        act_ref, qkv_ref, cosine_ref, sine_ref = refs[:4]
        heads_ref = refs[4 + arrays]
        columns_ref, held_ref, load_sem, head_send, head_recv, own_sem = refs[arrays + 8 :]
        refs = refs[4 : 4 + arrays] + refs[arrays + 5 : arrays + 8]
    array_fulls = refs[:arrays]
    send_sem, recv_sem, local_sem = refs[arrays:]
    shapes = [part[0] for part in parts]
    shard_refs = [array_shards[part[1]] for part in parts]
    full_refs = [array_fulls[part[1]] for part in parts]
    shards = lax.axis_size("fsdp")
    slices = lax.axis_size("ctx") // 2
    own_ctx, own_shard = (lax.axis_index("ctx"), lax.axis_index("fsdp"))
    core, chip = (own_ctx % 2, own_ctx // 2)
    barrier = pltpu.get_barrier_semaphore()
    partners = [{"fsdp": toggled(own_shard, bit)} for bit in (1, 2)]
    partners += [{"ctx": toggled(own_ctx, bit)} for bit in (1, 2, 4)]

    def owner_at(relation):
        owner = own_ctx
        for bit in (1, 2, 4):
            if relation & bit:
                owner = toggled(owner, bit)
        return owner

    if projects:
        partners += [{"ctx": owner_at(relation)} for relation in (3, 5, 6, 7)]
    for partner in partners:
        pl.semaphore_signal(
            barrier, inc=1, device_id=partner, device_id_type=pl.DeviceIdType.MESH
        )
    pl.semaphore_wait(barrier, len(partners))
    to_one, to_two, to_core, to_x, to_y = partners[:5]

    def shard_at(step):
        if step == 0:
            return own_shard
        if step == 3:
            return toggled(toggled(own_shard, 1), 2)
        return toggled(own_shard, step)

    def region(ref, weight, step, chip_at, half):
        if shapes[weight] == "small":
            return ref if len(ref.shape) == 2 else ref.at[shard_at(step)]
        if shapes[weight] == "rows":
            rows = ref.shape[-2]
            span = pl.ds(0, rows) if half is None else pl.ds(half * (rows // 2), rows // 2)
            columns = pl.ds(parts[weight][2], parts[weight][3])
            if len(ref.shape) == 4:
                return ref.at[core, chip_at, span, columns]
            return ref.at[shard_at(step), core, chip_at, span, columns]
        rows = ref.shape[-2]
        first = (rows // 2) // 16 * 16
        spans_of = {None: pl.ds(0, rows), 0: pl.ds(0, first), 1: pl.ds(first, rows - first)}
        width = ref.shape[-1] // (2 * slices)
        columns = pl.ds(pl.multiple_of((core * slices + chip_at) * width, width), width)
        if len(ref.shape) == 2:
            return ref.at[spans_of[half], columns]
        return ref.at[shard_at(step), spans_of[half], columns]

    def core_region(ref, weight, step):
        if shapes[weight] == "rows":
            return ref.at[shard_at(step), core, :, :, pl.ds(parts[weight][2], parts[weight][3])]
        width = ref.shape[-1] // 2
        return ref.at[shard_at(step), :, pl.ds(pl.multiple_of(core * width, width), width)]

    pending = []

    def send(source, target, slot, partner):
        copy = pltpu.make_async_remote_copy(
            src_ref=source,
            dst_ref=target,
            send_sem=send_sem.at[slot],
            recv_sem=recv_sem.at[slot],
            device_id=partner,
            device_id_type=pl.DeviceIdType.MESH,
        )
        copy.start()
        pending.append(copy)
        return copy

    copies = {}
    local = []

    def slot_of(weight, step, kind):
        return (weight * 3 + step - 1) * 8 + kind

    def shard_sends(weight):
        source = region(shard_refs[weight], weight, 0, chip, None)
        target = region(full_refs[weight], weight, 0, chip, None)
        copies[weight, 2, 0] = send(source, target, slot_of(weight, 2, 0), to_two)
        copies[weight, 1, 0] = send(source, target, slot_of(weight, 1, 0), to_one)
        if parts[weight][2] == 0:
            target = full_refs[weight].at[own_shard]
            copy = pltpu.make_async_copy(shard_refs[weight], target, local_sem.at[parts[weight][1]])
            copy.start()
            local.append(copy)

    def shard_forward(weight):
        copies[weight, 2, 0].wait_recv()
        piece = region(full_refs[weight], weight, 2, chip, None)
        copies[weight, 3, 0] = send(piece, piece, slot_of(weight, 3, 0), to_one)

    def plane_sends(weight, step):
        lead = region(full_refs[weight], weight, step, chip, 0)
        rest = region(full_refs[weight], weight, step, chip, 1)
        for kind, piece, partner in ((1, lead, to_x), (2, rest, to_y), (3, lead, to_y), (4, rest, to_x)):
            copies[weight, step, kind] = send(piece, piece, slot_of(weight, step, kind), partner)

    def plane_forward(weight, step):
        copies[weight, step, 1].wait_recv()
        lead = region(full_refs[weight], weight, step, toggled(chip, 1), 0)
        copies[weight, step, 5] = send(lead, lead, slot_of(weight, step, 5), to_y)
        copies[weight, step, 2].wait_recv()
        rest = region(full_refs[weight], weight, step, toggled(chip, 2), 1)
        copies[weight, step, 6] = send(rest, rest, slot_of(weight, step, 6), to_x)

    def core_send(weight, step):
        for kind in (3, 4, 5, 6):
            copies[weight, step, kind].wait_recv()
        piece = core_region(full_refs[weight], weight, step)
        copies[weight, step, 7] = send(piece, piece, slot_of(weight, step, 7), to_core)

    chip_order = (3, 1, 2, 0)

    def start_loads():
        loads = {}
        for chip_bits in chip_order:
            owner_chip = owner_at(2 * chip_bits) // 2
            for part in range(3):
                width = columns_ref.shape[2] // 3
                total = qkv_ref.shape[1] // 3
                first = pl.multiple_of(part * total + owner_chip * width, width)
                loads[chip_bits, part] = pltpu.make_async_copy(
                    qkv_ref.at[:, pl.ds(first, width)],
                    columns_ref.at[chip_bits, :, pl.ds(part * width, width)],
                    load_sem.at[chip_bits * 3 + part],
                )
                loads[chip_bits, part].start()
        return loads

    def project(chip_bits, loads):
        for part in range(3):
            loads[chip_bits, part].wait()
        rows, own_width = (act_ref.shape[0], held_ref.shape[2] // 3)
        product = jnp.dot(
            act_ref[...], columns_ref[chip_bits], preferred_element_type=jnp.float32
        )
        for core_at in (0, 1):
            slot = 2 * chip_bits + core + core_at - 2 * core * core_at
            for part in range(3):
                first = (2 * part + core_at) * own_width
                piece = product[:, first : first + own_width]
                if part < 2:
                    half = HEAD_WIDTH // 2
                    turned = []
                    for base in range(0, own_width, HEAD_WIDTH):
                        turned += [piece[:, base + half : base + HEAD_WIDTH], piece[:, base : base + half]]
                    piece = piece * cosine_ref[...] - jnp.concatenate(turned, axis=1) * sine_ref[...]
                held_ref[slot, :, part * own_width : (part + 1) * own_width] = piece.astype(jnp.bfloat16)
        target = heads_ref.at[pl.ds(pl.multiple_of(own_ctx * rows, rows), rows), :]
        for core_bit in (0, 1):
            relation = 2 * chip_bits + core_bit
            if relation == 0:
                copy = pltpu.make_async_copy(held_ref.at[0], target, own_sem.at[0])
                copy.start()
                local.append(copy)
                continue
            copy = pltpu.make_async_remote_copy(
                src_ref=held_ref.at[relation],
                dst_ref=target,
                send_sem=head_send.at[relation],
                recv_sem=head_recv.at[relation],
                device_id={"ctx": owner_at(relation)},
                device_id_type=pl.DeviceIdType.MESH,
            )
            copy.start()
            pending.append(copy)
            arriving.append(copy)

    arriving = []
    sent = 1
    if projects:
        loads = start_loads()
        for weight in range(count):
            shard_sends(weight)
        sent = count
        for chip_bits in chip_order:
            project(chip_bits, loads)
    else:
        shard_sends(0)
    for weight in range(count):
        if weight + 1 >= sent and weight + 1 < count:
            shard_sends(weight + 1)
        shard_forward(weight)
        copies[weight, 1, 0].wait_recv()
        if shapes[weight] == "small":
            copies[weight, 3, 0].wait_recv()
            continue
        plane_sends(weight, 1)
        plane_sends(weight, 2)
        copies[weight, 3, 0].wait_recv()
        plane_sends(weight, 3)
        for step in (1, 2, 3):
            plane_forward(weight, step)
        if weight > 0 and shapes[weight - 1] != "small":
            for step in (1, 2, 3):
                core_send(weight - 1, step)
    for step in (1, 2, 3):
        core_send(count - 1, step)
    for weight in range(count):
        if shapes[weight] != "small":
            for step in (1, 2, 3):
                copies[weight, step, 7].wait_recv()
    for copy in arriving:
        copy.wait_recv()
    for copy in pending:
        copy.wait_send()
    for copy in local:
        copy.wait()


def gather_weights(weights, projection=None):
    shards, ctx_count = (lax.axis_size("fsdp"), lax.axis_size("ctx"))
    slices = ctx_count // 2
    shapes, views, outs = ([], [], [])
    for weight in weights:
        rows, columns = weight.shape
        if rows % (32 * ctx_count) == 0:
            shapes.append("rows")
            views.append(weight.reshape(2, slices, rows // ctx_count, columns))
            outs.append((shards, 2, slices, rows // ctx_count, columns))
        elif rows == 16:
            shapes.append("small")
            views.append(weight)
            outs.append((shards, rows, columns))
        elif columns % (128 * ctx_count) == 0 and rows % 16 == 0:
            shapes.append("columns")
            views.append(weight)
            outs.append((shards, rows, columns))
    if shards != 4 or ctx_count != 8 or len(views) < len(weights):
        return [lax.all_gather(weight, "fsdp", axis=0, tiled=True) for weight in weights]
    parts = []
    for at in sorted(range(len(views)), key=lambda at: (shapes[at] != "small", -views[at].size, at)):
        columns = views[at].shape[-1]
        pieces = max(1, min(columns // 1024, views[at].size // (1 << 18))) if shapes[at] == "rows" else 1
        width = -(-columns // (128 * pieces)) * 128 if pieces > 1 else columns
        for first in range(0, columns, width):
            parts.append((shapes[at], at, first, min(width, columns - first)))
    arrays, slots = (len(views), len(parts) * 24)
    vmem, anywhere, dma = (
        pl.BlockSpec(memory_space=pltpu.VMEM),
        pl.BlockSpec(memory_space=pl.ANY),
        pltpu.SemaphoreType.DMA,
    )
    in_specs = [vmem] * len(views)
    scratch = [dma((slots,)), dma((slots,)), dma((len(views),))]
    if projection is not None:
        act_attn, qkv_full = projection[:2]
        rows, own_columns = (act_attn.shape[0], qkv_full.shape[1] // ctx_count)
        views += list(projection)
        in_specs += [vmem, anywhere, vmem, vmem]
        outs.append((ctx_count * rows, own_columns))
        scratch += [
            pltpu.VMEM((slices, qkv_full.shape[0], 2 * own_columns), jnp.bfloat16),
            pltpu.VMEM((ctx_count, rows, own_columns), jnp.bfloat16),
            dma((3 * slices,)),
            dma((ctx_count,)),
            dma((ctx_count,)),
            dma((1,)),
        ]
    held = pl.pallas_call(
        functools.partial(gather_kernel, arrays, parts, projection is not None),
        out_shape=tuple(jax.ShapeDtypeStruct(out, jnp.bfloat16) for out in outs),
        in_specs=in_specs,
        out_specs=tuple(anywhere for out in outs),
        scratch_shapes=scratch,
        compiler_params=pltpu.CompilerParams(
            collective_id=0 if projection is None else 2,
            has_side_effects=True,
            vmem_limit_bytes=60 * 1024 * 1024,
        ),
        name="gather_weights" if projection is None else "gather_and_project",
    )(*views)
    return [whole.reshape(-1, whole.shape[-1]) for whole in held]


def pair_steps(plan, lead_rows, left_refs, right_refs, turned_refs, whole_refs, sems, core, pending, send):
    pair_send, pair_recv, near_sem = sems
    to_core = {"ctx": toggled(lax.axis_index("ctx"), 1)}

    def send_core(source, target, sent, got, start=True):
        return send(source, target, sent, got, to_core, start)

    rows = left_refs[0].shape[0] if left_refs else 0
    pairs = []
    for w, entry in enumerate(plan):
        span, right = (plan_span(entry), right_refs[w])
        own_part, other_part = (whole_refs[w].at[pl.ds(0, rows)], whole_refs[w].at[pl.ds(rows, rows)])

        def exchange(own_half, other_half, start=True):
            near = pltpu.make_async_copy(own_half, own_part, near_sem.at[w])
            if start:
                near.start()
            sems = (pair_send.at[2 * w], pair_recv.at[2 * w])
            return [near, send_core(other_half, other_part, *sems, start)]

        if entry[5]:
            ways = [exchange(right[at], right[1 - at], False) for at in (0, 1)]
            for at in (0, 1):

                @pl.when(core == at)
                def begin():
                    for copy in ways[at]:
                        copy.start()

            pairs.append(ways[0])
            pending.append(ways[0][1])
        else:
            halves = [
                right.at[:, pl.ds(pl.multiple_of(at * span, span), span)] for at in (core, 1 - core)
            ]
            pairs.append(exchange(*halves))

    def turn(w):
        left, turned = (left_refs[w], turned_refs[w])
        block = 512
        for first in range(0, left.shape[1], block):
            last = min(first + block, left.shape[1])
            turned[first:last, :rows] = (
                left[:, first:last].astype(jnp.float32).T.astype(jnp.bfloat16)
            )
        pairs[w].append(
            send_core(
                turned.at[:, pl.ds(0, rows)],
                turned.at[:, pl.ds(rows, rows)],
                pair_send.at[2 * w + 1],
                pair_recv.at[2 * w + 1],
            )
        )

    def multiply(w, t, first, second):
        kind, count, width, deep, halves, parted = plan[w]
        if t == 0:
            near, far, turned = pairs[w]
            near.wait()
            far.wait_recv()
            turned.wait_recv()

        def each(z, carried):
            left = turned_refs[w][pl.ds(pl.multiple_of(z * deep, 16), deep), :]
            if kind == "rows":
                last = min((t + 1) * width, whole_refs[w].shape[1])
                part = jnp.dot(
                    left, whole_refs[w][:, t * width : last], preferred_element_type=jnp.float32
                ).astype(jnp.bfloat16)
                if last < (t + 1) * width:
                    empty = jnp.zeros((deep, (t + 1) * width - last), jnp.bfloat16)
                    part = jnp.concatenate([part, empty], axis=1)
                piece_rows = first.shape[3]
                for s in range(4):
                    first[z, s // 2, s % 2] = part[2 * s * piece_rows : (2 * s + 1) * piece_rows]
                    second[z, s // 2, s % 2] = part[(2 * s + 1) * piece_rows : (2 * s + 2) * piece_rows]
            else:
                part = jnp.dot(
                    left, whole_refs[w][...], preferred_element_type=jnp.float32
                ).astype(jnp.bfloat16)
                for s in range(4):
                    piece = part[:, s * width : (s + 1) * width]
                    first[z, s // 2, s % 2] = piece[:lead_rows]
                    second[z, s // 2, s % 2] = piece[lead_rows:]
            return carried

        lax.fori_loop(0, 4, each, 0)

    return (turn, multiply)


def remote_send(pending):
    def send(source, target, sent, got, partner, start=True):
        copy = pltpu.make_async_remote_copy(
            src_ref=source,
            dst_ref=target,
            send_sem=sent,
            recv_sem=got,
            device_id=partner,
            device_id_type=pl.DeviceIdType.MESH,
        )
        if start:
            copy.start()
            pending.append(copy)
        return copy

    return send


def product_kernel(plan, lead_rows, *refs):
    groups, places = early_places(plan)
    weights, outs = (len(plan), 4 * len(groups))
    left_refs, refs = (refs[:weights], refs[weights:])
    right_refs = []
    for entry in plan:
        held = 2 if entry[5] else 1
        right_refs.append(refs[:held] if held == 2 else refs[0])
        refs = refs[held:]
    out_refs = refs[:outs]
    scratch = list(refs[outs:])
    turned_refs = [scratch.pop(0) for weight in plan]
    whole_refs = [scratch.pop(0) for weight in plan]
    chunks = [(w, t) for w, entry in enumerate(plan) for t in range(entry[1])]
    held = [(scratch.pop(0), scratch.pop(0)) for chunk in chunks]
    pair_send, pair_recv, near_sem, store_sem = scratch
    own_ctx = lax.axis_index("ctx")
    core, chip = (own_ctx % 2, own_ctx // 2)
    own_x, own_y = (chip % 2, chip // 2)
    to_core = {"ctx": toggled(own_ctx, 1)}
    barrier = pltpu.get_barrier_semaphore()
    pl.semaphore_signal(barrier, inc=1, device_id=to_core, device_id_type=pl.DeviceIdType.MESH)
    pl.semaphore_wait(barrier, 1)
    pending = []
    send = remote_send(pending)
    turn, multiply = pair_steps(
        plan,
        lead_rows,
        left_refs,
        right_refs,
        turned_refs,
        whole_refs,
        (pair_send, pair_recv, near_sem),
        core,
        pending,
        send,
    )
    for w in range(weights):
        turn(w)
    stores = []
    for number, (w, t) in enumerate(chunks):
        first, second = held[number]
        multiply(w, t, first, second)
        group, offset = places[number]
        sides = (
            lambda at: first.at[:, at, own_x],
            lambda at: first.at[:, at, 1 - own_x],
            lambda at: second.at[:, own_y, at],
            lambda at: second.at[:, 1 - own_y, at],
        )
        for side, source_at in enumerate(sides):
            for at in (0, 1):
                copy = pltpu.make_async_copy(
                    source_at(at),
                    out_refs[4 * group + side].at[at, :, :, pl.ds(offset, plan[w][2])],
                    store_sem.at[8 * number + 2 * side + at],
                )
                copy.start()
                stores.append(copy)
    for copy in stores:
        copy.wait()
    for copy in pending:
        copy.wait_send()


def weight_plan(kind, left, right, count):
    deep = left.shape[1] // 4
    if kind == "rows":
        parted = isinstance(right, tuple)
        span = right[0].shape[1] if parted else right.shape[1] // 2
        width = -(-span // (128 * count)) * 128
        return (kind, count, width, deep, (deep // 8, deep // 8), span if parted else 0)
    lead_rows = deep // 2 // 16 * 16
    return (kind, count, right.shape[-1] // 8, deep, (lead_rows, deep - lead_rows), 0)


def early_places(plan):
    groups, places = ([], [])
    for kind, count, width, deep, halves, parted in plan:
        found = [at for at, group in enumerate(groups) if group[0] == halves]
        if not found:
            groups.append([halves, 0])
            found = [len(groups) - 1]
        for chunk in range(count):
            places.append((found[0], groups[found[0]][1]))
            groups[found[0]][1] += width
    return (groups, places)


def plan_span(entry):
    return entry[1] * entry[2] if entry[0] == "rows" else 4 * entry[2]


def plan_lead(plan):
    return max([0] + [entry[4][0] for entry in plan if entry[0] == "columns"])


def pair_scratch(plan, tokens):
    turned = [pltpu.VMEM((4 * entry[3], 2 * tokens), jnp.bfloat16) for entry in plan]
    return turned + [
        pltpu.VMEM((2 * tokens, entry[5] or plan_span(entry)), jnp.bfloat16) for entry in plan
    ]


def early_sums(products, held):
    plan = [weight_plan(*product) for product in products]
    lefts, rights = ([product[1] for product in products], [product[2] for product in products])
    vmem, anywhere, dma = (
        pl.BlockSpec(memory_space=pltpu.VMEM),
        pl.BlockSpec(memory_space=pl.ANY),
        pltpu.SemaphoreType.DMA,
    )
    rights = [part for right in rights for part in (right if isinstance(right, tuple) else [right])]
    groups = early_places(plan)[0]
    outs, units = ([], [])
    for halves, columns in groups:
        for half in halves:
            outs += [jax.ShapeDtypeStruct((2, 4, half, columns), jnp.bfloat16)] * 2
    for kind, count, width, deep, halves, parted in plan:
        for chunk in range(count):
            units += [pltpu.VMEM((4, 2, 2, half, width), jnp.bfloat16) for half in halves]
    chunk_count = sum(entry[1] for entry in plan)
    scratch = pair_scratch(plan, lefts[0].shape[0]) + units
    scratch += [dma((2 * len(plan),)), dma((2 * len(plan),)), dma((len(plan),)), dma((8 * chunk_count,))]
    sides = pl.pallas_call(
        functools.partial(product_kernel, plan, plan_lead(plan)),
        out_shape=tuple(outs),
        in_specs=[vmem] * len(plan) + [anywhere] * len(rights),
        out_specs=(anywhere,) * len(outs),
        scratch_shapes=scratch,
        compiler_params=pltpu.CompilerParams(
            collective_id=3, has_side_effects=True, vmem_limit_bytes=60 * 1024 * 1024
        ),
        name="early_products",
    )(*lefts, *rights)
    held, sides = lax.optimization_barrier((held, sides))
    arrays = []
    for group in range(len(groups)):
        for part, bit in ((0, 2), (2, 4)):
            kept, sent = sides[4 * group + part : 4 * group + part + 2]
            arrays.append((kept, swap(sent, "ctx", bit)))
    return (held, (plan, arrays))


def second_step(held, early):
    plan, arrays = early
    held, arrays = lax.optimization_barrier((held, arrays))
    chip = lax.axis_index("ctx") // 2
    flat = []
    for at, (kept, arrived) in enumerate(arrays):
        bit, own = ((4, chip // 2), (2, chip % 2))[at % 2]
        other = [
            lax.dynamic_index_in_dim(side, 1 - own, 0, keepdims=False).astype(jnp.float32)
            for side in (kept, arrived)
        ]
        flat += [kept, arrived, swap((other[0] + other[1]).astype(jnp.bfloat16), "ctx", bit)]
    return (held, (plan, flat))


def sum_kernel(early, late, lead_rows, *refs):
    weights, products = (len(early) + len(late), len(late))
    left_refs, right_refs = (refs[:products], refs[products : 2 * products])
    refs = refs[2 * products :]
    groups, places = early_places(early)
    early_refs, refs = (refs[: 6 * len(groups)], refs[6 * len(groups) :])
    small_ref, out_refs, small_out = (refs[0], refs[1 : weights + 1], refs[weights + 1])
    scratch = list(refs[weights + 2 :])
    turned_refs = [scratch.pop(0) for weight in late]
    whole_refs = [scratch.pop(0) for weight in late]
    plan = early + late
    chunks = [(w, t) for w, entry in enumerate(plan) for t in range(entry[1])]
    early_count = sum(entry[1] for entry in early)
    units = {}
    for number in range(len(chunks)):
        for half in (0, 1):
            units[number, half] = [scratch.pop(0) for stage in range(5)]
    small_held = scratch.pop(0)
    send_sem, recv_sem, local_sem, load_sem, pair_send, pair_recv, small_send, small_recv, near_sem = scratch
    own_ctx, own_shard = (lax.axis_index("ctx"), lax.axis_index("fsdp"))
    core, chip = (own_ctx % 2, own_ctx // 2)
    own_x, own_y = (chip % 2, chip // 2)
    low_bit, high_bit = (own_shard % 2, own_shard // 2)
    loads = {}
    for number in range(early_count):
        w, (group, offset) = (chunks[number][0], places[number])
        for half in (0, 1):
            own = own_y if half == 0 else own_x
            kept, arrived, twice = early_refs[6 * group + 3 * half : 6 * group + 3 * half + 3]
            columns = pl.ds(offset, plan[w][2])
            sources = (kept.at[own, :, :, columns], arrived.at[own, :, :, columns], twice.at[:, :, columns])
            for at, source in enumerate(sources):
                slot = (number * 2 + half) * 3 + at
                copy = pltpu.make_async_copy(source, units[number, half][at], load_sem.at[slot])
                copy.start()
                loads[number, half, at] = copy
    partners = [{"ctx": toggled(own_ctx, bit)} for bit in (1, 2, 4)]
    partners += [{"fsdp": toggled(own_shard, bit)} for bit in (1, 2)]
    barrier = pltpu.get_barrier_semaphore()
    for partner in partners:
        pl.semaphore_signal(
            barrier, inc=1, device_id=partner, device_id_type=pl.DeviceIdType.MESH
        )
    pl.semaphore_wait(barrier, len(partners))
    to_core, to_x, to_y, to_one, to_two = partners
    pending = []
    send = remote_send(pending)
    turn, multiply = pair_steps(
        late,
        lead_rows,
        left_refs,
        right_refs,
        turned_refs,
        whole_refs,
        (pair_send, pair_recv, near_sem),
        core,
        pending,
        send,
    )
    copies = {}

    def hop(number, half, stage, source, target, partner):
        slot = (number * 2 + half) * 8 + stage
        copies[number, half, stage] = send(
            source, target, send_sem.at[slot], recv_sem.at[slot], partner
        )

    def stage_one(number):
        w, t = chunks[number]
        multiply(w - len(early), t, units[number, 0][0], units[number, 1][0])
        hop(number, 0, 0, units[number, 0][0].at[:, :, 1 - own_x], units[number, 0][1], to_x)
        hop(number, 1, 0, units[number, 1][0].at[:, 1 - own_y], units[number, 1][1], to_y)

    def add(target, source_at, count):
        def each(i, carried):
            target[i] = (
                target[i].astype(jnp.float32) + source_at(i).astype(jnp.float32)
            ).astype(jnp.bfloat16)
            return carried

        lax.fori_loop(0, count, each, 0)

    def stage_two(number):
        held, got = (units[number, 0][0], units[number, 0][1])
        copies[number, 0, 0].wait_recv()
        add(got, lambda z: held[z, :, own_x], 4)
        held_b, got_b = (units[number, 1][0], units[number, 1][1])
        copies[number, 1, 0].wait_recv()
        add(got_b, lambda z: held_b[z, own_y], 4)
        hop(number, 0, 1, got.at[:, 1 - own_y], units[number, 0][2], to_y)
        hop(number, 1, 1, got_b.at[:, 1 - own_x], units[number, 1][2], to_x)

    def stage_three(number):
        for half in (0, 1):
            kept, held, got = units[number, half][:3]
            own = own_y if half == 0 else own_x
            if number < early_count:
                for at in range(3):
                    loads[number, half, at].wait()
                add(held, lambda z: kept[z], 4)
                add(got, lambda z: held[z], 4)
            else:
                copies[number, half, 1].wait_recv()
                add(got, lambda z: held[z, own], 4)
        for half in (0, 1):
            got = units[number, half][2]
            for high in (0, 1):
                hop(
                    number,
                    half,
                    2 + 4 * high,
                    got.at[2 * high + 1 - low_bit],
                    units[number, half][3].at[high],
                    to_one,
                )

    def stage_four(number):
        for half in (0, 1):
            held, got = (units[number, half][2], units[number, half][3])
            copies[number, half, 2].wait_recv()
            copies[number, half, 6].wait_recv()
            add(got, lambda high: held[2 * high + low_bit], 2)
        for half in (0, 1):
            got = units[number, half][3]
            hop(number, half, 3, got.at[1 - high_bit], units[number, half][4].at[0], to_two)

    def final_region(number, half, chip_at):
        w, t = chunks[number]
        kind, count, width = plan[w][:3]
        deep = units[number, half][4].shape[1]
        if kind == "rows":
            start = pl.multiple_of((2 * chip_at + half) * deep, deep)
            column = pl.multiple_of((core * count + t) * width, width)
            return out_refs[w].at[pl.ds(start, deep), pl.ds(column, width)]
        column = pl.multiple_of((core * 4 + chip_at) * width, width)
        return out_refs[w].at[pl.ds(half * lead_rows, deep), pl.ds(column, width)]

    local = {}

    def stage_five(number):
        for half in (0, 1):
            held, got = (units[number, half][3], units[number, half][4])
            copies[number, half, 3].wait_recv()
            add(got, lambda i: held[high_bit], 1)
        for half in (0, 1):
            got = units[number, half][4].at[0]
            target = final_region(number, half, chip)
            hop(number, half, 4, got, target, to_x if half == 0 else to_y)
            hop(number, half, 5, got, target, to_y if half == 0 else to_x)
            copy = pltpu.make_async_copy(got, target, local_sem.at[number * 2 + half])
            copy.start()
            local[number, half] = copy

    def stage_six(number):
        for half in (0, 1):
            copies[number, half, 4].wait_recv()
            piece = final_region(number, half, toggled(chip, 1 if half == 0 else 2))
            hop(number, half, 7, piece, piece, to_y if half == 0 else to_x)

    def stage_seven(number):
        w, t = chunks[number]
        kind, count, width = plan[w][:3]
        for half in (0, 1):
            copies[number, half, 5].wait_recv()
            copies[number, half, 7].wait_recv()
            local[number, half].wait()
        span = width if kind == "rows" else 4 * width
        at = core * count + t if kind == "rows" else core
        piece = out_refs[w].at[:, pl.ds(pl.multiple_of(at * span, span), span)]
        slot = len(chunks) * 16 + number
        copies[number, 2, 0] = send(
            piece, piece, send_sem.at[slot], recv_sem.at[slot], to_core
        )

    small_copies = []

    def small_step(step):
        if step > 0:
            small_copies[step - 1].wait_recv()
            small_held[2 * step] = small_held[2 * step - 2] + small_held[2 * step - 1]
            if step == 3:
                small_out[0] = small_held[6]
        else:
            small_held[0] = small_ref[...]
        if step < 5:
            small_copies.append(
                send(
                    small_held.at[2 * step],
                    small_held.at[2 * step + 1],
                    small_send.at[step],
                    small_recv.at[step],
                    partners[step],
                )
            )
        else:
            small_out[1] = small_held[10]

    stages = (stage_one, stage_two, stage_three, stage_four, stage_five, stage_six, stage_seven)
    small_at = 0
    stage_three(0)
    for w in range(len(late)):
        turn(w)
    for tick in range(len(chunks) + len(stages)):
        for lag, stage in enumerate(stages):
            for number in range(len(chunks)):
                start = number - 2 if number < early_count else number - early_count
                if start + lag == tick and (number >= early_count or (lag >= 2 and number + lag > 2)):
                    stage(number)
        if small_at < 6:
            small_step(small_at)
            small_at += 1
    for number in range(len(chunks)):
        copies[number, 2, 0].wait_recv()
    for copy in pending:
        copy.wait_send()


def sum_weights(early, early_arrays, products, small):
    late = [weight_plan(*product) for product in products]
    lefts, rights = ([product[1] for product in products], [product[2] for product in products])
    plan = early + late
    pieces = []
    for w, (kind, count, width, deep, halves, parted) in enumerate(plan):
        leads = [(4, 2, 2), (4, 2), (4,), (2,), (1,)]
        if w < len(early):
            leads[:2] = [(4,), (4,)]
        for chunk in range(count):
            for half in halves:
                pieces += [pltpu.VMEM(lead + (half, width), jnp.bfloat16) for lead in leads]
    outs = [jax.ShapeDtypeStruct((entry[3], 2 * plan_span(entry)), jnp.bfloat16) for entry in plan]
    chunk_count = sum(entry[1] for entry in plan)
    scratch = pair_scratch(late, lefts[0].shape[0]) + pieces
    scratch += [pltpu.VMEM((11,) + small.shape, jnp.float32)]
    dma = pltpu.SemaphoreType.DMA
    slots = chunk_count * 17
    scratch += [dma((slots,)), dma((slots,)), dma((2 * chunk_count,)), dma((6 * chunk_count,))]
    scratch += [dma((2 * len(late),)), dma((2 * len(late),)), dma((5,)), dma((5,)), dma((len(late),))]
    vmem, anywhere = (
        pl.BlockSpec(memory_space=pltpu.VMEM),
        pl.BlockSpec(memory_space=pl.ANY),
    )
    return pl.pallas_call(
        functools.partial(sum_kernel, early, late, plan_lead(plan)),
        out_shape=tuple(outs) + (jax.ShapeDtypeStruct((2,) + small.shape, jnp.float32),),
        in_specs=[vmem] * len(late) + [anywhere] * (len(late) + len(early_arrays)) + [vmem],
        out_specs=(anywhere,) * len(plan) + (vmem,),
        scratch_shapes=scratch,
        compiler_params=pltpu.CompilerParams(
            collective_id=1, has_side_effects=True, vmem_limit_bytes=60 * 1024 * 1024
        ),
        name="sum_weights",
    )(*lefts, *rights, *early_arrays, small)


def layer_norm(rows_in, gain_vec):
    row_mean = jnp.mean(rows_in, axis=-1, keepdims=True)
    centred = rows_in - row_mean
    variance = jnp.mean(centred * centred, axis=-1, keepdims=True)
    return centred * lax.rsqrt(variance + norm_eps) * gain_vec


def rotate(projected, cosine, sine):
    row_count, width = projected.shape
    half_width = HEAD_WIDTH // 2
    by_head = projected.reshape(row_count, width // HEAD_WIDTH, HEAD_WIDTH)
    turned = jnp.concatenate([by_head[..., half_width:], by_head[..., :half_width]], axis=-1)
    return (by_head * cosine[:, None, :] - turned * sine[:, None, :]).reshape(row_count, width)


def swap(value, axis, bit):
    pairs = [(i, i ^ bit) for i in range(lax.axis_size(axis))]
    return lax.ppermute(value, axis, pairs)


def bit_of(axis, bit):
    return (lax.axis_index(axis) // bit) % 2 == 1


def bits_below(count):
    return [1 << i for i in range(count.bit_length() - 1)]


def reduce_pieces(pieces, labels, order):
    labels = list(labels)
    for axis, bit in order:
        at = labels.index((axis, bit))
        labels.pop(at)
        first = lax.index_in_dim(pieces, 0, at, keepdims=False)
        second = lax.index_in_dim(pieces, 1, at, keepdims=False)
        upper = bit_of(axis, bit)
        arrived = swap(jnp.where(upper, first, second), axis, bit)
        kept = jnp.where(upper, second, first)
        pieces = (kept.astype(jnp.float32) + arrived.astype(jnp.float32)).astype(jnp.bfloat16)
    return pieces


def gather_pieces(piece, labels, order):
    held = []
    for axis, bit in reversed(order):
        arrived = swap(piece, axis, bit)
        upper = bit_of(axis, bit)
        held = [label for label in labels if label in held or label == (axis, bit)]
        piece = jnp.stack(
            [jnp.where(upper, arrived, piece), jnp.where(upper, piece, arrived)],
            axis=held.index((axis, bit)),
        )
    return piece


def keep_and_send(first, second):
    upper = bit_of("ctx", 1)
    return (jnp.where(upper, second, first), jnp.where(upper, first, second))


def core_product(left, first, second):
    kept, sent = keep_and_send(first, second)
    left_all = jnp.concatenate([left, swap(left, "ctx", 1)], axis=0)
    right_all = jnp.concatenate([kept, swap(sent, "ctx", 1)], axis=0)
    return lax.dot_general(
        left_all, right_all, (((0,), (0,)), ((), ())), preferred_element_type=jnp.float32
    ).astype(jnp.bfloat16)


def shard_sum(product, by_columns):
    shards = lax.axis_size("fsdp")
    slices = lax.axis_size("ctx") // 2
    rows, columns = product.shape
    shard_labels = [("fsdp", bit) for bit in reversed(bits_below(shards))]
    slice_labels = [("ctx", 2 * bit) for bit in reversed(bits_below(slices))]
    if by_columns:
        cut = product.reshape(shards, rows // shards, slices, columns // slices)
        cut = jnp.transpose(cut, (0, 2, 1, 3))
    else:
        cut = product.reshape(shards, slices, rows // shards // slices, columns)
    parts = []
    half = cut.shape[2] // 2
    tail = list(reversed(shard_labels))
    for lead, orders in (
        (cut[:, :, :half], list(reversed(slice_labels))),
        (cut[:, :, half:], slice_labels),
    ):
        pieces = lead.reshape((2,) * (len(shard_labels) + len(slice_labels)) + lead.shape[2:])
        piece = reduce_pieces(pieces, shard_labels + slice_labels, orders + tail)
        whole = gather_pieces(piece, slice_labels, orders)
        parts.append(whole.reshape((slices,) + piece.shape))
    both = jnp.concatenate(parts, axis=1)
    if by_columns:
        return jnp.transpose(both, (1, 0, 2)).reshape(rows // shards, columns)
    return both.reshape(rows // shards, columns)


def join_cores(own):
    other = swap(own, "ctx", 1)
    upper = bit_of("ctx", 1)
    return jnp.concatenate(
        [jnp.where(upper, other, own), jnp.where(upper, own, other)], axis=1
    ).astype(jnp.float32)


def sum_over(value, axes):
    for axis in axes:
        for bit in bits_below(lax.axis_size(axis)):
            value = value + swap(value, axis, bit)
    return value


def own_shard(vector):
    width = vector.shape[0] // lax.axis_size("fsdp")
    return lax.dynamic_slice_in_dim(vector, lax.axis_index("fsdp") * width, width, 0)


def weight_sums(
    hidden,
    grad_mlp_low,
    act_mlp,
    grad_leading,
    grad_trailing,
    act_attn,
    grad_projected,
    attn_low,
    grad_attn_low,
    small,
    early,
):
    shards, ctx_count = (lax.axis_size("fsdp"), lax.axis_size("ctx"))
    rows, ff_width = hidden.shape
    model_width = act_mlp.shape[1]
    if early is None:
        half, half_three = (model_width // 2, 3 * model_width // 2)
        pairs = (
            (hidden, grad_mlp_low[:, :half], grad_mlp_low[:, half:]),
            (act_mlp, grad_leading, grad_trailing),
            (act_attn, grad_projected[:, :half_three], grad_projected[:, half_three:]),
            (attn_low, grad_attn_low[:, :half], grad_attn_low[:, half:]),
        )
        totals = [
            join_cores(shard_sum(core_product(*pair), at == 0)) for at, pair in enumerate(pairs)
        ]
        over_pack = sum_over(small, ("ctx",))
        return totals + [jnp.stack([over_pack, sum_over(over_pack, ("fsdp",))])]
    total_out, total_in, total_attn, total_qkv, small_sums = sum_weights(
        *early, [("rows", act_attn, grad_projected, 3)], small
    )
    padded = total_in.shape[1] // 2
    total_in = jnp.concatenate(
        [total_in[:, :ff_width], total_in[:, padded : padded + ff_width]], axis=1
    )
    return [
        total.astype(jnp.float32) for total in (total_out, total_in, total_qkv, total_attn)
    ] + [small_sums]


def weight_sums_early(
    hidden, grad_mlp_low, act_mlp, grad_leading, grad_trailing, attn_low, grad_attn_low, held
):
    shards, ctx_count = (lax.axis_size("fsdp"), lax.axis_size("ctx"))
    ff_width = hidden.shape[1]
    if shards != 4 or ctx_count != 8 or act_mlp.shape[1] % 1024 != 0 or ff_width % 64 != 0:
        return (held, None)
    return early_sums(
        [
            ("columns", hidden, grad_mlp_low, 1),
            ("rows", act_mlp, (grad_leading, grad_trailing), 3),
            ("rows", attn_low, grad_attn_low, 1),
        ],
        held,
    )


def per_device(
    inputs,
    cotangent,
    lengths,
    piece_route,
    gain_one,
    qkv_weight,
    attn_out,
    gain_two,
    geglu_in,
    geglu_out,
):
    ctx_count = lax.axis_size("ctx")
    own_index = lax.axis_index("ctx")
    row_count = inputs.shape[1]
    model_width = inputs.shape[2]
    piece_rows = row_count // ctx_count
    tokens = row_count * ctx_count
    own_heads = model_width // HEAD_WIDTH // ctx_count
    own_width = own_heads * HEAD_WIDTH
    block_q = math.gcd(tokens, 256)
    block_k = math.gcd(tokens, 512)
    lengths_row = lengths[0]
    own_route = piece_route[0, 0]
    slot_ids = jnp.arange(ctx_count, dtype=jnp.int32)
    outgoing = jnp.sum(
        slot_ids[None, :] * (own_route[None, :] == slot_ids[:, None]).astype(jnp.int32), axis=1
    )

    def exchange(blocks):
        return lax.all_to_all(blocks, "ctx", split_axis=0, concat_axis=0, tiled=True)

    def to_slots(rows_in):
        return jnp.take(rows_in.reshape(ctx_count, piece_rows, model_width), outgoing, axis=0)

    def to_heads(rows_in):
        by_heads = rows_in.reshape(row_count, ctx_count, -1)
        return exchange(jnp.transpose(by_heads, (1, 0, 2))).reshape(tokens, -1)

    def to_rows(heads_in):
        return exchange(heads_in.reshape(ctx_count, row_count, -1))

    both_arrived = exchange(
        jnp.concatenate([to_slots(inputs[0]), to_slots(cotangent[0])], axis=1)
    )
    arrived, grad_arrived = (both_arrived[:, :piece_rows], both_arrived[:, piece_rows:])
    residual = arrived.reshape(row_count, model_width).astype(jnp.float32)
    places = own_index * row_count + jnp.arange(row_count, dtype=jnp.int32)
    unused_begin, unused_end, offset, is_valid = spans(places, lengths_row)
    pack_begin, pack_end, unused_offset, unused_valid = spans(
        jnp.arange(tokens, dtype=jnp.int32), lengths_row
    )
    grad_final = jnp.where(
        is_valid[:, None], grad_arrived.reshape(row_count, model_width).astype(jnp.float32), 0.0
    )
    gains = jnp.pad(jnp.stack([gain_one, gain_two]), ((0, 14), (0, 0)))
    gains_full, qkv_full = gather_weights([gains, qkv_weight])
    gains_full = gains_full.reshape(-1, 16, gains.shape[1])
    gain_attn = gains_full[:, 0].reshape(-1).astype(jnp.float32)
    gain_mlp = gains_full[:, 1].reshape(-1).astype(jnp.float32)
    act_attn = layer_norm(residual, gain_attn).astype(jnp.bfloat16)
    later = [attn_out, geglu_in, geglu_out]
    row_cosine, row_sine = rotary_tables(offset, own_heads)
    if lax.axis_size("fsdp") == 4 and ctx_count == 8 and own_width == 128:
        attn_full, in_full, out_full, qkv_heads = gather_weights(
            later, (act_attn, qkv_full, row_cosine, row_sine)
        )
    else:
        attn_full, in_full, out_full = gather_weights(later)
        projected = jnp.dot(act_attn, qkv_full, preferred_element_type=jnp.float32)
        cosine, sine = rotary_tables(offset, 1)
        queries, keys = (
            rotate(projected[:, :model_width], cosine, sine).astype(jnp.bfloat16),
            rotate(projected[:, model_width : 2 * model_width], cosine, sine).astype(jnp.bfloat16),
        )
        values = projected[:, 2 * model_width :].astype(jnp.bfloat16)
        joined = jnp.stack(
            [part.reshape(row_count, ctx_count, own_width) for part in (queries, keys, values)], axis=2
        )
        qkv_heads = to_heads(joined.reshape(row_count, -1))
    low, high = key_range(pack_begin, pack_end, block_q, block_k)
    pack_begin, pack_end = (pack_begin[None, :], pack_end[None, :])
    attended_heads, log_total = attention_forward(
        qkv_heads, pack_begin, pack_end, low, high, own_heads, block_q, block_k
    )
    attn_low = jnp.transpose(to_rows(attended_heads.astype(jnp.bfloat16)), (1, 0, 2)).reshape(
        row_count, model_width
    )
    branch_attn = jnp.dot(attn_low, attn_full, preferred_element_type=jnp.float32)
    middle = residual + branch_attn
    act_mlp = layer_norm(middle, gain_mlp).astype(jnp.bfloat16)
    up_both = jnp.dot(act_mlp, in_full, preferred_element_type=jnp.float32)
    ff_width = up_both.shape[1] // 2
    hidden = (jax.nn.gelu(up_both[:, :ff_width], approximate=False) * up_both[:, ff_width:]).astype(
        jnp.bfloat16
    )
    branch_mlp = jnp.dot(hidden, out_full, preferred_element_type=jnp.float32)
    final_rows = jnp.where(is_valid[:, None], middle + branch_mlp, 0.0)
    square_sums = jnp.stack(
        [
            jnp.sum(final_rows * final_rows),
            jnp.sum(jnp.where(is_valid[:, None], branch_attn * branch_attn, 0.0)),
            jnp.sum(jnp.where(is_valid[:, None], branch_mlp * branch_mlp, 0.0)),
        ]
    )
    out_slots = final_rows.astype(jnp.bfloat16).reshape(ctx_count, piece_rows, model_width)
    grad_mlp_low = grad_final.astype(jnp.bfloat16)
    grad_hidden = lax.dot_general(
        grad_mlp_low, out_full, NT, preferred_element_type=jnp.float32
    )

    def gated(leading, trailing):
        return jax.nn.gelu(leading, approximate=False) * trailing

    unused_gate, gate_back = jax.vjp(gated, up_both[:, :ff_width], up_both[:, ff_width:])
    grad_leading, grad_trailing = gate_back(grad_hidden)
    grad_leading, grad_trailing = (
        grad_leading.astype(jnp.bfloat16),
        grad_trailing.astype(jnp.bfloat16),
    )
    grad_up = jnp.concatenate([grad_leading, grad_trailing], axis=1)
    grad_act_mlp = lax.dot_general(grad_up, in_full, NT, preferred_element_type=jnp.float32)
    unused_norm, norm_back_mlp = jax.vjp(layer_norm, middle, gain_mlp)
    grad_middle_norm, grad_gain_mlp = norm_back_mlp(grad_act_mlp)
    grad_middle = grad_final + grad_middle_norm
    grad_attn_low = grad_middle.astype(jnp.bfloat16)
    grad_attended = lax.dot_general(
        grad_attn_low, attn_full, NT, preferred_element_type=jnp.float32
    ).astype(jnp.bfloat16)
    grad_attended_heads, early = weight_sums_early(
        hidden,
        grad_mlp_low,
        act_mlp,
        grad_leading,
        grad_trailing,
        attn_low,
        grad_attn_low,
        to_heads(grad_attended),
    )
    block_back = math.gcd(tokens, 256)
    low_back, high_back = key_range(pack_begin[0], pack_end[0], block_q, block_back)
    grad_heads = attention_backward(
        qkv_heads,
        attended_heads,
        grad_attended_heads,
        log_total,
        pack_begin,
        pack_end,
        low_back,
        high_back,
        [] if early is None else [early[1][0][0]],
        own_heads,
        block_q,
        block_back,
    )
    if early is not None:
        grad_heads, early = second_step(grad_heads, early)
    grad_rows = to_rows(grad_heads)
    if own_width % 128 == 0:
        grad_projected, grad_act_attn = finish_rows(
            grad_rows, row_cosine, row_sine, qkv_full, own_heads
        )
    else:
        by_part = jnp.transpose(
            grad_rows.reshape(ctx_count, row_count, 3, own_width), (2, 1, 0, 3)
        ).reshape(3, row_count, model_width)
        cosine, sine = rotary_tables(offset, 1)
        grad_projected = jnp.concatenate(
            [
                rotate(by_part[part].astype(jnp.float32), cosine, -sine).astype(jnp.bfloat16)
                for part in (0, 1)
            ]
            + [by_part[2]],
            axis=1,
        )
        grad_act_attn = lax.dot_general(
            grad_projected, qkv_full, NT, preferred_element_type=jnp.float32
        )
    unused_first, norm_back_attn = jax.vjp(layer_norm, residual, gain_attn)
    grad_resid_norm, grad_gain_attn = norm_back_attn(grad_act_attn)
    grad_residual = (grad_middle + grad_resid_norm).astype(jnp.bfloat16)
    grad_slots = grad_residual.reshape(ctx_count, piece_rows, model_width)
    back = exchange(jnp.concatenate([out_slots, grad_slots], axis=1))
    block_out, grad_inputs = (
        jnp.take(half, own_route, axis=0).reshape(1, row_count, model_width)
        for half in (back[:, :piece_rows], back[:, piece_rows:])
    )
    small = jnp.stack(
        [grad_gain_attn, grad_gain_mlp, jnp.pad(square_sums, (0, model_width - 3))]
        + [jnp.zeros((model_width,), jnp.float32)] * 5
    )
    total_out, total_in, total_qkv, total_attn, small_sums = weight_sums(
        hidden,
        grad_mlp_low,
        act_mlp,
        grad_leading,
        grad_trailing,
        act_attn,
        grad_projected,
        attn_low,
        grad_attn_low,
        small,
        early,
    )
    total_gain_one = own_shard(small_sums[1, 0])
    total_gain_two = own_shard(small_sums[1, 1])
    total_squares = small_sums[0, 2, :3]
    valid_count = jnp.sum(lengths_row).astype(jnp.float32)
    rms_stats = jnp.sqrt(total_squares / (valid_count * model_width))[None, :]
    return (
        block_out,
        grad_inputs,
        total_gain_one,
        total_qkv,
        total_attn,
        total_gain_two,
        total_in,
        total_out,
        rms_stats,
    )


def solution(mesh):
    placed = (
        P("fsdp", "ctx", None),
        P("fsdp", "ctx", None),
        P("fsdp", None),
        P("fsdp", "ctx", None),
        P("fsdp"),
        P("fsdp", None),
        P("fsdp", None),
        P("fsdp"),
        P("fsdp", None),
        P("fsdp", None),
    )
    return jax.shard_map(
        per_device,
        mesh=mesh,
        in_specs=placed,
        out_specs=(
            P("fsdp", "ctx", None),
            P("fsdp", "ctx", None),
            P("fsdp"),
            P("fsdp", None),
            P("fsdp", None),
            P("fsdp"),
            P("fsdp", None),
            P("fsdp", None),
            P("fsdp", None),
        ),
        check_vma=False,
    )
```

```python
import functools
import math
import jax
import jax.numpy as jnp
from jax import lax
from jax.experimental import pallas as pl
from jax.experimental.pallas import tpu as pltpu
from jax.sharding import PartitionSpec as P

HEAD_WIDTH = 64
norm_eps = 1e-05
masked_score = -1e30


def head_stack(rows_in, head_count):
    if head_count == 1:
        return rows_in
    lane_head = lax.broadcasted_iota(jnp.int32, rows_in.shape, 1) // HEAD_WIDTH
    zero = jnp.zeros_like(rows_in)
    return jnp.concatenate(
        [jnp.where(lane_head == h, rows_in, zero) for h in range(head_count)], axis=0
    )


def head_pick(stacked_t, head_count, block):
    return jnp.concatenate(
        [
            stacked_t[h * HEAD_WIDTH : (h + 1) * HEAD_WIDTH, h * block : (h + 1) * block]
            for h in range(head_count)
        ],
        axis=0,
    ).T


NT = (((1,), (1,)), ((), ()))


def forward_kernel(
    head_count, block_q, block_k, low_ref, high_ref, begin_ref, end_ref, qkv_ref, out_ref, low_out_ref, log_ref, turned_ref
):
    width = out_ref.shape[1]
    step = pl.program_id(0)

    @pl.when(step == 0)
    def prepare():
        turned_ref[...] = qkv_ref[:, 2 * width :].astype(jnp.float32).T.astype(jnp.bfloat16)

    rows = pl.ds(pl.multiple_of(step * block_q, block_q), block_q)
    scale = 1.0 / math.sqrt(HEAD_WIDTH)
    stacked = head_stack(qkv_ref[rows, :width] * jnp.asarray(scale, jnp.bfloat16), head_count)
    begin = jnp.concatenate([begin_ref[:, rows]] * head_count, axis=1)
    end = jnp.concatenate([end_ref[:, rows]] * head_count, axis=1)

    def body(index, carried):
        top, total, acc = carried
        first = pl.multiple_of(index * block_k, block_k)
        keys = qkv_ref[pl.ds(first, block_k), width : 2 * width]
        scores = lax.dot_general(keys, stacked, NT, preferred_element_type=jnp.float32)
        place = first + lax.broadcasted_iota(jnp.int32, scores.shape, 0)
        scores = jnp.where((place >= begin) & (place < end), scores, masked_score)
        new_top = jnp.maximum(top, jnp.max(scores, axis=0, keepdims=True))
        fresh = jnp.exp(scores - new_top)
        fade = jnp.exp(top - new_top)
        total = total * fade + jnp.sum(fresh, axis=0, keepdims=True)
        acc = acc * fade + jnp.dot(
            turned_ref[:, pl.ds(first, block_k)],
            fresh.astype(jnp.bfloat16),
            preferred_element_type=jnp.float32,
        )
        return (new_top, total, acc)

    lanes = head_count * block_q
    top, total, acc = lax.fori_loop(
        low_ref[step],
        high_ref[step],
        body,
        (
            jnp.full((1, lanes), masked_score, jnp.float32),
            jnp.zeros((1, lanes), jnp.float32),
            jnp.zeros((width, lanes), jnp.float32),
        ),
    )
    valid = end > begin
    safe = jnp.where(valid, total, 1.0)
    acc = jnp.where(valid, acc / safe, 0.0)
    log_total = jnp.where(valid, top + jnp.log(safe), 0.0)
    attended = head_pick(acc, head_count, block_q)
    out_ref[...] = attended
    low_out_ref[...] = attended.astype(jnp.bfloat16)
    log_ref[0] = log_total


def attention_forward(qkv, begin, end, low, high, head_count, block_q, block_k):
    tokens = qkv.shape[0]
    width = head_count * HEAD_WIDTH
    steps = tokens // block_q
    whole = lambda shape: pl.BlockSpec(shape, lambda i, *_: (0,) * len(shape))
    pairs = tokens * tokens // 4 * head_count
    return pl.pallas_call(
        functools.partial(forward_kernel, head_count, block_q, block_k),
        out_shape=(
            jax.ShapeDtypeStruct((tokens, width), jnp.float32),
            jax.ShapeDtypeStruct((tokens, width), jnp.bfloat16),
            jax.ShapeDtypeStruct((steps, 1, head_count * block_q), jnp.float32),
        ),
        grid_spec=pltpu.PrefetchScalarGridSpec(
            num_scalar_prefetch=2,
            grid=(steps,),
            in_specs=[whole((1, tokens)), whole((1, tokens)), whole((tokens, 3 * width))],
            out_specs=(
                pl.BlockSpec((block_q, width), lambda i, *_: (i, 0)),
                pl.BlockSpec((block_q, width), lambda i, *_: (i, 0)),
                pl.BlockSpec((1, 1, head_count * block_q), lambda i, *_: (i, 0, 0)),
            ),
            scratch_shapes=[pltpu.VMEM((width, tokens), jnp.bfloat16)],
        ),
        cost_estimate=pl.CostEstimate(
            flops=pairs * 512, bytes_accessed=tokens * width * 12, transcendentals=pairs
        ),
        name="attention_forward",
    )(low, high, begin, end, qkv)


def turn_back(grads, cosine, sine, head_count):
    half = HEAD_WIDTH // 2
    pieces = []
    for h in range(head_count):
        base = h * HEAD_WIDTH
        pieces += [grads[:, base + half : base + HEAD_WIDTH], grads[:, base : base + half]]
    return grads * cosine + jnp.concatenate(pieces, axis=1) * sine


def backward_kernel(
    head_count,
    block_q,
    block_k,
    low_ref,
    high_ref,
    begin_ref,
    end_ref,
    qkv_ref,
    attended_ref,
    grad_ref,
    log_ref,
    *refs,
):
    out_ref, turned_ref, key_acc, value_acc = refs[-4:]
    width = attended_ref.shape[1]
    step = pl.program_id(0)

    @pl.when(step == 0)
    def prepare():
        turned_ref[...] = qkv_ref[:, width : 2 * width].astype(jnp.float32).T.astype(jnp.bfloat16)
        key_acc[...] = jnp.zeros_like(key_acc)
        value_acc[...] = jnp.zeros_like(value_acc)

    rows = pl.ds(pl.multiple_of(step * block_q, block_q), block_q)
    scale = 1.0 / math.sqrt(HEAD_WIDTH)
    stacked = head_stack(qkv_ref[rows, :width] * jnp.asarray(scale, jnp.bfloat16), head_count)
    grads = grad_ref[rows, :]
    grad_stacked = head_stack(grads, head_count)
    begin = jnp.concatenate([begin_ref[:, rows]] * head_count, axis=1)
    end = jnp.concatenate([end_ref[:, rows]] * head_count, axis=1)
    product = (grads.astype(jnp.float32) * attended_ref[rows, :]).T
    delta = jnp.concatenate(
        [
            jnp.sum(product[h * HEAD_WIDTH : (h + 1) * HEAD_WIDTH], axis=0, keepdims=True)
            for h in range(head_count)
        ],
        axis=1,
    )
    log_total = log_ref[0]

    def body(index, acc):
        first = pl.multiple_of(index * block_k, block_k)
        span = pl.ds(first, block_k)
        keys = qkv_ref[span, width : 2 * width]
        values = qkv_ref[span, 2 * width :]
        scores = lax.dot_general(keys, stacked, NT, preferred_element_type=jnp.float32)
        grad_probs = lax.dot_general(values, grad_stacked, NT, preferred_element_type=jnp.float32)
        place = first + lax.broadcasted_iota(jnp.int32, scores.shape, 0)
        scores = jnp.where((place >= begin) & (place < end), scores, masked_score)
        probs = jnp.exp(scores - log_total)
        grad_scores = (probs * (grad_probs - delta)).astype(jnp.bfloat16)
        value_acc[span, :] += jnp.dot(
            probs.astype(jnp.bfloat16), grad_stacked, preferred_element_type=jnp.float32
        )
        key_acc[span, :] += jnp.dot(grad_scores, stacked, preferred_element_type=jnp.float32)
        return acc + jnp.dot(
            turned_ref[:, span], grad_scores, preferred_element_type=jnp.float32
        )

    acc = lax.fori_loop(
        low_ref[step],
        high_ref[step],
        body,
        jnp.zeros((width, head_count * block_q), jnp.float32),
    )
    grad_queries = head_pick(acc, head_count, block_q) * scale
    out_ref[rows, :width] = grad_queries.astype(jnp.bfloat16)

    @pl.when(step == pl.num_programs(0) - 1)
    def finish():
        @pl.loop(0, pl.num_programs(0))
        def each(index):
            span = pl.ds(pl.multiple_of(index * block_q, block_q), block_q)
            out_ref[span, width : 2 * width] = key_acc[span, :].astype(jnp.bfloat16)
            out_ref[span, 2 * width :] = value_acc[span, :].astype(jnp.bfloat16)


def attention_backward(
    qkv, attended, grads, log_total, begin, end, low, high, after, head_count, block_q, block_k
):
    tokens = qkv.shape[0]
    width = head_count * HEAD_WIDTH
    steps = tokens // block_q
    whole = lambda shape: pl.BlockSpec(shape, lambda i, *_: (0,) * len(shape))
    pairs = tokens * tokens // 4 * head_count
    return pl.pallas_call(
        functools.partial(backward_kernel, head_count, block_q, block_k),
        out_shape=jax.ShapeDtypeStruct((tokens, 3 * width), jnp.bfloat16),
        grid_spec=pltpu.PrefetchScalarGridSpec(
            num_scalar_prefetch=2,
            grid=(steps,),
            in_specs=[
                whole((1, tokens)),
                whole((1, tokens)),
                whole((tokens, 3 * width)),
                whole((tokens, width)),
                whole((tokens, width)),
                pl.BlockSpec((1, 1, head_count * block_q), lambda i, *_: (i, 0, 0)),
            ]
            + [pl.BlockSpec(memory_space=pl.ANY)] * len(after),
            out_specs=whole((tokens, 3 * width)),
            scratch_shapes=[
                pltpu.VMEM((width, tokens), jnp.bfloat16),
                pltpu.VMEM((tokens, width), jnp.float32),
                pltpu.VMEM((tokens, width), jnp.float32),
            ],
        ),
        cost_estimate=pl.CostEstimate(
            flops=pairs * 1280, bytes_accessed=tokens * width * 30, transcendentals=pairs
        ),
        name="attention_backward",
    )(low, high, begin, end, qkv, attended, grads, log_total, *after)


def rows_kernel(head_count, heads_ref, cosine_ref, sine_ref, query_ref, key_ref, value_ref, out_ref, act_ref):
    width = heads_ref.shape[2] // 3
    step = pl.program_id(0)
    total = out_ref.shape[1] // 3
    owners = heads_ref.shape[0]
    pieces = []
    for part in range(3):
        for owner in range(owners):
            piece = heads_ref[owner, :, part * width : (part + 1) * width]
            if part < 2:
                piece = turn_back(
                    piece.astype(jnp.float32), cosine_ref[...], sine_ref[...], head_count
                ).astype(jnp.bfloat16)
            first = pl.multiple_of(part * total + (step * owners + owner) * width, width)
            out_ref[:, pl.ds(first, width)] = piece
            pieces.append(piece)
    weights = jnp.concatenate([query_ref[...], key_ref[...], value_ref[...]], axis=1)
    product = lax.dot_general(
        jnp.concatenate(pieces, axis=1), weights, NT, preferred_element_type=jnp.float32
    )

    @pl.when(step == 0)
    def begin():
        act_ref[...] = product

    @pl.when(step > 0)
    def add():
        act_ref[...] += product


def finish_rows(heads, cosine, sine, qkv_full, head_count):
    owners, rows, columns = heads.shape
    width = columns // 3
    depth = qkv_full.shape[0]
    whole = lambda shape: pl.BlockSpec(shape, lambda i: (0,) * len(shape))
    steps = owners // 2
    part_of = lambda part: pl.BlockSpec((depth, 2 * width), lambda i: (0, part * steps + i))
    return pl.pallas_call(
        functools.partial(rows_kernel, head_count),
        out_shape=(
            jax.ShapeDtypeStruct((rows, owners * columns), jnp.bfloat16),
            jax.ShapeDtypeStruct((rows, depth), jnp.float32),
        ),
        grid=(steps,),
        in_specs=[
            pl.BlockSpec((2, rows, columns), lambda i: (i, 0, 0)),
            whole((rows, width)),
            whole((rows, width)),
            part_of(0),
            part_of(1),
            part_of(2),
        ],
        out_specs=(whole((rows, owners * columns)), whole((rows, depth))),
        cost_estimate=pl.CostEstimate(
            flops=2 * rows * depth * owners * columns,
            bytes_accessed=2 * depth * owners * columns + 4 * rows * owners * columns,
            transcendentals=0,
        ),
        name="finish_rows",
    )(heads, cosine, sine, qkv_full, qkv_full, qkv_full)


def spans(places, lengths_row):
    ends = jnp.cumsum(lengths_row)
    past = (places[:, None] >= ends[None, :]).astype(jnp.int32)
    begin = jnp.sum(past * lengths_row[None, :], axis=1)
    before = (places[:, None] >= (ends - lengths_row)[None, :]).astype(jnp.int32)
    end = jnp.sum(before * lengths_row[None, :], axis=1)
    valid = places < ends[-1]
    return (jnp.where(valid, begin, 0), jnp.where(valid, end, 0), places - begin, valid)


def key_range(begin, end, block_q, block_k):
    begin_blocks = jnp.where(end > begin, begin, jnp.int32(1 << 30)).reshape(-1, block_q)
    high = (jnp.max(end.reshape(-1, block_q), axis=1) + block_k - 1) // block_k
    low = jnp.minimum(jnp.min(begin_blocks, axis=1) // block_k, high)
    return (low, high)


def rotary_tables(offset, head_count):
    half = HEAD_WIDTH // 2
    inverse = 160000.0 ** (-2.0 * jnp.arange(half, dtype=jnp.float32) / HEAD_WIDTH)
    angles = offset.astype(jnp.float32)[:, None] * inverse[None, :]
    cosine, sine = (jnp.cos(angles), jnp.sin(angles))
    return (
        jnp.concatenate([cosine, cosine] * head_count, axis=1),
        jnp.concatenate([sine, -sine] * head_count, axis=1),
    )


def toggled(index, bit):
    return index + bit - 2 * bit * ((index // bit) % 2)


def gather_kernel(shapes, projects, *refs):
    count = len(shapes)
    shard_refs, refs = (refs[:count], refs[count:])
    if projects:
        act_ref, qkv_ref, cosine_ref, sine_ref = refs[:4]
        heads_ref = refs[4 + count]
        columns_ref, held_ref, load_sem, head_send, head_recv, own_sem = refs[count + 8 :]
        refs = refs[4 : 4 + count] + refs[count + 5 : count + 8]
    full_refs = refs[:count]
    send_sem, recv_sem, local_sem = refs[count:]
    shards = lax.axis_size("fsdp")
    slices = lax.axis_size("ctx") // 2
    own_ctx, own_shard = (lax.axis_index("ctx"), lax.axis_index("fsdp"))
    core, chip = (own_ctx % 2, own_ctx // 2)
    barrier = pltpu.get_barrier_semaphore()
    partners = [{"fsdp": toggled(own_shard, bit)} for bit in (1, 2)]
    partners += [{"ctx": toggled(own_ctx, bit)} for bit in (1, 2, 4)]

    def owner_at(relation):
        owner = own_ctx
        for bit in (1, 2, 4):
            if relation & bit:
                owner = toggled(owner, bit)
        return owner

    if projects:
        partners += [{"ctx": owner_at(relation)} for relation in (3, 5, 6, 7)]
    for partner in partners:
        pl.semaphore_signal(
            barrier, inc=1, device_id=partner, device_id_type=pl.DeviceIdType.MESH
        )
    pl.semaphore_wait(barrier, len(partners))
    to_one, to_two, to_core, to_x, to_y = partners[:5]

    def shard_at(step):
        if step == 0:
            return own_shard
        if step == 3:
            return toggled(toggled(own_shard, 1), 2)
        return toggled(own_shard, step)

    def region(ref, weight, step, chip_at, half):
        if shapes[weight] == "small":
            return ref if len(ref.shape) == 2 else ref.at[shard_at(step)]
        if shapes[weight] == "rows":
            rows = ref.shape[-2]
            span = pl.ds(0, rows) if half is None else pl.ds(half * (rows // 2), rows // 2)
            if len(ref.shape) == 4:
                return ref.at[core, chip_at, span, :]
            return ref.at[shard_at(step), core, chip_at, span, :]
        rows = ref.shape[-2]
        first = (rows // 2) // 16 * 16
        spans_of = {None: pl.ds(0, rows), 0: pl.ds(0, first), 1: pl.ds(first, rows - first)}
        width = ref.shape[-1] // (2 * slices)
        columns = pl.ds(pl.multiple_of((core * slices + chip_at) * width, width), width)
        if len(ref.shape) == 2:
            return ref.at[spans_of[half], columns]
        return ref.at[shard_at(step), spans_of[half], columns]

    def core_region(ref, weight, step):
        if shapes[weight] == "rows":
            return ref.at[shard_at(step), core]
        width = ref.shape[-1] // 2
        return ref.at[shard_at(step), :, pl.ds(pl.multiple_of(core * width, width), width)]

    pending = []

    def send(source, target, slot, partner):
        copy = pltpu.make_async_remote_copy(
            src_ref=source,
            dst_ref=target,
            send_sem=send_sem.at[slot],
            recv_sem=recv_sem.at[slot],
            device_id=partner,
            device_id_type=pl.DeviceIdType.MESH,
        )
        copy.start()
        pending.append(copy)
        return copy

    copies = {}
    local = []

    def slot_of(weight, step, kind):
        return (weight * 3 + step - 1) * 8 + kind

    def shard_sends(weight):
        source = region(shard_refs[weight], weight, 0, chip, None)
        target = region(full_refs[weight], weight, 0, chip, None)
        copies[weight, 2, 0] = send(source, target, slot_of(weight, 2, 0), to_two)
        copies[weight, 1, 0] = send(source, target, slot_of(weight, 1, 0), to_one)
        target = full_refs[weight].at[own_shard]
        copy = pltpu.make_async_copy(shard_refs[weight], target, local_sem.at[weight])
        copy.start()
        local.append(copy)

    def shard_forward(weight):
        copies[weight, 2, 0].wait_recv()
        piece = region(full_refs[weight], weight, 2, chip, None)
        copies[weight, 3, 0] = send(piece, piece, slot_of(weight, 3, 0), to_one)

    def plane_sends(weight, step):
        lead = region(full_refs[weight], weight, step, chip, 0)
        rest = region(full_refs[weight], weight, step, chip, 1)
        for kind, piece, partner in ((1, lead, to_x), (2, rest, to_y), (3, lead, to_y), (4, rest, to_x)):
            copies[weight, step, kind] = send(piece, piece, slot_of(weight, step, kind), partner)

    def plane_forward(weight, step):
        copies[weight, step, 1].wait_recv()
        lead = region(full_refs[weight], weight, step, toggled(chip, 1), 0)
        copies[weight, step, 5] = send(lead, lead, slot_of(weight, step, 5), to_y)
        copies[weight, step, 2].wait_recv()
        rest = region(full_refs[weight], weight, step, toggled(chip, 2), 1)
        copies[weight, step, 6] = send(rest, rest, slot_of(weight, step, 6), to_x)

    def core_send(weight, step):
        for kind in (3, 4, 5, 6):
            copies[weight, step, kind].wait_recv()
        piece = core_region(full_refs[weight], weight, step)
        copies[weight, step, 7] = send(piece, piece, slot_of(weight, step, 7), to_core)

    chip_order = (3, 1, 2, 0)

    def start_loads():
        loads = {}
        for chip_bits in chip_order:
            owner_chip = owner_at(2 * chip_bits) // 2
            for part in range(3):
                width = columns_ref.shape[2] // 3
                total = qkv_ref.shape[1] // 3
                first = pl.multiple_of(part * total + owner_chip * width, width)
                loads[chip_bits, part] = pltpu.make_async_copy(
                    qkv_ref.at[:, pl.ds(first, width)],
                    columns_ref.at[chip_bits, :, pl.ds(part * width, width)],
                    load_sem.at[chip_bits * 3 + part],
                )
                loads[chip_bits, part].start()
        return loads

    def project(chip_bits, loads):
        for part in range(3):
            loads[chip_bits, part].wait()
        rows, own_width = (act_ref.shape[0], held_ref.shape[2] // 3)
        product = jnp.dot(
            act_ref[...], columns_ref[chip_bits], preferred_element_type=jnp.float32
        )
        for core_at in (0, 1):
            slot = 2 * chip_bits + core + core_at - 2 * core * core_at
            for part in range(3):
                first = (2 * part + core_at) * own_width
                piece = product[:, first : first + own_width]
                if part < 2:
                    half = HEAD_WIDTH // 2
                    turned = []
                    for base in range(0, own_width, HEAD_WIDTH):
                        turned += [piece[:, base + half : base + HEAD_WIDTH], piece[:, base : base + half]]
                    piece = piece * cosine_ref[...] - jnp.concatenate(turned, axis=1) * sine_ref[...]
                held_ref[slot, :, part * own_width : (part + 1) * own_width] = piece.astype(jnp.bfloat16)
        target = heads_ref.at[pl.ds(pl.multiple_of(own_ctx * rows, rows), rows), :]
        for core_bit in (0, 1):
            relation = 2 * chip_bits + core_bit
            if relation == 0:
                copy = pltpu.make_async_copy(held_ref.at[0], target, own_sem.at[0])
                copy.start()
                local.append(copy)
                continue
            copy = pltpu.make_async_remote_copy(
                src_ref=held_ref.at[relation],
                dst_ref=target,
                send_sem=head_send.at[relation],
                recv_sem=head_recv.at[relation],
                device_id={"ctx": owner_at(relation)},
                device_id_type=pl.DeviceIdType.MESH,
            )
            copy.start()
            pending.append(copy)
            arriving.append(copy)

    arriving = []
    sent = 1
    if projects:
        loads = start_loads()
        for weight in range(count):
            shard_sends(weight)
        sent = count
        for chip_bits in chip_order:
            project(chip_bits, loads)
    else:
        shard_sends(0)
    for weight in range(count):
        if weight + 1 >= sent and weight + 1 < count:
            shard_sends(weight + 1)
        shard_forward(weight)
        copies[weight, 1, 0].wait_recv()
        if shapes[weight] == "small":
            copies[weight, 3, 0].wait_recv()
            continue
        plane_sends(weight, 1)
        plane_sends(weight, 2)
        copies[weight, 3, 0].wait_recv()
        plane_sends(weight, 3)
        for step in (1, 2, 3):
            plane_forward(weight, step)
        if weight > 0 and shapes[weight - 1] != "small":
            for step in (1, 2, 3):
                core_send(weight - 1, step)
    for step in (1, 2, 3):
        core_send(count - 1, step)
    for weight in range(count):
        if shapes[weight] != "small":
            for step in (1, 2, 3):
                copies[weight, step, 7].wait_recv()
    for copy in arriving:
        copy.wait_recv()
    for copy in pending:
        copy.wait_send()
    for copy in local:
        copy.wait()


def gather_weights(weights, projection=None):
    shards, ctx_count = (lax.axis_size("fsdp"), lax.axis_size("ctx"))
    slices = ctx_count // 2
    shapes, views, outs = ([], [], [])
    for weight in weights:
        rows, columns = weight.shape
        if rows % (32 * ctx_count) == 0:
            shapes.append("rows")
            views.append(weight.reshape(2, slices, rows // ctx_count, columns))
            outs.append((shards, 2, slices, rows // ctx_count, columns))
        elif rows == 16:
            shapes.append("small")
            views.append(weight)
            outs.append((shards, rows, columns))
        elif columns % (128 * ctx_count) == 0 and rows % 16 == 0:
            shapes.append("columns")
            views.append(weight)
            outs.append((shards, rows, columns))
    if shards != 4 or ctx_count != 8 or len(views) < len(weights):
        return [lax.all_gather(weight, "fsdp", axis=0, tiled=True) for weight in weights]
    slots = len(views) * 24
    vmem, anywhere, dma = (
        pl.BlockSpec(memory_space=pltpu.VMEM),
        pl.BlockSpec(memory_space=pl.ANY),
        pltpu.SemaphoreType.DMA,
    )
    in_specs = [vmem] * len(views)
    scratch = [dma((slots,)), dma((slots,)), dma((len(views),))]
    if projection is not None:
        act_attn, qkv_full = projection[:2]
        rows, own_columns = (act_attn.shape[0], qkv_full.shape[1] // ctx_count)
        views += list(projection)
        in_specs += [vmem, anywhere, vmem, vmem]
        outs.append((ctx_count * rows, own_columns))
        scratch += [
            pltpu.VMEM((slices, qkv_full.shape[0], 2 * own_columns), jnp.bfloat16),
            pltpu.VMEM((ctx_count, rows, own_columns), jnp.bfloat16),
            dma((3 * slices,)),
            dma((ctx_count,)),
            dma((ctx_count,)),
            dma((1,)),
        ]
    held = pl.pallas_call(
        functools.partial(gather_kernel, shapes, projection is not None),
        out_shape=tuple(jax.ShapeDtypeStruct(out, jnp.bfloat16) for out in outs),
        in_specs=in_specs,
        out_specs=tuple(anywhere for out in outs),
        scratch_shapes=scratch,
        compiler_params=pltpu.CompilerParams(
            collective_id=0 if projection is None else 2,
            has_side_effects=True,
            vmem_limit_bytes=60 * 1024 * 1024,
        ),
        name="gather_weights" if projection is None else "gather_and_project",
    )(*views)
    return [whole.reshape(-1, whole.shape[-1]) for whole in held]


def pair_steps(plan, lead_rows, left_refs, right_refs, turned_refs, whole_refs, sems, core, pending, send):
    pair_send, pair_recv, near_sem = sems
    to_core = {"ctx": toggled(lax.axis_index("ctx"), 1)}

    def send_core(source, target, sent, got, start=True):
        return send(source, target, sent, got, to_core, start)

    rows = left_refs[0].shape[0] if left_refs else 0
    pairs = []

    def begin(w):
        entry = plan[w]
        span, right = (plan_span(entry), right_refs[w])
        own_part, other_part = (whole_refs[w].at[pl.ds(0, rows)], whole_refs[w].at[pl.ds(rows, rows)])

        def exchange(own_half, other_half, start=True):
            near = pltpu.make_async_copy(own_half, own_part, near_sem.at[w])
            if start:
                near.start()
            sems = (pair_send.at[2 * w], pair_recv.at[2 * w])
            return [near, send_core(other_half, other_part, *sems, start)]

        if entry[5]:
            ways = [exchange(right[at], right[1 - at], False) for at in (0, 1)]
            for at in (0, 1):

                @pl.when(core == at)
                def start():
                    for copy in ways[at]:
                        copy.start()

            pairs.append(ways[0])
            pending.append(ways[0][1])
        else:
            halves = [
                right.at[:, pl.ds(pl.multiple_of(at * span, span), span)] for at in (core, 1 - core)
            ]
            pairs.append(exchange(*halves))

    def turn(w):
        left, turned = (left_refs[w], turned_refs[w])
        block = 512
        for first in range(0, left.shape[1], block):
            last = min(first + block, left.shape[1])
            turned[first:last, :rows] = (
                left[:, first:last].astype(jnp.float32).T.astype(jnp.bfloat16)
            )
        pairs[w].append(
            send_core(
                turned.at[:, pl.ds(0, rows)],
                turned.at[:, pl.ds(rows, rows)],
                pair_send.at[2 * w + 1],
                pair_recv.at[2 * w + 1],
            )
        )

    def multiply(w, t, first, second):
        kind, count, width, deep, halves, parted = plan[w]
        if t == 0:
            near, far, turned = pairs[w]
            near.wait()
            far.wait_recv()
            turned.wait_recv()

        def each(z, carried):
            left = turned_refs[w][pl.ds(pl.multiple_of(z * deep, 16), deep), :]
            if kind == "rows":
                last = min((t + 1) * width, whole_refs[w].shape[1])
                part = jnp.dot(
                    left, whole_refs[w][:, t * width : last], preferred_element_type=jnp.float32
                ).astype(jnp.bfloat16)
                if last < (t + 1) * width:
                    empty = jnp.zeros((deep, (t + 1) * width - last), jnp.bfloat16)
                    part = jnp.concatenate([part, empty], axis=1)
                piece_rows = first.shape[3]
                for s in range(4):
                    first[z, s // 2, s % 2] = part[2 * s * piece_rows : (2 * s + 1) * piece_rows]
                    second[z, s // 2, s % 2] = part[(2 * s + 1) * piece_rows : (2 * s + 2) * piece_rows]
            else:
                part = jnp.dot(
                    left, whole_refs[w][...], preferred_element_type=jnp.float32
                ).astype(jnp.bfloat16)
                for s in range(4):
                    piece = part[:, s * width : (s + 1) * width]
                    first[z, s // 2, s % 2] = piece[:lead_rows]
                    second[z, s // 2, s % 2] = piece[lead_rows:]
            return carried

        lax.fori_loop(0, 4, each, 0)

    return (begin, turn, multiply)


def remote_send(pending):
    def send(source, target, sent, got, partner, start=True):
        copy = pltpu.make_async_remote_copy(
            src_ref=source,
            dst_ref=target,
            send_sem=sent,
            recv_sem=got,
            device_id=partner,
            device_id_type=pl.DeviceIdType.MESH,
        )
        if start:
            copy.start()
            pending.append(copy)
        return copy

    return send


def product_kernel(plan, lead_rows, *refs):
    groups, places = early_places(plan)
    weights, outs = (len(plan), 4 * len(groups))
    left_refs, refs = (refs[:weights], refs[weights:])
    right_refs = []
    for entry in plan:
        held = 2 if entry[5] else 1
        right_refs.append(refs[:held] if held == 2 else refs[0])
        refs = refs[held:]
    out_refs = refs[:outs]
    scratch = list(refs[outs:])
    turned_refs = [scratch.pop(0) for weight in plan]
    whole_refs = [scratch.pop(0) for weight in plan]
    chunks = [(w, t) for w, entry in enumerate(plan) for t in range(entry[1])]
    held = [(scratch.pop(0), scratch.pop(0)) for chunk in chunks]
    pair_send, pair_recv, near_sem, store_sem = scratch
    own_ctx = lax.axis_index("ctx")
    core, chip = (own_ctx % 2, own_ctx // 2)
    own_x, own_y = (chip % 2, chip // 2)
    to_core = {"ctx": toggled(own_ctx, 1)}
    barrier = pltpu.get_barrier_semaphore()
    pl.semaphore_signal(barrier, inc=1, device_id=to_core, device_id_type=pl.DeviceIdType.MESH)
    pl.semaphore_wait(barrier, 1)
    pending = []
    send = remote_send(pending)
    begin, turn, multiply = pair_steps(
        plan,
        lead_rows,
        left_refs,
        right_refs,
        turned_refs,
        whole_refs,
        (pair_send, pair_recv, near_sem),
        core,
        pending,
        send,
    )
    for w in range(weights):
        begin(w)
        turn(w)
    stores = []
    for number, (w, t) in enumerate(chunks):
        first, second = held[number]
        multiply(w, t, first, second)
        group, offset = places[number]
        sides = (
            lambda at: first.at[:, at, own_x],
            lambda at: first.at[:, at, 1 - own_x],
            lambda at: second.at[:, own_y, at],
            lambda at: second.at[:, 1 - own_y, at],
        )
        for side, source_at in enumerate(sides):
            for at in (0, 1):
                copy = pltpu.make_async_copy(
                    source_at(at),
                    out_refs[4 * group + side].at[at, :, :, pl.ds(offset, plan[w][2])],
                    store_sem.at[8 * number + 2 * side + at],
                )
                copy.start()
                stores.append(copy)
    for copy in stores:
        copy.wait()
    for copy in pending:
        copy.wait_send()


def weight_plan(kind, left, right, count):
    deep = left.shape[1] // 4
    if kind == "rows":
        parted = isinstance(right, tuple)
        span = right[0].shape[1] if parted else right.shape[1] // 2
        width = -(-span // (128 * count)) * 128
        return (kind, count, width, deep, (deep // 8, deep // 8), span if parted else 0)
    lead_rows = deep // 2 // 16 * 16
    return (kind, count, right.shape[-1] // 8, deep, (lead_rows, deep - lead_rows), 0)


def early_places(plan):
    groups, places = ([], [])
    for kind, count, width, deep, halves, parted in plan:
        found = [at for at, group in enumerate(groups) if group[0] == halves]
        if not found:
            groups.append([halves, 0])
            found = [len(groups) - 1]
        for chunk in range(count):
            places.append((found[0], groups[found[0]][1]))
            groups[found[0]][1] += width
    return (groups, places)


def plan_span(entry):
    return entry[1] * entry[2] if entry[0] == "rows" else 4 * entry[2]


def plan_lead(plan):
    return max([0] + [entry[4][0] for entry in plan if entry[0] == "columns"])


def pair_scratch(plan, tokens):
    turned = [pltpu.VMEM((4 * entry[3], 2 * tokens), jnp.bfloat16) for entry in plan]
    return turned + [
        pltpu.VMEM((2 * tokens, entry[5] or plan_span(entry)), jnp.bfloat16) for entry in plan
    ]


def early_sums(products, held):
    plan = [weight_plan(*product) for product in products]
    lefts, rights = ([product[1] for product in products], [product[2] for product in products])
    vmem, anywhere, dma = (
        pl.BlockSpec(memory_space=pltpu.VMEM),
        pl.BlockSpec(memory_space=pl.ANY),
        pltpu.SemaphoreType.DMA,
    )
    rights = [part for right in rights for part in (right if isinstance(right, tuple) else [right])]
    groups = early_places(plan)[0]
    outs, units = ([], [])
    for halves, columns in groups:
        for half in halves:
            outs += [jax.ShapeDtypeStruct((2, 4, half, columns), jnp.bfloat16)] * 2
    for kind, count, width, deep, halves, parted in plan:
        for chunk in range(count):
            units += [pltpu.VMEM((4, 2, 2, half, width), jnp.bfloat16) for half in halves]
    chunk_count = sum(entry[1] for entry in plan)
    scratch = pair_scratch(plan, lefts[0].shape[0]) + units
    scratch += [dma((2 * len(plan),)), dma((2 * len(plan),)), dma((len(plan),)), dma((8 * chunk_count,))]
    sides = pl.pallas_call(
        functools.partial(product_kernel, plan, plan_lead(plan)),
        out_shape=tuple(outs),
        in_specs=[vmem] * len(plan) + [anywhere] * len(rights),
        out_specs=(anywhere,) * len(outs),
        scratch_shapes=scratch,
        compiler_params=pltpu.CompilerParams(
            collective_id=3, has_side_effects=True, vmem_limit_bytes=60 * 1024 * 1024
        ),
        name="early_products",
    )(*lefts, *rights)
    held, sides = lax.optimization_barrier((held, sides))
    arrays = []
    for group in range(len(groups)):
        for part, bit in ((0, 2), (2, 4)):
            kept, sent = sides[4 * group + part : 4 * group + part + 2]
            arrays.append((kept, swap(sent, "ctx", bit)))
    return (held, (plan, arrays))


def second_step(held, early):
    plan, arrays = early
    held, arrays = lax.optimization_barrier((held, arrays))
    chip = lax.axis_index("ctx") // 2
    flat = []
    for at, (kept, arrived) in enumerate(arrays):
        bit, own = ((4, chip // 2), (2, chip % 2))[at % 2]
        other = [
            lax.dynamic_index_in_dim(side, 1 - own, 0, keepdims=False).astype(jnp.float32)
            for side in (kept, arrived)
        ]
        flat += [kept, arrived, swap((other[0] + other[1]).astype(jnp.bfloat16), "ctx", bit)]
    return (held, (plan, flat))


def sum_kernel(early, late, lead_rows, *refs):
    weights, products = (len(early) + len(late), len(late))
    left_refs, right_refs = (refs[:products], refs[products : 2 * products])
    refs = refs[2 * products :]
    groups, places = early_places(early)
    early_refs, refs = (refs[: 6 * len(groups)], refs[6 * len(groups) :])
    small_ref, out_refs, small_out = (refs[0], refs[1 : weights + 1], refs[weights + 1])
    scratch = list(refs[weights + 2 :])
    turned_refs = [scratch.pop(0) for weight in late]
    whole_refs = [scratch.pop(0) for weight in late]
    plan = early + late
    chunks = [(w, t) for w, entry in enumerate(plan) for t in range(entry[1])]
    early_count = sum(entry[1] for entry in early)
    units = {}
    for number in range(len(chunks)):
        for half in (0, 1):
            units[number, half] = [scratch.pop(0) for stage in range(5)]
    sum_refs = [scratch.pop(0) for entry in plan]
    wide_refs = [scratch.pop(0) for entry in plan]
    small_held, wide_sem = (scratch.pop(0), scratch.pop(0))
    send_sem, recv_sem, local_sem, load_sem, pair_send, pair_recv, small_send, small_recv, near_sem = scratch
    own_ctx, own_shard = (lax.axis_index("ctx"), lax.axis_index("fsdp"))
    core, chip = (own_ctx % 2, own_ctx // 2)
    own_x, own_y = (chip % 2, chip // 2)
    low_bit, high_bit = (own_shard % 2, own_shard // 2)
    loads = {}
    for number in range(early_count):
        w, (group, offset) = (chunks[number][0], places[number])
        for half in (0, 1):
            own = own_y if half == 0 else own_x
            kept, arrived, twice = early_refs[6 * group + 3 * half : 6 * group + 3 * half + 3]
            columns = pl.ds(offset, plan[w][2])
            sources = (kept.at[own, :, :, columns], arrived.at[own, :, :, columns], twice.at[:, :, columns])
            for at, source in enumerate(sources):
                slot = (number * 2 + half) * 3 + at
                copy = pltpu.make_async_copy(source, units[number, half][at], load_sem.at[slot])
                copy.start()
                loads[number, half, at] = copy
    partners = [{"ctx": toggled(own_ctx, bit)} for bit in (1, 2, 4)]
    partners += [{"fsdp": toggled(own_shard, bit)} for bit in (1, 2)]
    barrier = pltpu.get_barrier_semaphore()
    for partner in partners:
        pl.semaphore_signal(
            barrier, inc=1, device_id=partner, device_id_type=pl.DeviceIdType.MESH
        )
    pl.semaphore_wait(barrier, len(partners))
    to_core, to_x, to_y, to_one, to_two = partners
    pending = []
    send = remote_send(pending)
    begin, turn, multiply = pair_steps(
        late,
        lead_rows,
        left_refs,
        right_refs,
        turned_refs,
        whole_refs,
        (pair_send, pair_recv, near_sem),
        core,
        pending,
        send,
    )
    for w in range(len(late)):
        begin(w)
    copies = {}

    def hop(number, half, stage, source, target, partner):
        slot = (number * 2 + half) * 8 + stage
        copies[number, half, stage] = send(
            source, target, send_sem.at[slot], recv_sem.at[slot], partner
        )

    def stage_one(number):
        w, t = chunks[number]
        multiply(w - len(early), t, units[number, 0][0], units[number, 1][0])
        hop(number, 0, 0, units[number, 0][0].at[:, :, 1 - own_x], units[number, 0][1], to_x)
        hop(number, 1, 0, units[number, 1][0].at[:, 1 - own_y], units[number, 1][1], to_y)

    def add(target, source_at, count):
        def each(i, carried):
            target[i] = (
                target[i].astype(jnp.float32) + source_at(i).astype(jnp.float32)
            ).astype(jnp.bfloat16)
            return carried

        lax.fori_loop(0, count, each, 0)

    def stage_two(number):
        held, got = (units[number, 0][0], units[number, 0][1])
        copies[number, 0, 0].wait_recv()
        add(got, lambda z: held[z, :, own_x], 4)
        held_b, got_b = (units[number, 1][0], units[number, 1][1])
        copies[number, 1, 0].wait_recv()
        add(got_b, lambda z: held_b[z, own_y], 4)
        hop(number, 0, 1, got.at[:, 1 - own_y], units[number, 0][2], to_y)
        hop(number, 1, 1, got_b.at[:, 1 - own_x], units[number, 1][2], to_x)

    def stage_three(number):
        for half in (0, 1):
            kept, held, got = units[number, half][:3]
            own = own_y if half == 0 else own_x
            if number < early_count:
                for at in range(3):
                    loads[number, half, at].wait()
                add(held, lambda z: kept[z], 4)
                add(got, lambda z: held[z], 4)
            else:
                copies[number, half, 1].wait_recv()
                add(got, lambda z: held[z, own], 4)
        for half in (0, 1):
            got = units[number, half][2]
            for high in (0, 1):
                hop(
                    number,
                    half,
                    2 + 4 * high,
                    got.at[2 * high + 1 - low_bit],
                    units[number, half][3].at[high],
                    to_one,
                )

    def stage_four(number):
        for half in (0, 1):
            held, got = (units[number, half][2], units[number, half][3])
            copies[number, half, 2].wait_recv()
            copies[number, half, 6].wait_recv()
            add(got, lambda high: held[2 * high + low_bit], 2)
        for half in (0, 1):
            got = units[number, half][3]
            hop(number, half, 3, got.at[1 - high_bit], units[number, half][4].at[0], to_two)

    def final_region(number, half, chip_at):
        w, t = chunks[number]
        kind, count, width = plan[w][:3]
        deep = units[number, half][4].shape[1]
        if kind == "rows":
            start = pl.multiple_of((2 * chip_at + half) * deep, deep)
            column = pl.multiple_of((core * count + t) * width, width)
            return sum_refs[w].at[pl.ds(start, deep), pl.ds(column, width)]
        column = pl.multiple_of((core * 4 + chip_at) * width, width)
        return sum_refs[w].at[pl.ds(half * lead_rows, deep), pl.ds(column, width)]

    local = {}

    def stage_five(number):
        for half in (0, 1):
            held, got = (units[number, half][3], units[number, half][4])
            copies[number, half, 3].wait_recv()
            add(got, lambda i: held[high_bit], 1)
        for half in (0, 1):
            got = units[number, half][4].at[0]
            target = final_region(number, half, chip)
            hop(number, half, 4, got, target, to_x if half == 0 else to_y)
            hop(number, half, 5, got, target, to_y if half == 0 else to_x)
            copy = pltpu.make_async_copy(got, target, local_sem.at[number * 2 + half])
            copy.start()
            local[number, half] = copy

    def stage_six(number):
        for half in (0, 1):
            copies[number, half, 4].wait_recv()
            piece = final_region(number, half, toggled(chip, 1 if half == 0 else 2))
            hop(number, half, 7, piece, piece, to_y if half == 0 else to_x)

    def stage_seven(number):
        w, t = chunks[number]
        kind, count, width = plan[w][:3]
        for half in (0, 1):
            copies[number, half, 5].wait_recv()
            copies[number, half, 7].wait_recv()
            local[number, half].wait()
        span = width if kind == "rows" else 4 * width
        at = core * count + t if kind == "rows" else core
        piece = sum_refs[w].at[:, pl.ds(pl.multiple_of(at * span, span), span)]
        slot = len(chunks) * 16 + number
        copies[number, 2, 0] = send(
            piece, piece, send_sem.at[slot], recv_sem.at[slot], to_core
        )

    written = []

    def write(number, source, target):
        copy = pltpu.make_async_copy(source, target, wide_sem.at[len(written)])
        copy.start()
        written.append(copy)

    def stage_eight(number):
        w, t = chunks[number]
        kind, count, width, deep, halves, parted = plan[w]
        copies[number, 2, 0].wait_recv()
        span = plan_span(plan[w])
        real, width = (parted or span, width if kind == "rows" else span)
        columns = min(width, real - t * width)
        starts = [(at * span + t * width, at * real + t * width) for at in (0, 1)]

        def each(i, carried):
            block = pl.ds(pl.multiple_of(16 * i, 16), 16)
            for source, target in starts:
                wide_refs[w][block, target : target + columns] = sum_refs[w][
                    block, source : source + columns
                ].astype(jnp.float32)
            return carried

        lax.fori_loop(0, deep // 16, each, 0)
        if real == span:
            for source, target in starts:
                place = pl.ds(target, columns)
                write(number, wide_refs[w].at[:, place], out_refs[w].at[:, place])
        elif t == count - 1:
            write(number, wide_refs[w], out_refs[w])

    small_copies = []

    def small_step(step):
        if step > 0:
            small_copies[step - 1].wait_recv()
            small_held[2 * step] = small_held[2 * step - 2] + small_held[2 * step - 1]
            if step == 3:
                small_out[0] = small_held[6]
        else:
            small_held[0] = small_ref[...]
        if step < 5:
            small_copies.append(
                send(
                    small_held.at[2 * step],
                    small_held.at[2 * step + 1],
                    small_send.at[step],
                    small_recv.at[step],
                    partners[step],
                )
            )
        else:
            small_out[1] = small_held[10]

    stages = (stage_one, stage_two, stage_three, stage_four, stage_five, stage_six, stage_seven)
    stages += (stage_eight,)
    small_at = 0
    stage_three(0)
    for w in range(len(late)):
        turn(w)
    for tick in range(len(chunks) + len(stages)):
        for lag, stage in enumerate(stages):
            for number in range(len(chunks)):
                start = number - 2 if number < early_count else number - early_count
                if start + lag == tick and (number >= early_count or (lag >= 2 and number + lag > 2)):
                    stage(number)
        if small_at < 6:
            small_step(small_at)
            small_at += 1
    for copy in written:
        copy.wait()
    for copy in pending:
        copy.wait_send()


def sum_weights(early, early_arrays, products, small):
    late = [weight_plan(*product) for product in products]
    lefts, rights = ([product[1] for product in products], [product[2] for product in products])
    plan = early + late
    pieces = []
    for w, (kind, count, width, deep, halves, parted) in enumerate(plan):
        leads = [(4, 2, 2), (4, 2), (4,), (2,), (1,)]
        if w < len(early):
            leads[:2] = [(4,), (4,)]
        for chunk in range(count):
            for half in halves:
                pieces += [pltpu.VMEM(lead + (half, width), jnp.bfloat16) for lead in leads]
    outs = [
        jax.ShapeDtypeStruct((entry[3], 2 * (entry[5] or plan_span(entry))), jnp.float32)
        for entry in plan
    ]
    chunk_count = sum(entry[1] for entry in plan)
    scratch = pair_scratch(late, lefts[0].shape[0]) + pieces
    dma = pltpu.SemaphoreType.DMA
    scratch += [pltpu.VMEM((entry[3], 2 * plan_span(entry)), jnp.bfloat16) for entry in plan]
    scratch += [pltpu.VMEM(out.shape, out.dtype) for out in outs]
    scratch += [pltpu.VMEM((11,) + small.shape, jnp.float32), dma((2 * chunk_count,))]
    slots = chunk_count * 17
    scratch += [dma((slots,)), dma((slots,)), dma((2 * chunk_count,)), dma((6 * chunk_count,))]
    scratch += [dma((2 * len(late),)), dma((2 * len(late),)), dma((5,)), dma((5,)), dma((len(late),))]
    vmem, anywhere = (
        pl.BlockSpec(memory_space=pltpu.VMEM),
        pl.BlockSpec(memory_space=pl.ANY),
    )
    return pl.pallas_call(
        functools.partial(sum_kernel, early, late, plan_lead(plan)),
        out_shape=tuple(outs) + (jax.ShapeDtypeStruct((2,) + small.shape, jnp.float32),),
        in_specs=[vmem] * len(late) + [anywhere] * (len(late) + len(early_arrays)) + [vmem],
        out_specs=(anywhere,) * len(plan) + (vmem,),
        scratch_shapes=scratch,
        compiler_params=pltpu.CompilerParams(
            collective_id=1, has_side_effects=True, vmem_limit_bytes=60 * 1024 * 1024
        ),
        name="sum_weights",
    )(*lefts, *rights, *early_arrays, small)


def layer_norm(rows_in, gain_vec):
    row_mean = jnp.mean(rows_in, axis=-1, keepdims=True)
    centred = rows_in - row_mean
    variance = jnp.mean(centred * centred, axis=-1, keepdims=True)
    return centred * lax.rsqrt(variance + norm_eps) * gain_vec


def rotate(projected, cosine, sine):
    row_count, width = projected.shape
    half_width = HEAD_WIDTH // 2
    by_head = projected.reshape(row_count, width // HEAD_WIDTH, HEAD_WIDTH)
    turned = jnp.concatenate([by_head[..., half_width:], by_head[..., :half_width]], axis=-1)
    return (by_head * cosine[:, None, :] - turned * sine[:, None, :]).reshape(row_count, width)


def swap(value, axis, bit):
    pairs = [(i, i ^ bit) for i in range(lax.axis_size(axis))]
    return lax.ppermute(value, axis, pairs)


def bit_of(axis, bit):
    return (lax.axis_index(axis) // bit) % 2 == 1


def bits_below(count):
    return [1 << i for i in range(count.bit_length() - 1)]


def reduce_pieces(pieces, labels, order):
    labels = list(labels)
    for axis, bit in order:
        at = labels.index((axis, bit))
        labels.pop(at)
        first = lax.index_in_dim(pieces, 0, at, keepdims=False)
        second = lax.index_in_dim(pieces, 1, at, keepdims=False)
        upper = bit_of(axis, bit)
        arrived = swap(jnp.where(upper, first, second), axis, bit)
        kept = jnp.where(upper, second, first)
        pieces = (kept.astype(jnp.float32) + arrived.astype(jnp.float32)).astype(jnp.bfloat16)
    return pieces


def gather_pieces(piece, labels, order):
    held = []
    for axis, bit in reversed(order):
        arrived = swap(piece, axis, bit)
        upper = bit_of(axis, bit)
        held = [label for label in labels if label in held or label == (axis, bit)]
        piece = jnp.stack(
            [jnp.where(upper, arrived, piece), jnp.where(upper, piece, arrived)],
            axis=held.index((axis, bit)),
        )
    return piece


def keep_and_send(first, second):
    upper = bit_of("ctx", 1)
    return (jnp.where(upper, second, first), jnp.where(upper, first, second))


def core_product(left, first, second):
    kept, sent = keep_and_send(first, second)
    left_all = jnp.concatenate([left, swap(left, "ctx", 1)], axis=0)
    right_all = jnp.concatenate([kept, swap(sent, "ctx", 1)], axis=0)
    return lax.dot_general(
        left_all, right_all, (((0,), (0,)), ((), ())), preferred_element_type=jnp.float32
    ).astype(jnp.bfloat16)


def shard_sum(product, by_columns):
    shards = lax.axis_size("fsdp")
    slices = lax.axis_size("ctx") // 2
    rows, columns = product.shape
    shard_labels = [("fsdp", bit) for bit in reversed(bits_below(shards))]
    slice_labels = [("ctx", 2 * bit) for bit in reversed(bits_below(slices))]
    if by_columns:
        cut = product.reshape(shards, rows // shards, slices, columns // slices)
        cut = jnp.transpose(cut, (0, 2, 1, 3))
    else:
        cut = product.reshape(shards, slices, rows // shards // slices, columns)
    parts = []
    half = cut.shape[2] // 2
    tail = list(reversed(shard_labels))
    for lead, orders in (
        (cut[:, :, :half], list(reversed(slice_labels))),
        (cut[:, :, half:], slice_labels),
    ):
        pieces = lead.reshape((2,) * (len(shard_labels) + len(slice_labels)) + lead.shape[2:])
        piece = reduce_pieces(pieces, shard_labels + slice_labels, orders + tail)
        whole = gather_pieces(piece, slice_labels, orders)
        parts.append(whole.reshape((slices,) + piece.shape))
    both = jnp.concatenate(parts, axis=1)
    if by_columns:
        return jnp.transpose(both, (1, 0, 2)).reshape(rows // shards, columns)
    return both.reshape(rows // shards, columns)


def join_cores(own):
    other = swap(own, "ctx", 1)
    upper = bit_of("ctx", 1)
    return jnp.concatenate(
        [jnp.where(upper, other, own), jnp.where(upper, own, other)], axis=1
    ).astype(jnp.float32)


def sum_over(value, axes):
    for axis in axes:
        for bit in bits_below(lax.axis_size(axis)):
            value = value + swap(value, axis, bit)
    return value


def own_shard(vector):
    width = vector.shape[0] // lax.axis_size("fsdp")
    return lax.dynamic_slice_in_dim(vector, lax.axis_index("fsdp") * width, width, 0)


def weight_sums(
    hidden,
    grad_mlp_low,
    act_mlp,
    grad_leading,
    grad_trailing,
    act_attn,
    grad_projected,
    attn_low,
    grad_attn_low,
    small,
    early,
):
    shards, ctx_count = (lax.axis_size("fsdp"), lax.axis_size("ctx"))
    rows, ff_width = hidden.shape
    model_width = act_mlp.shape[1]
    if early is None:
        half, half_three = (model_width // 2, 3 * model_width // 2)
        pairs = (
            (hidden, grad_mlp_low[:, :half], grad_mlp_low[:, half:]),
            (act_mlp, grad_leading, grad_trailing),
            (act_attn, grad_projected[:, :half_three], grad_projected[:, half_three:]),
            (attn_low, grad_attn_low[:, :half], grad_attn_low[:, half:]),
        )
        totals = [
            join_cores(shard_sum(core_product(*pair), at == 0)) for at, pair in enumerate(pairs)
        ]
        over_pack = sum_over(small, ("ctx",))
        return totals + [jnp.stack([over_pack, sum_over(over_pack, ("fsdp",))])]
    total_attn, total_in, total_out, total_qkv, small_sums = sum_weights(
        *early, [("rows", act_attn, grad_projected, 3)], small
    )
    return [total_out, total_in, total_qkv, total_attn, small_sums]


def weight_sums_early(
    hidden, grad_mlp_low, act_mlp, grad_leading, grad_trailing, attn_low, grad_attn_low, held
):
    shards, ctx_count = (lax.axis_size("fsdp"), lax.axis_size("ctx"))
    ff_width = hidden.shape[1]
    if shards != 4 or ctx_count != 8 or act_mlp.shape[1] % 1024 != 0 or ff_width % 64 != 0:
        return (held, None)
    return early_sums(
        [
            ("rows", attn_low, grad_attn_low, 1),
            ("rows", act_mlp, (grad_leading, grad_trailing), 3),
            ("columns", hidden, grad_mlp_low, 1),
        ],
        held,
    )


def per_device(
    inputs,
    cotangent,
    lengths,
    piece_route,
    gain_one,
    qkv_weight,
    attn_out,
    gain_two,
    geglu_in,
    geglu_out,
):
    ctx_count = lax.axis_size("ctx")
    own_index = lax.axis_index("ctx")
    row_count = inputs.shape[1]
    model_width = inputs.shape[2]
    piece_rows = row_count // ctx_count
    tokens = row_count * ctx_count
    own_heads = model_width // HEAD_WIDTH // ctx_count
    own_width = own_heads * HEAD_WIDTH
    block_q = math.gcd(tokens, 256)
    block_k = math.gcd(tokens, 512)
    lengths_row = lengths[0]
    own_route = piece_route[0, 0]
    slot_ids = jnp.arange(ctx_count, dtype=jnp.int32)
    outgoing = jnp.sum(
        slot_ids[None, :] * (own_route[None, :] == slot_ids[:, None]).astype(jnp.int32), axis=1
    )

    def exchange(blocks):
        return lax.all_to_all(blocks, "ctx", split_axis=0, concat_axis=0, tiled=True)

    def to_slots(rows_in):
        return jnp.take(rows_in.reshape(ctx_count, piece_rows, model_width), outgoing, axis=0)

    def to_heads(rows_in):
        by_heads = rows_in.reshape(row_count, ctx_count, -1)
        return exchange(jnp.transpose(by_heads, (1, 0, 2))).reshape(tokens, -1)

    def to_rows(heads_in):
        return exchange(heads_in.reshape(ctx_count, row_count, -1))

    both_arrived = exchange(
        jnp.concatenate([to_slots(inputs[0]), to_slots(cotangent[0])], axis=1)
    )
    arrived, grad_arrived = (both_arrived[:, :piece_rows], both_arrived[:, piece_rows:])
    residual = arrived.reshape(row_count, model_width).astype(jnp.float32)
    places = own_index * row_count + jnp.arange(row_count, dtype=jnp.int32)
    unused_begin, unused_end, offset, is_valid = spans(places, lengths_row)
    pack_begin, pack_end, unused_offset, unused_valid = spans(
        jnp.arange(tokens, dtype=jnp.int32), lengths_row
    )
    grad_final = jnp.where(
        is_valid[:, None], grad_arrived.reshape(row_count, model_width).astype(jnp.float32), 0.0
    )
    gains = jnp.pad(jnp.stack([gain_one, gain_two]), ((0, 14), (0, 0)))
    gains_full, qkv_full = gather_weights([gains, qkv_weight])
    gains_full = gains_full.reshape(-1, 16, gains.shape[1])
    gain_attn = gains_full[:, 0].reshape(-1).astype(jnp.float32)
    gain_mlp = gains_full[:, 1].reshape(-1).astype(jnp.float32)
    act_attn = layer_norm(residual, gain_attn).astype(jnp.bfloat16)
    later = [attn_out, geglu_in, geglu_out]
    row_cosine, row_sine = rotary_tables(offset, own_heads)
    if lax.axis_size("fsdp") == 4 and ctx_count == 8 and own_width == 128:
        attn_full, in_full, out_full, qkv_heads = gather_weights(
            later, (act_attn, qkv_full, row_cosine, row_sine)
        )
    else:
        attn_full, in_full, out_full = gather_weights(later)
        projected = jnp.dot(act_attn, qkv_full, preferred_element_type=jnp.float32)
        cosine, sine = rotary_tables(offset, 1)
        queries, keys = (
            rotate(projected[:, :model_width], cosine, sine).astype(jnp.bfloat16),
            rotate(projected[:, model_width : 2 * model_width], cosine, sine).astype(jnp.bfloat16),
        )
        values = projected[:, 2 * model_width :].astype(jnp.bfloat16)
        joined = jnp.stack(
            [part.reshape(row_count, ctx_count, own_width) for part in (queries, keys, values)], axis=2
        )
        qkv_heads = to_heads(joined.reshape(row_count, -1))
    low, high = key_range(pack_begin, pack_end, block_q, block_k)
    pack_begin, pack_end = (pack_begin[None, :], pack_end[None, :])
    attended_heads, attended_low, log_total = attention_forward(
        qkv_heads, pack_begin, pack_end, low, high, own_heads, block_q, block_k
    )
    attn_low = jnp.transpose(to_rows(attended_low), (1, 0, 2)).reshape(
        row_count, model_width
    )
    branch_attn = jnp.dot(attn_low, attn_full, preferred_element_type=jnp.float32)
    middle = residual + branch_attn
    act_mlp = layer_norm(middle, gain_mlp).astype(jnp.bfloat16)
    up_both = jnp.dot(act_mlp, in_full, preferred_element_type=jnp.float32)
    ff_width = up_both.shape[1] // 2
    hidden = (jax.nn.gelu(up_both[:, :ff_width], approximate=False) * up_both[:, ff_width:]).astype(
        jnp.bfloat16
    )
    branch_mlp = jnp.dot(hidden, out_full, preferred_element_type=jnp.float32)
    final_rows = jnp.where(is_valid[:, None], middle + branch_mlp, 0.0)
    square_sums = jnp.stack(
        [
            jnp.sum(final_rows * final_rows),
            jnp.sum(jnp.where(is_valid[:, None], branch_attn * branch_attn, 0.0)),
            jnp.sum(jnp.where(is_valid[:, None], branch_mlp * branch_mlp, 0.0)),
        ]
    )
    out_slots = final_rows.astype(jnp.bfloat16).reshape(ctx_count, piece_rows, model_width)
    grad_mlp_low = grad_final.astype(jnp.bfloat16)
    grad_hidden = lax.dot_general(
        grad_mlp_low, out_full, NT, preferred_element_type=jnp.float32
    )

    def gated(leading, trailing):
        return jax.nn.gelu(leading, approximate=False) * trailing

    unused_gate, gate_back = jax.vjp(gated, up_both[:, :ff_width], up_both[:, ff_width:])
    grad_leading, grad_trailing = gate_back(grad_hidden)
    grad_leading, grad_trailing = (
        grad_leading.astype(jnp.bfloat16),
        grad_trailing.astype(jnp.bfloat16),
    )
    grad_up = jnp.concatenate([grad_leading, grad_trailing], axis=1)
    grad_act_mlp = lax.dot_general(grad_up, in_full, NT, preferred_element_type=jnp.float32)
    unused_norm, norm_back_mlp = jax.vjp(layer_norm, middle, gain_mlp)
    grad_middle_norm, grad_gain_mlp = norm_back_mlp(grad_act_mlp)
    grad_middle = grad_final + grad_middle_norm
    grad_attn_low = grad_middle.astype(jnp.bfloat16)
    grad_attended = lax.dot_general(
        grad_attn_low, attn_full, NT, preferred_element_type=jnp.float32
    ).astype(jnp.bfloat16)
    grad_attended_heads, early = weight_sums_early(
        hidden,
        grad_mlp_low,
        act_mlp,
        grad_leading,
        grad_trailing,
        attn_low,
        grad_attn_low,
        to_heads(grad_attended),
    )
    block_back = math.gcd(tokens, 256)
    low_back, high_back = key_range(pack_begin[0], pack_end[0], block_q, block_back)
    grad_heads = attention_backward(
        qkv_heads,
        attended_heads,
        grad_attended_heads,
        log_total,
        pack_begin,
        pack_end,
        low_back,
        high_back,
        [] if early is None else [early[1][0][0]],
        own_heads,
        block_q,
        block_back,
    )
    if early is not None:
        grad_heads, early = second_step(grad_heads, early)
    grad_rows = to_rows(grad_heads)
    if own_width % 128 == 0:
        grad_projected, grad_act_attn = finish_rows(
            grad_rows, row_cosine, row_sine, qkv_full, own_heads
        )
    else:
        by_part = jnp.transpose(
            grad_rows.reshape(ctx_count, row_count, 3, own_width), (2, 1, 0, 3)
        ).reshape(3, row_count, model_width)
        cosine, sine = rotary_tables(offset, 1)
        grad_projected = jnp.concatenate(
            [
                rotate(by_part[part].astype(jnp.float32), cosine, -sine).astype(jnp.bfloat16)
                for part in (0, 1)
            ]
            + [by_part[2]],
            axis=1,
        )
        grad_act_attn = lax.dot_general(
            grad_projected, qkv_full, NT, preferred_element_type=jnp.float32
        )
    unused_first, norm_back_attn = jax.vjp(layer_norm, residual, gain_attn)
    grad_resid_norm, grad_gain_attn = norm_back_attn(grad_act_attn)
    grad_residual = (grad_middle + grad_resid_norm).astype(jnp.bfloat16)
    grad_slots = grad_residual.reshape(ctx_count, piece_rows, model_width)
    back = exchange(jnp.concatenate([out_slots, grad_slots], axis=1))
    block_out, grad_inputs = (
        jnp.take(half, own_route, axis=0).reshape(1, row_count, model_width)
        for half in (back[:, :piece_rows], back[:, piece_rows:])
    )
    small = jnp.stack(
        [grad_gain_attn, grad_gain_mlp, jnp.pad(square_sums, (0, model_width - 3))]
        + [jnp.zeros((model_width,), jnp.float32)] * 5
    )
    total_out, total_in, total_qkv, total_attn, small_sums = weight_sums(
        hidden,
        grad_mlp_low,
        act_mlp,
        grad_leading,
        grad_trailing,
        act_attn,
        grad_projected,
        attn_low,
        grad_attn_low,
        small,
        early,
    )
    total_gain_one = own_shard(small_sums[1, 0])
    total_gain_two = own_shard(small_sums[1, 1])
    total_squares = small_sums[0, 2, :3]
    valid_count = jnp.sum(lengths_row).astype(jnp.float32)
    rms_stats = jnp.sqrt(total_squares / (valid_count * model_width))[None, :]
    return (
        block_out,
        grad_inputs,
        total_gain_one,
        total_qkv,
        total_attn,
        total_gain_two,
        total_in,
        total_out,
        rms_stats,
    )


def solution(mesh):
    placed = (
        P("fsdp", "ctx", None),
        P("fsdp", "ctx", None),
        P("fsdp", None),
        P("fsdp", "ctx", None),
        P("fsdp"),
        P("fsdp", None),
        P("fsdp", None),
        P("fsdp"),
        P("fsdp", None),
        P("fsdp", None),
    )
    return jax.shard_map(
        per_device,
        mesh=mesh,
        in_specs=placed,
        out_specs=(
            P("fsdp", "ctx", None),
            P("fsdp", "ctx", None),
            P("fsdp"),
            P("fsdp", None),
            P("fsdp", None),
            P("fsdp"),
            P("fsdp", None),
            P("fsdp", None),
            P("fsdp", None),
        ),
        check_vma=False,
    )
```

```python
import functools
import math
import jax
import jax.numpy as jnp
from jax import lax
from jax.experimental import pallas as pl
from jax.experimental.pallas import tpu as pltpu
from jax.sharding import PartitionSpec as P

HEAD_WIDTH = 64
norm_eps = 1e-05
masked_score = -1e30


def head_stack(rows_in, head_count):
    if head_count == 1:
        return rows_in
    lane_head = lax.broadcasted_iota(jnp.int32, rows_in.shape, 1) // HEAD_WIDTH
    zero = jnp.zeros_like(rows_in)
    return jnp.concatenate(
        [jnp.where(lane_head == h, rows_in, zero) for h in range(head_count)], axis=0
    )


def head_pick(stacked_t, head_count, block):
    return jnp.concatenate(
        [
            stacked_t[h * HEAD_WIDTH : (h + 1) * HEAD_WIDTH, h * block : (h + 1) * block]
            for h in range(head_count)
        ],
        axis=0,
    ).T


NT = (((1,), (1,)), ((), ()))


def forward_kernel(
    head_count, block_q, block_k, low_ref, high_ref, begin_ref, end_ref, qkv_ref, out_ref, low_out_ref, log_ref, turned_ref
):
    width = out_ref.shape[1]
    step = pl.program_id(0)

    @pl.when(step == 0)
    def prepare():
        turned_ref[...] = qkv_ref[:, 2 * width :].astype(jnp.float32).T.astype(jnp.bfloat16)

    rows = pl.ds(pl.multiple_of(step * block_q, block_q), block_q)
    scale = 1.0 / math.sqrt(HEAD_WIDTH)
    stacked = head_stack(qkv_ref[rows, :width] * jnp.asarray(scale, jnp.bfloat16), head_count)
    begin = jnp.concatenate([begin_ref[:, rows]] * head_count, axis=1)
    end = jnp.concatenate([end_ref[:, rows]] * head_count, axis=1)

    def body(index, carried):
        top, total, acc = carried
        first = pl.multiple_of(index * block_k, block_k)
        keys = qkv_ref[pl.ds(first, block_k), width : 2 * width]
        scores = lax.dot_general(keys, stacked, NT, preferred_element_type=jnp.float32)
        place = first + lax.broadcasted_iota(jnp.int32, scores.shape, 0)
        scores = jnp.where((place >= begin) & (place < end), scores, masked_score)
        new_top = jnp.maximum(top, jnp.max(scores, axis=0, keepdims=True))
        fresh = jnp.exp(scores - new_top)
        fade = jnp.exp(top - new_top)
        total = total * fade + jnp.sum(fresh, axis=0, keepdims=True)
        acc = acc * fade + jnp.dot(
            turned_ref[:, pl.ds(first, block_k)],
            fresh.astype(jnp.bfloat16),
            preferred_element_type=jnp.float32,
        )
        return (new_top, total, acc)

    lanes = head_count * block_q
    top, total, acc = lax.fori_loop(
        low_ref[step],
        high_ref[step],
        body,
        (
            jnp.full((1, lanes), masked_score, jnp.float32),
            jnp.zeros((1, lanes), jnp.float32),
            jnp.zeros((width, lanes), jnp.float32),
        ),
    )
    valid = end > begin
    safe = jnp.where(valid, total, 1.0)
    acc = jnp.where(valid, acc / safe, 0.0)
    log_total = jnp.where(valid, top + jnp.log(safe), 0.0)
    attended = head_pick(acc, head_count, block_q)
    out_ref[...] = attended
    low_out_ref[...] = attended.astype(jnp.bfloat16)
    log_ref[0] = log_total


def attention_forward(qkv, begin, end, low, high, head_count, block_q, block_k):
    tokens = qkv.shape[0]
    width = head_count * HEAD_WIDTH
    steps = tokens // block_q
    whole = lambda shape: pl.BlockSpec(shape, lambda i, *_: (0,) * len(shape))
    pairs = tokens * tokens // 4 * head_count
    return pl.pallas_call(
        functools.partial(forward_kernel, head_count, block_q, block_k),
        out_shape=(
            jax.ShapeDtypeStruct((tokens, width), jnp.float32),
            jax.ShapeDtypeStruct((tokens, width), jnp.bfloat16),
            jax.ShapeDtypeStruct((steps, 1, head_count * block_q), jnp.float32),
        ),
        grid_spec=pltpu.PrefetchScalarGridSpec(
            num_scalar_prefetch=2,
            grid=(steps,),
            in_specs=[whole((1, tokens)), whole((1, tokens)), whole((tokens, 3 * width))],
            out_specs=(
                pl.BlockSpec((block_q, width), lambda i, *_: (i, 0)),
                pl.BlockSpec((block_q, width), lambda i, *_: (i, 0)),
                pl.BlockSpec((1, 1, head_count * block_q), lambda i, *_: (i, 0, 0)),
            ),
            scratch_shapes=[pltpu.VMEM((width, tokens), jnp.bfloat16)],
        ),
        cost_estimate=pl.CostEstimate(
            flops=pairs * 512, bytes_accessed=tokens * width * 12, transcendentals=pairs
        ),
        name="attention_forward",
    )(low, high, begin, end, qkv)


def turn_back(grads, cosine, sine, head_count):
    half = HEAD_WIDTH // 2
    pieces = []
    for h in range(head_count):
        base = h * HEAD_WIDTH
        pieces += [grads[:, base + half : base + HEAD_WIDTH], grads[:, base : base + half]]
    return grads * cosine + jnp.concatenate(pieces, axis=1) * sine


def backward_kernel(
    head_count,
    block_q,
    block_k,
    low_ref,
    high_ref,
    begin_ref,
    end_ref,
    qkv_ref,
    attended_ref,
    grad_ref,
    log_ref,
    *refs,
):
    out_ref, turned_ref, key_acc, value_acc = refs[-4:]
    width = attended_ref.shape[1]
    step = pl.program_id(0)

    @pl.when(step == 0)
    def prepare():
        turned_ref[...] = qkv_ref[:, width : 2 * width].astype(jnp.float32).T.astype(jnp.bfloat16)
        key_acc[...] = jnp.zeros_like(key_acc)
        value_acc[...] = jnp.zeros_like(value_acc)

    rows = pl.ds(pl.multiple_of(step * block_q, block_q), block_q)
    scale = 1.0 / math.sqrt(HEAD_WIDTH)
    stacked = head_stack(qkv_ref[rows, :width] * jnp.asarray(scale, jnp.bfloat16), head_count)
    grads = grad_ref[rows, :]
    grad_stacked = head_stack(grads, head_count)
    begin = jnp.concatenate([begin_ref[:, rows]] * head_count, axis=1)
    end = jnp.concatenate([end_ref[:, rows]] * head_count, axis=1)
    product = (grads.astype(jnp.float32) * attended_ref[rows, :]).T
    delta = jnp.concatenate(
        [
            jnp.sum(product[h * HEAD_WIDTH : (h + 1) * HEAD_WIDTH], axis=0, keepdims=True)
            for h in range(head_count)
        ],
        axis=1,
    )
    log_total = log_ref[0]

    def body(index, acc):
        first = pl.multiple_of(index * block_k, block_k)
        span = pl.ds(first, block_k)
        keys = qkv_ref[span, width : 2 * width]
        values = qkv_ref[span, 2 * width :]
        scores = lax.dot_general(keys, stacked, NT, preferred_element_type=jnp.float32)
        grad_probs = lax.dot_general(values, grad_stacked, NT, preferred_element_type=jnp.float32)
        place = first + lax.broadcasted_iota(jnp.int32, scores.shape, 0)
        scores = jnp.where((place >= begin) & (place < end), scores, masked_score)
        probs = jnp.exp(scores - log_total)
        grad_scores = (probs * (grad_probs - delta)).astype(jnp.bfloat16)
        value_acc[span, :] += jnp.dot(
            probs.astype(jnp.bfloat16), grad_stacked, preferred_element_type=jnp.float32
        )
        key_acc[span, :] += jnp.dot(grad_scores, stacked, preferred_element_type=jnp.float32)
        return acc + jnp.dot(
            turned_ref[:, span], grad_scores, preferred_element_type=jnp.float32
        )

    acc = lax.fori_loop(
        low_ref[step],
        high_ref[step],
        body,
        jnp.zeros((width, head_count * block_q), jnp.float32),
    )
    grad_queries = head_pick(acc, head_count, block_q) * scale
    out_ref[rows, :width] = grad_queries.astype(jnp.bfloat16)

    @pl.when(step == pl.num_programs(0) - 1)
    def finish():
        @pl.loop(0, pl.num_programs(0))
        def each(index):
            span = pl.ds(pl.multiple_of(index * block_q, block_q), block_q)
            out_ref[span, width : 2 * width] = key_acc[span, :].astype(jnp.bfloat16)
            out_ref[span, 2 * width :] = value_acc[span, :].astype(jnp.bfloat16)


def attention_backward(
    qkv, attended, grads, log_total, begin, end, low, high, after, head_count, block_q, block_k
):
    tokens = qkv.shape[0]
    width = head_count * HEAD_WIDTH
    steps = tokens // block_q
    whole = lambda shape: pl.BlockSpec(shape, lambda i, *_: (0,) * len(shape))
    pairs = tokens * tokens // 4 * head_count
    return pl.pallas_call(
        functools.partial(backward_kernel, head_count, block_q, block_k),
        out_shape=jax.ShapeDtypeStruct((tokens, 3 * width), jnp.bfloat16),
        grid_spec=pltpu.PrefetchScalarGridSpec(
            num_scalar_prefetch=2,
            grid=(steps,),
            in_specs=[
                whole((1, tokens)),
                whole((1, tokens)),
                whole((tokens, 3 * width)),
                whole((tokens, width)),
                whole((tokens, width)),
                pl.BlockSpec((1, 1, head_count * block_q), lambda i, *_: (i, 0, 0)),
            ]
            + [pl.BlockSpec(memory_space=pl.ANY)] * len(after),
            out_specs=whole((tokens, 3 * width)),
            scratch_shapes=[
                pltpu.VMEM((width, tokens), jnp.bfloat16),
                pltpu.VMEM((tokens, width), jnp.float32),
                pltpu.VMEM((tokens, width), jnp.float32),
            ],
        ),
        cost_estimate=pl.CostEstimate(
            flops=pairs * 1280, bytes_accessed=tokens * width * 30, transcendentals=pairs
        ),
        name="attention_backward",
    )(low, high, begin, end, qkv, attended, grads, log_total, *after)


def rows_kernel(head_count, heads_ref, cosine_ref, sine_ref, query_ref, key_ref, value_ref, out_ref, act_ref):
    width = heads_ref.shape[2] // 3
    step = pl.program_id(0)
    total = out_ref.shape[1] // 3
    owners = heads_ref.shape[0]
    pieces = []
    for part in range(3):
        for owner in range(owners):
            piece = heads_ref[owner, :, part * width : (part + 1) * width]
            if part < 2:
                piece = turn_back(
                    piece.astype(jnp.float32), cosine_ref[...], sine_ref[...], head_count
                ).astype(jnp.bfloat16)
            first = pl.multiple_of(part * total + (step * owners + owner) * width, width)
            out_ref[:, pl.ds(first, width)] = piece
            pieces.append(piece)
    weights = jnp.concatenate([query_ref[...], key_ref[...], value_ref[...]], axis=1)
    product = lax.dot_general(
        jnp.concatenate(pieces, axis=1), weights, NT, preferred_element_type=jnp.float32
    )

    @pl.when(step == 0)
    def begin():
        act_ref[...] = product

    @pl.when(step > 0)
    def add():
        act_ref[...] += product


def finish_rows(heads, cosine, sine, qkv_full, head_count):
    owners, rows, columns = heads.shape
    width = columns // 3
    depth = qkv_full.shape[0]
    whole = lambda shape: pl.BlockSpec(shape, lambda i: (0,) * len(shape))
    steps = owners // 2
    part_of = lambda part: pl.BlockSpec((depth, 2 * width), lambda i: (0, part * steps + i))
    return pl.pallas_call(
        functools.partial(rows_kernel, head_count),
        out_shape=(
            jax.ShapeDtypeStruct((rows, owners * columns), jnp.bfloat16),
            jax.ShapeDtypeStruct((rows, depth), jnp.float32),
        ),
        grid=(steps,),
        in_specs=[
            pl.BlockSpec((2, rows, columns), lambda i: (i, 0, 0)),
            whole((rows, width)),
            whole((rows, width)),
            part_of(0),
            part_of(1),
            part_of(2),
        ],
        out_specs=(whole((rows, owners * columns)), whole((rows, depth))),
        cost_estimate=pl.CostEstimate(
            flops=2 * rows * depth * owners * columns,
            bytes_accessed=2 * depth * owners * columns + 4 * rows * owners * columns,
            transcendentals=0,
        ),
        name="finish_rows",
    )(heads, cosine, sine, qkv_full, qkv_full, qkv_full)


def spans(places, lengths_row):
    ends = jnp.cumsum(lengths_row)
    past = (places[:, None] >= ends[None, :]).astype(jnp.int32)
    begin = jnp.sum(past * lengths_row[None, :], axis=1)
    before = (places[:, None] >= (ends - lengths_row)[None, :]).astype(jnp.int32)
    end = jnp.sum(before * lengths_row[None, :], axis=1)
    valid = places < ends[-1]
    return (jnp.where(valid, begin, 0), jnp.where(valid, end, 0), places - begin, valid)


def key_range(begin, end, block_q, block_k):
    begin_blocks = jnp.where(end > begin, begin, jnp.int32(1 << 30)).reshape(-1, block_q)
    high = (jnp.max(end.reshape(-1, block_q), axis=1) + block_k - 1) // block_k
    low = jnp.minimum(jnp.min(begin_blocks, axis=1) // block_k, high)
    return (low, high)


def rotary_tables(offset, head_count):
    half = HEAD_WIDTH // 2
    inverse = 160000.0 ** (-2.0 * jnp.arange(half, dtype=jnp.float32) / HEAD_WIDTH)
    angles = offset.astype(jnp.float32)[:, None] * inverse[None, :]
    cosine, sine = (jnp.cos(angles), jnp.sin(angles))
    return (
        jnp.concatenate([cosine, cosine] * head_count, axis=1),
        jnp.concatenate([sine, -sine] * head_count, axis=1),
    )


def toggled(index, bit):
    return index + bit - 2 * bit * ((index // bit) % 2)


def gather_kernel(shapes, projects, *refs):
    count = len(shapes)
    shard_refs, refs = (refs[:count], refs[count:])
    if projects:
        act_ref, qkv_ref, cosine_ref, sine_ref = refs[:4]
        heads_ref = refs[4 + count]
        columns_ref, held_ref, load_sem, head_send, head_recv, own_sem = refs[count + 8 :]
        refs = refs[4 : 4 + count] + refs[count + 5 : count + 8]
    full_refs = refs[:count]
    send_sem, recv_sem, local_sem = refs[count:]
    shards = lax.axis_size("fsdp")
    slices = lax.axis_size("ctx") // 2
    own_ctx, own_shard = (lax.axis_index("ctx"), lax.axis_index("fsdp"))
    core, chip = (own_ctx % 2, own_ctx // 2)
    barrier = pltpu.get_barrier_semaphore()
    partners = [{"fsdp": toggled(own_shard, bit)} for bit in (1, 2)]
    partners += [{"ctx": toggled(own_ctx, bit)} for bit in (1, 2, 4)]

    def owner_at(relation):
        owner = own_ctx
        for bit in (1, 2, 4):
            if relation & bit:
                owner = toggled(owner, bit)
        return owner

    if projects:
        partners += [{"ctx": owner_at(relation)} for relation in (3, 5, 6, 7)]
    for partner in partners:
        pl.semaphore_signal(
            barrier, inc=1, device_id=partner, device_id_type=pl.DeviceIdType.MESH
        )
    pl.semaphore_wait(barrier, len(partners))
    to_one, to_two, to_core, to_x, to_y = partners[:5]

    def shard_at(step):
        if step == 0:
            return own_shard
        if step == 3:
            return toggled(toggled(own_shard, 1), 2)
        return toggled(own_shard, step)

    def region(ref, weight, step, chip_at, half):
        if shapes[weight] == "small":
            return ref if len(ref.shape) == 2 else ref.at[shard_at(step)]
        if shapes[weight] == "rows":
            rows = ref.shape[-2]
            span = pl.ds(0, rows) if half is None else pl.ds(half * (rows // 2), rows // 2)
            if len(ref.shape) == 4:
                return ref.at[core, chip_at, span, :]
            return ref.at[shard_at(step), core, chip_at, span, :]
        rows = ref.shape[-2]
        first = (rows // 2) // 16 * 16
        spans_of = {None: pl.ds(0, rows), 0: pl.ds(0, first), 1: pl.ds(first, rows - first)}
        width = ref.shape[-1] // (2 * slices)
        columns = pl.ds(pl.multiple_of((core * slices + chip_at) * width, width), width)
        if len(ref.shape) == 2:
            return ref.at[spans_of[half], columns]
        return ref.at[shard_at(step), spans_of[half], columns]

    def core_region(ref, weight, step):
        if shapes[weight] == "rows":
            return ref.at[shard_at(step), core]
        width = ref.shape[-1] // 2
        return ref.at[shard_at(step), :, pl.ds(pl.multiple_of(core * width, width), width)]

    pending = []

    def send(source, target, slot, partner):
        copy = pltpu.make_async_remote_copy(
            src_ref=source,
            dst_ref=target,
            send_sem=send_sem.at[slot],
            recv_sem=recv_sem.at[slot],
            device_id=partner,
            device_id_type=pl.DeviceIdType.MESH,
        )
        copy.start()
        pending.append(copy)
        return copy

    copies = {}
    local = []

    def slot_of(weight, step, kind):
        return (weight * 3 + step - 1) * 8 + kind

    def shard_sends(weight):
        source = region(shard_refs[weight], weight, 0, chip, None)
        target = region(full_refs[weight], weight, 0, chip, None)
        copies[weight, 2, 0] = send(source, target, slot_of(weight, 2, 0), to_two)
        copies[weight, 1, 0] = send(source, target, slot_of(weight, 1, 0), to_one)
        target = full_refs[weight].at[own_shard]
        copy = pltpu.make_async_copy(shard_refs[weight], target, local_sem.at[weight])
        copy.start()
        local.append(copy)

    def shard_forward(weight):
        copies[weight, 2, 0].wait_recv()
        piece = region(full_refs[weight], weight, 2, chip, None)
        copies[weight, 3, 0] = send(piece, piece, slot_of(weight, 3, 0), to_one)

    def plane_sends(weight, step):
        lead = region(full_refs[weight], weight, step, chip, 0)
        rest = region(full_refs[weight], weight, step, chip, 1)
        for kind, piece, partner in ((1, lead, to_x), (2, rest, to_y), (3, lead, to_y), (4, rest, to_x)):
            copies[weight, step, kind] = send(piece, piece, slot_of(weight, step, kind), partner)

    def plane_forward(weight, step):
        copies[weight, step, 1].wait_recv()
        lead = region(full_refs[weight], weight, step, toggled(chip, 1), 0)
        copies[weight, step, 5] = send(lead, lead, slot_of(weight, step, 5), to_y)
        copies[weight, step, 2].wait_recv()
        rest = region(full_refs[weight], weight, step, toggled(chip, 2), 1)
        copies[weight, step, 6] = send(rest, rest, slot_of(weight, step, 6), to_x)

    def core_send(weight, step):
        for kind in (3, 4, 5, 6):
            copies[weight, step, kind].wait_recv()
        piece = core_region(full_refs[weight], weight, step)
        copies[weight, step, 7] = send(piece, piece, slot_of(weight, step, 7), to_core)

    chip_order = (3, 1, 2, 0)

    def start_loads():
        loads = {}
        for chip_bits in chip_order:
            owner_chip = owner_at(2 * chip_bits) // 2
            for part in range(3):
                width = columns_ref.shape[2] // 3
                total = qkv_ref.shape[1] // 3
                first = pl.multiple_of(part * total + owner_chip * width, width)
                loads[chip_bits, part] = pltpu.make_async_copy(
                    qkv_ref.at[:, pl.ds(first, width)],
                    columns_ref.at[chip_bits, :, pl.ds(part * width, width)],
                    load_sem.at[chip_bits * 3 + part],
                )
                loads[chip_bits, part].start()
        return loads

    def project(chip_bits, loads):
        for part in range(3):
            loads[chip_bits, part].wait()
        rows, own_width = (act_ref.shape[0], held_ref.shape[2] // 3)
        product = jnp.dot(
            act_ref[...], columns_ref[chip_bits], preferred_element_type=jnp.float32
        )
        for core_at in (0, 1):
            slot = 2 * chip_bits + core + core_at - 2 * core * core_at
            for part in range(3):
                first = (2 * part + core_at) * own_width
                piece = product[:, first : first + own_width]
                if part < 2:
                    half = HEAD_WIDTH // 2
                    turned = []
                    for base in range(0, own_width, HEAD_WIDTH):
                        turned += [piece[:, base + half : base + HEAD_WIDTH], piece[:, base : base + half]]
                    piece = piece * cosine_ref[...] - jnp.concatenate(turned, axis=1) * sine_ref[...]
                held_ref[slot, :, part * own_width : (part + 1) * own_width] = piece.astype(jnp.bfloat16)
        target = heads_ref.at[pl.ds(pl.multiple_of(own_ctx * rows, rows), rows), :]
        for core_bit in (0, 1):
            relation = 2 * chip_bits + core_bit
            if relation == 0:
                copy = pltpu.make_async_copy(held_ref.at[0], target, own_sem.at[0])
                copy.start()
                local.append(copy)
                continue
            copy = pltpu.make_async_remote_copy(
                src_ref=held_ref.at[relation],
                dst_ref=target,
                send_sem=head_send.at[relation],
                recv_sem=head_recv.at[relation],
                device_id={"ctx": owner_at(relation)},
                device_id_type=pl.DeviceIdType.MESH,
            )
            copy.start()
            pending.append(copy)
            arriving.append(copy)

    arriving = []
    sent = 1
    if projects:
        loads = start_loads()
        for weight in range(count):
            shard_sends(weight)
        sent = count
        for chip_bits in chip_order:
            project(chip_bits, loads)
    else:
        shard_sends(0)
    for weight in range(count):
        if weight + 1 >= sent and weight + 1 < count:
            shard_sends(weight + 1)
        shard_forward(weight)
        copies[weight, 1, 0].wait_recv()
        if shapes[weight] == "small":
            copies[weight, 3, 0].wait_recv()
            continue
        plane_sends(weight, 1)
        plane_sends(weight, 2)
        copies[weight, 3, 0].wait_recv()
        plane_sends(weight, 3)
        for step in (1, 2, 3):
            plane_forward(weight, step)
        if weight > 0 and shapes[weight - 1] != "small":
            for step in (1, 2, 3):
                core_send(weight - 1, step)
    for step in (1, 2, 3):
        core_send(count - 1, step)
    for weight in range(count):
        if shapes[weight] != "small":
            for step in (1, 2, 3):
                copies[weight, step, 7].wait_recv()
    for copy in arriving:
        copy.wait_recv()
    for copy in pending:
        copy.wait_send()
    for copy in local:
        copy.wait()


def gather_weights(weights, projection=None):
    shards, ctx_count = (lax.axis_size("fsdp"), lax.axis_size("ctx"))
    slices = ctx_count // 2
    shapes, views, outs = ([], [], [])
    for weight in weights:
        rows, columns = weight.shape
        if rows % (32 * ctx_count) == 0:
            shapes.append("rows")
            views.append(weight.reshape(2, slices, rows // ctx_count, columns))
            outs.append((shards, 2, slices, rows // ctx_count, columns))
        elif rows == 16:
            shapes.append("small")
            views.append(weight)
            outs.append((shards, rows, columns))
        elif columns % (128 * ctx_count) == 0 and rows % 16 == 0:
            shapes.append("columns")
            views.append(weight)
            outs.append((shards, rows, columns))
    if shards != 4 or ctx_count != 8 or len(views) < len(weights):
        return [lax.all_gather(weight, "fsdp", axis=0, tiled=True) for weight in weights]
    slots = len(views) * 24
    vmem, anywhere, dma = (
        pl.BlockSpec(memory_space=pltpu.VMEM),
        pl.BlockSpec(memory_space=pl.ANY),
        pltpu.SemaphoreType.DMA,
    )
    in_specs = [vmem] * len(views)
    scratch = [dma((slots,)), dma((slots,)), dma((len(views),))]
    if projection is not None:
        act_attn, qkv_full = projection[:2]
        rows, own_columns = (act_attn.shape[0], qkv_full.shape[1] // ctx_count)
        views += list(projection)
        in_specs += [vmem, anywhere, vmem, vmem]
        outs.append((ctx_count * rows, own_columns))
        scratch += [
            pltpu.VMEM((slices, qkv_full.shape[0], 2 * own_columns), jnp.bfloat16),
            pltpu.VMEM((ctx_count, rows, own_columns), jnp.bfloat16),
            dma((3 * slices,)),
            dma((ctx_count,)),
            dma((ctx_count,)),
            dma((1,)),
        ]
    held = pl.pallas_call(
        functools.partial(gather_kernel, shapes, projection is not None),
        out_shape=tuple(jax.ShapeDtypeStruct(out, jnp.bfloat16) for out in outs),
        in_specs=in_specs,
        out_specs=tuple(anywhere for out in outs),
        scratch_shapes=scratch,
        compiler_params=pltpu.CompilerParams(
            collective_id=0 if projection is None else 2,
            has_side_effects=True,
            vmem_limit_bytes=60 * 1024 * 1024,
        ),
        name="gather_weights" if projection is None else "gather_and_project",
    )(*views)
    return [whole.reshape(-1, whole.shape[-1]) for whole in held]


def pair_steps(plan, lead_rows, left_refs, right_refs, turned_refs, whole_refs, sems, core, pending, send):
    pair_send, pair_recv, near_sem = sems
    to_core = {"ctx": toggled(lax.axis_index("ctx"), 1)}

    def send_core(source, target, sent, got, start=True):
        return send(source, target, sent, got, to_core, start)

    rows = left_refs[0].shape[0] if left_refs else 0
    pairs = []

    def begin(w):
        entry = plan[w]
        span, right = (plan_span(entry), right_refs[w])
        own_part, other_part = (whole_refs[w].at[pl.ds(0, rows)], whole_refs[w].at[pl.ds(rows, rows)])

        def exchange(own_half, other_half, start=True):
            near = pltpu.make_async_copy(own_half, own_part, near_sem.at[w])
            if start:
                near.start()
            sems = (pair_send.at[2 * w], pair_recv.at[2 * w])
            return [near, send_core(other_half, other_part, *sems, start)]

        if entry[5]:
            ways = [exchange(right[at], right[1 - at], False) for at in (0, 1)]
            for at in (0, 1):

                @pl.when(core == at)
                def start():
                    for copy in ways[at]:
                        copy.start()

            pairs.append(ways[0])
            pending.append(ways[0][1])
        else:
            halves = [
                right.at[:, pl.ds(pl.multiple_of(at * span, span), span)] for at in (core, 1 - core)
            ]
            pairs.append(exchange(*halves))

    def turn(w):
        left, turned = (left_refs[w], turned_refs[w])
        block = 512
        for first in range(0, left.shape[1], block):
            last = min(first + block, left.shape[1])
            turned[first:last, :rows] = (
                left[:, first:last].astype(jnp.float32).T.astype(jnp.bfloat16)
            )
        pairs[w].append(
            send_core(
                turned.at[:, pl.ds(0, rows)],
                turned.at[:, pl.ds(rows, rows)],
                pair_send.at[2 * w + 1],
                pair_recv.at[2 * w + 1],
            )
        )

    def multiply(w, t, first, second):
        kind, count, width, deep, halves, parted = plan[w]
        if t == 0:
            near, far, turned = pairs[w]
            near.wait()
            far.wait_recv()
            turned.wait_recv()

        def each(z, carried):
            left = turned_refs[w][pl.ds(pl.multiple_of(z * deep, 16), deep), :]
            if kind == "rows":
                last = min((t + 1) * width, whole_refs[w].shape[1])
                part = jnp.dot(
                    left, whole_refs[w][:, t * width : last], preferred_element_type=jnp.float32
                ).astype(jnp.bfloat16)
                if last < (t + 1) * width:
                    empty = jnp.zeros((deep, (t + 1) * width - last), jnp.bfloat16)
                    part = jnp.concatenate([part, empty], axis=1)
                piece_rows = first.shape[3]
                for s in range(4):
                    first[z, s // 2, s % 2] = part[2 * s * piece_rows : (2 * s + 1) * piece_rows]
                    second[z, s // 2, s % 2] = part[(2 * s + 1) * piece_rows : (2 * s + 2) * piece_rows]
            else:
                part = jnp.dot(
                    left, whole_refs[w][...], preferred_element_type=jnp.float32
                ).astype(jnp.bfloat16)
                for s in range(4):
                    piece = part[:, s * width : (s + 1) * width]
                    first[z, s // 2, s % 2] = piece[:lead_rows]
                    second[z, s // 2, s % 2] = piece[lead_rows:]
            return carried

        lax.fori_loop(0, 4, each, 0)

    return (begin, turn, multiply)


def remote_send(pending):
    def send(source, target, sent, got, partner, start=True):
        copy = pltpu.make_async_remote_copy(
            src_ref=source,
            dst_ref=target,
            send_sem=sent,
            recv_sem=got,
            device_id=partner,
            device_id_type=pl.DeviceIdType.MESH,
        )
        if start:
            copy.start()
            pending.append(copy)
        return copy

    return send


def product_kernel(plan, lead_rows, *refs):
    groups, places = early_places(plan)
    weights, outs = (len(plan), 4 * len(groups))
    left_refs, refs = (refs[:weights], refs[weights:])
    right_refs = []
    for entry in plan:
        held = 2 if entry[5] else 1
        right_refs.append(refs[:held] if held == 2 else refs[0])
        refs = refs[held:]
    out_refs = refs[:outs]
    scratch = list(refs[outs:])
    turned_refs = [scratch.pop(0) for weight in plan]
    whole_refs = [scratch.pop(0) for weight in plan]
    chunks = [(w, t) for w, entry in enumerate(plan) for t in range(entry[1])]
    held = [(scratch.pop(0), scratch.pop(0)) for chunk in chunks]
    pair_send, pair_recv, near_sem, store_sem = scratch
    own_ctx = lax.axis_index("ctx")
    core, chip = (own_ctx % 2, own_ctx // 2)
    own_x, own_y = (chip % 2, chip // 2)
    to_core = {"ctx": toggled(own_ctx, 1)}
    barrier = pltpu.get_barrier_semaphore()
    pl.semaphore_signal(barrier, inc=1, device_id=to_core, device_id_type=pl.DeviceIdType.MESH)
    pl.semaphore_wait(barrier, 1)
    pending = []
    send = remote_send(pending)
    begin, turn, multiply = pair_steps(
        plan,
        lead_rows,
        left_refs,
        right_refs,
        turned_refs,
        whole_refs,
        (pair_send, pair_recv, near_sem),
        core,
        pending,
        send,
    )
    for w in range(weights):
        begin(w)
        turn(w)
    stores = []
    for number, (w, t) in enumerate(chunks):
        first, second = held[number]
        multiply(w, t, first, second)
        group, offset = places[number]
        sides = (
            lambda at: first.at[:, at, own_x],
            lambda at: first.at[:, at, 1 - own_x],
            lambda at: second.at[:, own_y, at],
            lambda at: second.at[:, 1 - own_y, at],
        )
        for side, source_at in enumerate(sides):
            for at in (0, 1):
                copy = pltpu.make_async_copy(
                    source_at(at),
                    out_refs[4 * group + side].at[at, :, :, pl.ds(offset, plan[w][2])],
                    store_sem.at[8 * number + 2 * side + at],
                )
                copy.start()
                stores.append(copy)
    for copy in stores:
        copy.wait()
    for copy in pending:
        copy.wait_send()


def weight_plan(kind, left, right, count):
    deep = left.shape[1] // 4
    if kind == "rows":
        parted = isinstance(right, tuple)
        span = right[0].shape[1] if parted else right.shape[1] // 2
        width = -(-span // (128 * count)) * 128
        return (kind, count, width, deep, (deep // 8, deep // 8), span if parted else 0)
    lead_rows = deep // 2 // 16 * 16
    return (kind, count, right.shape[-1] // 8, deep, (lead_rows, deep - lead_rows), 0)


def early_places(plan):
    groups, places = ([], [])
    for kind, count, width, deep, halves, parted in plan:
        found = [at for at, group in enumerate(groups) if group[0] == halves]
        if not found:
            groups.append([halves, 0])
            found = [len(groups) - 1]
        for chunk in range(count):
            places.append((found[0], groups[found[0]][1]))
            groups[found[0]][1] += width
    return (groups, places)


def plan_span(entry):
    return entry[1] * entry[2] if entry[0] == "rows" else 4 * entry[2]


def plan_lead(plan):
    return max([0] + [entry[4][0] for entry in plan if entry[0] == "columns"])


def pair_scratch(plan, tokens):
    turned = [pltpu.VMEM((4 * entry[3], 2 * tokens), jnp.bfloat16) for entry in plan]
    return turned + [
        pltpu.VMEM((2 * tokens, entry[5] or plan_span(entry)), jnp.bfloat16) for entry in plan
    ]


def early_sums(products, held):
    plan = [weight_plan(*product) for product in products]
    lefts, rights = ([product[1] for product in products], [product[2] for product in products])
    vmem, anywhere, dma = (
        pl.BlockSpec(memory_space=pltpu.VMEM),
        pl.BlockSpec(memory_space=pl.ANY),
        pltpu.SemaphoreType.DMA,
    )
    rights = [part for right in rights for part in (right if isinstance(right, tuple) else [right])]
    groups = early_places(plan)[0]
    outs, units = ([], [])
    for halves, columns in groups:
        for half in halves:
            outs += [jax.ShapeDtypeStruct((2, 4, half, columns), jnp.bfloat16)] * 2
    for kind, count, width, deep, halves, parted in plan:
        for chunk in range(count):
            units += [pltpu.VMEM((4, 2, 2, half, width), jnp.bfloat16) for half in halves]
    chunk_count = sum(entry[1] for entry in plan)
    scratch = pair_scratch(plan, lefts[0].shape[0]) + units
    scratch += [dma((2 * len(plan),)), dma((2 * len(plan),)), dma((len(plan),)), dma((8 * chunk_count,))]
    sides = pl.pallas_call(
        functools.partial(product_kernel, plan, plan_lead(plan)),
        out_shape=tuple(outs),
        in_specs=[vmem] * len(plan) + [anywhere] * len(rights),
        out_specs=(anywhere,) * len(outs),
        scratch_shapes=scratch,
        compiler_params=pltpu.CompilerParams(
            collective_id=3, has_side_effects=True, vmem_limit_bytes=60 * 1024 * 1024
        ),
        name="early_products",
    )(*lefts, *rights)
    held, sides = lax.optimization_barrier((held, sides))
    arrays = []
    for group in range(len(groups)):
        for part, bit in ((0, 2), (2, 4)):
            kept, sent = sides[4 * group + part : 4 * group + part + 2]
            arrays.append((kept, swap(sent, "ctx", bit)))
    return (held, (plan, arrays))


def second_step(held, early):
    plan, arrays = early
    held, arrays = lax.optimization_barrier((held, arrays))
    chip = lax.axis_index("ctx") // 2
    flat = []
    for at, (kept, arrived) in sorted(enumerate(arrays), key=lambda pair: (-(pair[0] // 2), pair[0])):
        bit, own = ((4, chip // 2), (2, chip % 2))[at % 2]
        other = [
            lax.dynamic_index_in_dim(side, 1 - own, 0, keepdims=False).astype(jnp.float32)
            for side in (kept, arrived)
        ]
        twice = swap((other[0] + other[1]).astype(jnp.bfloat16), "ctx", bit)
        flat.append((at, [kept, arrived, twice]))
    flat = [side for at, sides in sorted(flat, key=lambda pair: pair[0]) for side in sides]
    return (held, (plan, flat))


def sum_kernel(early, late, lead_rows, *refs):
    weights, products = (len(early) + len(late), len(late))
    left_refs, right_refs = (refs[:products], refs[products : 2 * products])
    refs = refs[2 * products :]
    groups, places = early_places(early)
    early_refs, refs = (refs[: 6 * len(groups)], refs[6 * len(groups) :])
    small_ref, out_refs, small_out = (refs[0], refs[1 : weights + 1], refs[weights + 1])
    scratch = list(refs[weights + 2 :])
    turned_refs = [scratch.pop(0) for weight in late]
    whole_refs = [scratch.pop(0) for weight in late]
    plan = early + late
    chunks = [(w, t) for w, entry in enumerate(plan) for t in range(entry[1])]
    early_count = sum(entry[1] for entry in early)
    units = {}
    for number in range(len(chunks)):
        for half in (0, 1):
            units[number, half] = [scratch.pop(0) for stage in range(5)]
    small_held = scratch.pop(0)
    send_sem, recv_sem, local_sem, load_sem, pair_send, pair_recv, small_send, small_recv, near_sem = scratch
    own_ctx, own_shard = (lax.axis_index("ctx"), lax.axis_index("fsdp"))
    core, chip = (own_ctx % 2, own_ctx // 2)
    own_x, own_y = (chip % 2, chip // 2)
    low_bit, high_bit = (own_shard % 2, own_shard // 2)
    loads = {}
    for number in range(early_count):
        w, (group, offset) = (chunks[number][0], places[number])
        for half in (0, 1):
            own = own_y if half == 0 else own_x
            kept, arrived, twice = early_refs[6 * group + 3 * half : 6 * group + 3 * half + 3]
            columns = pl.ds(offset, plan[w][2])
            sources = (kept.at[own, :, :, columns], arrived.at[own, :, :, columns], twice.at[:, :, columns])
            for at, source in enumerate(sources):
                slot = (number * 2 + half) * 3 + at
                copy = pltpu.make_async_copy(source, units[number, half][at], load_sem.at[slot])
                copy.start()
                loads[number, half, at] = copy
    partners = [{"ctx": toggled(own_ctx, bit)} for bit in (1, 2, 4)]
    partners += [{"fsdp": toggled(own_shard, bit)} for bit in (1, 2)]
    barrier = pltpu.get_barrier_semaphore()
    for partner in partners:
        pl.semaphore_signal(
            barrier, inc=1, device_id=partner, device_id_type=pl.DeviceIdType.MESH
        )
    pl.semaphore_wait(barrier, len(partners))
    to_core, to_x, to_y, to_one, to_two = partners
    pending = []
    send = remote_send(pending)
    begin, turn, multiply = pair_steps(
        late,
        lead_rows,
        left_refs,
        right_refs,
        turned_refs,
        whole_refs,
        (pair_send, pair_recv, near_sem),
        core,
        pending,
        send,
    )
    for w in range(len(late)):
        begin(w)
    copies = {}

    def hop(number, half, stage, source, target, partner):
        slot = (number * 2 + half) * 8 + stage
        copies[number, half, stage] = send(
            source, target, send_sem.at[slot], recv_sem.at[slot], partner
        )

    def stage_one(number):
        w, t = chunks[number]
        multiply(w - len(early), t, units[number, 0][0], units[number, 1][0])
        hop(number, 0, 0, units[number, 0][0].at[:, :, 1 - own_x], units[number, 0][1], to_x)
        hop(number, 1, 0, units[number, 1][0].at[:, 1 - own_y], units[number, 1][1], to_y)

    def add(target, source_at, count):
        def each(i, carried):
            target[i] = (
                target[i].astype(jnp.float32) + source_at(i).astype(jnp.float32)
            ).astype(jnp.bfloat16)
            return carried

        lax.fori_loop(0, count, each, 0)

    def stage_two(number):
        held, got = (units[number, 0][0], units[number, 0][1])
        copies[number, 0, 0].wait_recv()
        add(got, lambda z: held[z, :, own_x], 4)
        held_b, got_b = (units[number, 1][0], units[number, 1][1])
        copies[number, 1, 0].wait_recv()
        add(got_b, lambda z: held_b[z, own_y], 4)
        hop(number, 0, 1, got.at[:, 1 - own_y], units[number, 0][2], to_y)
        hop(number, 1, 1, got_b.at[:, 1 - own_x], units[number, 1][2], to_x)

    def stage_three(number):
        for half in (0, 1):
            kept, held, got = units[number, half][:3]
            own = own_y if half == 0 else own_x
            if number < early_count:
                for at in range(3):
                    loads[number, half, at].wait()
                add(held, lambda z: kept[z], 4)
                add(got, lambda z: held[z], 4)
            else:
                copies[number, half, 1].wait_recv()
                add(got, lambda z: held[z, own], 4)
        for half in (0, 1):
            got = units[number, half][2]
            for high in (0, 1):
                hop(
                    number,
                    half,
                    2 + 4 * high,
                    got.at[2 * high + 1 - low_bit],
                    units[number, half][3].at[high],
                    to_one,
                )

    def stage_four(number):
        for half in (0, 1):
            held, got = (units[number, half][2], units[number, half][3])
            copies[number, half, 2].wait_recv()
            copies[number, half, 6].wait_recv()
            add(got, lambda high: held[2 * high + low_bit], 2)
        for half in (0, 1):
            got = units[number, half][3]
            hop(number, half, 3, got.at[1 - high_bit], units[number, half][4].at[0], to_two)

    def final_region(number, half, chip_at):
        w, t = chunks[number]
        kind, count, width = plan[w][:3]
        deep = units[number, half][4].shape[1]
        if kind == "rows":
            start = pl.multiple_of((2 * chip_at + half) * deep, deep)
            column = pl.multiple_of((core * count + t) * width, width)
            return out_refs[w].at[pl.ds(start, deep), pl.ds(column, width)]
        column = pl.multiple_of((core * 4 + chip_at) * width, width)
        return out_refs[w].at[pl.ds(half * lead_rows, deep), pl.ds(column, width)]

    local = {}

    def stage_five(number):
        for half in (0, 1):
            held, got = (units[number, half][3], units[number, half][4])
            copies[number, half, 3].wait_recv()
            add(got, lambda i: held[high_bit], 1)
        for half in (0, 1):
            got = units[number, half][4].at[0]
            target = final_region(number, half, chip)
            hop(number, half, 4, got, target, to_x if half == 0 else to_y)
            hop(number, half, 5, got, target, to_y if half == 0 else to_x)
            copy = pltpu.make_async_copy(got, target, local_sem.at[number * 2 + half])
            copy.start()
            local[number, half] = copy

    def stage_six(number):
        for half in (0, 1):
            copies[number, half, 4].wait_recv()
            piece = final_region(number, half, toggled(chip, 1 if half == 0 else 2))
            hop(number, half, 7, piece, piece, to_y if half == 0 else to_x)

    def stage_seven(number):
        w, t = chunks[number]
        kind, count, width = plan[w][:3]
        for half in (0, 1):
            copies[number, half, 5].wait_recv()
            copies[number, half, 7].wait_recv()
            local[number, half].wait()
        span = width if kind == "rows" else 4 * width
        at = core * count + t if kind == "rows" else core
        piece = out_refs[w].at[:, pl.ds(pl.multiple_of(at * span, span), span)]
        slot = len(chunks) * 16 + number
        copies[number, 2, 0] = send(
            piece, piece, send_sem.at[slot], recv_sem.at[slot], to_core
        )

    small_copies = []

    def small_step(step):
        if step > 0:
            small_copies[step - 1].wait_recv()
            small_held[2 * step] = small_held[2 * step - 2] + small_held[2 * step - 1]
            if step == 3:
                small_out[0] = small_held[6]
        else:
            small_held[0] = small_ref[...]
        if step < 5:
            small_copies.append(
                send(
                    small_held.at[2 * step],
                    small_held.at[2 * step + 1],
                    small_send.at[step],
                    small_recv.at[step],
                    partners[step],
                )
            )
        else:
            small_out[1] = small_held[10]

    stages = (stage_one, stage_two, stage_three, stage_four, stage_five, stage_six, stage_seven)
    small_at = 0
    stage_three(0)
    for w in range(len(late)):
        turn(w)
    for tick in range(len(chunks) + len(stages)):
        for lag, stage in enumerate(stages):
            for number in range(len(chunks)):
                start = number - 2 if number < early_count else number - early_count
                if start + lag == tick and (number >= early_count or (lag >= 2 and number + lag > 2)):
                    stage(number)
        if small_at < 6:
            small_step(small_at)
            small_at += 1
    for number in range(len(chunks)):
        copies[number, 2, 0].wait_recv()
    for copy in pending:
        copy.wait_send()


def sum_weights(early, early_arrays, products, small):
    late = [weight_plan(*product) for product in products]
    lefts, rights = ([product[1] for product in products], [product[2] for product in products])
    plan = early + late
    pieces = []
    for w, (kind, count, width, deep, halves, parted) in enumerate(plan):
        leads = [(4, 2, 2), (4, 2), (4,), (2,), (1,)]
        if w < len(early):
            leads[:2] = [(4,), (4,)]
        for chunk in range(count):
            for half in halves:
                pieces += [pltpu.VMEM(lead + (half, width), jnp.bfloat16) for lead in leads]
    outs = [jax.ShapeDtypeStruct((entry[3], 2 * plan_span(entry)), jnp.bfloat16) for entry in plan]
    chunk_count = sum(entry[1] for entry in plan)
    scratch = pair_scratch(late, lefts[0].shape[0]) + pieces
    dma = pltpu.SemaphoreType.DMA
    scratch += [pltpu.VMEM((11,) + small.shape, jnp.float32)]
    slots = chunk_count * 17
    scratch += [dma((slots,)), dma((slots,)), dma((2 * chunk_count,)), dma((6 * chunk_count,))]
    scratch += [dma((2 * len(late),)), dma((2 * len(late),)), dma((5,)), dma((5,)), dma((len(late),))]
    vmem, anywhere = (
        pl.BlockSpec(memory_space=pltpu.VMEM),
        pl.BlockSpec(memory_space=pl.ANY),
    )
    return pl.pallas_call(
        functools.partial(sum_kernel, early, late, plan_lead(plan)),
        out_shape=tuple(outs) + (jax.ShapeDtypeStruct((2,) + small.shape, jnp.float32),),
        in_specs=[vmem] * len(late) + [anywhere] * (len(late) + len(early_arrays)) + [vmem],
        out_specs=(anywhere,) * len(plan) + (vmem,),
        scratch_shapes=scratch,
        compiler_params=pltpu.CompilerParams(
            collective_id=1, has_side_effects=True, vmem_limit_bytes=60 * 1024 * 1024
        ),
        name="sum_weights",
    )(*lefts, *rights, *early_arrays, small)


def layer_norm(rows_in, gain_vec):
    row_mean = jnp.mean(rows_in, axis=-1, keepdims=True)
    centred = rows_in - row_mean
    variance = jnp.mean(centred * centred, axis=-1, keepdims=True)
    return centred * lax.rsqrt(variance + norm_eps) * gain_vec


def rotate(projected, cosine, sine):
    row_count, width = projected.shape
    half_width = HEAD_WIDTH // 2
    by_head = projected.reshape(row_count, width // HEAD_WIDTH, HEAD_WIDTH)
    turned = jnp.concatenate([by_head[..., half_width:], by_head[..., :half_width]], axis=-1)
    return (by_head * cosine[:, None, :] - turned * sine[:, None, :]).reshape(row_count, width)


def swap(value, axis, bit):
    pairs = [(i, i ^ bit) for i in range(lax.axis_size(axis))]
    return lax.ppermute(value, axis, pairs)


def bit_of(axis, bit):
    return (lax.axis_index(axis) // bit) % 2 == 1


def bits_below(count):
    return [1 << i for i in range(count.bit_length() - 1)]


def reduce_pieces(pieces, labels, order):
    labels = list(labels)
    for axis, bit in order:
        at = labels.index((axis, bit))
        labels.pop(at)
        first = lax.index_in_dim(pieces, 0, at, keepdims=False)
        second = lax.index_in_dim(pieces, 1, at, keepdims=False)
        upper = bit_of(axis, bit)
        arrived = swap(jnp.where(upper, first, second), axis, bit)
        kept = jnp.where(upper, second, first)
        pieces = (kept.astype(jnp.float32) + arrived.astype(jnp.float32)).astype(jnp.bfloat16)
    return pieces


def gather_pieces(piece, labels, order):
    held = []
    for axis, bit in reversed(order):
        arrived = swap(piece, axis, bit)
        upper = bit_of(axis, bit)
        held = [label for label in labels if label in held or label == (axis, bit)]
        piece = jnp.stack(
            [jnp.where(upper, arrived, piece), jnp.where(upper, piece, arrived)],
            axis=held.index((axis, bit)),
        )
    return piece


def keep_and_send(first, second):
    upper = bit_of("ctx", 1)
    return (jnp.where(upper, second, first), jnp.where(upper, first, second))


def core_product(left, first, second):
    kept, sent = keep_and_send(first, second)
    left_all = jnp.concatenate([left, swap(left, "ctx", 1)], axis=0)
    right_all = jnp.concatenate([kept, swap(sent, "ctx", 1)], axis=0)
    return lax.dot_general(
        left_all, right_all, (((0,), (0,)), ((), ())), preferred_element_type=jnp.float32
    ).astype(jnp.bfloat16)


def shard_sum(product, by_columns):
    shards = lax.axis_size("fsdp")
    slices = lax.axis_size("ctx") // 2
    rows, columns = product.shape
    shard_labels = [("fsdp", bit) for bit in reversed(bits_below(shards))]
    slice_labels = [("ctx", 2 * bit) for bit in reversed(bits_below(slices))]
    if by_columns:
        cut = product.reshape(shards, rows // shards, slices, columns // slices)
        cut = jnp.transpose(cut, (0, 2, 1, 3))
    else:
        cut = product.reshape(shards, slices, rows // shards // slices, columns)
    parts = []
    half = cut.shape[2] // 2
    tail = list(reversed(shard_labels))
    for lead, orders in (
        (cut[:, :, :half], list(reversed(slice_labels))),
        (cut[:, :, half:], slice_labels),
    ):
        pieces = lead.reshape((2,) * (len(shard_labels) + len(slice_labels)) + lead.shape[2:])
        piece = reduce_pieces(pieces, shard_labels + slice_labels, orders + tail)
        whole = gather_pieces(piece, slice_labels, orders)
        parts.append(whole.reshape((slices,) + piece.shape))
    both = jnp.concatenate(parts, axis=1)
    if by_columns:
        return jnp.transpose(both, (1, 0, 2)).reshape(rows // shards, columns)
    return both.reshape(rows // shards, columns)


def join_cores(own):
    other = swap(own, "ctx", 1)
    upper = bit_of("ctx", 1)
    return jnp.concatenate(
        [jnp.where(upper, other, own), jnp.where(upper, own, other)], axis=1
    ).astype(jnp.float32)


def sum_over(value, axes):
    for axis in axes:
        for bit in bits_below(lax.axis_size(axis)):
            value = value + swap(value, axis, bit)
    return value


def own_shard(vector):
    width = vector.shape[0] // lax.axis_size("fsdp")
    return lax.dynamic_slice_in_dim(vector, lax.axis_index("fsdp") * width, width, 0)


def weight_sums(
    hidden,
    grad_mlp_low,
    act_mlp,
    grad_leading,
    grad_trailing,
    act_attn,
    grad_projected,
    attn_low,
    grad_attn_low,
    small,
    early,
):
    shards, ctx_count = (lax.axis_size("fsdp"), lax.axis_size("ctx"))
    rows, ff_width = hidden.shape
    model_width = act_mlp.shape[1]
    if early is None:
        half, half_three = (model_width // 2, 3 * model_width // 2)
        pairs = (
            (hidden, grad_mlp_low[:, :half], grad_mlp_low[:, half:]),
            (act_mlp, grad_leading, grad_trailing),
            (act_attn, grad_projected[:, :half_three], grad_projected[:, half_three:]),
            (attn_low, grad_attn_low[:, :half], grad_attn_low[:, half:]),
        )
        totals = [
            join_cores(shard_sum(core_product(*pair), at == 0)) for at, pair in enumerate(pairs)
        ]
        over_pack = sum_over(small, ("ctx",))
        return totals + [jnp.stack([over_pack, sum_over(over_pack, ("fsdp",))])]
    total_attn, total_in, total_out, total_qkv, small_sums = sum_weights(
        *early, [("rows", act_attn, grad_projected, 3)], small
    )
    padded = total_in.shape[1] // 2
    total_in = jnp.concatenate(
        [total_in[:, :ff_width], total_in[:, padded : padded + ff_width]], axis=1
    )
    return [
        total.astype(jnp.float32) for total in (total_out, total_in, total_qkv, total_attn)
    ] + [small_sums]


def weight_sums_early(
    hidden, grad_mlp_low, act_mlp, grad_leading, grad_trailing, attn_low, grad_attn_low, held
):
    shards, ctx_count = (lax.axis_size("fsdp"), lax.axis_size("ctx"))
    ff_width = hidden.shape[1]
    if shards != 4 or ctx_count != 8 or act_mlp.shape[1] % 1024 != 0 or ff_width % 64 != 0:
        return (held, None)
    return early_sums(
        [
            ("rows", attn_low, grad_attn_low, 1),
            ("rows", act_mlp, (grad_leading, grad_trailing), 3),
            ("columns", hidden, grad_mlp_low, 1),
        ],
        held,
    )


def per_device(
    inputs,
    cotangent,
    lengths,
    piece_route,
    gain_one,
    qkv_weight,
    attn_out,
    gain_two,
    geglu_in,
    geglu_out,
):
    ctx_count = lax.axis_size("ctx")
    own_index = lax.axis_index("ctx")
    row_count = inputs.shape[1]
    model_width = inputs.shape[2]
    piece_rows = row_count // ctx_count
    tokens = row_count * ctx_count
    own_heads = model_width // HEAD_WIDTH // ctx_count
    own_width = own_heads * HEAD_WIDTH
    block_q = math.gcd(tokens, 256)
    block_k = math.gcd(tokens, 512)
    lengths_row = lengths[0]
    own_route = piece_route[0, 0]
    slot_ids = jnp.arange(ctx_count, dtype=jnp.int32)
    outgoing = jnp.sum(
        slot_ids[None, :] * (own_route[None, :] == slot_ids[:, None]).astype(jnp.int32), axis=1
    )

    def exchange(blocks):
        return lax.all_to_all(blocks, "ctx", split_axis=0, concat_axis=0, tiled=True)

    def to_slots(rows_in):
        return jnp.take(rows_in.reshape(ctx_count, piece_rows, model_width), outgoing, axis=0)

    def to_heads(rows_in):
        by_heads = rows_in.reshape(row_count, ctx_count, -1)
        return exchange(jnp.transpose(by_heads, (1, 0, 2))).reshape(tokens, -1)

    def to_rows(heads_in):
        return exchange(heads_in.reshape(ctx_count, row_count, -1))

    both_arrived = exchange(
        jnp.concatenate([to_slots(inputs[0]), to_slots(cotangent[0])], axis=1)
    )
    arrived, grad_arrived = (both_arrived[:, :piece_rows], both_arrived[:, piece_rows:])
    residual = arrived.reshape(row_count, model_width).astype(jnp.float32)
    places = own_index * row_count + jnp.arange(row_count, dtype=jnp.int32)
    unused_begin, unused_end, offset, is_valid = spans(places, lengths_row)
    pack_begin, pack_end, unused_offset, unused_valid = spans(
        jnp.arange(tokens, dtype=jnp.int32), lengths_row
    )
    grad_final = jnp.where(
        is_valid[:, None], grad_arrived.reshape(row_count, model_width).astype(jnp.float32), 0.0
    )
    gains = jnp.pad(jnp.stack([gain_one, gain_two]), ((0, 14), (0, 0)))
    gains_full, qkv_full = gather_weights([gains, qkv_weight])
    gains_full = gains_full.reshape(-1, 16, gains.shape[1])
    gain_attn = gains_full[:, 0].reshape(-1).astype(jnp.float32)
    gain_mlp = gains_full[:, 1].reshape(-1).astype(jnp.float32)
    act_attn = layer_norm(residual, gain_attn).astype(jnp.bfloat16)
    later = [attn_out, geglu_in, geglu_out]
    row_cosine, row_sine = rotary_tables(offset, own_heads)
    if lax.axis_size("fsdp") == 4 and ctx_count == 8 and own_width == 128:
        attn_full, in_full, out_full, qkv_heads = gather_weights(
            later, (act_attn, qkv_full, row_cosine, row_sine)
        )
    else:
        attn_full, in_full, out_full = gather_weights(later)
        projected = jnp.dot(act_attn, qkv_full, preferred_element_type=jnp.float32)
        cosine, sine = rotary_tables(offset, 1)
        queries, keys = (
            rotate(projected[:, :model_width], cosine, sine).astype(jnp.bfloat16),
            rotate(projected[:, model_width : 2 * model_width], cosine, sine).astype(jnp.bfloat16),
        )
        values = projected[:, 2 * model_width :].astype(jnp.bfloat16)
        joined = jnp.stack(
            [part.reshape(row_count, ctx_count, own_width) for part in (queries, keys, values)], axis=2
        )
        qkv_heads = to_heads(joined.reshape(row_count, -1))
    low, high = key_range(pack_begin, pack_end, block_q, block_k)
    pack_begin, pack_end = (pack_begin[None, :], pack_end[None, :])
    attended_heads, attended_low, log_total = attention_forward(
        qkv_heads, pack_begin, pack_end, low, high, own_heads, block_q, block_k
    )
    attn_low = jnp.transpose(to_rows(attended_low), (1, 0, 2)).reshape(
        row_count, model_width
    )
    branch_attn = jnp.dot(attn_low, attn_full, preferred_element_type=jnp.float32)
    middle = residual + branch_attn
    act_mlp = layer_norm(middle, gain_mlp).astype(jnp.bfloat16)
    up_both = jnp.dot(act_mlp, in_full, preferred_element_type=jnp.float32)
    ff_width = up_both.shape[1] // 2
    hidden = (jax.nn.gelu(up_both[:, :ff_width], approximate=False) * up_both[:, ff_width:]).astype(
        jnp.bfloat16
    )
    branch_mlp = jnp.dot(hidden, out_full, preferred_element_type=jnp.float32)
    final_rows = jnp.where(is_valid[:, None], middle + branch_mlp, 0.0)
    square_sums = jnp.stack(
        [
            jnp.sum(final_rows * final_rows),
            jnp.sum(jnp.where(is_valid[:, None], branch_attn * branch_attn, 0.0)),
            jnp.sum(jnp.where(is_valid[:, None], branch_mlp * branch_mlp, 0.0)),
        ]
    )
    out_slots = final_rows.astype(jnp.bfloat16).reshape(ctx_count, piece_rows, model_width)
    grad_mlp_low = grad_final.astype(jnp.bfloat16)
    grad_hidden = lax.dot_general(
        grad_mlp_low, out_full, NT, preferred_element_type=jnp.float32
    )

    def gated(leading, trailing):
        return jax.nn.gelu(leading, approximate=False) * trailing

    unused_gate, gate_back = jax.vjp(gated, up_both[:, :ff_width], up_both[:, ff_width:])
    grad_leading, grad_trailing = gate_back(grad_hidden)
    grad_leading, grad_trailing = (
        grad_leading.astype(jnp.bfloat16),
        grad_trailing.astype(jnp.bfloat16),
    )
    grad_up = jnp.concatenate([grad_leading, grad_trailing], axis=1)
    grad_act_mlp = lax.dot_general(grad_up, in_full, NT, preferred_element_type=jnp.float32)
    unused_norm, norm_back_mlp = jax.vjp(layer_norm, middle, gain_mlp)
    grad_middle_norm, grad_gain_mlp = norm_back_mlp(grad_act_mlp)
    grad_middle = grad_final + grad_middle_norm
    grad_attn_low = grad_middle.astype(jnp.bfloat16)
    grad_attended = lax.dot_general(
        grad_attn_low, attn_full, NT, preferred_element_type=jnp.float32
    ).astype(jnp.bfloat16)
    grad_attended_heads, early = weight_sums_early(
        hidden,
        grad_mlp_low,
        act_mlp,
        grad_leading,
        grad_trailing,
        attn_low,
        grad_attn_low,
        to_heads(grad_attended),
    )
    block_back = math.gcd(tokens, 256)
    low_back, high_back = key_range(pack_begin[0], pack_end[0], block_q, block_back)
    grad_heads = attention_backward(
        qkv_heads,
        attended_heads,
        grad_attended_heads,
        log_total,
        pack_begin,
        pack_end,
        low_back,
        high_back,
        [] if early is None else [early[1][0][0]],
        own_heads,
        block_q,
        block_back,
    )
    if early is not None:
        grad_heads, early = second_step(grad_heads, early)
    grad_rows = to_rows(grad_heads)
    if own_width % 128 == 0:
        grad_projected, grad_act_attn = finish_rows(
            grad_rows, row_cosine, row_sine, qkv_full, own_heads
        )
    else:
        by_part = jnp.transpose(
            grad_rows.reshape(ctx_count, row_count, 3, own_width), (2, 1, 0, 3)
        ).reshape(3, row_count, model_width)
        cosine, sine = rotary_tables(offset, 1)
        grad_projected = jnp.concatenate(
            [
                rotate(by_part[part].astype(jnp.float32), cosine, -sine).astype(jnp.bfloat16)
                for part in (0, 1)
            ]
            + [by_part[2]],
            axis=1,
        )
        grad_act_attn = lax.dot_general(
            grad_projected, qkv_full, NT, preferred_element_type=jnp.float32
        )
    unused_first, norm_back_attn = jax.vjp(layer_norm, residual, gain_attn)
    grad_resid_norm, grad_gain_attn = norm_back_attn(grad_act_attn)
    grad_residual = (grad_middle + grad_resid_norm).astype(jnp.bfloat16)
    grad_slots = grad_residual.reshape(ctx_count, piece_rows, model_width)
    back = exchange(jnp.concatenate([out_slots, grad_slots], axis=1))
    block_out, grad_inputs = (
        jnp.take(half, own_route, axis=0).reshape(1, row_count, model_width)
        for half in (back[:, :piece_rows], back[:, piece_rows:])
    )
    small = jnp.stack(
        [grad_gain_attn, grad_gain_mlp, jnp.pad(square_sums, (0, model_width - 3))]
        + [jnp.zeros((model_width,), jnp.float32)] * 5
    )
    total_out, total_in, total_qkv, total_attn, small_sums = weight_sums(
        hidden,
        grad_mlp_low,
        act_mlp,
        grad_leading,
        grad_trailing,
        act_attn,
        grad_projected,
        attn_low,
        grad_attn_low,
        small,
        early,
    )
    total_gain_one = own_shard(small_sums[1, 0])
    total_gain_two = own_shard(small_sums[1, 1])
    total_squares = small_sums[0, 2, :3]
    valid_count = jnp.sum(lengths_row).astype(jnp.float32)
    rms_stats = jnp.sqrt(total_squares / (valid_count * model_width))[None, :]
    return (
        block_out,
        grad_inputs,
        total_gain_one,
        total_qkv,
        total_attn,
        total_gain_two,
        total_in,
        total_out,
        rms_stats,
    )


def solution(mesh):
    placed = (
        P("fsdp", "ctx", None),
        P("fsdp", "ctx", None),
        P("fsdp", None),
        P("fsdp", "ctx", None),
        P("fsdp"),
        P("fsdp", None),
        P("fsdp", None),
        P("fsdp"),
        P("fsdp", None),
        P("fsdp", None),
    )
    return jax.shard_map(
        per_device,
        mesh=mesh,
        in_specs=placed,
        out_specs=(
            P("fsdp", "ctx", None),
            P("fsdp", "ctx", None),
            P("fsdp"),
            P("fsdp", None),
            P("fsdp", None),
            P("fsdp"),
            P("fsdp", None),
            P("fsdp", None),
            P("fsdp", None),
        ),
        check_vma=False,
    )
```

```python
import functools
import math
import jax
import jax.numpy as jnp
from jax import lax
from jax.experimental import pallas as pl
from jax.experimental.pallas import tpu as pltpu
from jax.sharding import PartitionSpec as P

HEAD_WIDTH = 64
norm_eps = 1e-05
masked_score = -1e30


def head_stack(rows_in, head_count):
    if head_count == 1:
        return rows_in
    lane_head = lax.broadcasted_iota(jnp.int32, rows_in.shape, 1) // HEAD_WIDTH
    zero = jnp.zeros_like(rows_in)
    return jnp.concatenate(
        [jnp.where(lane_head == h, rows_in, zero) for h in range(head_count)], axis=0
    )


def head_pick(stacked_t, head_count, block):
    return jnp.concatenate(
        [
            stacked_t[h * HEAD_WIDTH : (h + 1) * HEAD_WIDTH, h * block : (h + 1) * block]
            for h in range(head_count)
        ],
        axis=0,
    ).T


NT = (((1,), (1,)), ((), ()))


def forward_kernel(
    head_count, block_q, block_k, low_ref, high_ref, begin_ref, end_ref, qkv_ref, out_ref, low_out_ref, log_ref, turned_ref
):
    width = out_ref.shape[1]
    step = pl.program_id(0)

    @pl.when(step == 0)
    def prepare():
        turned_ref[...] = qkv_ref[:, 2 * width :].astype(jnp.float32).T.astype(jnp.bfloat16)

    rows = pl.ds(pl.multiple_of(step * block_q, block_q), block_q)
    scale = 1.0 / math.sqrt(HEAD_WIDTH)
    stacked = head_stack(qkv_ref[rows, :width] * jnp.asarray(scale, jnp.bfloat16), head_count)
    begin = jnp.concatenate([begin_ref[:, rows]] * head_count, axis=1)
    end = jnp.concatenate([end_ref[:, rows]] * head_count, axis=1)

    def body(index, carried):
        top, total, acc = carried
        first = pl.multiple_of(index * block_k, block_k)
        keys = qkv_ref[pl.ds(first, block_k), width : 2 * width]
        scores = lax.dot_general(keys, stacked, NT, preferred_element_type=jnp.float32)
        place = first + lax.broadcasted_iota(jnp.int32, scores.shape, 0)
        scores = jnp.where((place >= begin) & (place < end), scores, masked_score)
        new_top = jnp.maximum(top, jnp.max(scores, axis=0, keepdims=True))
        fresh = jnp.exp(scores - new_top)
        fade = jnp.exp(top - new_top)
        total = total * fade + jnp.sum(fresh, axis=0, keepdims=True)
        acc = acc * fade + jnp.dot(
            turned_ref[:, pl.ds(first, block_k)],
            fresh.astype(jnp.bfloat16),
            preferred_element_type=jnp.float32,
        )
        return (new_top, total, acc)

    lanes = head_count * block_q
    top, total, acc = lax.fori_loop(
        low_ref[step],
        high_ref[step],
        body,
        (
            jnp.full((1, lanes), masked_score, jnp.float32),
            jnp.zeros((1, lanes), jnp.float32),
            jnp.zeros((width, lanes), jnp.float32),
        ),
    )
    valid = end > begin
    safe = jnp.where(valid, total, 1.0)
    acc = jnp.where(valid, acc / safe, 0.0)
    log_total = jnp.where(valid, top + jnp.log(safe), 0.0)
    attended = head_pick(acc, head_count, block_q)
    out_ref[...] = attended
    low_out_ref[...] = attended.astype(jnp.bfloat16)
    log_ref[0] = log_total


def attention_forward(qkv, begin, end, low, high, head_count, block_q, block_k):
    tokens = qkv.shape[0]
    width = head_count * HEAD_WIDTH
    steps = tokens // block_q
    whole = lambda shape: pl.BlockSpec(shape, lambda i, *_: (0,) * len(shape))
    pairs = tokens * tokens // 4 * head_count
    return pl.pallas_call(
        functools.partial(forward_kernel, head_count, block_q, block_k),
        out_shape=(
            jax.ShapeDtypeStruct((tokens, width), jnp.float32),
            jax.ShapeDtypeStruct((tokens, width), jnp.bfloat16),
            jax.ShapeDtypeStruct((steps, 1, head_count * block_q), jnp.float32),
        ),
        grid_spec=pltpu.PrefetchScalarGridSpec(
            num_scalar_prefetch=2,
            grid=(steps,),
            in_specs=[whole((1, tokens)), whole((1, tokens)), whole((tokens, 3 * width))],
            out_specs=(
                pl.BlockSpec((block_q, width), lambda i, *_: (i, 0)),
                pl.BlockSpec((block_q, width), lambda i, *_: (i, 0)),
                pl.BlockSpec((1, 1, head_count * block_q), lambda i, *_: (i, 0, 0)),
            ),
            scratch_shapes=[pltpu.VMEM((width, tokens), jnp.bfloat16)],
        ),
        cost_estimate=pl.CostEstimate(
            flops=pairs * 512, bytes_accessed=tokens * width * 12, transcendentals=pairs
        ),
        name="attention_forward",
    )(low, high, begin, end, qkv)


def turn_back(grads, cosine, sine, head_count):
    half = HEAD_WIDTH // 2
    pieces = []
    for h in range(head_count):
        base = h * HEAD_WIDTH
        pieces += [grads[:, base + half : base + HEAD_WIDTH], grads[:, base : base + half]]
    return grads * cosine + jnp.concatenate(pieces, axis=1) * sine


def backward_kernel(
    head_count,
    block_q,
    block_k,
    low_ref,
    high_ref,
    begin_ref,
    end_ref,
    qkv_ref,
    attended_ref,
    grad_ref,
    log_ref,
    *refs,
):
    out_ref, turned_ref, key_acc, value_acc = refs[-4:]
    width = attended_ref.shape[1]
    step = pl.program_id(0)

    @pl.when(step == 0)
    def prepare():
        turned_ref[...] = qkv_ref[:, width : 2 * width].astype(jnp.float32).T.astype(jnp.bfloat16)
        key_acc[...] = jnp.zeros_like(key_acc)
        value_acc[...] = jnp.zeros_like(value_acc)

    rows = pl.ds(pl.multiple_of(step * block_q, block_q), block_q)
    scale = 1.0 / math.sqrt(HEAD_WIDTH)
    stacked = head_stack(qkv_ref[rows, :width] * jnp.asarray(scale, jnp.bfloat16), head_count)
    grads = grad_ref[rows, :]
    grad_stacked = head_stack(grads, head_count)
    begin = jnp.concatenate([begin_ref[:, rows]] * head_count, axis=1)
    end = jnp.concatenate([end_ref[:, rows]] * head_count, axis=1)
    product = (grads.astype(jnp.float32) * attended_ref[rows, :]).T
    delta = jnp.concatenate(
        [
            jnp.sum(product[h * HEAD_WIDTH : (h + 1) * HEAD_WIDTH], axis=0, keepdims=True)
            for h in range(head_count)
        ],
        axis=1,
    )
    log_total = log_ref[0]

    def body(index, acc):
        first = pl.multiple_of(index * block_k, block_k)
        span = pl.ds(first, block_k)
        keys = qkv_ref[span, width : 2 * width]
        values = qkv_ref[span, 2 * width :]
        scores = lax.dot_general(keys, stacked, NT, preferred_element_type=jnp.float32)
        grad_probs = lax.dot_general(values, grad_stacked, NT, preferred_element_type=jnp.float32)
        place = first + lax.broadcasted_iota(jnp.int32, scores.shape, 0)
        scores = jnp.where((place >= begin) & (place < end), scores, masked_score)
        probs = jnp.exp(scores - log_total)
        grad_scores = (probs * (grad_probs - delta)).astype(jnp.bfloat16)
        value_acc[span, :] += jnp.dot(
            probs.astype(jnp.bfloat16), grad_stacked, preferred_element_type=jnp.float32
        )
        key_acc[span, :] += jnp.dot(grad_scores, stacked, preferred_element_type=jnp.float32)
        return acc + jnp.dot(
            turned_ref[:, span], grad_scores, preferred_element_type=jnp.float32
        )

    acc = lax.fori_loop(
        low_ref[step],
        high_ref[step],
        body,
        jnp.zeros((width, head_count * block_q), jnp.float32),
    )
    grad_queries = head_pick(acc, head_count, block_q) * scale
    out_ref[rows, :width] = grad_queries.astype(jnp.bfloat16)

    @pl.when(step == pl.num_programs(0) - 1)
    def finish():
        @pl.loop(0, pl.num_programs(0))
        def each(index):
            span = pl.ds(pl.multiple_of(index * block_q, block_q), block_q)
            out_ref[span, width : 2 * width] = key_acc[span, :].astype(jnp.bfloat16)
            out_ref[span, 2 * width :] = value_acc[span, :].astype(jnp.bfloat16)


def attention_backward(
    qkv, attended, grads, log_total, begin, end, low, high, after, head_count, block_q, block_k
):
    tokens = qkv.shape[0]
    width = head_count * HEAD_WIDTH
    steps = tokens // block_q
    whole = lambda shape: pl.BlockSpec(shape, lambda i, *_: (0,) * len(shape))
    pairs = tokens * tokens // 4 * head_count
    return pl.pallas_call(
        functools.partial(backward_kernel, head_count, block_q, block_k),
        out_shape=jax.ShapeDtypeStruct((tokens, 3 * width), jnp.bfloat16),
        grid_spec=pltpu.PrefetchScalarGridSpec(
            num_scalar_prefetch=2,
            grid=(steps,),
            in_specs=[
                whole((1, tokens)),
                whole((1, tokens)),
                whole((tokens, 3 * width)),
                whole((tokens, width)),
                whole((tokens, width)),
                pl.BlockSpec((1, 1, head_count * block_q), lambda i, *_: (i, 0, 0)),
            ]
            + [pl.BlockSpec(memory_space=pl.ANY)] * len(after),
            out_specs=whole((tokens, 3 * width)),
            scratch_shapes=[
                pltpu.VMEM((width, tokens), jnp.bfloat16),
                pltpu.VMEM((tokens, width), jnp.float32),
                pltpu.VMEM((tokens, width), jnp.float32),
            ],
        ),
        cost_estimate=pl.CostEstimate(
            flops=pairs * 1280, bytes_accessed=tokens * width * 30, transcendentals=pairs
        ),
        name="attention_backward",
    )(low, high, begin, end, qkv, attended, grads, log_total, *after)


def rows_kernel(head_count, heads_ref, cosine_ref, sine_ref, query_ref, key_ref, value_ref, out_ref, act_ref):
    width = heads_ref.shape[2] // 3
    step = pl.program_id(0)
    total = out_ref.shape[1] // 3
    owners = heads_ref.shape[0]
    pieces = []
    for part in range(3):
        for owner in range(owners):
            piece = heads_ref[owner, :, part * width : (part + 1) * width]
            if part < 2:
                piece = turn_back(
                    piece.astype(jnp.float32), cosine_ref[...], sine_ref[...], head_count
                ).astype(jnp.bfloat16)
            first = pl.multiple_of(part * total + (step * owners + owner) * width, width)
            out_ref[:, pl.ds(first, width)] = piece
            pieces.append(piece)
    weights = jnp.concatenate([query_ref[...], key_ref[...], value_ref[...]], axis=1)
    product = lax.dot_general(
        jnp.concatenate(pieces, axis=1), weights, NT, preferred_element_type=jnp.float32
    )

    @pl.when(step == 0)
    def begin():
        act_ref[...] = product

    @pl.when(step > 0)
    def add():
        act_ref[...] += product


def finish_rows(heads, cosine, sine, qkv_full, head_count):
    owners, rows, columns = heads.shape
    width = columns // 3
    depth = qkv_full.shape[0]
    whole = lambda shape: pl.BlockSpec(shape, lambda i: (0,) * len(shape))
    steps = owners // 2
    part_of = lambda part: pl.BlockSpec((depth, 2 * width), lambda i: (0, part * steps + i))
    return pl.pallas_call(
        functools.partial(rows_kernel, head_count),
        out_shape=(
            jax.ShapeDtypeStruct((rows, owners * columns), jnp.bfloat16),
            jax.ShapeDtypeStruct((rows, depth), jnp.float32),
        ),
        grid=(steps,),
        in_specs=[
            pl.BlockSpec((2, rows, columns), lambda i: (i, 0, 0)),
            whole((rows, width)),
            whole((rows, width)),
            part_of(0),
            part_of(1),
            part_of(2),
        ],
        out_specs=(whole((rows, owners * columns)), whole((rows, depth))),
        cost_estimate=pl.CostEstimate(
            flops=2 * rows * depth * owners * columns,
            bytes_accessed=2 * depth * owners * columns + 4 * rows * owners * columns,
            transcendentals=0,
        ),
        name="finish_rows",
    )(heads, cosine, sine, qkv_full, qkv_full, qkv_full)


def spans(places, lengths_row):
    ends = jnp.cumsum(lengths_row)
    past = (places[:, None] >= ends[None, :]).astype(jnp.int32)
    begin = jnp.sum(past * lengths_row[None, :], axis=1)
    before = (places[:, None] >= (ends - lengths_row)[None, :]).astype(jnp.int32)
    end = jnp.sum(before * lengths_row[None, :], axis=1)
    valid = places < ends[-1]
    return (jnp.where(valid, begin, 0), jnp.where(valid, end, 0), places - begin, valid)


def key_range(begin, end, block_q, block_k):
    begin_blocks = jnp.where(end > begin, begin, jnp.int32(1 << 30)).reshape(-1, block_q)
    high = (jnp.max(end.reshape(-1, block_q), axis=1) + block_k - 1) // block_k
    low = jnp.minimum(jnp.min(begin_blocks, axis=1) // block_k, high)
    return (low, high)


def rotary_tables(offset, head_count):
    half = HEAD_WIDTH // 2
    inverse = 160000.0 ** (-2.0 * jnp.arange(half, dtype=jnp.float32) / HEAD_WIDTH)
    angles = offset.astype(jnp.float32)[:, None] * inverse[None, :]
    cosine, sine = (jnp.cos(angles), jnp.sin(angles))
    return (
        jnp.concatenate([cosine, cosine] * head_count, axis=1),
        jnp.concatenate([sine, -sine] * head_count, axis=1),
    )


def toggled(index, bit):
    return index + bit - 2 * bit * ((index // bit) % 2)


def gather_kernel(shapes, projects, *refs):
    count = len(shapes)
    shard_refs, refs = (refs[:count], refs[count:])
    if projects:
        act_ref, qkv_ref, cosine_ref, sine_ref = refs[:4]
        heads_ref = refs[4 + count]
        columns_ref, held_ref, load_sem, head_send, head_recv, own_sem = refs[count + 8 :]
        refs = refs[4 : 4 + count] + refs[count + 5 : count + 8]
    full_refs = refs[:count]
    send_sem, recv_sem, local_sem = refs[count:]
    shards = lax.axis_size("fsdp")
    slices = lax.axis_size("ctx") // 2
    own_ctx, own_shard = (lax.axis_index("ctx"), lax.axis_index("fsdp"))
    core, chip = (own_ctx % 2, own_ctx // 2)
    barrier = pltpu.get_barrier_semaphore()
    partners = [{"fsdp": toggled(own_shard, bit)} for bit in (1, 2)]
    partners += [{"ctx": toggled(own_ctx, bit)} for bit in (1, 2, 4)]

    def owner_at(relation):
        owner = own_ctx
        for bit in (1, 2, 4):
            if relation & bit:
                owner = toggled(owner, bit)
        return owner

    if projects:
        partners += [{"ctx": owner_at(relation)} for relation in (3, 5, 6, 7)]
    for partner in partners:
        pl.semaphore_signal(
            barrier, inc=1, device_id=partner, device_id_type=pl.DeviceIdType.MESH
        )
    pl.semaphore_wait(barrier, len(partners))
    to_one, to_two, to_core, to_x, to_y = partners[:5]

    def shard_at(step):
        if step == 0:
            return own_shard
        if step == 3:
            return toggled(toggled(own_shard, 1), 2)
        return toggled(own_shard, step)

    def region(ref, weight, step, chip_at, half):
        if shapes[weight] == "small":
            return ref if len(ref.shape) == 2 else ref.at[shard_at(step)]
        if shapes[weight] == "rows":
            rows = ref.shape[-2]
            span = pl.ds(0, rows) if half is None else pl.ds(half * (rows // 2), rows // 2)
            if len(ref.shape) == 4:
                return ref.at[core, chip_at, span, :]
            return ref.at[shard_at(step), core, chip_at, span, :]
        rows = ref.shape[-2]
        first = (rows // 2) // 16 * 16
        spans_of = {None: pl.ds(0, rows), 0: pl.ds(0, first), 1: pl.ds(first, rows - first)}
        width = ref.shape[-1] // (2 * slices)
        columns = pl.ds(pl.multiple_of((core * slices + chip_at) * width, width), width)
        if len(ref.shape) == 2:
            return ref.at[spans_of[half], columns]
        return ref.at[shard_at(step), spans_of[half], columns]

    def core_region(ref, weight, step):
        if shapes[weight] == "rows":
            return ref.at[shard_at(step), core]
        width = ref.shape[-1] // 2
        return ref.at[shard_at(step), :, pl.ds(pl.multiple_of(core * width, width), width)]

    pending = []

    def send(source, target, slot, partner):
        copy = pltpu.make_async_remote_copy(
            src_ref=source,
            dst_ref=target,
            send_sem=send_sem.at[slot],
            recv_sem=recv_sem.at[slot],
            device_id=partner,
            device_id_type=pl.DeviceIdType.MESH,
        )
        copy.start()
        pending.append(copy)
        return copy

    copies = {}
    local = []

    def slot_of(weight, step, kind):
        return (weight * 3 + step - 1) * 8 + kind

    def shard_sends(weight):
        source = region(shard_refs[weight], weight, 0, chip, None)
        target = region(full_refs[weight], weight, 0, chip, None)
        copies[weight, 2, 0] = send(source, target, slot_of(weight, 2, 0), to_two)
        copies[weight, 1, 0] = send(source, target, slot_of(weight, 1, 0), to_one)
        target = full_refs[weight].at[own_shard]
        copy = pltpu.make_async_copy(shard_refs[weight], target, local_sem.at[weight])
        copy.start()
        local.append(copy)

    def shard_forward(weight):
        copies[weight, 2, 0].wait_recv()
        piece = region(full_refs[weight], weight, 2, chip, None)
        copies[weight, 3, 0] = send(piece, piece, slot_of(weight, 3, 0), to_one)

    def plane_sends(weight, step):
        lead = region(full_refs[weight], weight, step, chip, 0)
        rest = region(full_refs[weight], weight, step, chip, 1)
        for kind, piece, partner in ((1, lead, to_x), (2, rest, to_y), (3, lead, to_y), (4, rest, to_x)):
            copies[weight, step, kind] = send(piece, piece, slot_of(weight, step, kind), partner)

    def plane_forward(weight, step):
        copies[weight, step, 1].wait_recv()
        lead = region(full_refs[weight], weight, step, toggled(chip, 1), 0)
        copies[weight, step, 5] = send(lead, lead, slot_of(weight, step, 5), to_y)
        copies[weight, step, 2].wait_recv()
        rest = region(full_refs[weight], weight, step, toggled(chip, 2), 1)
        copies[weight, step, 6] = send(rest, rest, slot_of(weight, step, 6), to_x)

    def core_send(weight, step):
        for kind in (3, 4, 5, 6):
            copies[weight, step, kind].wait_recv()
        piece = core_region(full_refs[weight], weight, step)
        copies[weight, step, 7] = send(piece, piece, slot_of(weight, step, 7), to_core)

    chip_order = (3, 1, 2, 0)

    def start_loads():
        loads = {}
        for chip_bits in chip_order:
            owner_chip = owner_at(2 * chip_bits) // 2
            for part in range(3):
                width = columns_ref.shape[2] // 3
                total = qkv_ref.shape[1] // 3
                first = pl.multiple_of(part * total + owner_chip * width, width)
                loads[chip_bits, part] = pltpu.make_async_copy(
                    qkv_ref.at[:, pl.ds(first, width)],
                    columns_ref.at[chip_bits, :, pl.ds(part * width, width)],
                    load_sem.at[chip_bits * 3 + part],
                )
                loads[chip_bits, part].start()
        return loads

    def project(chip_bits, loads):
        for part in range(3):
            loads[chip_bits, part].wait()
        rows, own_width = (act_ref.shape[0], held_ref.shape[2] // 3)
        product = jnp.dot(
            act_ref[...], columns_ref[chip_bits], preferred_element_type=jnp.float32
        )
        for core_at in (0, 1):
            slot = 2 * chip_bits + core + core_at - 2 * core * core_at
            for part in range(3):
                first = (2 * part + core_at) * own_width
                piece = product[:, first : first + own_width]
                if part < 2:
                    half = HEAD_WIDTH // 2
                    turned = []
                    for base in range(0, own_width, HEAD_WIDTH):
                        turned += [piece[:, base + half : base + HEAD_WIDTH], piece[:, base : base + half]]
                    piece = piece * cosine_ref[...] - jnp.concatenate(turned, axis=1) * sine_ref[...]
                held_ref[slot, :, part * own_width : (part + 1) * own_width] = piece.astype(jnp.bfloat16)
        target = heads_ref.at[pl.ds(pl.multiple_of(own_ctx * rows, rows), rows), :]
        for core_bit in (0, 1):
            relation = 2 * chip_bits + core_bit
            if relation == 0:
                copy = pltpu.make_async_copy(held_ref.at[0], target, own_sem.at[0])
                copy.start()
                local.append(copy)
                continue
            copy = pltpu.make_async_remote_copy(
                src_ref=held_ref.at[relation],
                dst_ref=target,
                send_sem=head_send.at[relation],
                recv_sem=head_recv.at[relation],
                device_id={"ctx": owner_at(relation)},
                device_id_type=pl.DeviceIdType.MESH,
            )
            copy.start()
            pending.append(copy)
            arriving.append(copy)

    arriving = []
    sent = 1
    if projects:
        loads = start_loads()
        for weight in range(count):
            shard_sends(weight)
        sent = count
        for chip_bits in chip_order:
            project(chip_bits, loads)
    else:
        shard_sends(0)
    for weight in range(count):
        if weight + 1 >= sent and weight + 1 < count:
            shard_sends(weight + 1)
        shard_forward(weight)
        copies[weight, 1, 0].wait_recv()
        if shapes[weight] == "small":
            copies[weight, 3, 0].wait_recv()
            continue
        plane_sends(weight, 1)
        plane_sends(weight, 2)
        copies[weight, 3, 0].wait_recv()
        plane_sends(weight, 3)
        for step in (1, 2, 3):
            plane_forward(weight, step)
        if weight > 0 and shapes[weight - 1] != "small":
            for step in (1, 2, 3):
                core_send(weight - 1, step)
    for step in (1, 2, 3):
        core_send(count - 1, step)
    for weight in range(count):
        if shapes[weight] != "small":
            for step in (1, 2, 3):
                copies[weight, step, 7].wait_recv()
    for copy in arriving:
        copy.wait_recv()
    for copy in pending:
        copy.wait_send()
    for copy in local:
        copy.wait()


def gather_weights(weights, projection=None):
    shards, ctx_count = (lax.axis_size("fsdp"), lax.axis_size("ctx"))
    slices = ctx_count // 2
    shapes, views, outs = ([], [], [])
    for weight in weights:
        rows, columns = weight.shape
        if rows % (32 * ctx_count) == 0:
            shapes.append("rows")
            views.append(weight.reshape(2, slices, rows // ctx_count, columns))
            outs.append((shards, 2, slices, rows // ctx_count, columns))
        elif rows == 16:
            shapes.append("small")
            views.append(weight)
            outs.append((shards, rows, columns))
        elif columns % (128 * ctx_count) == 0 and rows % 16 == 0:
            shapes.append("columns")
            views.append(weight)
            outs.append((shards, rows, columns))
    if shards != 4 or ctx_count != 8 or len(views) < len(weights):
        return [lax.all_gather(weight, "fsdp", axis=0, tiled=True) for weight in weights]
    slots = len(views) * 24
    vmem, anywhere, dma = (
        pl.BlockSpec(memory_space=pltpu.VMEM),
        pl.BlockSpec(memory_space=pl.ANY),
        pltpu.SemaphoreType.DMA,
    )
    in_specs = [vmem] * len(views)
    scratch = [dma((slots,)), dma((slots,)), dma((len(views),))]
    if projection is not None:
        act_attn, qkv_full = projection[:2]
        rows, own_columns = (act_attn.shape[0], qkv_full.shape[1] // ctx_count)
        views += list(projection)
        in_specs += [vmem, anywhere, vmem, vmem]
        outs.append((ctx_count * rows, own_columns))
        scratch += [
            pltpu.VMEM((slices, qkv_full.shape[0], 2 * own_columns), jnp.bfloat16),
            pltpu.VMEM((ctx_count, rows, own_columns), jnp.bfloat16),
            dma((3 * slices,)),
            dma((ctx_count,)),
            dma((ctx_count,)),
            dma((1,)),
        ]
    held = pl.pallas_call(
        functools.partial(gather_kernel, shapes, projection is not None),
        out_shape=tuple(jax.ShapeDtypeStruct(out, jnp.bfloat16) for out in outs),
        in_specs=in_specs,
        out_specs=tuple(anywhere for out in outs),
        scratch_shapes=scratch,
        compiler_params=pltpu.CompilerParams(
            collective_id=0 if projection is None else 2,
            has_side_effects=True,
            vmem_limit_bytes=60 * 1024 * 1024,
        ),
        name="gather_weights" if projection is None else "gather_and_project",
    )(*views)
    return [whole.reshape(-1, whole.shape[-1]) for whole in held]


def pair_steps(plan, lead_rows, left_refs, right_refs, turned_refs, whole_refs, sems, core, pending, send):
    pair_send, pair_recv, near_sem = sems
    to_core = {"ctx": toggled(lax.axis_index("ctx"), 1)}

    def send_core(source, target, sent, got, start=True):
        return send(source, target, sent, got, to_core, start)

    rows = left_refs[0].shape[0] if left_refs else 0
    pairs = []

    def begin(w):
        entry = plan[w]
        span, right = (plan_span(entry), right_refs[w])
        own_part, other_part = (whole_refs[w].at[pl.ds(0, rows)], whole_refs[w].at[pl.ds(rows, rows)])

        def exchange(own_half, other_half, start=True):
            near = pltpu.make_async_copy(own_half, own_part, near_sem.at[w])
            if start:
                near.start()
            sems = (pair_send.at[2 * w], pair_recv.at[2 * w])
            return [near, send_core(other_half, other_part, *sems, start)]

        if entry[5]:
            ways = [exchange(right[at], right[1 - at], False) for at in (0, 1)]
            for at in (0, 1):

                @pl.when(core == at)
                def start():
                    for copy in ways[at]:
                        copy.start()

            pairs.append(ways[0])
            pending.append(ways[0][1])
        else:
            halves = [
                right.at[:, pl.ds(pl.multiple_of(at * span, span), span)] for at in (core, 1 - core)
            ]
            pairs.append(exchange(*halves))

    def turn(w):
        left, turned = (left_refs[w], turned_refs[w])
        block = 512
        for first in range(0, left.shape[1], block):
            last = min(first + block, left.shape[1])
            turned[first:last, :rows] = (
                left[:, first:last].astype(jnp.float32).T.astype(jnp.bfloat16)
            )
        pairs[w].append(
            send_core(
                turned.at[:, pl.ds(0, rows)],
                turned.at[:, pl.ds(rows, rows)],
                pair_send.at[2 * w + 1],
                pair_recv.at[2 * w + 1],
            )
        )

    def multiply(w, t, first, second):
        kind, count, width, deep, halves, parted = plan[w]
        if t == 0:
            near, far, turned = pairs[w]
            near.wait()
            far.wait_recv()
            turned.wait_recv()

        def each(z, carried):
            left = turned_refs[w][pl.ds(pl.multiple_of(z * deep, 16), deep), :]
            if kind == "rows":
                last = min((t + 1) * width, whole_refs[w].shape[1])
                part = jnp.dot(
                    left, whole_refs[w][:, t * width : last], preferred_element_type=jnp.float32
                ).astype(jnp.bfloat16)
                if last < (t + 1) * width:
                    empty = jnp.zeros((deep, (t + 1) * width - last), jnp.bfloat16)
                    part = jnp.concatenate([part, empty], axis=1)
                piece_rows = first.shape[3]
                for s in range(4):
                    first[z, s // 2, s % 2] = part[2 * s * piece_rows : (2 * s + 1) * piece_rows]
                    second[z, s // 2, s % 2] = part[(2 * s + 1) * piece_rows : (2 * s + 2) * piece_rows]
            else:
                part = jnp.dot(
                    left, whole_refs[w][...], preferred_element_type=jnp.float32
                ).astype(jnp.bfloat16)
                for s in range(4):
                    piece = part[:, s * width : (s + 1) * width]
                    first[z, s // 2, s % 2] = piece[:lead_rows]
                    second[z, s // 2, s % 2] = piece[lead_rows:]
            return carried

        lax.fori_loop(0, 4, each, 0)

    return (begin, turn, multiply)


def remote_send(pending):
    def send(source, target, sent, got, partner, start=True):
        copy = pltpu.make_async_remote_copy(
            src_ref=source,
            dst_ref=target,
            send_sem=sent,
            recv_sem=got,
            device_id=partner,
            device_id_type=pl.DeviceIdType.MESH,
        )
        if start:
            copy.start()
            pending.append(copy)
        return copy

    return send


def product_kernel(plan, lead_rows, *refs):
    groups, places = early_places(plan)
    weights, outs = (len(plan), 4 * len(groups))
    left_refs, refs = (refs[:weights], refs[weights:])
    right_refs = []
    for entry in plan:
        held = 2 if entry[5] else 1
        right_refs.append(refs[:held] if held == 2 else refs[0])
        refs = refs[held:]
    out_refs = refs[:outs]
    scratch = list(refs[outs:])
    turned_refs = [scratch.pop(0) for weight in plan]
    whole_refs = [scratch.pop(0) for weight in plan]
    chunks = [(w, t) for w, entry in enumerate(plan) for t in range(entry[1])]
    held = [(scratch.pop(0), scratch.pop(0)) for chunk in chunks]
    pair_send, pair_recv, near_sem, store_sem = scratch
    own_ctx = lax.axis_index("ctx")
    core, chip = (own_ctx % 2, own_ctx // 2)
    own_x, own_y = (chip % 2, chip // 2)
    to_core = {"ctx": toggled(own_ctx, 1)}
    barrier = pltpu.get_barrier_semaphore()
    pl.semaphore_signal(barrier, inc=1, device_id=to_core, device_id_type=pl.DeviceIdType.MESH)
    pl.semaphore_wait(barrier, 1)
    pending = []
    send = remote_send(pending)
    begin, turn, multiply = pair_steps(
        plan,
        lead_rows,
        left_refs,
        right_refs,
        turned_refs,
        whole_refs,
        (pair_send, pair_recv, near_sem),
        core,
        pending,
        send,
    )
    for w in range(weights):
        begin(w)
        turn(w)
    stores = []
    for number, (w, t) in enumerate(chunks):
        first, second = held[number]
        multiply(w, t, first, second)
        group, offset = places[number]
        sides = (
            lambda at: first.at[:, at, own_x],
            lambda at: first.at[:, at, 1 - own_x],
            lambda at: second.at[:, own_y, at],
            lambda at: second.at[:, 1 - own_y, at],
        )
        for side, source_at in enumerate(sides):
            for at in (0, 1):
                copy = pltpu.make_async_copy(
                    source_at(at),
                    out_refs[4 * group + side].at[at, :, :, pl.ds(offset, plan[w][2])],
                    store_sem.at[8 * number + 2 * side + at],
                )
                copy.start()
                stores.append(copy)
    for copy in stores:
        copy.wait()
    for copy in pending:
        copy.wait_send()


def weight_plan(kind, left, right, count):
    deep = left.shape[1] // 4
    if kind == "rows":
        parted = isinstance(right, tuple)
        span = right[0].shape[1] if parted else right.shape[1] // 2
        width = -(-span // (128 * count)) * 128
        return (kind, count, width, deep, (deep // 8, deep // 8), span if parted else 0)
    lead_rows = deep // 2 // 16 * 16
    return (kind, count, right.shape[-1] // 8, deep, (lead_rows, deep - lead_rows), 0)


def early_places(plan):
    groups, places = ([], [])
    for kind, count, width, deep, halves, parted in plan:
        found = [at for at, group in enumerate(groups) if group[0] == halves]
        if not found:
            groups.append([halves, 0])
            found = [len(groups) - 1]
        for chunk in range(count):
            places.append((found[0], groups[found[0]][1]))
            groups[found[0]][1] += width
    return (groups, places)


def plan_span(entry):
    return entry[1] * entry[2] if entry[0] == "rows" else 4 * entry[2]


def plan_lead(plan):
    return max([0] + [entry[4][0] for entry in plan if entry[0] == "columns"])


def pair_scratch(plan, tokens):
    turned = [pltpu.VMEM((4 * entry[3], 2 * tokens), jnp.bfloat16) for entry in plan]
    return turned + [
        pltpu.VMEM((2 * tokens, entry[5] or plan_span(entry)), jnp.bfloat16) for entry in plan
    ]


def early_sums(products, held):
    plan = [weight_plan(*product) for product in products]
    lefts, rights = ([product[1] for product in products], [product[2] for product in products])
    vmem, anywhere, dma = (
        pl.BlockSpec(memory_space=pltpu.VMEM),
        pl.BlockSpec(memory_space=pl.ANY),
        pltpu.SemaphoreType.DMA,
    )
    rights = [part for right in rights for part in (right if isinstance(right, tuple) else [right])]
    groups = early_places(plan)[0]
    outs, units = ([], [])
    for halves, columns in groups:
        for half in halves:
            outs += [jax.ShapeDtypeStruct((2, 4, half, columns), jnp.bfloat16)] * 2
    for kind, count, width, deep, halves, parted in plan:
        for chunk in range(count):
            units += [pltpu.VMEM((4, 2, 2, half, width), jnp.bfloat16) for half in halves]
    chunk_count = sum(entry[1] for entry in plan)
    scratch = pair_scratch(plan, lefts[0].shape[0]) + units
    scratch += [dma((2 * len(plan),)), dma((2 * len(plan),)), dma((len(plan),)), dma((8 * chunk_count,))]
    sides = pl.pallas_call(
        functools.partial(product_kernel, plan, plan_lead(plan)),
        out_shape=tuple(outs),
        in_specs=[vmem] * len(plan) + [anywhere] * len(rights),
        out_specs=(anywhere,) * len(outs),
        scratch_shapes=scratch,
        compiler_params=pltpu.CompilerParams(
            collective_id=3, has_side_effects=True, vmem_limit_bytes=60 * 1024 * 1024
        ),
        name="early_products",
    )(*lefts, *rights)
    held, sides = lax.optimization_barrier((held, sides))
    arrays = []
    for group in range(len(groups)):
        for part, bit in ((0, 2), (2, 4)):
            kept, sent = sides[4 * group + part : 4 * group + part + 2]
            arrays.append((kept, swap(sent, "ctx", bit)))
    return (held, (plan, arrays))


def second_step(held, early):
    plan, arrays = early
    held, arrays = lax.optimization_barrier((held, arrays))
    chip = lax.axis_index("ctx") // 2
    flat = []
    for at, (kept, arrived) in sorted(enumerate(arrays), key=lambda pair: (-(pair[0] // 2), pair[0])):
        bit, own = ((4, chip // 2), (2, chip % 2))[at % 2]
        other = [
            lax.dynamic_index_in_dim(side, 1 - own, 0, keepdims=False).astype(jnp.float32)
            for side in (kept, arrived)
        ]
        twice = swap((other[0] + other[1]).astype(jnp.bfloat16), "ctx", bit)
        flat.append((at, [kept, arrived, twice]))
    flat = [side for at, sides in sorted(flat, key=lambda pair: pair[0]) for side in sides]
    return (held, (plan, flat))


def sum_kernel(early, late, lead_rows, *refs):
    weights, products = (len(early) + len(late), len(late))
    left_refs, right_refs = (refs[:products], refs[products : 2 * products])
    refs = refs[2 * products :]
    groups, places = early_places(early)
    early_refs, refs = (refs[: 6 * len(groups)], refs[6 * len(groups) :])
    small_ref, out_refs, small_out = (refs[0], refs[1 : weights + 1], refs[weights + 1])
    scratch = list(refs[weights + 2 :])
    turned_refs = [scratch.pop(0) for weight in late]
    whole_refs = [scratch.pop(0) for weight in late]
    plan = early + late
    chunks = [(w, t) for w, entry in enumerate(plan) for t in range(entry[1])]
    early_count = sum(entry[1] for entry in early)
    order = sorted(range(early_count), key=lambda number: (-chunks[number][0], number))
    units = {}
    for number in range(len(chunks)):
        for half in (0, 1):
            units[number, half] = [scratch.pop(0) for stage in range(5)]
    small_held = scratch.pop(0)
    send_sem, recv_sem, local_sem, load_sem, pair_send, pair_recv, small_send, small_recv, near_sem = scratch
    own_ctx, own_shard = (lax.axis_index("ctx"), lax.axis_index("fsdp"))
    core, chip = (own_ctx % 2, own_ctx // 2)
    own_x, own_y = (chip % 2, chip // 2)
    low_bit, high_bit = (own_shard % 2, own_shard // 2)
    loads = {}
    for number in order:
        w, (group, offset) = (chunks[number][0], places[number])
        for half in (0, 1):
            own = own_y if half == 0 else own_x
            kept, arrived, twice = early_refs[6 * group + 3 * half : 6 * group + 3 * half + 3]
            columns = pl.ds(offset, plan[w][2])
            sources = (kept.at[own, :, :, columns], arrived.at[own, :, :, columns], twice.at[:, :, columns])
            for at, source in enumerate(sources):
                slot = (number * 2 + half) * 3 + at
                copy = pltpu.make_async_copy(source, units[number, half][at], load_sem.at[slot])
                copy.start()
                loads[number, half, at] = copy
    partners = [{"ctx": toggled(own_ctx, bit)} for bit in (1, 2, 4)]
    partners += [{"fsdp": toggled(own_shard, bit)} for bit in (1, 2)]
    barrier = pltpu.get_barrier_semaphore()
    for partner in partners:
        pl.semaphore_signal(
            barrier, inc=1, device_id=partner, device_id_type=pl.DeviceIdType.MESH
        )
    pl.semaphore_wait(barrier, len(partners))
    to_core, to_x, to_y, to_one, to_two = partners
    pending = []
    send = remote_send(pending)
    begin, turn, multiply = pair_steps(
        late,
        lead_rows,
        left_refs,
        right_refs,
        turned_refs,
        whole_refs,
        (pair_send, pair_recv, near_sem),
        core,
        pending,
        send,
    )
    for w in range(len(late)):
        begin(w)
    copies = {}

    def hop(number, half, stage, source, target, partner):
        slot = (number * 2 + half) * 8 + stage
        copies[number, half, stage] = send(
            source, target, send_sem.at[slot], recv_sem.at[slot], partner
        )

    def stage_one(number):
        w, t = chunks[number]
        multiply(w - len(early), t, units[number, 0][0], units[number, 1][0])
        hop(number, 0, 0, units[number, 0][0].at[:, :, 1 - own_x], units[number, 0][1], to_x)
        hop(number, 1, 0, units[number, 1][0].at[:, 1 - own_y], units[number, 1][1], to_y)

    def add(target, source_at, count):
        def each(i, carried):
            target[i] = (
                target[i].astype(jnp.float32) + source_at(i).astype(jnp.float32)
            ).astype(jnp.bfloat16)
            return carried

        lax.fori_loop(0, count, each, 0)

    def stage_two(number):
        held, got = (units[number, 0][0], units[number, 0][1])
        copies[number, 0, 0].wait_recv()
        add(got, lambda z: held[z, :, own_x], 4)
        held_b, got_b = (units[number, 1][0], units[number, 1][1])
        copies[number, 1, 0].wait_recv()
        add(got_b, lambda z: held_b[z, own_y], 4)
        hop(number, 0, 1, got.at[:, 1 - own_y], units[number, 0][2], to_y)
        hop(number, 1, 1, got_b.at[:, 1 - own_x], units[number, 1][2], to_x)

    def stage_three(number):
        for half in (0, 1):
            kept, held, got = units[number, half][:3]
            own = own_y if half == 0 else own_x
            if number < early_count:
                for at in range(3):
                    loads[number, half, at].wait()
                add(held, lambda z: kept[z], 4)
                add(got, lambda z: held[z], 4)
            else:
                copies[number, half, 1].wait_recv()
                add(got, lambda z: held[z, own], 4)
        for half in (0, 1):
            got = units[number, half][2]
            for high in (0, 1):
                hop(
                    number,
                    half,
                    2 + 4 * high,
                    got.at[2 * high + 1 - low_bit],
                    units[number, half][3].at[high],
                    to_one,
                )

    def stage_four(number):
        for half in (0, 1):
            held, got = (units[number, half][2], units[number, half][3])
            copies[number, half, 2].wait_recv()
            copies[number, half, 6].wait_recv()
            add(got, lambda high: held[2 * high + low_bit], 2)
        for half in (0, 1):
            got = units[number, half][3]
            hop(number, half, 3, got.at[1 - high_bit], units[number, half][4].at[0], to_two)

    def final_region(number, half, chip_at):
        w, t = chunks[number]
        kind, count, width = plan[w][:3]
        deep = units[number, half][4].shape[1]
        if kind == "rows":
            start = pl.multiple_of((2 * chip_at + half) * deep, deep)
            column = pl.multiple_of((core * count + t) * width, width)
            return out_refs[w].at[pl.ds(start, deep), pl.ds(column, width)]
        column = pl.multiple_of((core * 4 + chip_at) * width, width)
        return out_refs[w].at[pl.ds(half * lead_rows, deep), pl.ds(column, width)]

    local = {}

    def stage_five(number):
        for half in (0, 1):
            held, got = (units[number, half][3], units[number, half][4])
            copies[number, half, 3].wait_recv()
            add(got, lambda i: held[high_bit], 1)
        for half in (0, 1):
            got = units[number, half][4].at[0]
            target = final_region(number, half, chip)
            hop(number, half, 4, got, target, to_x if half == 0 else to_y)
            hop(number, half, 5, got, target, to_y if half == 0 else to_x)
            copy = pltpu.make_async_copy(got, target, local_sem.at[number * 2 + half])
            copy.start()
            local[number, half] = copy

    def stage_six(number):
        for half in (0, 1):
            copies[number, half, 4].wait_recv()
            piece = final_region(number, half, toggled(chip, 1 if half == 0 else 2))
            hop(number, half, 7, piece, piece, to_y if half == 0 else to_x)

    def stage_seven(number):
        w, t = chunks[number]
        kind, count, width = plan[w][:3]
        for half in (0, 1):
            copies[number, half, 5].wait_recv()
            copies[number, half, 7].wait_recv()
            local[number, half].wait()
        span = width if kind == "rows" else 4 * width
        at = core * count + t if kind == "rows" else core
        piece = out_refs[w].at[:, pl.ds(pl.multiple_of(at * span, span), span)]
        slot = len(chunks) * 16 + number
        copies[number, 2, 0] = send(
            piece, piece, send_sem.at[slot], recv_sem.at[slot], to_core
        )

    small_copies = []

    def small_step(step):
        if step > 0:
            small_copies[step - 1].wait_recv()
            small_held[2 * step] = small_held[2 * step - 2] + small_held[2 * step - 1]
            if step == 3:
                small_out[0] = small_held[6]
        else:
            small_held[0] = small_ref[...]
        if step < 5:
            small_copies.append(
                send(
                    small_held.at[2 * step],
                    small_held.at[2 * step + 1],
                    small_send.at[step],
                    small_recv.at[step],
                    partners[step],
                )
            )
        else:
            small_out[1] = small_held[10]

    stages = (stage_one, stage_two, stage_three, stage_four, stage_five, stage_six, stage_seven)
    small_at = 0
    stage_three(order[0])
    for w in range(len(late)):
        turn(w)
    for tick in range(len(chunks) + len(stages)):
        for lag, stage in enumerate(stages):
            for number in range(len(chunks)):
                if number >= early_count:
                    due = number - early_count + lag == tick
                else:
                    rank = order.index(number)
                    due = rank - 2 + lag == tick and lag >= 2 and rank + lag > 2
                if due:
                    stage(number)
        if small_at < 6:
            small_step(small_at)
            small_at += 1
    for number in range(len(chunks)):
        copies[number, 2, 0].wait_recv()
    for copy in pending:
        copy.wait_send()


def sum_weights(early, early_arrays, products, small):
    late = [weight_plan(*product) for product in products]
    lefts, rights = ([product[1] for product in products], [product[2] for product in products])
    plan = early + late
    pieces = []
    for w, (kind, count, width, deep, halves, parted) in enumerate(plan):
        leads = [(4, 2, 2), (4, 2), (4,), (2,), (1,)]
        if w < len(early):
            leads[:2] = [(4,), (4,)]
        for chunk in range(count):
            for half in halves:
                pieces += [pltpu.VMEM(lead + (half, width), jnp.bfloat16) for lead in leads]
    outs = [jax.ShapeDtypeStruct((entry[3], 2 * plan_span(entry)), jnp.bfloat16) for entry in plan]
    chunk_count = sum(entry[1] for entry in plan)
    scratch = pair_scratch(late, lefts[0].shape[0]) + pieces
    dma = pltpu.SemaphoreType.DMA
    scratch += [pltpu.VMEM((11,) + small.shape, jnp.float32)]
    slots = chunk_count * 17
    scratch += [dma((slots,)), dma((slots,)), dma((2 * chunk_count,)), dma((6 * chunk_count,))]
    scratch += [dma((2 * len(late),)), dma((2 * len(late),)), dma((5,)), dma((5,)), dma((len(late),))]
    vmem, anywhere = (
        pl.BlockSpec(memory_space=pltpu.VMEM),
        pl.BlockSpec(memory_space=pl.ANY),
    )
    return pl.pallas_call(
        functools.partial(sum_kernel, early, late, plan_lead(plan)),
        out_shape=tuple(outs) + (jax.ShapeDtypeStruct((2,) + small.shape, jnp.float32),),
        in_specs=[vmem] * len(late) + [anywhere] * (len(late) + len(early_arrays)) + [vmem],
        out_specs=(anywhere,) * len(plan) + (vmem,),
        scratch_shapes=scratch,
        compiler_params=pltpu.CompilerParams(
            collective_id=1, has_side_effects=True, vmem_limit_bytes=60 * 1024 * 1024
        ),
        name="sum_weights",
    )(*lefts, *rights, *early_arrays, small)


def layer_norm(rows_in, gain_vec):
    row_mean = jnp.mean(rows_in, axis=-1, keepdims=True)
    centred = rows_in - row_mean
    variance = jnp.mean(centred * centred, axis=-1, keepdims=True)
    return centred * lax.rsqrt(variance + norm_eps) * gain_vec


def rotate(projected, cosine, sine):
    row_count, width = projected.shape
    half_width = HEAD_WIDTH // 2
    by_head = projected.reshape(row_count, width // HEAD_WIDTH, HEAD_WIDTH)
    turned = jnp.concatenate([by_head[..., half_width:], by_head[..., :half_width]], axis=-1)
    return (by_head * cosine[:, None, :] - turned * sine[:, None, :]).reshape(row_count, width)


def swap(value, axis, bit):
    pairs = [(i, i ^ bit) for i in range(lax.axis_size(axis))]
    return lax.ppermute(value, axis, pairs)


def bit_of(axis, bit):
    return (lax.axis_index(axis) // bit) % 2 == 1


def bits_below(count):
    return [1 << i for i in range(count.bit_length() - 1)]


def reduce_pieces(pieces, labels, order):
    labels = list(labels)
    for axis, bit in order:
        at = labels.index((axis, bit))
        labels.pop(at)
        first = lax.index_in_dim(pieces, 0, at, keepdims=False)
        second = lax.index_in_dim(pieces, 1, at, keepdims=False)
        upper = bit_of(axis, bit)
        arrived = swap(jnp.where(upper, first, second), axis, bit)
        kept = jnp.where(upper, second, first)
        pieces = (kept.astype(jnp.float32) + arrived.astype(jnp.float32)).astype(jnp.bfloat16)
    return pieces


def gather_pieces(piece, labels, order):
    held = []
    for axis, bit in reversed(order):
        arrived = swap(piece, axis, bit)
        upper = bit_of(axis, bit)
        held = [label for label in labels if label in held or label == (axis, bit)]
        piece = jnp.stack(
            [jnp.where(upper, arrived, piece), jnp.where(upper, piece, arrived)],
            axis=held.index((axis, bit)),
        )
    return piece


def keep_and_send(first, second):
    upper = bit_of("ctx", 1)
    return (jnp.where(upper, second, first), jnp.where(upper, first, second))


def core_product(left, first, second):
    kept, sent = keep_and_send(first, second)
    left_all = jnp.concatenate([left, swap(left, "ctx", 1)], axis=0)
    right_all = jnp.concatenate([kept, swap(sent, "ctx", 1)], axis=0)
    return lax.dot_general(
        left_all, right_all, (((0,), (0,)), ((), ())), preferred_element_type=jnp.float32
    ).astype(jnp.bfloat16)


def shard_sum(product, by_columns):
    shards = lax.axis_size("fsdp")
    slices = lax.axis_size("ctx") // 2
    rows, columns = product.shape
    shard_labels = [("fsdp", bit) for bit in reversed(bits_below(shards))]
    slice_labels = [("ctx", 2 * bit) for bit in reversed(bits_below(slices))]
    if by_columns:
        cut = product.reshape(shards, rows // shards, slices, columns // slices)
        cut = jnp.transpose(cut, (0, 2, 1, 3))
    else:
        cut = product.reshape(shards, slices, rows // shards // slices, columns)
    parts = []
    half = cut.shape[2] // 2
    tail = list(reversed(shard_labels))
    for lead, orders in (
        (cut[:, :, :half], list(reversed(slice_labels))),
        (cut[:, :, half:], slice_labels),
    ):
        pieces = lead.reshape((2,) * (len(shard_labels) + len(slice_labels)) + lead.shape[2:])
        piece = reduce_pieces(pieces, shard_labels + slice_labels, orders + tail)
        whole = gather_pieces(piece, slice_labels, orders)
        parts.append(whole.reshape((slices,) + piece.shape))
    both = jnp.concatenate(parts, axis=1)
    if by_columns:
        return jnp.transpose(both, (1, 0, 2)).reshape(rows // shards, columns)
    return both.reshape(rows // shards, columns)


def join_cores(own):
    other = swap(own, "ctx", 1)
    upper = bit_of("ctx", 1)
    return jnp.concatenate(
        [jnp.where(upper, other, own), jnp.where(upper, own, other)], axis=1
    ).astype(jnp.float32)


def sum_over(value, axes):
    for axis in axes:
        for bit in bits_below(lax.axis_size(axis)):
            value = value + swap(value, axis, bit)
    return value


def own_shard(vector):
    width = vector.shape[0] // lax.axis_size("fsdp")
    return lax.dynamic_slice_in_dim(vector, lax.axis_index("fsdp") * width, width, 0)


def weight_sums(
    hidden,
    grad_mlp_low,
    act_mlp,
    grad_leading,
    grad_trailing,
    act_attn,
    grad_projected,
    attn_low,
    grad_attn_low,
    small,
    early,
):
    shards, ctx_count = (lax.axis_size("fsdp"), lax.axis_size("ctx"))
    rows, ff_width = hidden.shape
    model_width = act_mlp.shape[1]
    if early is None:
        half, half_three = (model_width // 2, 3 * model_width // 2)
        pairs = (
            (hidden, grad_mlp_low[:, :half], grad_mlp_low[:, half:]),
            (act_mlp, grad_leading, grad_trailing),
            (act_attn, grad_projected[:, :half_three], grad_projected[:, half_three:]),
            (attn_low, grad_attn_low[:, :half], grad_attn_low[:, half:]),
        )
        totals = [
            join_cores(shard_sum(core_product(*pair), at == 0)) for at, pair in enumerate(pairs)
        ]
        over_pack = sum_over(small, ("ctx",))
        return totals + [jnp.stack([over_pack, sum_over(over_pack, ("fsdp",))])]
    total_attn, total_in, total_out, total_qkv, small_sums = sum_weights(
        *early, [("rows", act_attn, grad_projected, 3)], small
    )
    padded = total_in.shape[1] // 2
    total_in = jnp.concatenate(
        [total_in[:, :ff_width], total_in[:, padded : padded + ff_width]], axis=1
    )
    return [
        total.astype(jnp.float32) for total in (total_out, total_in, total_qkv, total_attn)
    ] + [small_sums]


def weight_sums_early(
    hidden, grad_mlp_low, act_mlp, grad_leading, grad_trailing, attn_low, grad_attn_low, held
):
    shards, ctx_count = (lax.axis_size("fsdp"), lax.axis_size("ctx"))
    ff_width = hidden.shape[1]
    if shards != 4 or ctx_count != 8 or act_mlp.shape[1] % 1024 != 0 or ff_width % 64 != 0:
        return (held, None)
    return early_sums(
        [
            ("rows", attn_low, grad_attn_low, 1),
            ("rows", act_mlp, (grad_leading, grad_trailing), 3),
            ("columns", hidden, grad_mlp_low, 1),
        ],
        held,
    )


def per_device(
    inputs,
    cotangent,
    lengths,
    piece_route,
    gain_one,
    qkv_weight,
    attn_out,
    gain_two,
    geglu_in,
    geglu_out,
):
    ctx_count = lax.axis_size("ctx")
    own_index = lax.axis_index("ctx")
    row_count = inputs.shape[1]
    model_width = inputs.shape[2]
    piece_rows = row_count // ctx_count
    tokens = row_count * ctx_count
    own_heads = model_width // HEAD_WIDTH // ctx_count
    own_width = own_heads * HEAD_WIDTH
    block_q = math.gcd(tokens, 256)
    block_k = math.gcd(tokens, 512)
    lengths_row = lengths[0]
    own_route = piece_route[0, 0]
    slot_ids = jnp.arange(ctx_count, dtype=jnp.int32)
    outgoing = jnp.sum(
        slot_ids[None, :] * (own_route[None, :] == slot_ids[:, None]).astype(jnp.int32), axis=1
    )

    def exchange(blocks):
        return lax.all_to_all(blocks, "ctx", split_axis=0, concat_axis=0, tiled=True)

    def to_slots(rows_in):
        return jnp.take(rows_in.reshape(ctx_count, piece_rows, model_width), outgoing, axis=0)

    def to_heads(rows_in):
        by_heads = rows_in.reshape(row_count, ctx_count, -1)
        return exchange(jnp.transpose(by_heads, (1, 0, 2))).reshape(tokens, -1)

    def to_rows(heads_in):
        return exchange(heads_in.reshape(ctx_count, row_count, -1))

    both_arrived = exchange(
        jnp.concatenate([to_slots(inputs[0]), to_slots(cotangent[0])], axis=1)
    )
    arrived, grad_arrived = (both_arrived[:, :piece_rows], both_arrived[:, piece_rows:])
    residual = arrived.reshape(row_count, model_width).astype(jnp.float32)
    places = own_index * row_count + jnp.arange(row_count, dtype=jnp.int32)
    unused_begin, unused_end, offset, is_valid = spans(places, lengths_row)
    pack_begin, pack_end, unused_offset, unused_valid = spans(
        jnp.arange(tokens, dtype=jnp.int32), lengths_row
    )
    grad_final = jnp.where(
        is_valid[:, None], grad_arrived.reshape(row_count, model_width).astype(jnp.float32), 0.0
    )
    gains = jnp.pad(jnp.stack([gain_one, gain_two]), ((0, 14), (0, 0)))
    gains_full, qkv_full = gather_weights([gains, qkv_weight])
    gains_full = gains_full.reshape(-1, 16, gains.shape[1])
    gain_attn = gains_full[:, 0].reshape(-1).astype(jnp.float32)
    gain_mlp = gains_full[:, 1].reshape(-1).astype(jnp.float32)
    act_attn = layer_norm(residual, gain_attn).astype(jnp.bfloat16)
    later = [attn_out, geglu_in, geglu_out]
    row_cosine, row_sine = rotary_tables(offset, own_heads)
    if lax.axis_size("fsdp") == 4 and ctx_count == 8 and own_width == 128:
        attn_full, in_full, out_full, qkv_heads = gather_weights(
            later, (act_attn, qkv_full, row_cosine, row_sine)
        )
    else:
        attn_full, in_full, out_full = gather_weights(later)
        projected = jnp.dot(act_attn, qkv_full, preferred_element_type=jnp.float32)
        cosine, sine = rotary_tables(offset, 1)
        queries, keys = (
            rotate(projected[:, :model_width], cosine, sine).astype(jnp.bfloat16),
            rotate(projected[:, model_width : 2 * model_width], cosine, sine).astype(jnp.bfloat16),
        )
        values = projected[:, 2 * model_width :].astype(jnp.bfloat16)
        joined = jnp.stack(
            [part.reshape(row_count, ctx_count, own_width) for part in (queries, keys, values)], axis=2
        )
        qkv_heads = to_heads(joined.reshape(row_count, -1))
    low, high = key_range(pack_begin, pack_end, block_q, block_k)
    pack_begin, pack_end = (pack_begin[None, :], pack_end[None, :])
    attended_heads, attended_low, log_total = attention_forward(
        qkv_heads, pack_begin, pack_end, low, high, own_heads, block_q, block_k
    )
    attn_low = jnp.transpose(to_rows(attended_low), (1, 0, 2)).reshape(
        row_count, model_width
    )
    branch_attn = jnp.dot(attn_low, attn_full, preferred_element_type=jnp.float32)
    middle = residual + branch_attn
    act_mlp = layer_norm(middle, gain_mlp).astype(jnp.bfloat16)
    up_both = jnp.dot(act_mlp, in_full, preferred_element_type=jnp.float32)
    ff_width = up_both.shape[1] // 2
    hidden = (jax.nn.gelu(up_both[:, :ff_width], approximate=False) * up_both[:, ff_width:]).astype(
        jnp.bfloat16
    )
    branch_mlp = jnp.dot(hidden, out_full, preferred_element_type=jnp.float32)
    final_rows = jnp.where(is_valid[:, None], middle + branch_mlp, 0.0)
    square_sums = jnp.stack(
        [
            jnp.sum(final_rows * final_rows),
            jnp.sum(jnp.where(is_valid[:, None], branch_attn * branch_attn, 0.0)),
            jnp.sum(jnp.where(is_valid[:, None], branch_mlp * branch_mlp, 0.0)),
        ]
    )
    out_slots = final_rows.astype(jnp.bfloat16).reshape(ctx_count, piece_rows, model_width)
    grad_mlp_low = grad_final.astype(jnp.bfloat16)
    grad_hidden = lax.dot_general(
        grad_mlp_low, out_full, NT, preferred_element_type=jnp.float32
    )

    def gated(leading, trailing):
        return jax.nn.gelu(leading, approximate=False) * trailing

    unused_gate, gate_back = jax.vjp(gated, up_both[:, :ff_width], up_both[:, ff_width:])
    grad_leading, grad_trailing = gate_back(grad_hidden)
    grad_leading, grad_trailing = (
        grad_leading.astype(jnp.bfloat16),
        grad_trailing.astype(jnp.bfloat16),
    )
    grad_up = jnp.concatenate([grad_leading, grad_trailing], axis=1)
    grad_act_mlp = lax.dot_general(grad_up, in_full, NT, preferred_element_type=jnp.float32)
    unused_norm, norm_back_mlp = jax.vjp(layer_norm, middle, gain_mlp)
    grad_middle_norm, grad_gain_mlp = norm_back_mlp(grad_act_mlp)
    grad_middle = grad_final + grad_middle_norm
    grad_attn_low = grad_middle.astype(jnp.bfloat16)
    grad_attended = lax.dot_general(
        grad_attn_low, attn_full, NT, preferred_element_type=jnp.float32
    ).astype(jnp.bfloat16)
    grad_attended_heads, early = weight_sums_early(
        hidden,
        grad_mlp_low,
        act_mlp,
        grad_leading,
        grad_trailing,
        attn_low,
        grad_attn_low,
        to_heads(grad_attended),
    )
    block_back = math.gcd(tokens, 256)
    low_back, high_back = key_range(pack_begin[0], pack_end[0], block_q, block_back)
    grad_heads = attention_backward(
        qkv_heads,
        attended_heads,
        grad_attended_heads,
        log_total,
        pack_begin,
        pack_end,
        low_back,
        high_back,
        [] if early is None else [early[1][0][0]],
        own_heads,
        block_q,
        block_back,
    )
    if early is not None:
        grad_heads, early = second_step(grad_heads, early)
    grad_rows = to_rows(grad_heads)
    if own_width % 128 == 0:
        grad_projected, grad_act_attn = finish_rows(
            grad_rows, row_cosine, row_sine, qkv_full, own_heads
        )
    else:
        by_part = jnp.transpose(
            grad_rows.reshape(ctx_count, row_count, 3, own_width), (2, 1, 0, 3)
        ).reshape(3, row_count, model_width)
        cosine, sine = rotary_tables(offset, 1)
        grad_projected = jnp.concatenate(
            [
                rotate(by_part[part].astype(jnp.float32), cosine, -sine).astype(jnp.bfloat16)
                for part in (0, 1)
            ]
            + [by_part[2]],
            axis=1,
        )
        grad_act_attn = lax.dot_general(
            grad_projected, qkv_full, NT, preferred_element_type=jnp.float32
        )
    unused_first, norm_back_attn = jax.vjp(layer_norm, residual, gain_attn)
    grad_resid_norm, grad_gain_attn = norm_back_attn(grad_act_attn)
    grad_residual = (grad_middle + grad_resid_norm).astype(jnp.bfloat16)
    grad_slots = grad_residual.reshape(ctx_count, piece_rows, model_width)
    back = exchange(jnp.concatenate([out_slots, grad_slots], axis=1))
    block_out, grad_inputs = (
        jnp.take(half, own_route, axis=0).reshape(1, row_count, model_width)
        for half in (back[:, :piece_rows], back[:, piece_rows:])
    )
    small = jnp.stack(
        [grad_gain_attn, grad_gain_mlp, jnp.pad(square_sums, (0, model_width - 3))]
        + [jnp.zeros((model_width,), jnp.float32)] * 5
    )
    total_out, total_in, total_qkv, total_attn, small_sums = weight_sums(
        hidden,
        grad_mlp_low,
        act_mlp,
        grad_leading,
        grad_trailing,
        act_attn,
        grad_projected,
        attn_low,
        grad_attn_low,
        small,
        early,
    )
    total_gain_one = own_shard(small_sums[1, 0])
    total_gain_two = own_shard(small_sums[1, 1])
    total_squares = small_sums[0, 2, :3]
    valid_count = jnp.sum(lengths_row).astype(jnp.float32)
    rms_stats = jnp.sqrt(total_squares / (valid_count * model_width))[None, :]
    return (
        block_out,
        grad_inputs,
        total_gain_one,
        total_qkv,
        total_attn,
        total_gain_two,
        total_in,
        total_out,
        rms_stats,
    )


def solution(mesh):
    placed = (
        P("fsdp", "ctx", None),
        P("fsdp", "ctx", None),
        P("fsdp", None),
        P("fsdp", "ctx", None),
        P("fsdp"),
        P("fsdp", None),
        P("fsdp", None),
        P("fsdp"),
        P("fsdp", None),
        P("fsdp", None),
    )
    return jax.shard_map(
        per_device,
        mesh=mesh,
        in_specs=placed,
        out_specs=(
            P("fsdp", "ctx", None),
            P("fsdp", "ctx", None),
            P("fsdp"),
            P("fsdp", None),
            P("fsdp", None),
            P("fsdp"),
            P("fsdp", None),
            P("fsdp", None),
            P("fsdp", None),
        ),
        check_vma=False,
    )
```

```python
import functools
import math
import jax
import jax.numpy as jnp
from jax import lax
from jax.experimental import pallas as pl
from jax.experimental.pallas import tpu as pltpu
from jax.sharding import PartitionSpec as P

HEAD_WIDTH = 64
norm_eps = 1e-05
masked_score = -1e30


def head_stack(rows_in, head_count):
    if head_count == 1:
        return rows_in
    lane_head = lax.broadcasted_iota(jnp.int32, rows_in.shape, 1) // HEAD_WIDTH
    zero = jnp.zeros_like(rows_in)
    return jnp.concatenate(
        [jnp.where(lane_head == h, rows_in, zero) for h in range(head_count)], axis=0
    )


def head_pick(stacked_t, head_count, block):
    return jnp.concatenate(
        [
            stacked_t[h * HEAD_WIDTH : (h + 1) * HEAD_WIDTH, h * block : (h + 1) * block]
            for h in range(head_count)
        ],
        axis=0,
    ).T


NT = (((1,), (1,)), ((), ()))


def forward_kernel(
    head_count, block_q, block_k, low_ref, high_ref, begin_ref, end_ref, qkv_ref, out_ref, low_out_ref, log_ref, turned_ref
):
    width = out_ref.shape[1]
    step = pl.program_id(0)

    @pl.when(step == 0)
    def prepare():
        turned_ref[...] = qkv_ref[:, 2 * width :].astype(jnp.float32).T.astype(jnp.bfloat16)

    rows = pl.ds(pl.multiple_of(step * block_q, block_q), block_q)
    scale = 1.0 / math.sqrt(HEAD_WIDTH)
    stacked = head_stack(qkv_ref[rows, :width] * jnp.asarray(scale, jnp.bfloat16), head_count)
    begin = jnp.concatenate([begin_ref[:, rows]] * head_count, axis=1)
    end = jnp.concatenate([end_ref[:, rows]] * head_count, axis=1)

    def body(index, carried):
        top, total, acc = carried
        first = pl.multiple_of(index * block_k, block_k)
        keys = qkv_ref[pl.ds(first, block_k), width : 2 * width]
        scores = lax.dot_general(keys, stacked, NT, preferred_element_type=jnp.float32)
        place = first + lax.broadcasted_iota(jnp.int32, scores.shape, 0)
        scores = jnp.where((place >= begin) & (place < end), scores, masked_score)
        new_top = jnp.maximum(top, jnp.max(scores, axis=0, keepdims=True))
        fresh = jnp.exp(scores - new_top)
        fade = jnp.exp(top - new_top)
        total = total * fade + jnp.sum(fresh, axis=0, keepdims=True)
        acc = acc * fade + jnp.dot(
            turned_ref[:, pl.ds(first, block_k)],
            fresh.astype(jnp.bfloat16),
            preferred_element_type=jnp.float32,
        )
        return (new_top, total, acc)

    lanes = head_count * block_q
    top, total, acc = lax.fori_loop(
        low_ref[step],
        high_ref[step],
        body,
        (
            jnp.full((1, lanes), masked_score, jnp.float32),
            jnp.zeros((1, lanes), jnp.float32),
            jnp.zeros((width, lanes), jnp.float32),
        ),
    )
    valid = end > begin
    safe = jnp.where(valid, total, 1.0)
    acc = jnp.where(valid, acc / safe, 0.0)
    log_total = jnp.where(valid, top + jnp.log(safe), 0.0)
    attended = head_pick(acc, head_count, block_q)
    out_ref[...] = attended
    low_out_ref[...] = attended.astype(jnp.bfloat16)
    log_ref[0] = log_total


def attention_forward(qkv, begin, end, low, high, head_count, block_q, block_k):
    tokens = qkv.shape[0]
    width = head_count * HEAD_WIDTH
    steps = tokens // block_q
    whole = lambda shape: pl.BlockSpec(shape, lambda i, *_: (0,) * len(shape))
    pairs = tokens * tokens // 4 * head_count
    return pl.pallas_call(
        functools.partial(forward_kernel, head_count, block_q, block_k),
        out_shape=(
            jax.ShapeDtypeStruct((tokens, width), jnp.float32),
            jax.ShapeDtypeStruct((tokens, width), jnp.bfloat16),
            jax.ShapeDtypeStruct((steps, 1, head_count * block_q), jnp.float32),
        ),
        grid_spec=pltpu.PrefetchScalarGridSpec(
            num_scalar_prefetch=2,
            grid=(steps,),
            in_specs=[whole((1, tokens)), whole((1, tokens)), whole((tokens, 3 * width))],
            out_specs=(
                pl.BlockSpec((block_q, width), lambda i, *_: (i, 0)),
                pl.BlockSpec((block_q, width), lambda i, *_: (i, 0)),
                pl.BlockSpec((1, 1, head_count * block_q), lambda i, *_: (i, 0, 0)),
            ),
            scratch_shapes=[pltpu.VMEM((width, tokens), jnp.bfloat16)],
        ),
        cost_estimate=pl.CostEstimate(
            flops=pairs * 512, bytes_accessed=tokens * width * 12, transcendentals=pairs
        ),
        name="attention_forward",
    )(low, high, begin, end, qkv)


def turn_back(grads, cosine, sine, head_count):
    half = HEAD_WIDTH // 2
    pieces = []
    for h in range(head_count):
        base = h * HEAD_WIDTH
        pieces += [grads[:, base + half : base + HEAD_WIDTH], grads[:, base : base + half]]
    return grads * cosine + jnp.concatenate(pieces, axis=1) * sine


def backward_kernel(
    head_count,
    block_q,
    block_k,
    low_ref,
    high_ref,
    begin_ref,
    end_ref,
    qkv_ref,
    attended_ref,
    grad_ref,
    log_ref,
    *refs,
):
    out_ref, turned_ref, key_acc, value_acc = refs[-4:]
    width = attended_ref.shape[1]
    step = pl.program_id(0)

    @pl.when(step == 0)
    def prepare():
        turned_ref[...] = qkv_ref[:, width : 2 * width].astype(jnp.float32).T.astype(jnp.bfloat16)
        key_acc[...] = jnp.zeros_like(key_acc)
        value_acc[...] = jnp.zeros_like(value_acc)

    rows = pl.ds(pl.multiple_of(step * block_q, block_q), block_q)
    scale = 1.0 / math.sqrt(HEAD_WIDTH)
    stacked = head_stack(qkv_ref[rows, :width] * jnp.asarray(scale, jnp.bfloat16), head_count)
    grads = grad_ref[rows, :]
    grad_stacked = head_stack(grads, head_count)
    begin = jnp.concatenate([begin_ref[:, rows]] * head_count, axis=1)
    end = jnp.concatenate([end_ref[:, rows]] * head_count, axis=1)
    product = (grads.astype(jnp.float32) * attended_ref[rows, :]).T
    delta = jnp.concatenate(
        [
            jnp.sum(product[h * HEAD_WIDTH : (h + 1) * HEAD_WIDTH], axis=0, keepdims=True)
            for h in range(head_count)
        ],
        axis=1,
    )
    log_total = log_ref[0]

    def body(index, acc):
        first = pl.multiple_of(index * block_k, block_k)
        span = pl.ds(first, block_k)
        keys = qkv_ref[span, width : 2 * width]
        values = qkv_ref[span, 2 * width :]
        scores = lax.dot_general(keys, stacked, NT, preferred_element_type=jnp.float32)
        grad_probs = lax.dot_general(values, grad_stacked, NT, preferred_element_type=jnp.float32)
        place = first + lax.broadcasted_iota(jnp.int32, scores.shape, 0)
        scores = jnp.where((place >= begin) & (place < end), scores, masked_score)
        probs = jnp.exp(scores - log_total)
        grad_scores = (probs * (grad_probs - delta)).astype(jnp.bfloat16)
        value_acc[span, :] += jnp.dot(
            probs.astype(jnp.bfloat16), grad_stacked, preferred_element_type=jnp.float32
        )
        key_acc[span, :] += jnp.dot(grad_scores, stacked, preferred_element_type=jnp.float32)
        return acc + jnp.dot(
            turned_ref[:, span], grad_scores, preferred_element_type=jnp.float32
        )

    acc = lax.fori_loop(
        low_ref[step],
        high_ref[step],
        body,
        jnp.zeros((width, head_count * block_q), jnp.float32),
    )
    grad_queries = head_pick(acc, head_count, block_q) * scale
    out_ref[rows, :width] = grad_queries.astype(jnp.bfloat16)

    @pl.when(step == pl.num_programs(0) - 1)
    def finish():
        @pl.loop(0, pl.num_programs(0))
        def each(index):
            span = pl.ds(pl.multiple_of(index * block_q, block_q), block_q)
            out_ref[span, width : 2 * width] = key_acc[span, :].astype(jnp.bfloat16)
            out_ref[span, 2 * width :] = value_acc[span, :].astype(jnp.bfloat16)


def attention_backward(
    qkv, attended, grads, log_total, begin, end, low, high, after, head_count, block_q, block_k
):
    tokens = qkv.shape[0]
    width = head_count * HEAD_WIDTH
    steps = tokens // block_q
    whole = lambda shape: pl.BlockSpec(shape, lambda i, *_: (0,) * len(shape))
    pairs = tokens * tokens // 4 * head_count
    return pl.pallas_call(
        functools.partial(backward_kernel, head_count, block_q, block_k),
        out_shape=jax.ShapeDtypeStruct((tokens, 3 * width), jnp.bfloat16),
        grid_spec=pltpu.PrefetchScalarGridSpec(
            num_scalar_prefetch=2,
            grid=(steps,),
            in_specs=[
                whole((1, tokens)),
                whole((1, tokens)),
                whole((tokens, 3 * width)),
                whole((tokens, width)),
                whole((tokens, width)),
                pl.BlockSpec((1, 1, head_count * block_q), lambda i, *_: (i, 0, 0)),
            ]
            + [pl.BlockSpec(memory_space=pl.ANY)] * len(after),
            out_specs=whole((tokens, 3 * width)),
            scratch_shapes=[
                pltpu.VMEM((width, tokens), jnp.bfloat16),
                pltpu.VMEM((tokens, width), jnp.float32),
                pltpu.VMEM((tokens, width), jnp.float32),
            ],
        ),
        cost_estimate=pl.CostEstimate(
            flops=pairs * 1280, bytes_accessed=tokens * width * 30, transcendentals=pairs
        ),
        name="attention_backward",
    )(low, high, begin, end, qkv, attended, grads, log_total, *after)


def rows_kernel(head_count, heads_ref, cosine_ref, sine_ref, query_ref, key_ref, value_ref, out_ref, act_ref):
    width = heads_ref.shape[2] // 3
    step = pl.program_id(0)
    total = out_ref.shape[1] // 3
    owners = heads_ref.shape[0]
    pieces = []
    for part in range(3):
        for owner in range(owners):
            piece = heads_ref[owner, :, part * width : (part + 1) * width]
            if part < 2:
                piece = turn_back(
                    piece.astype(jnp.float32), cosine_ref[...], sine_ref[...], head_count
                ).astype(jnp.bfloat16)
            first = pl.multiple_of(part * total + (step * owners + owner) * width, width)
            out_ref[:, pl.ds(first, width)] = piece
            pieces.append(piece)
    weights = jnp.concatenate([query_ref[...], key_ref[...], value_ref[...]], axis=1)
    product = lax.dot_general(
        jnp.concatenate(pieces, axis=1), weights, NT, preferred_element_type=jnp.float32
    )

    @pl.when(step == 0)
    def begin():
        act_ref[...] = product

    @pl.when(step > 0)
    def add():
        act_ref[...] += product


def finish_rows(heads, cosine, sine, qkv_full, head_count):
    owners, rows, columns = heads.shape
    width = columns // 3
    depth = qkv_full.shape[0]
    whole = lambda shape: pl.BlockSpec(shape, lambda i: (0,) * len(shape))
    steps = owners // 2
    part_of = lambda part: pl.BlockSpec((depth, 2 * width), lambda i: (0, part * steps + i))
    return pl.pallas_call(
        functools.partial(rows_kernel, head_count),
        out_shape=(
            jax.ShapeDtypeStruct((rows, owners * columns), jnp.bfloat16),
            jax.ShapeDtypeStruct((rows, depth), jnp.float32),
        ),
        grid=(steps,),
        in_specs=[
            pl.BlockSpec((2, rows, columns), lambda i: (i, 0, 0)),
            whole((rows, width)),
            whole((rows, width)),
            part_of(0),
            part_of(1),
            part_of(2),
        ],
        out_specs=(whole((rows, owners * columns)), whole((rows, depth))),
        cost_estimate=pl.CostEstimate(
            flops=2 * rows * depth * owners * columns,
            bytes_accessed=2 * depth * owners * columns + 4 * rows * owners * columns,
            transcendentals=0,
        ),
        name="finish_rows",
    )(heads, cosine, sine, qkv_full, qkv_full, qkv_full)


def spans(places, lengths_row):
    ends = jnp.cumsum(lengths_row)
    past = (places[:, None] >= ends[None, :]).astype(jnp.int32)
    begin = jnp.sum(past * lengths_row[None, :], axis=1)
    before = (places[:, None] >= (ends - lengths_row)[None, :]).astype(jnp.int32)
    end = jnp.sum(before * lengths_row[None, :], axis=1)
    valid = places < ends[-1]
    return (jnp.where(valid, begin, 0), jnp.where(valid, end, 0), places - begin, valid)


def key_range(begin, end, block_q, block_k):
    begin_blocks = jnp.where(end > begin, begin, jnp.int32(1 << 30)).reshape(-1, block_q)
    high = (jnp.max(end.reshape(-1, block_q), axis=1) + block_k - 1) // block_k
    low = jnp.minimum(jnp.min(begin_blocks, axis=1) // block_k, high)
    return (low, high)


def rotary_tables(offset, head_count):
    half = HEAD_WIDTH // 2
    inverse = 160000.0 ** (-2.0 * jnp.arange(half, dtype=jnp.float32) / HEAD_WIDTH)
    angles = offset.astype(jnp.float32)[:, None] * inverse[None, :]
    cosine, sine = (jnp.cos(angles), jnp.sin(angles))
    return (
        jnp.concatenate([cosine, cosine] * head_count, axis=1),
        jnp.concatenate([sine, -sine] * head_count, axis=1),
    )


def toggled(index, bit):
    return index + bit - 2 * bit * ((index // bit) % 2)


def gather_kernel(shapes, projects, *refs):
    count = len(shapes)
    shard_refs, refs = (refs[:count], refs[count:])
    if projects:
        act_ref, qkv_ref, cosine_ref, sine_ref = refs[:4]
        heads_ref = refs[4 + count]
        columns_ref, held_ref, load_sem, head_send, head_recv, own_sem = refs[count + 8 :]
        refs = refs[4 : 4 + count] + refs[count + 5 : count + 8]
    full_refs = refs[:count]
    send_sem, recv_sem, local_sem = refs[count:]
    shards = lax.axis_size("fsdp")
    slices = lax.axis_size("ctx") // 2
    own_ctx, own_shard = (lax.axis_index("ctx"), lax.axis_index("fsdp"))
    core, chip = (own_ctx % 2, own_ctx // 2)
    barrier = pltpu.get_barrier_semaphore()
    partners = [{"fsdp": toggled(own_shard, bit)} for bit in (1, 2)]
    partners += [{"ctx": toggled(own_ctx, bit)} for bit in (1, 2, 4)]

    def owner_at(relation):
        owner = own_ctx
        for bit in (1, 2, 4):
            if relation & bit:
                owner = toggled(owner, bit)
        return owner

    if projects:
        partners += [{"ctx": owner_at(relation)} for relation in (3, 5, 6, 7)]
    for partner in partners:
        pl.semaphore_signal(
            barrier, inc=1, device_id=partner, device_id_type=pl.DeviceIdType.MESH
        )
    pl.semaphore_wait(barrier, len(partners))
    to_one, to_two, to_core, to_x, to_y = partners[:5]

    def shard_at(step):
        if step == 0:
            return own_shard
        if step == 3:
            return toggled(toggled(own_shard, 1), 2)
        return toggled(own_shard, step)

    def region(ref, weight, step, chip_at, half):
        if shapes[weight] == "small":
            return ref if len(ref.shape) == 2 else ref.at[shard_at(step)]
        if shapes[weight] == "rows":
            rows = ref.shape[-2]
            span = pl.ds(0, rows) if half is None else pl.ds(half * (rows // 2), rows // 2)
            if len(ref.shape) == 4:
                return ref.at[core, chip_at, span, :]
            return ref.at[shard_at(step), core, chip_at, span, :]
        rows = ref.shape[-2]
        first = (rows // 2) // 16 * 16
        spans_of = {None: pl.ds(0, rows), 0: pl.ds(0, first), 1: pl.ds(first, rows - first)}
        width = ref.shape[-1] // (2 * slices)
        columns = pl.ds(pl.multiple_of((core * slices + chip_at) * width, width), width)
        if len(ref.shape) == 2:
            return ref.at[spans_of[half], columns]
        return ref.at[shard_at(step), spans_of[half], columns]

    def core_region(ref, weight, step):
        if shapes[weight] == "rows":
            return ref.at[shard_at(step), core]
        width = ref.shape[-1] // 2
        return ref.at[shard_at(step), :, pl.ds(pl.multiple_of(core * width, width), width)]

    pending = []

    def send(source, target, slot, partner):
        copy = pltpu.make_async_remote_copy(
            src_ref=source,
            dst_ref=target,
            send_sem=send_sem.at[slot],
            recv_sem=recv_sem.at[slot],
            device_id=partner,
            device_id_type=pl.DeviceIdType.MESH,
        )
        copy.start()
        pending.append(copy)
        return copy

    copies = {}
    local = []

    def slot_of(weight, step, kind):
        return (weight * 3 + step - 1) * 8 + kind

    def shard_sends(weight):
        source = region(shard_refs[weight], weight, 0, chip, None)
        target = region(full_refs[weight], weight, 0, chip, None)
        copies[weight, 2, 0] = send(source, target, slot_of(weight, 2, 0), to_two)
        copies[weight, 1, 0] = send(source, target, slot_of(weight, 1, 0), to_one)
        target = full_refs[weight].at[own_shard]
        copy = pltpu.make_async_copy(shard_refs[weight], target, local_sem.at[weight])
        copy.start()
        local.append(copy)

    def shard_forward(weight):
        copies[weight, 2, 0].wait_recv()
        piece = region(full_refs[weight], weight, 2, chip, None)
        copies[weight, 3, 0] = send(piece, piece, slot_of(weight, 3, 0), to_one)

    def plane_sends(weight, step):
        lead = region(full_refs[weight], weight, step, chip, 0)
        rest = region(full_refs[weight], weight, step, chip, 1)
        for kind, piece, partner in ((1, lead, to_x), (2, rest, to_y), (3, lead, to_y), (4, rest, to_x)):
            copies[weight, step, kind] = send(piece, piece, slot_of(weight, step, kind), partner)

    def plane_forward(weight, step):
        copies[weight, step, 1].wait_recv()
        lead = region(full_refs[weight], weight, step, toggled(chip, 1), 0)
        copies[weight, step, 5] = send(lead, lead, slot_of(weight, step, 5), to_y)
        copies[weight, step, 2].wait_recv()
        rest = region(full_refs[weight], weight, step, toggled(chip, 2), 1)
        copies[weight, step, 6] = send(rest, rest, slot_of(weight, step, 6), to_x)

    def core_send(weight, step):
        for kind in (3, 4, 5, 6):
            copies[weight, step, kind].wait_recv()
        piece = core_region(full_refs[weight], weight, step)
        copies[weight, step, 7] = send(piece, piece, slot_of(weight, step, 7), to_core)

    chip_order = (3, 1, 2, 0)

    def start_loads():
        loads = {}
        for chip_bits in chip_order:
            owner_chip = owner_at(2 * chip_bits) // 2
            for part in range(3):
                width = columns_ref.shape[2] // 3
                total = qkv_ref.shape[1] // 3
                first = pl.multiple_of(part * total + owner_chip * width, width)
                loads[chip_bits, part] = pltpu.make_async_copy(
                    qkv_ref.at[:, pl.ds(first, width)],
                    columns_ref.at[chip_bits, :, pl.ds(part * width, width)],
                    load_sem.at[chip_bits * 3 + part],
                )
                loads[chip_bits, part].start()
        return loads

    def project(chip_bits, loads):
        for part in range(3):
            loads[chip_bits, part].wait()
        rows, own_width = (act_ref.shape[0], held_ref.shape[2] // 3)
        product = jnp.dot(
            act_ref[...], columns_ref[chip_bits], preferred_element_type=jnp.float32
        )
        for core_at in (0, 1):
            slot = 2 * chip_bits + core + core_at - 2 * core * core_at
            for part in range(3):
                first = (2 * part + core_at) * own_width
                piece = product[:, first : first + own_width]
                if part < 2:
                    half = HEAD_WIDTH // 2
                    turned = []
                    for base in range(0, own_width, HEAD_WIDTH):
                        turned += [piece[:, base + half : base + HEAD_WIDTH], piece[:, base : base + half]]
                    piece = piece * cosine_ref[...] - jnp.concatenate(turned, axis=1) * sine_ref[...]
                held_ref[slot, :, part * own_width : (part + 1) * own_width] = piece.astype(jnp.bfloat16)
        target = heads_ref.at[pl.ds(pl.multiple_of(own_ctx * rows, rows), rows), :]
        for core_bit in (0, 1):
            relation = 2 * chip_bits + core_bit
            if relation == 0:
                copy = pltpu.make_async_copy(held_ref.at[0], target, own_sem.at[0])
                copy.start()
                local.append(copy)
                continue
            copy = pltpu.make_async_remote_copy(
                src_ref=held_ref.at[relation],
                dst_ref=target,
                send_sem=head_send.at[relation],
                recv_sem=head_recv.at[relation],
                device_id={"ctx": owner_at(relation)},
                device_id_type=pl.DeviceIdType.MESH,
            )
            copy.start()
            pending.append(copy)
            arriving.append(copy)

    arriving = []
    sent = 1
    if projects:
        loads = start_loads()
        for weight in range(count):
            shard_sends(weight)
        sent = count
        for chip_bits in chip_order:
            project(chip_bits, loads)
    else:
        shard_sends(0)
    for weight in range(count):
        if weight + 1 >= sent and weight + 1 < count:
            shard_sends(weight + 1)
        shard_forward(weight)
        copies[weight, 1, 0].wait_recv()
        if shapes[weight] == "small":
            copies[weight, 3, 0].wait_recv()
            continue
        plane_sends(weight, 1)
        plane_sends(weight, 2)
        copies[weight, 3, 0].wait_recv()
        plane_sends(weight, 3)
        for step in (1, 2, 3):
            plane_forward(weight, step)
        if weight > 0 and shapes[weight - 1] != "small":
            for step in (1, 2, 3):
                core_send(weight - 1, step)
    for step in (1, 2, 3):
        core_send(count - 1, step)
    for weight in range(count):
        if shapes[weight] != "small":
            for step in (1, 2, 3):
                copies[weight, step, 7].wait_recv()
    for copy in arriving:
        copy.wait_recv()
    for copy in pending:
        copy.wait_send()
    for copy in local:
        copy.wait()


def gather_weights(weights, projection=None):
    shards, ctx_count = (lax.axis_size("fsdp"), lax.axis_size("ctx"))
    slices = ctx_count // 2
    shapes, views, outs = ([], [], [])
    for weight in weights:
        rows, columns = weight.shape
        if rows % (32 * ctx_count) == 0:
            shapes.append("rows")
            views.append(weight.reshape(2, slices, rows // ctx_count, columns))
            outs.append((shards, 2, slices, rows // ctx_count, columns))
        elif rows == 16:
            shapes.append("small")
            views.append(weight)
            outs.append((shards, rows, columns))
        elif columns % (128 * ctx_count) == 0 and rows % 16 == 0:
            shapes.append("columns")
            views.append(weight)
            outs.append((shards, rows, columns))
    if shards != 4 or ctx_count != 8 or len(views) < len(weights):
        return [lax.all_gather(weight, "fsdp", axis=0, tiled=True) for weight in weights]
    slots = len(views) * 24
    vmem, anywhere, dma = (
        pl.BlockSpec(memory_space=pltpu.VMEM),
        pl.BlockSpec(memory_space=pl.ANY),
        pltpu.SemaphoreType.DMA,
    )
    in_specs = [vmem] * len(views)
    scratch = [dma((slots,)), dma((slots,)), dma((len(views),))]
    if projection is not None:
        act_attn, qkv_full = projection[:2]
        rows, own_columns = (act_attn.shape[0], qkv_full.shape[1] // ctx_count)
        views += list(projection)
        in_specs += [vmem, anywhere, vmem, vmem]
        outs.append((ctx_count * rows, own_columns))
        scratch += [
            pltpu.VMEM((slices, qkv_full.shape[0], 2 * own_columns), jnp.bfloat16),
            pltpu.VMEM((ctx_count, rows, own_columns), jnp.bfloat16),
            dma((3 * slices,)),
            dma((ctx_count,)),
            dma((ctx_count,)),
            dma((1,)),
        ]
    held = pl.pallas_call(
        functools.partial(gather_kernel, shapes, projection is not None),
        out_shape=tuple(jax.ShapeDtypeStruct(out, jnp.bfloat16) for out in outs),
        in_specs=in_specs,
        out_specs=tuple(anywhere for out in outs),
        scratch_shapes=scratch,
        compiler_params=pltpu.CompilerParams(
            collective_id=0 if projection is None else 2,
            has_side_effects=True,
            vmem_limit_bytes=60 * 1024 * 1024,
        ),
        name="gather_weights" if projection is None else "gather_and_project",
    )(*views)
    return [whole.reshape(-1, whole.shape[-1]) for whole in held]


def pair_steps(plan, lead_rows, left_refs, right_refs, turned_refs, whole_refs, sems, core, pending, send):
    pair_send, pair_recv, near_sem = sems
    to_core = {"ctx": toggled(lax.axis_index("ctx"), 1)}

    def send_core(source, target, sent, got, start=True):
        return send(source, target, sent, got, to_core, start)

    rows = left_refs[0].shape[0] if left_refs else 0
    pairs = []

    def begin(w):
        entry = plan[w]
        span, right = (plan_span(entry), right_refs[w])
        own_part, other_part = (whole_refs[w].at[pl.ds(0, rows)], whole_refs[w].at[pl.ds(rows, rows)])

        def exchange(own_half, other_half, start=True):
            near = pltpu.make_async_copy(own_half, own_part, near_sem.at[w])
            if start:
                near.start()
            sems = (pair_send.at[2 * w], pair_recv.at[2 * w])
            return [near, send_core(other_half, other_part, *sems, start)]

        if entry[5]:
            ways = [exchange(right[at], right[1 - at], False) for at in (0, 1)]
            for at in (0, 1):

                @pl.when(core == at)
                def start():
                    for copy in ways[at]:
                        copy.start()

            pairs.append(ways[0])
            pending.append(ways[0][1])
        else:
            halves = [
                right.at[:, pl.ds(pl.multiple_of(at * span, span), span)] for at in (core, 1 - core)
            ]
            pairs.append(exchange(*halves))

    def turn(w):
        left, turned = (left_refs[w], turned_refs[w])
        block = 512
        for first in range(0, left.shape[1], block):
            last = min(first + block, left.shape[1])
            turned[first:last, :rows] = (
                left[:, first:last].astype(jnp.float32).T.astype(jnp.bfloat16)
            )
        pairs[w].append(
            send_core(
                turned.at[:, pl.ds(0, rows)],
                turned.at[:, pl.ds(rows, rows)],
                pair_send.at[2 * w + 1],
                pair_recv.at[2 * w + 1],
            )
        )

    def multiply(w, t, first, second):
        kind, count, width, deep, halves, parted = plan[w]
        if t == 0:
            near, far, turned = pairs[w]
            near.wait()
            far.wait_recv()
            turned.wait_recv()

        def each(z, carried):
            left = turned_refs[w][pl.ds(pl.multiple_of(z * deep, 16), deep), :]
            if kind == "rows":
                last = min((t + 1) * width, whole_refs[w].shape[1])
                part = jnp.dot(
                    left, whole_refs[w][:, t * width : last], preferred_element_type=jnp.float32
                ).astype(jnp.bfloat16)
                if last < (t + 1) * width:
                    empty = jnp.zeros((deep, (t + 1) * width - last), jnp.bfloat16)
                    part = jnp.concatenate([part, empty], axis=1)
                piece_rows = first.shape[3]
                for s in range(4):
                    first[z, s // 2, s % 2] = part[2 * s * piece_rows : (2 * s + 1) * piece_rows]
                    second[z, s // 2, s % 2] = part[(2 * s + 1) * piece_rows : (2 * s + 2) * piece_rows]
            else:
                part = jnp.dot(
                    left, whole_refs[w][...], preferred_element_type=jnp.float32
                ).astype(jnp.bfloat16)
                for s in range(4):
                    piece = part[:, s * width : (s + 1) * width]
                    first[z, s // 2, s % 2] = piece[:lead_rows]
                    second[z, s // 2, s % 2] = piece[lead_rows:]
            return carried

        lax.fori_loop(0, 4, each, 0)

    return (begin, turn, multiply)


def remote_send(pending):
    def send(source, target, sent, got, partner, start=True):
        copy = pltpu.make_async_remote_copy(
            src_ref=source,
            dst_ref=target,
            send_sem=sent,
            recv_sem=got,
            device_id=partner,
            device_id_type=pl.DeviceIdType.MESH,
        )
        if start:
            copy.start()
            pending.append(copy)
        return copy

    return send


def product_kernel(plan, lead_rows, *refs):
    groups, places = early_places(plan)
    weights, outs = (len(plan), 4 * len(groups))
    left_refs, refs = (refs[:weights], refs[weights:])
    right_refs = []
    for entry in plan:
        held = 2 if entry[5] else 1
        right_refs.append(refs[:held] if held == 2 else refs[0])
        refs = refs[held:]
    out_refs = refs[:outs]
    scratch = list(refs[outs:])
    turned_refs = [scratch.pop(0) for weight in plan]
    whole_refs = [scratch.pop(0) for weight in plan]
    chunks = [(w, t) for w, entry in enumerate(plan) for t in range(entry[1])]
    held = [(scratch.pop(0), scratch.pop(0)) for chunk in chunks]
    pair_send, pair_recv, near_sem, store_sem = scratch
    own_ctx = lax.axis_index("ctx")
    core, chip = (own_ctx % 2, own_ctx // 2)
    own_x, own_y = (chip % 2, chip // 2)
    to_core = {"ctx": toggled(own_ctx, 1)}
    barrier = pltpu.get_barrier_semaphore()
    pl.semaphore_signal(barrier, inc=1, device_id=to_core, device_id_type=pl.DeviceIdType.MESH)
    pl.semaphore_wait(barrier, 1)
    pending = []
    send = remote_send(pending)
    begin, turn, multiply = pair_steps(
        plan,
        lead_rows,
        left_refs,
        right_refs,
        turned_refs,
        whole_refs,
        (pair_send, pair_recv, near_sem),
        core,
        pending,
        send,
    )
    for w in range(weights):
        begin(w)
        turn(w)
    stores = []
    for number, (w, t) in enumerate(chunks):
        first, second = held[number]
        multiply(w, t, first, second)
        group, offset = places[number]
        sides = (
            lambda at: first.at[:, at, own_x],
            lambda at: first.at[:, at, 1 - own_x],
            lambda at: second.at[:, own_y, at],
            lambda at: second.at[:, 1 - own_y, at],
        )
        for side, source_at in enumerate(sides):
            for at in (0, 1):
                copy = pltpu.make_async_copy(
                    source_at(at),
                    out_refs[4 * group + side].at[at, :, :, pl.ds(offset, plan[w][2])],
                    store_sem.at[8 * number + 2 * side + at],
                )
                copy.start()
                stores.append(copy)
    for copy in stores:
        copy.wait()
    for copy in pending:
        copy.wait_send()


def weight_plan(kind, left, right, count):
    deep = left.shape[1] // 4
    if kind == "rows":
        parted = isinstance(right, tuple)
        span = right[0].shape[1] if parted else right.shape[1] // 2
        width = -(-span // (128 * count)) * 128
        return (kind, count, width, deep, (deep // 8, deep // 8), span if parted else 0)
    lead_rows = deep // 2 // 16 * 16
    return (kind, count, right.shape[-1] // 8, deep, (lead_rows, deep - lead_rows), 0)


def early_places(plan):
    groups, places = ([], [])
    for kind, count, width, deep, halves, parted in plan:
        found = [at for at, group in enumerate(groups) if group[0] == halves]
        if not found:
            groups.append([halves, 0])
            found = [len(groups) - 1]
        for chunk in range(count):
            places.append((found[0], groups[found[0]][1]))
            groups[found[0]][1] += width
    return (groups, places)


def plan_span(entry):
    return entry[1] * entry[2] if entry[0] == "rows" else 4 * entry[2]


def plan_lead(plan):
    return max([0] + [entry[4][0] for entry in plan if entry[0] == "columns"])


def pair_scratch(plan, tokens):
    turned = [pltpu.VMEM((4 * entry[3], 2 * tokens), jnp.bfloat16) for entry in plan]
    return turned + [
        pltpu.VMEM((2 * tokens, entry[5] or plan_span(entry)), jnp.bfloat16) for entry in plan
    ]


def early_sums(products, held):
    plan = [weight_plan(*product) for product in products]
    lefts, rights = ([product[1] for product in products], [product[2] for product in products])
    vmem, anywhere, dma = (
        pl.BlockSpec(memory_space=pltpu.VMEM),
        pl.BlockSpec(memory_space=pl.ANY),
        pltpu.SemaphoreType.DMA,
    )
    rights = [part for right in rights for part in (right if isinstance(right, tuple) else [right])]
    groups = early_places(plan)[0]
    outs, units = ([], [])
    for halves, columns in groups:
        for half in halves:
            outs += [jax.ShapeDtypeStruct((2, 4, half, columns), jnp.bfloat16)] * 2
    for kind, count, width, deep, halves, parted in plan:
        for chunk in range(count):
            units += [pltpu.VMEM((4, 2, 2, half, width), jnp.bfloat16) for half in halves]
    chunk_count = sum(entry[1] for entry in plan)
    scratch = pair_scratch(plan, lefts[0].shape[0]) + units
    scratch += [dma((2 * len(plan),)), dma((2 * len(plan),)), dma((len(plan),)), dma((8 * chunk_count,))]
    sides = pl.pallas_call(
        functools.partial(product_kernel, plan, plan_lead(plan)),
        out_shape=tuple(outs),
        in_specs=[vmem] * len(plan) + [anywhere] * len(rights),
        out_specs=(anywhere,) * len(outs),
        scratch_shapes=scratch,
        compiler_params=pltpu.CompilerParams(
            collective_id=3, has_side_effects=True, vmem_limit_bytes=60 * 1024 * 1024
        ),
        name="early_products",
    )(*lefts, *rights)
    held, sides = lax.optimization_barrier((held, sides))
    arrays = []
    for group in range(len(groups)):
        for part, bit in ((0, 2), (2, 4)):
            kept, sent = sides[4 * group + part : 4 * group + part + 2]
            arrays.append((kept, swap(sent, "ctx", bit)))
    return (held, (plan, arrays))


def second_step(held, early):
    plan, arrays = early
    held, arrays = lax.optimization_barrier((held, arrays))
    chip = lax.axis_index("ctx") // 2
    flat = []
    for at, (kept, arrived) in sorted(enumerate(arrays), key=lambda pair: (-(pair[0] // 2), pair[0])):
        bit, own = ((4, chip // 2), (2, chip % 2))[at % 2]
        other = [
            lax.dynamic_index_in_dim(side, 1 - own, 0, keepdims=False).astype(jnp.float32)
            for side in (kept, arrived)
        ]
        twice = swap((other[0] + other[1]).astype(jnp.bfloat16), "ctx", bit)
        flat.append((at, [kept, arrived, twice]))
    flat = [side for at, sides in sorted(flat, key=lambda pair: pair[0]) for side in sides]
    return (held, (plan, flat))


def sum_kernel(early, late, lead_rows, *refs):
    weights, products = (len(early) + len(late), len(late))
    left_refs, right_refs = (refs[:products], refs[products : 2 * products])
    refs = refs[2 * products :]
    groups, places = early_places(early)
    early_refs, refs = (refs[: 6 * len(groups)], refs[6 * len(groups) :])
    small_ref, out_refs, small_out = (refs[0], refs[1 : weights + 1], refs[weights + 1])
    scratch = list(refs[weights + 2 :])
    turned_refs = [scratch.pop(0) for weight in late]
    whole_refs = [scratch.pop(0) for weight in late]
    plan = early + late
    chunks = [(w, t) for w, entry in enumerate(plan) for t in range(entry[1])]
    early_count = sum(entry[1] for entry in early)
    order = sorted(range(early_count), key=lambda number: (-chunks[number][0], number))
    units = {}
    for number in range(len(chunks)):
        for half in (0, 1):
            units[number, half] = [scratch.pop(0) for stage in range(5)]
    small_held = scratch.pop(0)
    send_sem, recv_sem, local_sem, load_sem, pair_send, pair_recv, small_send, small_recv, near_sem = scratch
    own_ctx, own_shard = (lax.axis_index("ctx"), lax.axis_index("fsdp"))
    core, chip = (own_ctx % 2, own_ctx // 2)
    own_x, own_y = (chip % 2, chip // 2)
    low_bit, high_bit = (own_shard % 2, own_shard // 2)
    loads = {}
    for number in order:
        w, (group, offset) = (chunks[number][0], places[number])
        for half in (0, 1):
            own = own_y if half == 0 else own_x
            kept, arrived, twice = early_refs[6 * group + 3 * half : 6 * group + 3 * half + 3]
            columns = pl.ds(offset, plan[w][2])
            sources = (kept.at[own, :, :, columns], arrived.at[own, :, :, columns], twice.at[:, :, columns])
            for at, source in enumerate(sources):
                slot = (number * 2 + half) * 3 + at
                copy = pltpu.make_async_copy(source, units[number, half][at], load_sem.at[slot])
                copy.start()
                loads[number, half, at] = copy
    partners = [{"ctx": toggled(own_ctx, bit)} for bit in (1, 2, 4)]
    partners += [{"fsdp": toggled(own_shard, bit)} for bit in (1, 2)]
    barrier = pltpu.get_barrier_semaphore()
    for partner in partners:
        pl.semaphore_signal(
            barrier, inc=1, device_id=partner, device_id_type=pl.DeviceIdType.MESH
        )
    pl.semaphore_wait(barrier, len(partners))
    to_core, to_x, to_y, to_one, to_two = partners
    pending = []
    send = remote_send(pending)
    begin, turn, multiply = pair_steps(
        late,
        lead_rows,
        left_refs,
        right_refs,
        turned_refs,
        whole_refs,
        (pair_send, pair_recv, near_sem),
        core,
        pending,
        send,
    )
    for w in range(len(late)):
        begin(w)
    copies = {}

    def hop(number, half, stage, source, target, partner):
        slot = (number * 2 + half) * 8 + stage
        copies[number, half, stage] = send(
            source, target, send_sem.at[slot], recv_sem.at[slot], partner
        )

    def stage_one(number):
        w, t = chunks[number]
        multiply(w - len(early), t, units[number, 0][0], units[number, 1][0])
        hop(number, 0, 0, units[number, 0][0].at[:, :, 1 - own_x], units[number, 0][1], to_x)
        hop(number, 1, 0, units[number, 1][0].at[:, 1 - own_y], units[number, 1][1], to_y)

    def add(target, source_at, count):
        def each(i, carried):
            target[i] = (
                target[i].astype(jnp.float32) + source_at(i).astype(jnp.float32)
            ).astype(jnp.bfloat16)
            return carried

        lax.fori_loop(0, count, each, 0)

    def stage_two(number):
        held, got = (units[number, 0][0], units[number, 0][1])
        copies[number, 0, 0].wait_recv()
        add(got, lambda z: held[z, :, own_x], 4)
        held_b, got_b = (units[number, 1][0], units[number, 1][1])
        copies[number, 1, 0].wait_recv()
        add(got_b, lambda z: held_b[z, own_y], 4)
        hop(number, 0, 1, got.at[:, 1 - own_y], units[number, 0][2], to_y)
        hop(number, 1, 1, got_b.at[:, 1 - own_x], units[number, 1][2], to_x)

    def stage_three(number):
        for half in (0, 1):
            kept, held, got = units[number, half][:3]
            own = own_y if half == 0 else own_x
            if number < early_count:
                for at in range(3):
                    loads[number, half, at].wait()
                add(held, lambda z: kept[z], 4)
                add(got, lambda z: held[z], 4)
            else:
                copies[number, half, 1].wait_recv()
                add(got, lambda z: held[z, own], 4)
        for half in (0, 1):
            got = units[number, half][2]
            for high in (0, 1):
                hop(
                    number,
                    half,
                    2 + 4 * high,
                    got.at[2 * high + 1 - low_bit],
                    units[number, half][3].at[high],
                    to_one,
                )

    def stage_four(number):
        for half in (0, 1):
            held, got = (units[number, half][2], units[number, half][3])
            copies[number, half, 2].wait_recv()
            copies[number, half, 6].wait_recv()
            add(got, lambda high: held[2 * high + low_bit], 2)
        for half in (0, 1):
            got = units[number, half][3]
            hop(number, half, 3, got.at[1 - high_bit], units[number, half][4].at[0], to_two)

    def final_region(number, half, chip_at):
        w, t = chunks[number]
        kind, count, width = plan[w][:3]
        deep = units[number, half][4].shape[1]
        if kind == "rows":
            start = pl.multiple_of((2 * chip_at + half) * deep, deep)
            column = pl.multiple_of((core * count + t) * width, width)
            return out_refs[w].at[pl.ds(start, deep), pl.ds(column, width)]
        column = pl.multiple_of((core * 4 + chip_at) * width, width)
        return out_refs[w].at[pl.ds(half * lead_rows, deep), pl.ds(column, width)]

    local = {}

    def stage_five(number):
        for half in (0, 1):
            held, got = (units[number, half][3], units[number, half][4])
            copies[number, half, 3].wait_recv()
            add(got, lambda i: held[high_bit], 1)
        for half in (0, 1):
            got = units[number, half][4].at[0]
            target = final_region(number, half, chip)
            hop(number, half, 4, got, target, to_x if half == 0 else to_y)
            hop(number, half, 5, got, target, to_y if half == 0 else to_x)
            copy = pltpu.make_async_copy(got, target, local_sem.at[number * 2 + half])
            copy.start()
            local[number, half] = copy

    def stage_six(number):
        for half in (0, 1):
            copies[number, half, 4].wait_recv()
            piece = final_region(number, half, toggled(chip, 1 if half == 0 else 2))
            hop(number, half, 7, piece, piece, to_y if half == 0 else to_x)

    def stage_seven(number):
        w, t = chunks[number]
        kind, count, width = plan[w][:3]
        for half in (0, 1):
            copies[number, half, 5].wait_recv()
            copies[number, half, 7].wait_recv()
            local[number, half].wait()
        span = width if kind == "rows" else 4 * width
        at = core * count + t if kind == "rows" else core
        piece = out_refs[w].at[:, pl.ds(pl.multiple_of(at * span, span), span)]
        slot = len(chunks) * 16 + number
        copies[number, 2, 0] = send(
            piece, piece, send_sem.at[slot], recv_sem.at[slot], to_core
        )

    small_copies = []

    def small_step(step):
        if step > 0:
            small_copies[step - 1].wait_recv()
            small_held[2 * step] = small_held[2 * step - 2] + small_held[2 * step - 1]
            if step == 3:
                small_out[0] = small_held[6]
        else:
            small_held[0] = small_ref[...]
        if step < 5:
            small_copies.append(
                send(
                    small_held.at[2 * step],
                    small_held.at[2 * step + 1],
                    small_send.at[step],
                    small_recv.at[step],
                    partners[step],
                )
            )
        else:
            small_out[1] = small_held[10]

    stages = (stage_one, stage_two, stage_three, stage_four, stage_five, stage_six, stage_seven)
    small_at = 0
    stage_three(order[0])
    for w in range(len(late)):
        turn(w)
    for tick in range(len(chunks) + len(stages)):
        for lag, stage in enumerate(stages):
            for number in range(len(chunks)):
                if number >= early_count:
                    due = number - early_count + lag == tick
                else:
                    rank = order.index(number)
                    due = rank - 2 + lag == tick and lag >= 2 and rank + lag > 2
                if due:
                    stage(number)
        if small_at < 6:
            small_step(small_at)
            small_at += 1
    for number in range(len(chunks)):
        copies[number, 2, 0].wait_recv()
    for copy in pending:
        copy.wait_send()


def sum_weights(early, early_arrays, products, small):
    late = [weight_plan(*product) for product in products]
    lefts, rights = ([product[1] for product in products], [product[2] for product in products])
    plan = early + late
    pieces = []
    for w, (kind, count, width, deep, halves, parted) in enumerate(plan):
        leads = [(4, 2, 2), (4, 2), (4,), (2,), (1,)]
        if w < len(early):
            leads[:2] = [(4,), (4,)]
        for chunk in range(count):
            for half in halves:
                pieces += [pltpu.VMEM(lead + (half, width), jnp.bfloat16) for lead in leads]
    outs = [jax.ShapeDtypeStruct((entry[3], 2 * plan_span(entry)), jnp.bfloat16) for entry in plan]
    chunk_count = sum(entry[1] for entry in plan)
    scratch = pair_scratch(late, lefts[0].shape[0]) + pieces
    dma = pltpu.SemaphoreType.DMA
    scratch += [pltpu.VMEM((11,) + small.shape, jnp.float32)]
    slots = chunk_count * 17
    scratch += [dma((slots,)), dma((slots,)), dma((2 * chunk_count,)), dma((6 * chunk_count,))]
    scratch += [dma((2 * len(late),)), dma((2 * len(late),)), dma((5,)), dma((5,)), dma((len(late),))]
    vmem, anywhere = (
        pl.BlockSpec(memory_space=pltpu.VMEM),
        pl.BlockSpec(memory_space=pl.ANY),
    )
    return pl.pallas_call(
        functools.partial(sum_kernel, early, late, plan_lead(plan)),
        out_shape=tuple(outs) + (jax.ShapeDtypeStruct((2,) + small.shape, jnp.float32),),
        in_specs=[vmem] * len(late) + [anywhere] * (len(late) + len(early_arrays)) + [vmem],
        out_specs=(anywhere,) * len(plan) + (vmem,),
        scratch_shapes=scratch,
        compiler_params=pltpu.CompilerParams(
            collective_id=1, has_side_effects=True, vmem_limit_bytes=60 * 1024 * 1024
        ),
        name="sum_weights",
    )(*lefts, *rights, *early_arrays, small)


def layer_norm(rows_in, gain_vec):
    row_mean = jnp.mean(rows_in, axis=-1, keepdims=True)
    centred = rows_in - row_mean
    variance = jnp.mean(centred * centred, axis=-1, keepdims=True)
    return centred * lax.rsqrt(variance + norm_eps) * gain_vec


def rotate(projected, cosine, sine):
    row_count, width = projected.shape
    half_width = HEAD_WIDTH // 2
    by_head = projected.reshape(row_count, width // HEAD_WIDTH, HEAD_WIDTH)
    turned = jnp.concatenate([by_head[..., half_width:], by_head[..., :half_width]], axis=-1)
    return (by_head * cosine[:, None, :] - turned * sine[:, None, :]).reshape(row_count, width)


def swap(value, axis, bit):
    pairs = [(i, i ^ bit) for i in range(lax.axis_size(axis))]
    return lax.ppermute(value, axis, pairs)


def bit_of(axis, bit):
    return (lax.axis_index(axis) // bit) % 2 == 1


def bits_below(count):
    return [1 << i for i in range(count.bit_length() - 1)]


def reduce_pieces(pieces, labels, order):
    labels = list(labels)
    for axis, bit in order:
        at = labels.index((axis, bit))
        labels.pop(at)
        first = lax.index_in_dim(pieces, 0, at, keepdims=False)
        second = lax.index_in_dim(pieces, 1, at, keepdims=False)
        upper = bit_of(axis, bit)
        arrived = swap(jnp.where(upper, first, second), axis, bit)
        kept = jnp.where(upper, second, first)
        pieces = (kept.astype(jnp.float32) + arrived.astype(jnp.float32)).astype(jnp.bfloat16)
    return pieces


def gather_pieces(piece, labels, order):
    held = []
    for axis, bit in reversed(order):
        arrived = swap(piece, axis, bit)
        upper = bit_of(axis, bit)
        held = [label for label in labels if label in held or label == (axis, bit)]
        piece = jnp.stack(
            [jnp.where(upper, arrived, piece), jnp.where(upper, piece, arrived)],
            axis=held.index((axis, bit)),
        )
    return piece


def keep_and_send(first, second):
    upper = bit_of("ctx", 1)
    return (jnp.where(upper, second, first), jnp.where(upper, first, second))


def core_product(left, first, second):
    kept, sent = keep_and_send(first, second)
    left_all = jnp.concatenate([left, swap(left, "ctx", 1)], axis=0)
    right_all = jnp.concatenate([kept, swap(sent, "ctx", 1)], axis=0)
    return lax.dot_general(
        left_all, right_all, (((0,), (0,)), ((), ())), preferred_element_type=jnp.float32
    ).astype(jnp.bfloat16)


def shard_sum(product, by_columns):
    shards = lax.axis_size("fsdp")
    slices = lax.axis_size("ctx") // 2
    rows, columns = product.shape
    shard_labels = [("fsdp", bit) for bit in reversed(bits_below(shards))]
    slice_labels = [("ctx", 2 * bit) for bit in reversed(bits_below(slices))]
    if by_columns:
        cut = product.reshape(shards, rows // shards, slices, columns // slices)
        cut = jnp.transpose(cut, (0, 2, 1, 3))
    else:
        cut = product.reshape(shards, slices, rows // shards // slices, columns)
    parts = []
    half = cut.shape[2] // 2
    tail = list(reversed(shard_labels))
    for lead, orders in (
        (cut[:, :, :half], list(reversed(slice_labels))),
        (cut[:, :, half:], slice_labels),
    ):
        pieces = lead.reshape((2,) * (len(shard_labels) + len(slice_labels)) + lead.shape[2:])
        piece = reduce_pieces(pieces, shard_labels + slice_labels, orders + tail)
        whole = gather_pieces(piece, slice_labels, orders)
        parts.append(whole.reshape((slices,) + piece.shape))
    both = jnp.concatenate(parts, axis=1)
    if by_columns:
        return jnp.transpose(both, (1, 0, 2)).reshape(rows // shards, columns)
    return both.reshape(rows // shards, columns)


def join_cores(own):
    other = swap(own, "ctx", 1)
    upper = bit_of("ctx", 1)
    return jnp.concatenate(
        [jnp.where(upper, other, own), jnp.where(upper, own, other)], axis=1
    ).astype(jnp.float32)


def sum_over(value, axes):
    for axis in axes:
        for bit in bits_below(lax.axis_size(axis)):
            value = value + swap(value, axis, bit)
    return value


def own_shard(vector):
    width = vector.shape[0] // lax.axis_size("fsdp")
    return lax.dynamic_slice_in_dim(vector, lax.axis_index("fsdp") * width, width, 0)


def weight_sums(
    hidden,
    grad_mlp_low,
    act_mlp,
    grad_leading,
    grad_trailing,
    act_attn,
    grad_projected,
    attn_low,
    grad_attn_low,
    small,
    early,
):
    shards, ctx_count = (lax.axis_size("fsdp"), lax.axis_size("ctx"))
    rows, ff_width = hidden.shape
    model_width = act_mlp.shape[1]
    if early is None:
        half, half_three = (model_width // 2, 3 * model_width // 2)
        pairs = (
            (hidden, grad_mlp_low[:, :half], grad_mlp_low[:, half:]),
            (act_mlp, grad_leading, grad_trailing),
            (act_attn, grad_projected[:, :half_three], grad_projected[:, half_three:]),
            (attn_low, grad_attn_low[:, :half], grad_attn_low[:, half:]),
        )
        totals = [
            join_cores(shard_sum(core_product(*pair), at == 0)) for at, pair in enumerate(pairs)
        ]
        over_pack = sum_over(small, ("ctx",))
        return totals + [jnp.stack([over_pack, sum_over(over_pack, ("fsdp",))])]
    total_attn, total_in, total_out, total_qkv, small_sums = sum_weights(
        *early, [("rows", act_attn, grad_projected, 3)], small
    )
    padded = total_in.shape[1] // 2
    total_in = jnp.concatenate(
        [total_in[:, :ff_width], total_in[:, padded : padded + ff_width]], axis=1
    )
    return [
        total.astype(jnp.float32) for total in (total_out, total_in, total_qkv, total_attn)
    ] + [small_sums]


def weight_sums_early(
    hidden, grad_mlp_low, act_mlp, grad_leading, grad_trailing, attn_low, grad_attn_low, held
):
    shards, ctx_count = (lax.axis_size("fsdp"), lax.axis_size("ctx"))
    ff_width = hidden.shape[1]
    if shards != 4 or ctx_count != 8 or act_mlp.shape[1] % 1024 != 0 or ff_width % 64 != 0:
        return (held, None)
    return early_sums(
        [
            ("rows", attn_low, grad_attn_low, 1),
            ("rows", act_mlp, (grad_leading, grad_trailing), 3),
            ("columns", hidden, grad_mlp_low, 1),
        ],
        held,
    )


def per_device(
    inputs,
    cotangent,
    lengths,
    piece_route,
    gain_one,
    qkv_weight,
    attn_out,
    gain_two,
    geglu_in,
    geglu_out,
):
    ctx_count = lax.axis_size("ctx")
    own_index = lax.axis_index("ctx")
    row_count = inputs.shape[1]
    model_width = inputs.shape[2]
    piece_rows = row_count // ctx_count
    tokens = row_count * ctx_count
    own_heads = model_width // HEAD_WIDTH // ctx_count
    own_width = own_heads * HEAD_WIDTH
    block_q = math.gcd(tokens, 384)
    block_k = math.gcd(tokens, 512)
    lengths_row = lengths[0]
    own_route = piece_route[0, 0]
    slot_ids = jnp.arange(ctx_count, dtype=jnp.int32)
    outgoing = jnp.sum(
        slot_ids[None, :] * (own_route[None, :] == slot_ids[:, None]).astype(jnp.int32), axis=1
    )

    def exchange(blocks):
        return lax.all_to_all(blocks, "ctx", split_axis=0, concat_axis=0, tiled=True)

    def to_slots(rows_in):
        return jnp.take(rows_in.reshape(ctx_count, piece_rows, model_width), outgoing, axis=0)

    def to_heads(rows_in):
        by_heads = rows_in.reshape(row_count, ctx_count, -1)
        return exchange(jnp.transpose(by_heads, (1, 0, 2))).reshape(tokens, -1)

    def to_rows(heads_in):
        return exchange(heads_in.reshape(ctx_count, row_count, -1))

    both_arrived = exchange(
        jnp.concatenate([to_slots(inputs[0]), to_slots(cotangent[0])], axis=1)
    )
    arrived, grad_arrived = (both_arrived[:, :piece_rows], both_arrived[:, piece_rows:])
    residual = arrived.reshape(row_count, model_width).astype(jnp.float32)
    places = own_index * row_count + jnp.arange(row_count, dtype=jnp.int32)
    unused_begin, unused_end, offset, is_valid = spans(places, lengths_row)
    pack_begin, pack_end, unused_offset, unused_valid = spans(
        jnp.arange(tokens, dtype=jnp.int32), lengths_row
    )
    grad_final = jnp.where(
        is_valid[:, None], grad_arrived.reshape(row_count, model_width).astype(jnp.float32), 0.0
    )
    gains = jnp.pad(jnp.stack([gain_one, gain_two]), ((0, 14), (0, 0)))
    gains_full, qkv_full = gather_weights([gains, qkv_weight])
    gains_full = gains_full.reshape(-1, 16, gains.shape[1])
    gain_attn = gains_full[:, 0].reshape(-1).astype(jnp.float32)
    gain_mlp = gains_full[:, 1].reshape(-1).astype(jnp.float32)
    act_attn = layer_norm(residual, gain_attn).astype(jnp.bfloat16)
    later = [attn_out, geglu_in, geglu_out]
    row_cosine, row_sine = rotary_tables(offset, own_heads)
    if lax.axis_size("fsdp") == 4 and ctx_count == 8 and own_width == 128:
        attn_full, in_full, out_full, qkv_heads = gather_weights(
            later, (act_attn, qkv_full, row_cosine, row_sine)
        )
    else:
        attn_full, in_full, out_full = gather_weights(later)
        projected = jnp.dot(act_attn, qkv_full, preferred_element_type=jnp.float32)
        cosine, sine = rotary_tables(offset, 1)
        queries, keys = (
            rotate(projected[:, :model_width], cosine, sine).astype(jnp.bfloat16),
            rotate(projected[:, model_width : 2 * model_width], cosine, sine).astype(jnp.bfloat16),
        )
        values = projected[:, 2 * model_width :].astype(jnp.bfloat16)
        joined = jnp.stack(
            [part.reshape(row_count, ctx_count, own_width) for part in (queries, keys, values)], axis=2
        )
        qkv_heads = to_heads(joined.reshape(row_count, -1))
    low, high = key_range(pack_begin, pack_end, block_q, block_k)
    pack_begin, pack_end = (pack_begin[None, :], pack_end[None, :])
    attended_heads, attended_low, log_total = attention_forward(
        qkv_heads, pack_begin, pack_end, low, high, own_heads, block_q, block_k
    )
    attn_low = jnp.transpose(to_rows(attended_low), (1, 0, 2)).reshape(
        row_count, model_width
    )
    branch_attn = jnp.dot(attn_low, attn_full, preferred_element_type=jnp.float32)
    middle = residual + branch_attn
    act_mlp = layer_norm(middle, gain_mlp).astype(jnp.bfloat16)
    up_both = jnp.dot(act_mlp, in_full, preferred_element_type=jnp.float32)
    ff_width = up_both.shape[1] // 2
    hidden = (jax.nn.gelu(up_both[:, :ff_width], approximate=False) * up_both[:, ff_width:]).astype(
        jnp.bfloat16
    )
    branch_mlp = jnp.dot(hidden, out_full, preferred_element_type=jnp.float32)
    final_rows = jnp.where(is_valid[:, None], middle + branch_mlp, 0.0)
    square_sums = jnp.stack(
        [
            jnp.sum(final_rows * final_rows),
            jnp.sum(jnp.where(is_valid[:, None], branch_attn * branch_attn, 0.0)),
            jnp.sum(jnp.where(is_valid[:, None], branch_mlp * branch_mlp, 0.0)),
        ]
    )
    out_slots = final_rows.astype(jnp.bfloat16).reshape(ctx_count, piece_rows, model_width)
    grad_mlp_low = grad_final.astype(jnp.bfloat16)
    grad_hidden = lax.dot_general(
        grad_mlp_low, out_full, NT, preferred_element_type=jnp.float32
    )

    def gated(leading, trailing):
        return jax.nn.gelu(leading, approximate=False) * trailing

    unused_gate, gate_back = jax.vjp(gated, up_both[:, :ff_width], up_both[:, ff_width:])
    grad_leading, grad_trailing = gate_back(grad_hidden)
    grad_leading, grad_trailing = (
        grad_leading.astype(jnp.bfloat16),
        grad_trailing.astype(jnp.bfloat16),
    )
    grad_up = jnp.concatenate([grad_leading, grad_trailing], axis=1)
    grad_act_mlp = lax.dot_general(grad_up, in_full, NT, preferred_element_type=jnp.float32)
    unused_norm, norm_back_mlp = jax.vjp(layer_norm, middle, gain_mlp)
    grad_middle_norm, grad_gain_mlp = norm_back_mlp(grad_act_mlp)
    grad_middle = grad_final + grad_middle_norm
    grad_attn_low = grad_middle.astype(jnp.bfloat16)
    grad_attended = lax.dot_general(
        grad_attn_low, attn_full, NT, preferred_element_type=jnp.float32
    ).astype(jnp.bfloat16)
    grad_attended_heads, early = weight_sums_early(
        hidden,
        grad_mlp_low,
        act_mlp,
        grad_leading,
        grad_trailing,
        attn_low,
        grad_attn_low,
        to_heads(grad_attended),
    )
    block_back = math.gcd(tokens, 256)
    low_back, high_back = key_range(pack_begin[0], pack_end[0], block_q, block_back)
    grad_heads = attention_backward(
        qkv_heads,
        attended_heads,
        grad_attended_heads,
        log_total,
        pack_begin,
        pack_end,
        low_back,
        high_back,
        [] if early is None else [early[1][0][0]],
        own_heads,
        block_q,
        block_back,
    )
    if early is not None:
        grad_heads, early = second_step(grad_heads, early)
    grad_rows = to_rows(grad_heads)
    if own_width % 128 == 0:
        grad_projected, grad_act_attn = finish_rows(
            grad_rows, row_cosine, row_sine, qkv_full, own_heads
        )
    else:
        by_part = jnp.transpose(
            grad_rows.reshape(ctx_count, row_count, 3, own_width), (2, 1, 0, 3)
        ).reshape(3, row_count, model_width)
        cosine, sine = rotary_tables(offset, 1)
        grad_projected = jnp.concatenate(
            [
                rotate(by_part[part].astype(jnp.float32), cosine, -sine).astype(jnp.bfloat16)
                for part in (0, 1)
            ]
            + [by_part[2]],
            axis=1,
        )
        grad_act_attn = lax.dot_general(
            grad_projected, qkv_full, NT, preferred_element_type=jnp.float32
        )
    unused_first, norm_back_attn = jax.vjp(layer_norm, residual, gain_attn)
    grad_resid_norm, grad_gain_attn = norm_back_attn(grad_act_attn)
    grad_residual = (grad_middle + grad_resid_norm).astype(jnp.bfloat16)
    grad_slots = grad_residual.reshape(ctx_count, piece_rows, model_width)
    back = exchange(jnp.concatenate([out_slots, grad_slots], axis=1))
    block_out, grad_inputs = (
        jnp.take(half, own_route, axis=0).reshape(1, row_count, model_width)
        for half in (back[:, :piece_rows], back[:, piece_rows:])
    )
    small = jnp.stack(
        [grad_gain_attn, grad_gain_mlp, jnp.pad(square_sums, (0, model_width - 3))]
        + [jnp.zeros((model_width,), jnp.float32)] * 5
    )
    total_out, total_in, total_qkv, total_attn, small_sums = weight_sums(
        hidden,
        grad_mlp_low,
        act_mlp,
        grad_leading,
        grad_trailing,
        act_attn,
        grad_projected,
        attn_low,
        grad_attn_low,
        small,
        early,
    )
    total_gain_one = own_shard(small_sums[1, 0])
    total_gain_two = own_shard(small_sums[1, 1])
    total_squares = small_sums[0, 2, :3]
    valid_count = jnp.sum(lengths_row).astype(jnp.float32)
    rms_stats = jnp.sqrt(total_squares / (valid_count * model_width))[None, :]
    return (
        block_out,
        grad_inputs,
        total_gain_one,
        total_qkv,
        total_attn,
        total_gain_two,
        total_in,
        total_out,
        rms_stats,
    )


def solution(mesh):
    placed = (
        P("fsdp", "ctx", None),
        P("fsdp", "ctx", None),
        P("fsdp", None),
        P("fsdp", "ctx", None),
        P("fsdp"),
        P("fsdp", None),
        P("fsdp", None),
        P("fsdp"),
        P("fsdp", None),
        P("fsdp", None),
    )
    return jax.shard_map(
        per_device,
        mesh=mesh,
        in_specs=placed,
        out_specs=(
            P("fsdp", "ctx", None),
            P("fsdp", "ctx", None),
            P("fsdp"),
            P("fsdp", None),
            P("fsdp", None),
            P("fsdp"),
            P("fsdp", None),
            P("fsdp", None),
            P("fsdp", None),
        ),
        check_vma=False,
    )
```

```python
import functools
import math
import jax
import jax.numpy as jnp
from jax import lax
from jax.experimental import pallas as pl
from jax.experimental.pallas import tpu as pltpu
from jax.sharding import PartitionSpec as P

HEAD_WIDTH = 64
norm_eps = 1e-05
masked_score = -1e30


def head_stack(rows_in, head_count):
    if head_count == 1:
        return rows_in
    lane_head = lax.broadcasted_iota(jnp.int32, rows_in.shape, 1) // HEAD_WIDTH
    zero = jnp.zeros_like(rows_in)
    return jnp.concatenate(
        [jnp.where(lane_head == h, rows_in, zero) for h in range(head_count)], axis=0
    )


def head_pick(stacked_t, head_count, block):
    return jnp.concatenate(
        [
            stacked_t[h * HEAD_WIDTH : (h + 1) * HEAD_WIDTH, h * block : (h + 1) * block]
            for h in range(head_count)
        ],
        axis=0,
    ).T


NT = (((1,), (1,)), ((), ()))


def forward_kernel(
    head_count, block_q, block_k, low_ref, high_ref, begin_ref, end_ref, qkv_ref, out_ref, low_out_ref, log_ref, turned_ref
):
    width = out_ref.shape[1]
    step = pl.program_id(0)

    @pl.when(step == 0)
    def prepare():
        turned_ref[...] = qkv_ref[:, 2 * width :].astype(jnp.float32).T.astype(jnp.bfloat16)

    rows = pl.ds(pl.multiple_of(step * block_q, block_q), block_q)
    scale = 1.0 / math.sqrt(HEAD_WIDTH)
    stacked = head_stack(qkv_ref[rows, :width] * jnp.asarray(scale, jnp.bfloat16), head_count)
    begin = jnp.concatenate([begin_ref[:, rows]] * head_count, axis=1)
    end = jnp.concatenate([end_ref[:, rows]] * head_count, axis=1)

    def body(index, carried):
        top, total, acc = carried
        first = pl.multiple_of(index * block_k, block_k)
        keys = qkv_ref[pl.ds(first, block_k), width : 2 * width]
        scores = lax.dot_general(keys, stacked, NT, preferred_element_type=jnp.float32)
        place = first + lax.broadcasted_iota(jnp.int32, scores.shape, 0)
        scores = jnp.where((place >= begin) & (place < end), scores, masked_score)
        new_top = jnp.maximum(top, jnp.max(scores, axis=0, keepdims=True))
        fresh = jnp.exp(scores - new_top)
        fade = jnp.exp(top - new_top)
        total = total * fade + jnp.sum(fresh, axis=0, keepdims=True)
        acc = acc * fade + jnp.dot(
            turned_ref[:, pl.ds(first, block_k)],
            fresh.astype(jnp.bfloat16),
            preferred_element_type=jnp.float32,
        )
        return (new_top, total, acc)

    lanes = head_count * block_q
    top, total, acc = lax.fori_loop(
        low_ref[step],
        high_ref[step],
        body,
        (
            jnp.full((1, lanes), masked_score, jnp.float32),
            jnp.zeros((1, lanes), jnp.float32),
            jnp.zeros((width, lanes), jnp.float32),
        ),
    )
    valid = end > begin
    safe = jnp.where(valid, total, 1.0)
    acc = jnp.where(valid, acc / safe, 0.0)
    log_total = jnp.where(valid, top + jnp.log(safe), 0.0)
    attended = head_pick(acc, head_count, block_q)
    out_ref[...] = attended
    low_out_ref[...] = attended.astype(jnp.bfloat16)
    log_ref[0] = log_total


def attention_forward(qkv, begin, end, low, high, head_count, block_q, block_k):
    tokens = qkv.shape[0]
    width = head_count * HEAD_WIDTH
    steps = tokens // block_q
    whole = lambda shape: pl.BlockSpec(shape, lambda i, *_: (0,) * len(shape))
    pairs = tokens * tokens // 4 * head_count
    return pl.pallas_call(
        functools.partial(forward_kernel, head_count, block_q, block_k),
        out_shape=(
            jax.ShapeDtypeStruct((tokens, width), jnp.float32),
            jax.ShapeDtypeStruct((tokens, width), jnp.bfloat16),
            jax.ShapeDtypeStruct((steps, 1, head_count * block_q), jnp.float32),
        ),
        grid_spec=pltpu.PrefetchScalarGridSpec(
            num_scalar_prefetch=2,
            grid=(steps,),
            in_specs=[whole((1, tokens)), whole((1, tokens)), whole((tokens, 3 * width))],
            out_specs=(
                pl.BlockSpec((block_q, width), lambda i, *_: (i, 0)),
                pl.BlockSpec((block_q, width), lambda i, *_: (i, 0)),
                pl.BlockSpec((1, 1, head_count * block_q), lambda i, *_: (i, 0, 0)),
            ),
            scratch_shapes=[pltpu.VMEM((width, tokens), jnp.bfloat16)],
        ),
        cost_estimate=pl.CostEstimate(
            flops=pairs * 512, bytes_accessed=tokens * width * 12, transcendentals=pairs
        ),
        name="attention_forward",
    )(low, high, begin, end, qkv)


def turn_back(grads, cosine, sine, head_count):
    half = HEAD_WIDTH // 2
    pieces = []
    for h in range(head_count):
        base = h * HEAD_WIDTH
        pieces += [grads[:, base + half : base + HEAD_WIDTH], grads[:, base : base + half]]
    return grads * cosine + jnp.concatenate(pieces, axis=1) * sine


def backward_kernel(
    head_count,
    block_q,
    block_k,
    low_ref,
    high_ref,
    begin_ref,
    end_ref,
    qkv_ref,
    attended_ref,
    grad_ref,
    log_ref,
    *refs,
):
    out_ref, turned_ref, key_acc, value_acc = refs[-4:]
    width = attended_ref.shape[1]
    step = pl.program_id(0)

    @pl.when(step == 0)
    def prepare():
        turned_ref[...] = qkv_ref[:, width : 2 * width].astype(jnp.float32).T.astype(jnp.bfloat16)
        key_acc[...] = jnp.zeros_like(key_acc)
        value_acc[...] = jnp.zeros_like(value_acc)

    rows = pl.ds(pl.multiple_of(step * block_q, block_q), block_q)
    scale = 1.0 / math.sqrt(HEAD_WIDTH)
    stacked = head_stack(qkv_ref[rows, :width] * jnp.asarray(scale, jnp.bfloat16), head_count)
    grads = grad_ref[rows, :]
    grad_stacked = head_stack(grads, head_count)
    begin = jnp.concatenate([begin_ref[:, rows]] * head_count, axis=1)
    end = jnp.concatenate([end_ref[:, rows]] * head_count, axis=1)
    product = (grads.astype(jnp.float32) * attended_ref[rows, :]).T
    delta = jnp.concatenate(
        [
            jnp.sum(product[h * HEAD_WIDTH : (h + 1) * HEAD_WIDTH], axis=0, keepdims=True)
            for h in range(head_count)
        ],
        axis=1,
    )
    log_total = log_ref[0]

    def body(index, acc):
        first = pl.multiple_of(index * block_k, block_k)
        span = pl.ds(first, block_k)
        keys = qkv_ref[span, width : 2 * width]
        values = qkv_ref[span, 2 * width :]
        scores = lax.dot_general(keys, stacked, NT, preferred_element_type=jnp.float32)
        grad_probs = lax.dot_general(values, grad_stacked, NT, preferred_element_type=jnp.float32)
        place = first + lax.broadcasted_iota(jnp.int32, scores.shape, 0)
        scores = jnp.where((place >= begin) & (place < end), scores, masked_score)
        probs = jnp.exp(scores - log_total)
        grad_scores = (probs * (grad_probs - delta)).astype(jnp.bfloat16)
        value_acc[span, :] += jnp.dot(
            probs.astype(jnp.bfloat16), grad_stacked, preferred_element_type=jnp.float32
        )
        key_acc[span, :] += jnp.dot(grad_scores, stacked, preferred_element_type=jnp.float32)
        return acc + jnp.dot(
            turned_ref[:, span], grad_scores, preferred_element_type=jnp.float32
        )

    acc = lax.fori_loop(
        low_ref[step],
        high_ref[step],
        body,
        jnp.zeros((width, head_count * block_q), jnp.float32),
    )
    grad_queries = head_pick(acc, head_count, block_q) * scale
    out_ref[rows, :width] = grad_queries.astype(jnp.bfloat16)

    @pl.when(step == pl.num_programs(0) - 1)
    def finish():
        @pl.loop(0, pl.num_programs(0))
        def each(index):
            span = pl.ds(pl.multiple_of(index * block_q, block_q), block_q)
            out_ref[span, width : 2 * width] = key_acc[span, :].astype(jnp.bfloat16)
            out_ref[span, 2 * width :] = value_acc[span, :].astype(jnp.bfloat16)


def attention_backward(
    qkv, attended, grads, log_total, begin, end, low, high, after, head_count, block_q, block_k
):
    tokens = qkv.shape[0]
    width = head_count * HEAD_WIDTH
    steps = tokens // block_q
    whole = lambda shape: pl.BlockSpec(shape, lambda i, *_: (0,) * len(shape))
    pairs = tokens * tokens // 4 * head_count
    return pl.pallas_call(
        functools.partial(backward_kernel, head_count, block_q, block_k),
        out_shape=jax.ShapeDtypeStruct((tokens, 3 * width), jnp.bfloat16),
        grid_spec=pltpu.PrefetchScalarGridSpec(
            num_scalar_prefetch=2,
            grid=(steps,),
            in_specs=[
                whole((1, tokens)),
                whole((1, tokens)),
                whole((tokens, 3 * width)),
                whole((tokens, width)),
                whole((tokens, width)),
                pl.BlockSpec((1, 1, head_count * block_q), lambda i, *_: (i, 0, 0)),
            ]
            + [pl.BlockSpec(memory_space=pl.ANY)] * len(after),
            out_specs=whole((tokens, 3 * width)),
            scratch_shapes=[
                pltpu.VMEM((width, tokens), jnp.bfloat16),
                pltpu.VMEM((tokens, width), jnp.float32),
                pltpu.VMEM((tokens, width), jnp.float32),
            ],
        ),
        cost_estimate=pl.CostEstimate(
            flops=pairs * 1280, bytes_accessed=tokens * width * 30, transcendentals=pairs
        ),
        name="attention_backward",
    )(low, high, begin, end, qkv, attended, grads, log_total, *after)


def rows_kernel(head_count, heads_ref, cosine_ref, sine_ref, query_ref, key_ref, value_ref, out_ref, act_ref):
    width = heads_ref.shape[2] // 3
    step = pl.program_id(0)
    total = out_ref.shape[1] // 3
    owners = heads_ref.shape[0]
    pieces = []
    for part in range(3):
        for owner in range(owners):
            piece = heads_ref[owner, :, part * width : (part + 1) * width]
            if part < 2:
                piece = turn_back(
                    piece.astype(jnp.float32), cosine_ref[...], sine_ref[...], head_count
                ).astype(jnp.bfloat16)
            first = pl.multiple_of(part * total + (step * owners + owner) * width, width)
            out_ref[:, pl.ds(first, width)] = piece
            pieces.append(piece)
    weights = jnp.concatenate([query_ref[...], key_ref[...], value_ref[...]], axis=1)
    product = lax.dot_general(
        jnp.concatenate(pieces, axis=1), weights, NT, preferred_element_type=jnp.float32
    )

    @pl.when(step == 0)
    def begin():
        act_ref[...] = product

    @pl.when(step > 0)
    def add():
        act_ref[...] += product


def finish_rows(heads, cosine, sine, qkv_full, head_count):
    owners, rows, columns = heads.shape
    width = columns // 3
    depth = qkv_full.shape[0]
    whole = lambda shape: pl.BlockSpec(shape, lambda i: (0,) * len(shape))
    steps = owners // 2
    part_of = lambda part: pl.BlockSpec((depth, 2 * width), lambda i: (0, part * steps + i))
    return pl.pallas_call(
        functools.partial(rows_kernel, head_count),
        out_shape=(
            jax.ShapeDtypeStruct((rows, owners * columns), jnp.bfloat16),
            jax.ShapeDtypeStruct((rows, depth), jnp.float32),
        ),
        grid=(steps,),
        in_specs=[
            pl.BlockSpec((2, rows, columns), lambda i: (i, 0, 0)),
            whole((rows, width)),
            whole((rows, width)),
            part_of(0),
            part_of(1),
            part_of(2),
        ],
        out_specs=(whole((rows, owners * columns)), whole((rows, depth))),
        cost_estimate=pl.CostEstimate(
            flops=2 * rows * depth * owners * columns,
            bytes_accessed=2 * depth * owners * columns + 4 * rows * owners * columns,
            transcendentals=0,
        ),
        name="finish_rows",
    )(heads, cosine, sine, qkv_full, qkv_full, qkv_full)


def spans(places, lengths_row):
    ends = jnp.cumsum(lengths_row)
    past = (places[:, None] >= ends[None, :]).astype(jnp.int32)
    begin = jnp.sum(past * lengths_row[None, :], axis=1)
    before = (places[:, None] >= (ends - lengths_row)[None, :]).astype(jnp.int32)
    end = jnp.sum(before * lengths_row[None, :], axis=1)
    valid = places < ends[-1]
    return (jnp.where(valid, begin, 0), jnp.where(valid, end, 0), places - begin, valid)


def key_range(begin, end, block_q, block_k):
    begin_blocks = jnp.where(end > begin, begin, jnp.int32(1 << 30)).reshape(-1, block_q)
    high = (jnp.max(end.reshape(-1, block_q), axis=1) + block_k - 1) // block_k
    low = jnp.minimum(jnp.min(begin_blocks, axis=1) // block_k, high)
    return (low, high)


def rotary_tables(offset, head_count):
    half = HEAD_WIDTH // 2
    inverse = 160000.0 ** (-2.0 * jnp.arange(half, dtype=jnp.float32) / HEAD_WIDTH)
    angles = offset.astype(jnp.float32)[:, None] * inverse[None, :]
    cosine, sine = (jnp.cos(angles), jnp.sin(angles))
    return (
        jnp.concatenate([cosine, cosine] * head_count, axis=1),
        jnp.concatenate([sine, -sine] * head_count, axis=1),
    )


def toggled(index, bit):
    return index + bit - 2 * bit * ((index // bit) % 2)


def gather_kernel(shapes, projects, *refs):
    count = len(shapes)
    shard_refs, refs = (refs[:count], refs[count:])
    if projects:
        act_ref, qkv_ref, cosine_ref, sine_ref = refs[:4]
        heads_ref = refs[4 + count]
        columns_ref, held_ref, load_sem, head_send, head_recv, own_sem = refs[count + 8 :]
        refs = refs[4 : 4 + count] + refs[count + 5 : count + 8]
    full_refs = refs[:count]
    send_sem, recv_sem, local_sem = refs[count:]
    shards = lax.axis_size("fsdp")
    slices = lax.axis_size("ctx") // 2
    own_ctx, own_shard = (lax.axis_index("ctx"), lax.axis_index("fsdp"))
    core, chip = (own_ctx % 2, own_ctx // 2)
    barrier = pltpu.get_barrier_semaphore()
    partners = [{"fsdp": toggled(own_shard, bit)} for bit in (1, 2)]
    partners += [{"ctx": toggled(own_ctx, bit)} for bit in (1, 2, 4)]

    def owner_at(relation):
        owner = own_ctx
        for bit in (1, 2, 4):
            if relation & bit:
                owner = toggled(owner, bit)
        return owner

    if projects:
        partners += [{"ctx": owner_at(relation)} for relation in (3, 5, 6, 7)]
    for partner in partners:
        pl.semaphore_signal(
            barrier, inc=1, device_id=partner, device_id_type=pl.DeviceIdType.MESH
        )
    pl.semaphore_wait(barrier, len(partners))
    to_one, to_two, to_core, to_x, to_y = partners[:5]

    def shard_at(step):
        if step == 0:
            return own_shard
        if step == 3:
            return toggled(toggled(own_shard, 1), 2)
        return toggled(own_shard, step)

    def region(ref, weight, step, chip_at, half):
        if shapes[weight] == "small":
            return ref if len(ref.shape) == 2 else ref.at[shard_at(step)]
        if shapes[weight] == "rows":
            rows = ref.shape[-2]
            span = pl.ds(0, rows) if half is None else pl.ds(half * (rows // 2), rows // 2)
            if len(ref.shape) == 4:
                return ref.at[core, chip_at, span, :]
            return ref.at[shard_at(step), core, chip_at, span, :]
        rows = ref.shape[-2]
        first = (rows // 2) // 16 * 16
        spans_of = {None: pl.ds(0, rows), 0: pl.ds(0, first), 1: pl.ds(first, rows - first)}
        width = ref.shape[-1] // (2 * slices)
        columns = pl.ds(pl.multiple_of((core * slices + chip_at) * width, width), width)
        if len(ref.shape) == 2:
            return ref.at[spans_of[half], columns]
        return ref.at[shard_at(step), spans_of[half], columns]

    def core_region(ref, weight, step):
        if shapes[weight] == "rows":
            return ref.at[shard_at(step), core]
        width = ref.shape[-1] // 2
        return ref.at[shard_at(step), :, pl.ds(pl.multiple_of(core * width, width), width)]

    pending = []

    def send(source, target, slot, partner):
        copy = pltpu.make_async_remote_copy(
            src_ref=source,
            dst_ref=target,
            send_sem=send_sem.at[slot],
            recv_sem=recv_sem.at[slot],
            device_id=partner,
            device_id_type=pl.DeviceIdType.MESH,
        )
        copy.start()
        pending.append(copy)
        return copy

    copies = {}
    local = []

    def slot_of(weight, step, kind):
        return (weight * 3 + step - 1) * 8 + kind

    def shard_sends(weight):
        source = region(shard_refs[weight], weight, 0, chip, None)
        target = region(full_refs[weight], weight, 0, chip, None)
        copies[weight, 2, 0] = send(source, target, slot_of(weight, 2, 0), to_two)
        copies[weight, 1, 0] = send(source, target, slot_of(weight, 1, 0), to_one)
        target = full_refs[weight].at[own_shard]
        copy = pltpu.make_async_copy(shard_refs[weight], target, local_sem.at[weight])
        copy.start()
        local.append(copy)

    def shard_forward(weight):
        copies[weight, 2, 0].wait_recv()
        piece = region(full_refs[weight], weight, 2, chip, None)
        copies[weight, 3, 0] = send(piece, piece, slot_of(weight, 3, 0), to_one)

    def plane_sends(weight, step):
        lead = region(full_refs[weight], weight, step, chip, 0)
        rest = region(full_refs[weight], weight, step, chip, 1)
        for kind, piece, partner in ((1, lead, to_x), (2, rest, to_y), (3, lead, to_y), (4, rest, to_x)):
            copies[weight, step, kind] = send(piece, piece, slot_of(weight, step, kind), partner)

    def plane_forward(weight, step):
        copies[weight, step, 1].wait_recv()
        lead = region(full_refs[weight], weight, step, toggled(chip, 1), 0)
        copies[weight, step, 5] = send(lead, lead, slot_of(weight, step, 5), to_y)
        copies[weight, step, 2].wait_recv()
        rest = region(full_refs[weight], weight, step, toggled(chip, 2), 1)
        copies[weight, step, 6] = send(rest, rest, slot_of(weight, step, 6), to_x)

    def core_send(weight, step):
        for kind in (3, 4, 5, 6):
            copies[weight, step, kind].wait_recv()
        piece = core_region(full_refs[weight], weight, step)
        copies[weight, step, 7] = send(piece, piece, slot_of(weight, step, 7), to_core)

    chip_order = (3, 1, 2, 0)

    def start_loads():
        loads = {}
        for chip_bits in chip_order:
            owner_chip = owner_at(2 * chip_bits) // 2
            for part in range(3):
                width = columns_ref.shape[2] // 3
                total = qkv_ref.shape[1] // 3
                first = pl.multiple_of(part * total + owner_chip * width, width)
                loads[chip_bits, part] = pltpu.make_async_copy(
                    qkv_ref.at[:, pl.ds(first, width)],
                    columns_ref.at[chip_bits, :, pl.ds(part * width, width)],
                    load_sem.at[chip_bits * 3 + part],
                )
                loads[chip_bits, part].start()
        return loads

    def project(chip_bits, loads):
        for part in range(3):
            loads[chip_bits, part].wait()
        rows, own_width = (act_ref.shape[0], held_ref.shape[2] // 3)
        product = jnp.dot(
            act_ref[...], columns_ref[chip_bits], preferred_element_type=jnp.float32
        )
        for core_at in (0, 1):
            slot = 2 * chip_bits + core + core_at - 2 * core * core_at
            for part in range(3):
                first = (2 * part + core_at) * own_width
                piece = product[:, first : first + own_width]
                if part < 2:
                    half = HEAD_WIDTH // 2
                    turned = []
                    for base in range(0, own_width, HEAD_WIDTH):
                        turned += [piece[:, base + half : base + HEAD_WIDTH], piece[:, base : base + half]]
                    piece = piece * cosine_ref[...] - jnp.concatenate(turned, axis=1) * sine_ref[...]
                held_ref[slot, :, part * own_width : (part + 1) * own_width] = piece.astype(jnp.bfloat16)
        target = heads_ref.at[pl.ds(pl.multiple_of(own_ctx * rows, rows), rows), :]
        for core_bit in (0, 1):
            relation = 2 * chip_bits + core_bit
            if relation == 0:
                copy = pltpu.make_async_copy(held_ref.at[0], target, own_sem.at[0])
                copy.start()
                local.append(copy)
                continue
            copy = pltpu.make_async_remote_copy(
                src_ref=held_ref.at[relation],
                dst_ref=target,
                send_sem=head_send.at[relation],
                recv_sem=head_recv.at[relation],
                device_id={"ctx": owner_at(relation)},
                device_id_type=pl.DeviceIdType.MESH,
            )
            copy.start()
            pending.append(copy)
            arriving.append(copy)

    arriving = []
    sent = 1
    if projects:
        loads = start_loads()
        for weight in range(count):
            shard_sends(weight)
        sent = count
        for chip_bits in chip_order:
            project(chip_bits, loads)
    else:
        shard_sends(0)
    for weight in range(count):
        if weight + 1 >= sent and weight + 1 < count:
            shard_sends(weight + 1)
        shard_forward(weight)
        copies[weight, 1, 0].wait_recv()
        if shapes[weight] == "small":
            copies[weight, 3, 0].wait_recv()
            continue
        plane_sends(weight, 1)
        plane_sends(weight, 2)
        copies[weight, 3, 0].wait_recv()
        plane_sends(weight, 3)
        for step in (1, 2, 3):
            plane_forward(weight, step)
        if weight > 0 and shapes[weight - 1] != "small":
            for step in (1, 2, 3):
                core_send(weight - 1, step)
    for step in (1, 2, 3):
        core_send(count - 1, step)
    for weight in range(count):
        if shapes[weight] != "small":
            for step in (1, 2, 3):
                copies[weight, step, 7].wait_recv()
    for copy in arriving:
        copy.wait_recv()
    for copy in pending:
        copy.wait_send()
    for copy in local:
        copy.wait()


def gather_weights(weights, projection=None):
    shards, ctx_count = (lax.axis_size("fsdp"), lax.axis_size("ctx"))
    slices = ctx_count // 2
    shapes, views, outs = ([], [], [])
    for weight in weights:
        rows, columns = weight.shape
        if rows % (32 * ctx_count) == 0:
            shapes.append("rows")
            views.append(weight.reshape(2, slices, rows // ctx_count, columns))
            outs.append((shards, 2, slices, rows // ctx_count, columns))
        elif rows == 16:
            shapes.append("small")
            views.append(weight)
            outs.append((shards, rows, columns))
        elif columns % (128 * ctx_count) == 0 and rows % 16 == 0:
            shapes.append("columns")
            views.append(weight)
            outs.append((shards, rows, columns))
    if shards != 4 or ctx_count != 8 or len(views) < len(weights):
        return [lax.all_gather(weight, "fsdp", axis=0, tiled=True) for weight in weights]
    slots = len(views) * 24
    vmem, anywhere, dma = (
        pl.BlockSpec(memory_space=pltpu.VMEM),
        pl.BlockSpec(memory_space=pl.ANY),
        pltpu.SemaphoreType.DMA,
    )
    in_specs = [vmem] * len(views)
    scratch = [dma((slots,)), dma((slots,)), dma((len(views),))]
    if projection is not None:
        act_attn, qkv_full = projection[:2]
        rows, own_columns = (act_attn.shape[0], qkv_full.shape[1] // ctx_count)
        views += list(projection)
        in_specs += [vmem, anywhere, vmem, vmem]
        outs.append((ctx_count * rows, own_columns))
        scratch += [
            pltpu.VMEM((slices, qkv_full.shape[0], 2 * own_columns), jnp.bfloat16),
            pltpu.VMEM((ctx_count, rows, own_columns), jnp.bfloat16),
            dma((3 * slices,)),
            dma((ctx_count,)),
            dma((ctx_count,)),
            dma((1,)),
        ]
    held = pl.pallas_call(
        functools.partial(gather_kernel, shapes, projection is not None),
        out_shape=tuple(jax.ShapeDtypeStruct(out, jnp.bfloat16) for out in outs),
        in_specs=in_specs,
        out_specs=tuple(anywhere for out in outs),
        scratch_shapes=scratch,
        compiler_params=pltpu.CompilerParams(
            collective_id=0 if projection is None else 2,
            has_side_effects=True,
            vmem_limit_bytes=60 * 1024 * 1024,
        ),
        name="gather_weights" if projection is None else "gather_and_project",
    )(*views)
    return [whole.reshape(-1, whole.shape[-1]) for whole in held]


def pair_steps(plan, lead_rows, left_refs, right_refs, turned_refs, whole_refs, sems, core, pending, send):
    pair_send, pair_recv, near_sem = sems
    to_core = {"ctx": toggled(lax.axis_index("ctx"), 1)}

    def send_core(source, target, sent, got, start=True):
        return send(source, target, sent, got, to_core, start)

    rows = left_refs[0].shape[0] if left_refs else 0
    pairs = []

    def begin(w):
        entry = plan[w]
        span, right = (plan_span(entry), right_refs[w])
        own_part, other_part = (whole_refs[w].at[pl.ds(0, rows)], whole_refs[w].at[pl.ds(rows, rows)])

        def exchange(own_half, other_half, start=True):
            near = pltpu.make_async_copy(own_half, own_part, near_sem.at[w])
            if start:
                near.start()
            sems = (pair_send.at[2 * w], pair_recv.at[2 * w])
            return [near, send_core(other_half, other_part, *sems, start)]

        if entry[5]:
            ways = [exchange(right[at], right[1 - at], False) for at in (0, 1)]
            for at in (0, 1):

                @pl.when(core == at)
                def start():
                    for copy in ways[at]:
                        copy.start()

            pairs.append(ways[0])
            pending.append(ways[0][1])
        else:
            halves = [
                right.at[:, pl.ds(pl.multiple_of(at * span, span), span)] for at in (core, 1 - core)
            ]
            pairs.append(exchange(*halves))

    def turn(w):
        left, turned = (left_refs[w], turned_refs[w])
        block = 512
        for first in range(0, left.shape[1], block):
            last = min(first + block, left.shape[1])
            turned[first:last, :rows] = (
                left[:, first:last].astype(jnp.float32).T.astype(jnp.bfloat16)
            )
        pairs[w].append(
            send_core(
                turned.at[:, pl.ds(0, rows)],
                turned.at[:, pl.ds(rows, rows)],
                pair_send.at[2 * w + 1],
                pair_recv.at[2 * w + 1],
            )
        )

    def multiply(w, t, first, second):
        kind, count, width, deep, halves, parted = plan[w]
        if t == 0:
            near, far, turned = pairs[w]
            near.wait()
            far.wait_recv()
            turned.wait_recv()

        def each(z, carried):
            left = turned_refs[w][pl.ds(pl.multiple_of(z * deep, 16), deep), :]
            if kind == "rows":
                last = min((t + 1) * width, whole_refs[w].shape[1])
                part = jnp.dot(
                    left, whole_refs[w][:, t * width : last], preferred_element_type=jnp.float32
                ).astype(jnp.bfloat16)
                if last < (t + 1) * width:
                    empty = jnp.zeros((deep, (t + 1) * width - last), jnp.bfloat16)
                    part = jnp.concatenate([part, empty], axis=1)
                piece_rows = first.shape[3]
                for s in range(4):
                    first[z, s // 2, s % 2] = part[2 * s * piece_rows : (2 * s + 1) * piece_rows]
                    second[z, s // 2, s % 2] = part[(2 * s + 1) * piece_rows : (2 * s + 2) * piece_rows]
            else:
                part = jnp.dot(
                    left, whole_refs[w][...], preferred_element_type=jnp.float32
                ).astype(jnp.bfloat16)
                for s in range(4):
                    piece = part[:, s * width : (s + 1) * width]
                    first[z, s // 2, s % 2] = piece[:lead_rows]
                    second[z, s // 2, s % 2] = piece[lead_rows:]
            return carried

        lax.fori_loop(0, 4, each, 0)

    return (begin, turn, multiply)


def remote_send(pending):
    def send(source, target, sent, got, partner, start=True):
        copy = pltpu.make_async_remote_copy(
            src_ref=source,
            dst_ref=target,
            send_sem=sent,
            recv_sem=got,
            device_id=partner,
            device_id_type=pl.DeviceIdType.MESH,
        )
        if start:
            copy.start()
            pending.append(copy)
        return copy

    return send


def product_kernel(plan, lead_rows, *refs):
    groups, places = early_places(plan)
    weights, outs = (len(plan), 4 * len(groups))
    left_refs, refs = (refs[:weights], refs[weights:])
    right_refs = []
    for entry in plan:
        held = 2 if entry[5] else 1
        right_refs.append(refs[:held] if held == 2 else refs[0])
        refs = refs[held:]
    out_refs = refs[:outs]
    scratch = list(refs[outs:])
    turned_refs = [scratch.pop(0) for weight in plan]
    whole_refs = [scratch.pop(0) for weight in plan]
    chunks = [(w, t) for w, entry in enumerate(plan) for t in range(entry[1])]
    held = [(scratch.pop(0), scratch.pop(0)) for chunk in chunks]
    pair_send, pair_recv, near_sem, store_sem = scratch
    own_ctx = lax.axis_index("ctx")
    core, chip = (own_ctx % 2, own_ctx // 2)
    own_x, own_y = (chip % 2, chip // 2)
    to_core = {"ctx": toggled(own_ctx, 1)}
    barrier = pltpu.get_barrier_semaphore()
    pl.semaphore_signal(barrier, inc=1, device_id=to_core, device_id_type=pl.DeviceIdType.MESH)
    pl.semaphore_wait(barrier, 1)
    pending = []
    send = remote_send(pending)
    begin, turn, multiply = pair_steps(
        plan,
        lead_rows,
        left_refs,
        right_refs,
        turned_refs,
        whole_refs,
        (pair_send, pair_recv, near_sem),
        core,
        pending,
        send,
    )
    for w in range(weights):
        begin(w)
        turn(w)
    stores = []
    for number, (w, t) in enumerate(chunks):
        first, second = held[number]
        multiply(w, t, first, second)
        group, offset = places[number]
        sides = (
            lambda at: first.at[:, at, own_x],
            lambda at: first.at[:, at, 1 - own_x],
            lambda at: second.at[:, own_y, at],
            lambda at: second.at[:, 1 - own_y, at],
        )
        for side, source_at in enumerate(sides):
            for at in (0, 1):
                copy = pltpu.make_async_copy(
                    source_at(at),
                    out_refs[4 * group + side].at[at, :, :, pl.ds(offset, plan[w][2])],
                    store_sem.at[8 * number + 2 * side + at],
                )
                copy.start()
                stores.append(copy)
    for copy in stores:
        copy.wait()
    for copy in pending:
        copy.wait_send()


def weight_plan(kind, left, right, count):
    deep = left.shape[1] // 4
    if kind == "rows":
        parted = isinstance(right, tuple)
        span = right[0].shape[1] if parted else right.shape[1] // 2
        width = -(-span // (128 * count)) * 128
        return (kind, count, width, deep, (deep // 8, deep // 8), span if parted else 0)
    lead_rows = deep // 2 // 16 * 16
    return (kind, count, right.shape[-1] // 8, deep, (lead_rows, deep - lead_rows), 0)


def early_places(plan):
    groups, places = ([], [])
    for kind, count, width, deep, halves, parted in plan:
        found = [at for at, group in enumerate(groups) if group[0] == halves]
        if not found:
            groups.append([halves, 0])
            found = [len(groups) - 1]
        for chunk in range(count):
            places.append((found[0], groups[found[0]][1]))
            groups[found[0]][1] += width
    return (groups, places)


def plan_span(entry):
    return entry[1] * entry[2] if entry[0] == "rows" else 4 * entry[2]


def plan_lead(plan):
    return max([0] + [entry[4][0] for entry in plan if entry[0] == "columns"])


def pair_scratch(plan, tokens):
    turned = [pltpu.VMEM((4 * entry[3], 2 * tokens), jnp.bfloat16) for entry in plan]
    return turned + [
        pltpu.VMEM((2 * tokens, entry[5] or plan_span(entry)), jnp.bfloat16) for entry in plan
    ]


def early_sums(products, held):
    plan = [weight_plan(*product) for product in products]
    lefts, rights = ([product[1] for product in products], [product[2] for product in products])
    vmem, anywhere, dma = (
        pl.BlockSpec(memory_space=pltpu.VMEM),
        pl.BlockSpec(memory_space=pl.ANY),
        pltpu.SemaphoreType.DMA,
    )
    rights = [part for right in rights for part in (right if isinstance(right, tuple) else [right])]
    groups = early_places(plan)[0]
    outs, units = ([], [])
    for halves, columns in groups:
        for half in halves:
            outs += [jax.ShapeDtypeStruct((2, 4, half, columns), jnp.bfloat16)] * 2
    for kind, count, width, deep, halves, parted in plan:
        for chunk in range(count):
            units += [pltpu.VMEM((4, 2, 2, half, width), jnp.bfloat16) for half in halves]
    chunk_count = sum(entry[1] for entry in plan)
    scratch = pair_scratch(plan, lefts[0].shape[0]) + units
    scratch += [dma((2 * len(plan),)), dma((2 * len(plan),)), dma((len(plan),)), dma((8 * chunk_count,))]
    sides = pl.pallas_call(
        functools.partial(product_kernel, plan, plan_lead(plan)),
        out_shape=tuple(outs),
        in_specs=[vmem] * len(plan) + [anywhere] * len(rights),
        out_specs=(anywhere,) * len(outs),
        scratch_shapes=scratch,
        compiler_params=pltpu.CompilerParams(
            collective_id=3, has_side_effects=True, vmem_limit_bytes=60 * 1024 * 1024
        ),
        name="early_products",
    )(*lefts, *rights)
    held, sides = lax.optimization_barrier((held, sides))
    arrays = []
    for group in range(len(groups)):
        for part, bit in ((0, 2), (2, 4)):
            kept, sent = sides[4 * group + part : 4 * group + part + 2]
            arrays.append((kept, swap(sent, "ctx", bit)))
    return (held, (plan, arrays))


def second_step(held, early):
    plan, arrays = early
    held, arrays = lax.optimization_barrier((held, arrays))
    chip = lax.axis_index("ctx") // 2
    flat = []
    for at, (kept, arrived) in sorted(enumerate(arrays), key=lambda pair: (-(pair[0] // 2), pair[0])):
        bit, own = ((4, chip // 2), (2, chip % 2))[at % 2]
        other = [
            lax.dynamic_index_in_dim(side, 1 - own, 0, keepdims=False).astype(jnp.float32)
            for side in (kept, arrived)
        ]
        twice = swap((other[0] + other[1]).astype(jnp.bfloat16), "ctx", bit)
        flat.append((at, [kept, arrived, twice]))
    flat = [side for at, sides in sorted(flat, key=lambda pair: pair[0]) for side in sides]
    return (held, (plan, flat))


def sum_kernel(early, late, lead_rows, *refs):
    weights, products = (len(early) + len(late), len(late))
    left_refs, right_refs = (refs[:products], refs[products : 2 * products])
    refs = refs[2 * products :]
    groups, places = early_places(early)
    early_refs, refs = (refs[: 6 * len(groups)], refs[6 * len(groups) :])
    small_ref, out_refs, small_out = (refs[0], refs[1 : weights + 1], refs[weights + 1])
    scratch = list(refs[weights + 2 :])
    turned_refs = [scratch.pop(0) for weight in late]
    whole_refs = [scratch.pop(0) for weight in late]
    plan = early + late
    chunks = [(w, t) for w, entry in enumerate(plan) for t in range(entry[1])]
    early_count = sum(entry[1] for entry in early)
    order = sorted(range(early_count), key=lambda number: (-chunks[number][0], number))
    units = {}
    for number in range(len(chunks)):
        for half in (0, 1):
            units[number, half] = [scratch.pop(0) for stage in range(5)]
    small_held = scratch.pop(0)
    send_sem, recv_sem, local_sem, load_sem, pair_send, pair_recv, small_send, small_recv, near_sem = scratch
    own_ctx, own_shard = (lax.axis_index("ctx"), lax.axis_index("fsdp"))
    core, chip = (own_ctx % 2, own_ctx // 2)
    own_x, own_y = (chip % 2, chip // 2)
    low_bit, high_bit = (own_shard % 2, own_shard // 2)
    loads = {}
    for number in order:
        w, (group, offset) = (chunks[number][0], places[number])
        for half in (0, 1):
            own = own_y if half == 0 else own_x
            kept, arrived, twice = early_refs[6 * group + 3 * half : 6 * group + 3 * half + 3]
            columns = pl.ds(offset, plan[w][2])
            sources = (kept.at[own, :, :, columns], arrived.at[own, :, :, columns], twice.at[:, :, columns])
            for at, source in enumerate(sources):
                slot = (number * 2 + half) * 3 + at
                copy = pltpu.make_async_copy(source, units[number, half][at], load_sem.at[slot])
                copy.start()
                loads[number, half, at] = copy
    partners = [{"ctx": toggled(own_ctx, bit)} for bit in (1, 2, 4)]
    partners += [{"fsdp": toggled(own_shard, bit)} for bit in (1, 2)]
    barrier = pltpu.get_barrier_semaphore()
    for partner in partners:
        pl.semaphore_signal(
            barrier, inc=1, device_id=partner, device_id_type=pl.DeviceIdType.MESH
        )
    pl.semaphore_wait(barrier, len(partners))
    to_core, to_x, to_y, to_one, to_two = partners
    pending = []
    send = remote_send(pending)
    begin, turn, multiply = pair_steps(
        late,
        lead_rows,
        left_refs,
        right_refs,
        turned_refs,
        whole_refs,
        (pair_send, pair_recv, near_sem),
        core,
        pending,
        send,
    )
    for w in range(len(late)):
        begin(w)
    copies = {}

    def hop(number, half, stage, source, target, partner):
        slot = (number * 2 + half) * 8 + stage
        copies[number, half, stage] = send(
            source, target, send_sem.at[slot], recv_sem.at[slot], partner
        )

    def stage_one(number):
        w, t = chunks[number]
        multiply(w - len(early), t, units[number, 0][0], units[number, 1][0])
        hop(number, 0, 0, units[number, 0][0].at[:, :, 1 - own_x], units[number, 0][1], to_x)
        hop(number, 1, 0, units[number, 1][0].at[:, 1 - own_y], units[number, 1][1], to_y)

    def add(target, source_at, count):
        def each(i, carried):
            target[i] = (
                target[i].astype(jnp.float32) + source_at(i).astype(jnp.float32)
            ).astype(jnp.bfloat16)
            return carried

        lax.fori_loop(0, count, each, 0)

    def stage_two(number):
        held, got = (units[number, 0][0], units[number, 0][1])
        copies[number, 0, 0].wait_recv()
        add(got, lambda z: held[z, :, own_x], 4)
        held_b, got_b = (units[number, 1][0], units[number, 1][1])
        copies[number, 1, 0].wait_recv()
        add(got_b, lambda z: held_b[z, own_y], 4)
        hop(number, 0, 1, got.at[:, 1 - own_y], units[number, 0][2], to_y)
        hop(number, 1, 1, got_b.at[:, 1 - own_x], units[number, 1][2], to_x)

    def stage_three(number):
        for half in (0, 1):
            kept, held, got = units[number, half][:3]
            own = own_y if half == 0 else own_x
            if number < early_count:
                for at in range(3):
                    loads[number, half, at].wait()
                add(held, lambda z: kept[z], 4)
                add(got, lambda z: held[z], 4)
            else:
                copies[number, half, 1].wait_recv()
                add(got, lambda z: held[z, own], 4)
        for half in (0, 1):
            got = units[number, half][2]
            for high in (0, 1):
                hop(
                    number,
                    half,
                    2 + 4 * high,
                    got.at[2 * high + 1 - low_bit],
                    units[number, half][3].at[high],
                    to_one,
                )

    def stage_four(number):
        for half in (0, 1):
            held, got = (units[number, half][2], units[number, half][3])
            copies[number, half, 2].wait_recv()
            copies[number, half, 6].wait_recv()
            add(got, lambda high: held[2 * high + low_bit], 2)
        for half in (0, 1):
            got = units[number, half][3]
            hop(number, half, 3, got.at[1 - high_bit], units[number, half][4].at[0], to_two)

    def final_region(number, half, chip_at):
        w, t = chunks[number]
        kind, count, width = plan[w][:3]
        deep = units[number, half][4].shape[1]
        if kind == "rows":
            start = pl.multiple_of((2 * chip_at + half) * deep, deep)
            column = pl.multiple_of((core * count + t) * width, width)
            return out_refs[w].at[pl.ds(start, deep), pl.ds(column, width)]
        column = pl.multiple_of((core * 4 + chip_at) * width, width)
        return out_refs[w].at[pl.ds(half * lead_rows, deep), pl.ds(column, width)]

    local = {}

    def stage_five(number):
        for half in (0, 1):
            held, got = (units[number, half][3], units[number, half][4])
            copies[number, half, 3].wait_recv()
            add(got, lambda i: held[high_bit], 1)
        for half in (0, 1):
            got = units[number, half][4].at[0]
            target = final_region(number, half, chip)
            hop(number, half, 4, got, target, to_x if half == 0 else to_y)
            hop(number, half, 5, got, target, to_y if half == 0 else to_x)
            copy = pltpu.make_async_copy(got, target, local_sem.at[number * 2 + half])
            copy.start()
            local[number, half] = copy

    def stage_six(number):
        for half in (0, 1):
            copies[number, half, 4].wait_recv()
            piece = final_region(number, half, toggled(chip, 1 if half == 0 else 2))
            hop(number, half, 7, piece, piece, to_y if half == 0 else to_x)

    def stage_seven(number):
        w, t = chunks[number]
        kind, count, width = plan[w][:3]
        for half in (0, 1):
            copies[number, half, 5].wait_recv()
            copies[number, half, 7].wait_recv()
            local[number, half].wait()
        span = width if kind == "rows" else 4 * width
        at = core * count + t if kind == "rows" else core
        piece = out_refs[w].at[:, pl.ds(pl.multiple_of(at * span, span), span)]
        slot = len(chunks) * 16 + number
        copies[number, 2, 0] = send(
            piece, piece, send_sem.at[slot], recv_sem.at[slot], to_core
        )

    small_copies = []

    def small_step(step):
        if step > 0:
            small_copies[step - 1].wait_recv()
            small_held[2 * step] = small_held[2 * step - 2] + small_held[2 * step - 1]
            if step == 3:
                small_out[0] = small_held[6]
        else:
            small_held[0] = small_ref[...]
        if step < 5:
            small_copies.append(
                send(
                    small_held.at[2 * step],
                    small_held.at[2 * step + 1],
                    small_send.at[step],
                    small_recv.at[step],
                    partners[step],
                )
            )
        else:
            small_out[1] = small_held[10]

    stages = (stage_one, stage_two, stage_three, stage_four, stage_five, stage_six, stage_seven)
    small_at = 0
    stage_three(order[0])
    for w in range(len(late)):
        turn(w)
    for tick in range(len(chunks) + len(stages)):
        for lag, stage in enumerate(stages):
            for number in range(len(chunks)):
                if number >= early_count:
                    due = number - early_count + lag == tick
                else:
                    rank = order.index(number)
                    due = rank - 2 + lag == tick and lag >= 2 and rank + lag > 2
                if due:
                    stage(number)
        if small_at < 6:
            small_step(small_at)
            small_at += 1
    for number in range(len(chunks)):
        copies[number, 2, 0].wait_recv()
    for copy in pending:
        copy.wait_send()


def sum_weights(early, early_arrays, products, small):
    late = [weight_plan(*product) for product in products]
    lefts, rights = ([product[1] for product in products], [product[2] for product in products])
    plan = early + late
    pieces = []
    for w, (kind, count, width, deep, halves, parted) in enumerate(plan):
        leads = [(4, 2, 2), (4, 2), (4,), (2,), (1,)]
        if w < len(early):
            leads[:2] = [(4,), (4,)]
        for chunk in range(count):
            for half in halves:
                pieces += [pltpu.VMEM(lead + (half, width), jnp.bfloat16) for lead in leads]
    outs = [jax.ShapeDtypeStruct((entry[3], 2 * plan_span(entry)), jnp.bfloat16) for entry in plan]
    chunk_count = sum(entry[1] for entry in plan)
    scratch = pair_scratch(late, lefts[0].shape[0]) + pieces
    dma = pltpu.SemaphoreType.DMA
    scratch += [pltpu.VMEM((11,) + small.shape, jnp.float32)]
    slots = chunk_count * 17
    scratch += [dma((slots,)), dma((slots,)), dma((2 * chunk_count,)), dma((6 * chunk_count,))]
    scratch += [dma((2 * len(late),)), dma((2 * len(late),)), dma((5,)), dma((5,)), dma((len(late),))]
    vmem, anywhere = (
        pl.BlockSpec(memory_space=pltpu.VMEM),
        pl.BlockSpec(memory_space=pl.ANY),
    )
    return pl.pallas_call(
        functools.partial(sum_kernel, early, late, plan_lead(plan)),
        out_shape=tuple(outs) + (jax.ShapeDtypeStruct((2,) + small.shape, jnp.float32),),
        in_specs=[vmem] * len(late) + [anywhere] * (len(late) + len(early_arrays)) + [vmem],
        out_specs=(anywhere,) * len(plan) + (vmem,),
        scratch_shapes=scratch,
        compiler_params=pltpu.CompilerParams(
            collective_id=1, has_side_effects=True, vmem_limit_bytes=60 * 1024 * 1024
        ),
        name="sum_weights",
    )(*lefts, *rights, *early_arrays, small)


def layer_norm(rows_in, gain_vec):
    row_mean = jnp.mean(rows_in, axis=-1, keepdims=True)
    centred = rows_in - row_mean
    variance = jnp.mean(centred * centred, axis=-1, keepdims=True)
    return centred * lax.rsqrt(variance + norm_eps) * gain_vec


def rotate(projected, cosine, sine):
    row_count, width = projected.shape
    half_width = HEAD_WIDTH // 2
    by_head = projected.reshape(row_count, width // HEAD_WIDTH, HEAD_WIDTH)
    turned = jnp.concatenate([by_head[..., half_width:], by_head[..., :half_width]], axis=-1)
    return (by_head * cosine[:, None, :] - turned * sine[:, None, :]).reshape(row_count, width)


def swap(value, axis, bit):
    pairs = [(i, i ^ bit) for i in range(lax.axis_size(axis))]
    return lax.ppermute(value, axis, pairs)


def bit_of(axis, bit):
    return (lax.axis_index(axis) // bit) % 2 == 1


def bits_below(count):
    return [1 << i for i in range(count.bit_length() - 1)]


def reduce_pieces(pieces, labels, order):
    labels = list(labels)
    for axis, bit in order:
        at = labels.index((axis, bit))
        labels.pop(at)
        first = lax.index_in_dim(pieces, 0, at, keepdims=False)
        second = lax.index_in_dim(pieces, 1, at, keepdims=False)
        upper = bit_of(axis, bit)
        arrived = swap(jnp.where(upper, first, second), axis, bit)
        kept = jnp.where(upper, second, first)
        pieces = (kept.astype(jnp.float32) + arrived.astype(jnp.float32)).astype(jnp.bfloat16)
    return pieces


def gather_pieces(piece, labels, order):
    held = []
    for axis, bit in reversed(order):
        arrived = swap(piece, axis, bit)
        upper = bit_of(axis, bit)
        held = [label for label in labels if label in held or label == (axis, bit)]
        piece = jnp.stack(
            [jnp.where(upper, arrived, piece), jnp.where(upper, piece, arrived)],
            axis=held.index((axis, bit)),
        )
    return piece


def keep_and_send(first, second):
    upper = bit_of("ctx", 1)
    return (jnp.where(upper, second, first), jnp.where(upper, first, second))


def core_product(left, first, second):
    kept, sent = keep_and_send(first, second)
    left_all = jnp.concatenate([left, swap(left, "ctx", 1)], axis=0)
    right_all = jnp.concatenate([kept, swap(sent, "ctx", 1)], axis=0)
    return lax.dot_general(
        left_all, right_all, (((0,), (0,)), ((), ())), preferred_element_type=jnp.float32
    ).astype(jnp.bfloat16)


def shard_sum(product, by_columns):
    shards = lax.axis_size("fsdp")
    slices = lax.axis_size("ctx") // 2
    rows, columns = product.shape
    shard_labels = [("fsdp", bit) for bit in reversed(bits_below(shards))]
    slice_labels = [("ctx", 2 * bit) for bit in reversed(bits_below(slices))]
    if by_columns:
        cut = product.reshape(shards, rows // shards, slices, columns // slices)
        cut = jnp.transpose(cut, (0, 2, 1, 3))
    else:
        cut = product.reshape(shards, slices, rows // shards // slices, columns)
    parts = []
    half = cut.shape[2] // 2
    tail = list(reversed(shard_labels))
    for lead, orders in (
        (cut[:, :, :half], list(reversed(slice_labels))),
        (cut[:, :, half:], slice_labels),
    ):
        pieces = lead.reshape((2,) * (len(shard_labels) + len(slice_labels)) + lead.shape[2:])
        piece = reduce_pieces(pieces, shard_labels + slice_labels, orders + tail)
        whole = gather_pieces(piece, slice_labels, orders)
        parts.append(whole.reshape((slices,) + piece.shape))
    both = jnp.concatenate(parts, axis=1)
    if by_columns:
        return jnp.transpose(both, (1, 0, 2)).reshape(rows // shards, columns)
    return both.reshape(rows // shards, columns)


def join_cores(own):
    other = swap(own, "ctx", 1)
    upper = bit_of("ctx", 1)
    return jnp.concatenate(
        [jnp.where(upper, other, own), jnp.where(upper, own, other)], axis=1
    ).astype(jnp.float32)


def sum_over(value, axes):
    for axis in axes:
        for bit in bits_below(lax.axis_size(axis)):
            value = value + swap(value, axis, bit)
    return value


def own_shard(vector):
    width = vector.shape[0] // lax.axis_size("fsdp")
    return lax.dynamic_slice_in_dim(vector, lax.axis_index("fsdp") * width, width, 0)


def weight_sums(
    hidden,
    grad_mlp_low,
    act_mlp,
    grad_leading,
    grad_trailing,
    act_attn,
    grad_projected,
    attn_low,
    grad_attn_low,
    small,
    early,
):
    shards, ctx_count = (lax.axis_size("fsdp"), lax.axis_size("ctx"))
    rows, ff_width = hidden.shape
    model_width = act_mlp.shape[1]
    if early is None:
        half, half_three = (model_width // 2, 3 * model_width // 2)
        pairs = (
            (hidden, grad_mlp_low[:, :half], grad_mlp_low[:, half:]),
            (act_mlp, grad_leading, grad_trailing),
            (act_attn, grad_projected[:, :half_three], grad_projected[:, half_three:]),
            (attn_low, grad_attn_low[:, :half], grad_attn_low[:, half:]),
        )
        totals = [
            join_cores(shard_sum(core_product(*pair), at == 0)) for at, pair in enumerate(pairs)
        ]
        over_pack = sum_over(small, ("ctx",))
        return totals + [jnp.stack([over_pack, sum_over(over_pack, ("fsdp",))])]
    total_attn, total_in, total_out, total_qkv, small_sums = sum_weights(
        *early, [("rows", act_attn, grad_projected, 4)], small
    )
    padded = total_in.shape[1] // 2
    total_in = jnp.concatenate(
        [total_in[:, :ff_width], total_in[:, padded : padded + ff_width]], axis=1
    )
    return [
        total.astype(jnp.float32) for total in (total_out, total_in, total_qkv, total_attn)
    ] + [small_sums]


def weight_sums_early(
    hidden, grad_mlp_low, act_mlp, grad_leading, grad_trailing, attn_low, grad_attn_low, held
):
    shards, ctx_count = (lax.axis_size("fsdp"), lax.axis_size("ctx"))
    ff_width = hidden.shape[1]
    if shards != 4 or ctx_count != 8 or act_mlp.shape[1] % 1024 != 0 or ff_width % 64 != 0:
        return (held, None)
    return early_sums(
        [
            ("rows", attn_low, grad_attn_low, 1),
            ("rows", act_mlp, (grad_leading, grad_trailing), 3),
            ("columns", hidden, grad_mlp_low, 1),
        ],
        held,
    )


def per_device(
    inputs,
    cotangent,
    lengths,
    piece_route,
    gain_one,
    qkv_weight,
    attn_out,
    gain_two,
    geglu_in,
    geglu_out,
):
    ctx_count = lax.axis_size("ctx")
    own_index = lax.axis_index("ctx")
    row_count = inputs.shape[1]
    model_width = inputs.shape[2]
    piece_rows = row_count // ctx_count
    tokens = row_count * ctx_count
    own_heads = model_width // HEAD_WIDTH // ctx_count
    own_width = own_heads * HEAD_WIDTH
    block_q = math.gcd(tokens, 384)
    block_k = math.gcd(tokens, 512)
    lengths_row = lengths[0]
    own_route = piece_route[0, 0]
    slot_ids = jnp.arange(ctx_count, dtype=jnp.int32)
    outgoing = jnp.sum(
        slot_ids[None, :] * (own_route[None, :] == slot_ids[:, None]).astype(jnp.int32), axis=1
    )

    def exchange(blocks):
        return lax.all_to_all(blocks, "ctx", split_axis=0, concat_axis=0, tiled=True)

    def to_slots(rows_in):
        return jnp.take(rows_in.reshape(ctx_count, piece_rows, model_width), outgoing, axis=0)

    def to_heads(rows_in):
        by_heads = rows_in.reshape(row_count, ctx_count, -1)
        return exchange(jnp.transpose(by_heads, (1, 0, 2))).reshape(tokens, -1)

    def to_rows(heads_in):
        return exchange(heads_in.reshape(ctx_count, row_count, -1))

    both_arrived = exchange(
        jnp.concatenate([to_slots(inputs[0]), to_slots(cotangent[0])], axis=1)
    )
    arrived, grad_arrived = (both_arrived[:, :piece_rows], both_arrived[:, piece_rows:])
    residual = arrived.reshape(row_count, model_width).astype(jnp.float32)
    places = own_index * row_count + jnp.arange(row_count, dtype=jnp.int32)
    unused_begin, unused_end, offset, is_valid = spans(places, lengths_row)
    pack_begin, pack_end, unused_offset, unused_valid = spans(
        jnp.arange(tokens, dtype=jnp.int32), lengths_row
    )
    grad_final = jnp.where(
        is_valid[:, None], grad_arrived.reshape(row_count, model_width).astype(jnp.float32), 0.0
    )
    gains = jnp.pad(jnp.stack([gain_one, gain_two]), ((0, 14), (0, 0)))
    gains_full, qkv_full = gather_weights([gains, qkv_weight])
    gains_full = gains_full.reshape(-1, 16, gains.shape[1])
    gain_attn = gains_full[:, 0].reshape(-1).astype(jnp.float32)
    gain_mlp = gains_full[:, 1].reshape(-1).astype(jnp.float32)
    act_attn = layer_norm(residual, gain_attn).astype(jnp.bfloat16)
    later = [attn_out, geglu_in, geglu_out]
    row_cosine, row_sine = rotary_tables(offset, own_heads)
    if lax.axis_size("fsdp") == 4 and ctx_count == 8 and own_width == 128:
        attn_full, in_full, out_full, qkv_heads = gather_weights(
            later, (act_attn, qkv_full, row_cosine, row_sine)
        )
    else:
        attn_full, in_full, out_full = gather_weights(later)
        projected = jnp.dot(act_attn, qkv_full, preferred_element_type=jnp.float32)
        cosine, sine = rotary_tables(offset, 1)
        queries, keys = (
            rotate(projected[:, :model_width], cosine, sine).astype(jnp.bfloat16),
            rotate(projected[:, model_width : 2 * model_width], cosine, sine).astype(jnp.bfloat16),
        )
        values = projected[:, 2 * model_width :].astype(jnp.bfloat16)
        joined = jnp.stack(
            [part.reshape(row_count, ctx_count, own_width) for part in (queries, keys, values)], axis=2
        )
        qkv_heads = to_heads(joined.reshape(row_count, -1))
    low, high = key_range(pack_begin, pack_end, block_q, block_k)
    pack_begin, pack_end = (pack_begin[None, :], pack_end[None, :])
    attended_heads, attended_low, log_total = attention_forward(
        qkv_heads, pack_begin, pack_end, low, high, own_heads, block_q, block_k
    )
    attn_low = jnp.transpose(to_rows(attended_low), (1, 0, 2)).reshape(
        row_count, model_width
    )
    branch_attn = jnp.dot(attn_low, attn_full, preferred_element_type=jnp.float32)
    middle = residual + branch_attn
    act_mlp = layer_norm(middle, gain_mlp).astype(jnp.bfloat16)
    up_both = jnp.dot(act_mlp, in_full, preferred_element_type=jnp.float32)
    ff_width = up_both.shape[1] // 2
    hidden = (jax.nn.gelu(up_both[:, :ff_width], approximate=False) * up_both[:, ff_width:]).astype(
        jnp.bfloat16
    )
    branch_mlp = jnp.dot(hidden, out_full, preferred_element_type=jnp.float32)
    final_rows = jnp.where(is_valid[:, None], middle + branch_mlp, 0.0)
    square_sums = jnp.stack(
        [
            jnp.sum(final_rows * final_rows),
            jnp.sum(jnp.where(is_valid[:, None], branch_attn * branch_attn, 0.0)),
            jnp.sum(jnp.where(is_valid[:, None], branch_mlp * branch_mlp, 0.0)),
        ]
    )
    out_slots = final_rows.astype(jnp.bfloat16).reshape(ctx_count, piece_rows, model_width)
    grad_mlp_low = grad_final.astype(jnp.bfloat16)
    grad_hidden = lax.dot_general(
        grad_mlp_low, out_full, NT, preferred_element_type=jnp.float32
    )

    def gated(leading, trailing):
        return jax.nn.gelu(leading, approximate=False) * trailing

    unused_gate, gate_back = jax.vjp(gated, up_both[:, :ff_width], up_both[:, ff_width:])
    grad_leading, grad_trailing = gate_back(grad_hidden)
    grad_leading, grad_trailing = (
        grad_leading.astype(jnp.bfloat16),
        grad_trailing.astype(jnp.bfloat16),
    )
    grad_up = jnp.concatenate([grad_leading, grad_trailing], axis=1)
    grad_act_mlp = lax.dot_general(grad_up, in_full, NT, preferred_element_type=jnp.float32)
    unused_norm, norm_back_mlp = jax.vjp(layer_norm, middle, gain_mlp)
    grad_middle_norm, grad_gain_mlp = norm_back_mlp(grad_act_mlp)
    grad_middle = grad_final + grad_middle_norm
    grad_attn_low = grad_middle.astype(jnp.bfloat16)
    grad_attended = lax.dot_general(
        grad_attn_low, attn_full, NT, preferred_element_type=jnp.float32
    ).astype(jnp.bfloat16)
    grad_attended_heads, early = weight_sums_early(
        hidden,
        grad_mlp_low,
        act_mlp,
        grad_leading,
        grad_trailing,
        attn_low,
        grad_attn_low,
        to_heads(grad_attended),
    )
    block_back = math.gcd(tokens, 256)
    low_back, high_back = key_range(pack_begin[0], pack_end[0], block_q, block_back)
    grad_heads = attention_backward(
        qkv_heads,
        attended_heads,
        grad_attended_heads,
        log_total,
        pack_begin,
        pack_end,
        low_back,
        high_back,
        [] if early is None else [early[1][0][0]],
        own_heads,
        block_q,
        block_back,
    )
    if early is not None:
        grad_heads, early = second_step(grad_heads, early)
    grad_rows = to_rows(grad_heads)
    if own_width % 128 == 0:
        grad_projected, grad_act_attn = finish_rows(
            grad_rows, row_cosine, row_sine, qkv_full, own_heads
        )
    else:
        by_part = jnp.transpose(
            grad_rows.reshape(ctx_count, row_count, 3, own_width), (2, 1, 0, 3)
        ).reshape(3, row_count, model_width)
        cosine, sine = rotary_tables(offset, 1)
        grad_projected = jnp.concatenate(
            [
                rotate(by_part[part].astype(jnp.float32), cosine, -sine).astype(jnp.bfloat16)
                for part in (0, 1)
            ]
            + [by_part[2]],
            axis=1,
        )
        grad_act_attn = lax.dot_general(
            grad_projected, qkv_full, NT, preferred_element_type=jnp.float32
        )
    unused_first, norm_back_attn = jax.vjp(layer_norm, residual, gain_attn)
    grad_resid_norm, grad_gain_attn = norm_back_attn(grad_act_attn)
    grad_residual = (grad_middle + grad_resid_norm).astype(jnp.bfloat16)
    grad_slots = grad_residual.reshape(ctx_count, piece_rows, model_width)
    back = exchange(jnp.concatenate([out_slots, grad_slots], axis=1))
    block_out, grad_inputs = (
        jnp.take(half, own_route, axis=0).reshape(1, row_count, model_width)
        for half in (back[:, :piece_rows], back[:, piece_rows:])
    )
    small = jnp.stack(
        [grad_gain_attn, grad_gain_mlp, jnp.pad(square_sums, (0, model_width - 3))]
        + [jnp.zeros((model_width,), jnp.float32)] * 5
    )
    total_out, total_in, total_qkv, total_attn, small_sums = weight_sums(
        hidden,
        grad_mlp_low,
        act_mlp,
        grad_leading,
        grad_trailing,
        act_attn,
        grad_projected,
        attn_low,
        grad_attn_low,
        small,
        early,
    )
    total_gain_one = own_shard(small_sums[1, 0])
    total_gain_two = own_shard(small_sums[1, 1])
    total_squares = small_sums[0, 2, :3]
    valid_count = jnp.sum(lengths_row).astype(jnp.float32)
    rms_stats = jnp.sqrt(total_squares / (valid_count * model_width))[None, :]
    return (
        block_out,
        grad_inputs,
        total_gain_one,
        total_qkv,
        total_attn,
        total_gain_two,
        total_in,
        total_out,
        rms_stats,
    )


def solution(mesh):
    placed = (
        P("fsdp", "ctx", None),
        P("fsdp", "ctx", None),
        P("fsdp", None),
        P("fsdp", "ctx", None),
        P("fsdp"),
        P("fsdp", None),
        P("fsdp", None),
        P("fsdp"),
        P("fsdp", None),
        P("fsdp", None),
    )
    return jax.shard_map(
        per_device,
        mesh=mesh,
        in_specs=placed,
        out_specs=(
            P("fsdp", "ctx", None),
            P("fsdp", "ctx", None),
            P("fsdp"),
            P("fsdp", None),
            P("fsdp", None),
            P("fsdp"),
            P("fsdp", None),
            P("fsdp", None),
            P("fsdp", None),
        ),
        check_vma=False,
    )
```
